32 devices in a mesh: shard: 2 (over core), rep: 16 (over z, y, x).
Axes of the slice: x: 2, y: 2, z: 4, core: 2. Of those that a mesh axis runs over, the one named last changes fastest.
Arguments:
- noisy_patches: bfloat16 [128, 4096], P(('shard', 'rep')), may hold values from -6 to 6
- targets: float32 [128, 4096], P(('shard', 'rep')), may hold values from -6 to 6
- timesteps: int32 [128], P(('shard', 'rep')), may hold values from 0 to 999
- labels: int32 [128], P(('shard', 'rep')), may hold values from 0 to 999
- master_big: float32 [768, 16384], P(None, 'shard'), may hold values from -0.57735027 to 0.57735027
- moment_big: float32 [768, 16384], P(None, 'shard'), may hold values from -0.00021362305 to 0.00021362305
- error_big: float32 [16, 768, 16384], P('rep', None, 'shard'), may hold values from -5.340576e-05 to 5.340576e-05
- factor_right: float32 [16384, 8], P('shard'), may hold values from -6 to 6
- master_small: float32 [768, 1032], replicated, may hold values from -4 to 4
- moment_small: float32 [768, 1032], replicated, may hold values from -0.0017089844 to 0.0017089844
- biases: float32 [14608], replicated, may hold values from -1.25 to 1.25
- moment_bias: float32 [14608], replicated, may hold values from -0.0017089844 to 0.0017089844
- step_rates: float32 [2], replicated, may hold values from 362.03867 to 724.07733
Outputs:
- total_loss: float32 [], replicated
- new_master_big: float32 [768, 16384], P(None, 'shard')
- new_moment_big: float32 [768, 16384], P(None, 'shard')
- new_error_big: float32 [16, 768, 16384], P('rep', None, 'shard')
- new_factor_right: float32 [16384, 8], P('shard')
- new_master_small: float32 [768, 1032], replicated
- new_moment_small: float32 [768, 1032], replicated
- new_biases: float32 [14608], replicated
- new_moment_bias: float32 [14608], replicated
The draws below stay inside these ranges and needn't reach their ends.
All inputs are finite; a program needn't handle non-finite values.
Results may differ from the reference program's by a relative error of at most 0.011.
The reference program's roundings to bfloat16 on the way count: a program that leaves them out, or rounds other values in their place, can miss the bound.
Values may be sent and summed in bfloat16 or wider, within the bound.
A program may use at most 384 MiB of HBM per device.

```python
import math
import jax
import jax.numpy as jnp
from jax import lax

D = 768
HEADS = 12
HEAD_DIM = 64
FF = 3072
GRID = 16
FREQ = 256
NCLASS = 1000
P_DIM = 16
RANK = 8
IMG_DEV = 4
SEQ = 256
REPLICAS = 16
IMAGES = 128
TOKENS = 32768
WCOLS = 16384
WIDTH = 8192
SCOLS = 1032
BCOLS = 14608
N_SHARD = 2
N_REP = 16


def draw_master_big(key, part):
    column = jnp.arange(WCOLS, dtype=jnp.int32)
    scales = jnp.full((WCOLS,), D ** (-0.5), jnp.float32)
    scales = jnp.where((column >= 3 * D) & (column < 4 * D), 4.0 * D ** (-0.5), scales)
    scales = jnp.where((column >= 4 * D + FF) & (column < 4 * D + 2 * FF), FF ** (-0.5), scales)
    scales = jnp.where(column >= 13 * D + 2 * FF, FREQ ** (-0.5), scales)
    values = jax.random.truncated_normal(key, -4.0, 4.0, (D, WCOLS), jnp.float32)
    return values * scales[None, :]


def draw_master_small(key, part):
    column = jnp.arange(SCOLS, dtype=jnp.int32)
    scales = jnp.full((SCOLS,), D ** (-0.5), jnp.float32)
    scales = jnp.where(column < P_DIM + NCLASS, 1.0, scales)
    scales = jnp.where(column < P_DIM, P_DIM ** (-0.5), scales)
    values = jax.random.truncated_normal(key, -4.0, 4.0, (D, SCOLS), jnp.float32)
    return values * scales[None, :]


def touch_ends(entries, key, least, top_value):
    longest = entries.shape.index(max(entries.shape))
    spots = []
    for shift in (0, 1):
        where = [jax.random.randint(jax.random.fold_in(key, axis), (), 0, length) for axis, length in enumerate(entries.shape)]
        where[longest] = (where[longest] + shift) % entries.shape[longest]
        spots.append(tuple(where))
    return entries.at[spots[0]].set(least).at[spots[1]].set(top_value)


def levels(own_key, shape, cuts, least, high):
    def one(dim, shards_of):
        draws = jax.random.uniform(jax.random.fold_in(jax.random.fold_in(own_key, 6), dim), (shards_of,), jnp.float32, least / len(cuts), high / len(cuts))
        return jnp.repeat(jnp.exp(draws), shape[dim] // shards_of).reshape((-1,) + (1,) * (len(shape) - dim - 1))

    level = one(*cuts[0])
    for cut in cuts[1:]:
        level = level * one(*cut)
    return level


def noise(rng, extent, width, reach, cuts=(), kind=jnp.bfloat16):
    array = width * jax.random.normal(rng, extent, jnp.float32)
    if cuts:
        array = array * levels(rng, extent, cuts, -0.22, 0.18)
    return jnp.clip(array, -reach, reach).astype(kind)


def setup_inputs(seed: int = 0) -> dict:
    keys = jax.random.split(jax.random.key(seed), 14)
    noisy_patches = noise(keys[0], (IMAGES, SEQ * P_DIM), 1.0, 6.0, ((0, 32),))
    targets = noise(keys[1], (IMAGES, SEQ * P_DIM), 1.0, 6.0, ((0, 32),), jnp.float32)
    timesteps = touch_ends(jax.random.randint(keys[2], (IMAGES,), 0, 1000), jax.random.fold_in(keys[2], 1), 0, 999).astype(jnp.int32)
    labels = touch_ends(jax.random.randint(keys[3], (IMAGES,), 0, NCLASS), jax.random.fold_in(keys[3], 1), 0, NCLASS - 1).astype(jnp.int32)
    master_big = draw_master_big(jax.random.fold_in(keys[13], 71), 0)
    moment_big = noise(keys[5], (D, WCOLS), (0.006 * TOKENS ** -0.5), 0.00021362305, ((1, 2),), jnp.float32)
    error_big = noise(keys[6], (REPLICAS, D, WCOLS), (0.006 * (TOKENS * REPLICAS) ** -0.5), 5.340576171875e-05, ((0, 16), (2, 2)), jnp.float32)
    factor_right = noise(keys[7], (WCOLS, RANK), 1.0, 6.0, ((0, 2),), jnp.float32)
    master_small = draw_master_small(jax.random.fold_in(keys[13], 71), 0)
    moment_small = noise(keys[9], (D, SCOLS), (0.05 * TOKENS ** -0.5), 0.0017089844, (), jnp.float32)
    biases = noise(keys[10], (BCOLS,), 0.2, 1.25, (), jnp.float32)
    moment_bias = noise(keys[11], (BCOLS,), (0.05 * TOKENS ** -0.5), 0.0017089844, (), jnp.float32)
    step_rates = jnp.clip(jax.random.uniform(keys[12], (2,), jnp.float32, 362.03867, 724.07733), 362.03867, 724.07733)
    return {"noisy_patches": noisy_patches, "targets": targets, "timesteps": timesteps, "labels": labels, "master_big": master_big, "moment_big": moment_big, "error_big": error_big, "factor_right": factor_right, "master_small": master_small, "moment_small": moment_small, "biases": biases, "moment_bias": moment_bias, "step_rates": step_rates}


@jax.custom_vjp
def low(v):
    return lax.optimization_barrier(v.astype(jnp.bfloat16)).astype(jnp.float32)

@jax.custom_vjp
def low_back(v):
    return v

def low_keep(v):
    return (low(v), None)

def low_pass(kept, grad):
    return (grad,)

def back_keep(v):
    return (v, None)

def back_low(kept, grad):
    return (low(grad),)
low.defvjp(low_keep, low_pass)
low_back.defvjp(back_keep, back_low)
highest = lax.Precision.HIGHEST
epsilon = 1e-06
tiny_value = 1e-30
momentum_decay = 0.9

def matmul(left_side, right_side):
    return jnp.dot(left_side, right_side, precision=highest, preferred_element_type=jnp.float32)

def normalize(values):
    center = values - lax.optimization_barrier(jnp.mean(values, axis=-1, keepdims=True))
    return center * lax.rsqrt(lax.optimization_barrier(jnp.mean(center * center, axis=-1, keepdims=True)) + epsilon)

def timestep_features(steps):
    half_count = FREQ // 2
    freqs = jnp.exp(-math.log(10000.0) * jnp.arange(half_count, dtype=jnp.float32) / half_count)
    angles = steps.astype(jnp.float32)[:, None] * freqs[None, :]
    return jnp.concatenate([jnp.cos(angles), jnp.sin(angles)], axis=1)

def position_table():
    quarter = D // 4
    omega = 1.0 / 10000.0 ** (jnp.arange(quarter, dtype=jnp.float32) / quarter)
    cells = jnp.arange(SEQ, dtype=jnp.int32)
    across = (cells % GRID).astype(jnp.float32)[:, None] * omega[None, :]
    downward = (cells // GRID).astype(jnp.float32)[:, None] * omega[None, :]
    return jnp.concatenate([jnp.sin(across), jnp.cos(across), jnp.sin(downward), jnp.cos(downward)], axis=1)

def split_at(matrix, edges):
    return tuple((matrix[..., edges[place]:edges[place + 1]] for place in range(len(edges) - 1)))

def split_big(matrix):
    return split_at(matrix, [0, 3 * D, 4 * D, 4 * D + FF, 4 * D + 2 * FF, 10 * D + 2 * FF, 12 * D + 2 * FF, 13 * D + 2 * FF, 13 * D + 2 * FF + FREQ])

def split_small(matrix):
    return split_at(matrix, [0, P_DIM, P_DIM + NCLASS, 2 * P_DIM + NCLASS])

def split_bias(vector):
    return split_at(vector, [0, D, 2 * D, 3 * D, 3 * D + FF, 4 * D + FF, 10 * D + FF, 12 * D + FF, 13 * D + FF, 14 * D + FF, 15 * D + FF, 15 * D + FF + P_DIM])

def orthonormal(factor):
    columns = []
    for place in range(factor.shape[-1]):
        vector = factor[..., place]
        for earlier in columns:
            vector = vector - lax.optimization_barrier(jnp.sum(earlier * vector, axis=-1, keepdims=True)) * earlier
        vector = vector * lax.rsqrt(lax.optimization_barrier(jnp.sum(vector * vector, axis=-1, keepdims=True)) + tiny_value)
        columns.append(vector)
    return jnp.stack(columns, axis=-1)

def block_loss(params, noisy, target_rows, steps, labels):
    master_big, master_small, biases = params
    attend_weight, output_weight, up_weight, down_weight, modulate_weight, final_weight, embed_second, embed_first = split_big(low(master_big))
    patch_weight, unused_table, head_weight = split_small(low(master_small))
    class_table = split_small(master_small)[1]
    query_bias, value_bias, output_bias, up_bias, down_bias, modulate_bias, final_bias, second_bias, first_bias, patch_bias, head_bias = split_bias(biases)
    images = noisy.shape[0]
    tokens = images * SEQ
    frequency = low(timestep_features(steps))
    embed_pre = low_back(matmul(frequency, embed_first.T) + first_bias)
    embed_hidden = low(jax.nn.silu(embed_pre))
    time_embed = low_back(matmul(embed_hidden, embed_second) + second_bias)
    condition = time_embed + jnp.take(class_table, labels, axis=1).T
    active = low(jax.nn.silu(condition))
    modulation = low_back(matmul(active, modulate_weight) + modulate_bias)
    final_mod = low_back(matmul(active, final_weight) + final_bias)
    patches = low(noisy.reshape(tokens, P_DIM))
    start = low_back(matmul(patches, patch_weight.T) + patch_bias)
    stream_in = start.reshape(images, SEQ, D) + position_table()[None]
    shift_attn, scale_attn, gate_attn, shift_mlp, scale_mlp, gate_mlp = jnp.split(modulation[:, None, :], 6, axis=2)
    shift_final, scale_final = jnp.split(final_mod[:, None, :], 2, axis=2)
    attn_in = low(normalize(stream_in) * (1.0 + scale_attn) + shift_attn).reshape(tokens, D)
    qkv_bias = jnp.concatenate([query_bias, jnp.zeros_like(query_bias), value_bias])
    projected = low(low_back(matmul(attn_in, attend_weight) + qkv_bias))
    queries, key_rows, value_rows = [piece.reshape(images, SEQ, HEADS, HEAD_DIM) for piece in jnp.split(projected, 3, axis=1)]
    scores = low_back(jnp.einsum('nqhd,nkhd->nhqk', queries, key_rows, precision=highest) / math.sqrt(HEAD_DIM))
    shifted = jnp.exp(scores - lax.optimization_barrier(jnp.max(scores, axis=-1, keepdims=True)))
    probs_low = low(shifted / lax.optimization_barrier(jnp.sum(shifted, axis=-1, keepdims=True)))
    mixed_rows = jnp.einsum('nhqk,nkhd->nqhd', probs_low, value_rows, precision=highest).reshape(tokens, D)
    mixed_rows = low(low_back(mixed_rows))
    attended = low_back(matmul(mixed_rows, output_weight) + output_bias).reshape(images, SEQ, D)
    stream_mid = stream_in + gate_attn * attended
    mlp_in = low(normalize(stream_mid) * (1.0 + scale_mlp) + shift_mlp).reshape(tokens, D)
    hidden_pre = low_back(matmul(mlp_in, up_weight) + up_bias)
    hidden = low(jax.nn.gelu(hidden_pre, approximate=True))
    mlp_out = low_back(matmul(hidden, down_weight.T) + down_bias).reshape(images, SEQ, D)
    stream_out = stream_mid + gate_mlp * mlp_out
    final_in = low(normalize(stream_out) * (1.0 + scale_final) + shift_final).reshape(tokens, D)
    output = low_back(matmul(final_in, head_weight) + head_bias)
    error = output - target_rows.reshape(tokens, P_DIM)
    return jnp.sum(error * error) / (IMAGES * SEQ * P_DIM)

def reference(noisy_patches, targets, timesteps, labels, master_big, moment_big, error_big, factor_right, master_small, moment_small, biases, moment_bias, step_rates):
    params = (master_big, master_small, biases)

    def arrange(values):
        shaped = values.reshape((N_SHARD, N_REP, IMG_DEV) + values.shape[1:])
        return jnp.swapaxes(shaped, 0, 1)
    per_replica = (arrange(noisy_patches.astype(jnp.float32)), arrange(targets), arrange(timesteps), arrange(labels))

    def replica_grads(replica):

        def replica_loss(weights):

            def advance(running, portion):
                return (running + jax.checkpoint(block_loss)(weights, *portion), None)
            running, unused = lax.scan(advance, jnp.zeros((), jnp.float32), replica)
            return running
        result, pullback = jax.vjp(replica_loss, params)
        return (result, pullback(jnp.ones((), jnp.float32))[0])
    losses, grads = lax.map(replica_grads, per_replica)
    grad_big, grad_small, grad_bias = grads
    total_loss = jnp.sum(losses)
    matrices = (grad_big + error_big).reshape(N_REP, D, N_SHARD, WIDTH)
    factors = factor_right.reshape(N_SHARD, WIDTH, RANK)
    left_sum = jnp.einsum('rdsw,swk->sdk', matrices, factors, precision=highest)
    basis = orthonormal(left_sum)
    right_sum = jnp.einsum('rdsw,sdk->swk', matrices, basis, precision=highest)
    approx = jnp.einsum('sdk,swk->dsw', basis, right_sum, precision=highest).reshape(D, WCOLS)
    new_error = matrices.reshape(N_REP, D, WCOLS) - approx[None] / N_REP
    new_moment = momentum_decay * moment_big + approx
    new_master = master_big - step_rates[0] * new_moment
    small_grad = lax.optimization_barrier(jnp.sum(grad_small, axis=0))
    bias_grad = lax.optimization_barrier(jnp.sum(grad_bias, axis=0))
    new_moment_small = momentum_decay * moment_small + small_grad
    new_master_small = master_small - step_rates[1] * new_moment_small
    new_moment_bias = momentum_decay * moment_bias + bias_grad
    new_biases = biases - step_rates[1] * new_moment_bias
    return (total_loss, new_master, new_moment, new_error, right_sum.reshape(WCOLS, RANK), new_master_small, new_moment_small, new_biases, new_moment_bias)
```

```python
import functools
import math

import jax
import jax.numpy as jnp
from jax import lax
from jax.experimental import pallas as pl
from jax.experimental.pallas import tpu as pltpu
from jax.sharding import PartitionSpec as P

D = 768
HEADS = 12
HEAD_DIM = 64
FF = 3072
GRID = 16
FREQ = 256
NCLASS = 1000
P_DIM = 16
SEQ = 256


highest = lax.Precision.HIGHEST
epsilon = 1e-06
tiny_value = 1e-30
momentum_decay = 0.9
half_type = jnp.bfloat16


def multiply(left_side, right_side):
    return jnp.dot(left_side, right_side, preferred_element_type=jnp.float32)


def multiply_trans(left_side, right_side):
    return lax.dot_general(
        left_side, right_side, (((1,), (1,)), ((), ())), preferred_element_type=jnp.float32
    )


def outer_sum(left_side, right_side):
    return lax.dot_general(
        left_side, right_side, (((0,), (0,)), ((), ())), preferred_element_type=jnp.float32
    )


def exact_outer(left_side, right_side):
    return lax.dot_general(
        left_side,
        right_side,
        (((0,), (0,)), ((), ())),
        precision=highest,
        preferred_element_type=jnp.float32,
    )


def normalize(values):
    center = values - jnp.mean(values, axis=-1, keepdims=True)
    return center * lax.rsqrt(jnp.mean(center * center, axis=-1, keepdims=True) + epsilon)


def gelu_tanh(values):
    return jax.nn.gelu(values, approximate=True)


def slope(function, values, grad):
    unused, pullback = jax.vjp(function, values)
    return pullback(grad)[0]


def timestep_features(steps):
    half_count = FREQ // 2
    freqs = jnp.exp(-math.log(10000.0) * jnp.arange(half_count, dtype=jnp.float32) / half_count)
    angles = steps.astype(jnp.float32)[:, None] * freqs[None, :]
    return jnp.concatenate([jnp.cos(angles), jnp.sin(angles)], axis=1)


def position_table():
    quarter = D // 4
    omega = 1.0 / 10000.0 ** (jnp.arange(quarter, dtype=jnp.float32) / quarter)
    cells = jnp.arange(SEQ, dtype=jnp.int32)
    across = (cells % GRID).astype(jnp.float32)[:, None] * omega[None, :]
    downward = (cells // GRID).astype(jnp.float32)[:, None] * omega[None, :]
    return jnp.concatenate(
        [jnp.sin(across), jnp.cos(across), jnp.sin(downward), jnp.cos(downward)], axis=1
    )


def split_at(matrix, edges):
    return tuple((matrix[..., edges[place] : edges[place + 1]] for place in range(len(edges) - 1)))


def split_big(matrix):
    return split_at(
        matrix,
        [
            0,
            3 * D,
            4 * D,
            4 * D + FF,
            4 * D + 2 * FF,
            10 * D + 2 * FF,
            12 * D + 2 * FF,
            13 * D + 2 * FF,
            13 * D + 2 * FF + FREQ,
        ],
    )


def split_small(matrix):
    return split_at(matrix, [0, P_DIM, P_DIM + NCLASS, 2 * P_DIM + NCLASS])


def split_bias(vector):
    return split_at(
        vector,
        [
            0,
            D,
            2 * D,
            3 * D,
            3 * D + FF,
            4 * D + FF,
            10 * D + FF,
            12 * D + FF,
            13 * D + FF,
            14 * D + FF,
            15 * D + FF,
            15 * D + FF + P_DIM,
        ],
    )


def orthonormal(factor):
    columns = []
    for place in range(factor.shape[-1]):
        vector = factor[..., place]
        for earlier in columns:
            vector = vector - jnp.sum(earlier * vector, axis=-1, keepdims=True) * earlier
        vector = vector * lax.rsqrt(jnp.sum(vector * vector, axis=-1, keepdims=True) + tiny_value)
        columns.append(vector)
    return jnp.stack(columns, axis=-1)


def column_sums(grad):
    return jnp.sum(grad.astype(jnp.float32), axis=0)


def forward(gathered, master_small, biases, noisy_patches, timesteps, labels):
    (
        attend_weight,
        output_weight,
        up_weight,
        down_weight,
        modulate_weight,
        final_weight,
        embed_second,
        embed_first,
    ) = split_big(gathered)
    patch_weight, unused_table, head_weight = split_small(master_small.astype(half_type))
    class_table = split_small(master_small)[1]
    (
        query_bias,
        value_bias,
        output_bias,
        up_bias,
        down_bias,
        modulate_bias,
        final_bias,
        second_bias,
        first_bias,
        patch_bias,
        head_bias,
    ) = split_bias(biases)
    images = noisy_patches.shape[0]
    tokens = images * SEQ
    frequency = timestep_features(timesteps).astype(half_type)
    embed_pre = multiply_trans(frequency, embed_first) + first_bias
    embed_hidden = jax.nn.silu(embed_pre).astype(half_type)
    time_embed = multiply(embed_hidden, embed_second) + second_bias
    chosen = (labels[:, None] == jnp.arange(NCLASS, dtype=jnp.int32)[None, :]).astype(jnp.float32)
    condition = time_embed + lax.dot_general(
        chosen,
        class_table,
        (((1,), (1,)), ((), ())),
        precision=highest,
        preferred_element_type=jnp.float32,
    )
    active = jax.nn.silu(condition).astype(half_type)
    modulation = multiply(active, modulate_weight) + modulate_bias
    final_mod = multiply(active, final_weight) + final_bias
    patches = noisy_patches.reshape(tokens, P_DIM)
    stream_in = (multiply_trans(patches, patch_weight) + patch_bias).reshape(
        images, SEQ, D
    ) + position_table()[None]
    shift_attn, scale_attn, gate_attn, shift_mlp, scale_mlp, gate_mlp = jnp.split(
        modulation[:, None, :], 6, axis=2
    )
    shift_final, scale_final = jnp.split(final_mod[:, None, :], 2, axis=2)
    attn_in = (
        (normalize(stream_in) * (1.0 + scale_attn) + shift_attn)
        .astype(half_type)
        .reshape(tokens, D)
    )
    qkv_bias = jnp.concatenate([query_bias, jnp.zeros_like(query_bias), value_bias])
    projected = (multiply(attn_in, attend_weight) + qkv_bias).astype(half_type)
    queries, key_rows, value_rows = [
        piece.reshape(images, SEQ, HEADS, HEAD_DIM) for piece in jnp.split(projected, 3, axis=1)
    ]
    scores = jnp.einsum(
        "nqhd,nkhd->nhqk", queries, key_rows, preferred_element_type=jnp.float32
    ) / math.sqrt(HEAD_DIM)
    highest_score = jnp.max(scores, axis=-1, keepdims=True)
    logsum = highest_score + jnp.log(
        jnp.sum(jnp.exp(scores - highest_score), axis=-1, keepdims=True)
    )
    probs_low = jnp.exp(scores - logsum).astype(half_type)
    mixed_rows = (
        jnp.einsum("nhqk,nkhd->nqhd", probs_low, value_rows, preferred_element_type=jnp.float32)
        .astype(half_type)
        .reshape(tokens, D)
    )
    attended = (multiply(mixed_rows, output_weight) + output_bias).reshape(images, SEQ, D)
    stream_mid = stream_in + gate_attn * attended
    mlp_in = (
        (normalize(stream_mid) * (1.0 + scale_mlp) + shift_mlp).astype(half_type).reshape(tokens, D)
    )
    hidden_pre = multiply(mlp_in, up_weight) + up_bias
    hidden = gelu_tanh(hidden_pre).astype(half_type)
    mlp_out = (multiply_trans(hidden, down_weight) + down_bias).reshape(images, SEQ, D)
    stream_out = stream_mid + gate_mlp * mlp_out
    final_in = (
        (normalize(stream_out) * (1.0 + scale_final) + shift_final)
        .astype(half_type)
        .reshape(tokens, D)
    )
    output = multiply(final_in, head_weight) + head_bias
    kept = dict(
        frequency=frequency,
        embed_pre=embed_pre,
        embed_hidden=embed_hidden,
        chosen=chosen,
        condition=condition,
        active=active,
        modulation=modulation,
        final_mod=final_mod,
        patches=patches,
        stream_in=stream_in,
        attn_in=attn_in,
        queries=queries,
        key_rows=key_rows,
        value_rows=value_rows,
        logsum=logsum,
        mixed_rows=mixed_rows,
        attended=attended,
        stream_mid=stream_mid,
        mlp_in=mlp_in,
        hidden_pre=hidden_pre,
        hidden=hidden,
        mlp_out=mlp_out,
        stream_out=stream_out,
        final_in=final_in,
    )
    return (output, kept)


def backward(gathered, master_small, kept, grad_output):
    (
        attend_weight,
        output_weight,
        up_weight,
        down_weight,
        modulate_weight,
        final_weight,
        embed_second,
        embed_first,
    ) = split_big(gathered)
    patch_weight, unused_table, head_weight = split_small(master_small.astype(half_type))
    images = kept["stream_in"].shape[0]
    tokens = images * SEQ
    shift_attn, scale_attn, gate_attn, shift_mlp, scale_mlp, gate_mlp = jnp.split(
        kept["modulation"][:, None, :], 6, axis=2
    )
    shift_final, scale_final = jnp.split(kept["final_mod"][:, None, :], 2, axis=2)
    grad_out = grad_output.astype(half_type)
    grad_head = outer_sum(kept["final_in"], grad_out)
    bias_head = column_sums(grad_out)
    grad_final = multiply_trans(grad_out, head_weight).reshape(images, SEQ, D)
    grad_shift_final = jnp.sum(grad_final, axis=1)
    grad_scale_final = jnp.sum(grad_final * normalize(kept["stream_out"]), axis=1)
    grad_stream = slope(normalize, kept["stream_out"], grad_final * (1.0 + scale_final))
    grad_gate_mlp = jnp.sum(grad_stream * kept["mlp_out"], axis=1)
    grad_mlp = (grad_stream * gate_mlp).reshape(tokens, D).astype(half_type)
    bias_down = column_sums(grad_mlp)
    grad_down = outer_sum(grad_mlp, kept["hidden"])
    grad_hidden = multiply(grad_mlp, down_weight)
    grad_pre = slope(gelu_tanh, kept["hidden_pre"], grad_hidden).astype(half_type)
    bias_up = column_sums(grad_pre)
    grad_up = outer_sum(kept["mlp_in"], grad_pre)
    grad_mlp_in = multiply_trans(grad_pre, up_weight).reshape(images, SEQ, D)
    grad_shift_mlp = jnp.sum(grad_mlp_in, axis=1)
    grad_scale_mlp = jnp.sum(grad_mlp_in * normalize(kept["stream_mid"]), axis=1)
    grad_stream = grad_stream + slope(
        normalize, kept["stream_mid"], grad_mlp_in * (1.0 + scale_mlp)
    )
    grad_gate_attn = jnp.sum(grad_stream * kept["attended"], axis=1)
    grad_attn = (grad_stream * gate_attn).reshape(tokens, D).astype(half_type)
    bias_output = column_sums(grad_attn)
    grad_output_weight = outer_sum(kept["mixed_rows"], grad_attn)
    grad_mixed = (
        multiply_trans(grad_attn, output_weight)
        .astype(half_type)
        .reshape(images, SEQ, HEADS, HEAD_DIM)
    )
    inverse_root = 1.0 / math.sqrt(HEAD_DIM)
    scores = (
        jnp.einsum(
            "nqhd,nkhd->nhqk", kept["queries"], kept["key_rows"], preferred_element_type=jnp.float32
        )
        * inverse_root
    )
    probs = jnp.exp(scores - kept["logsum"])
    grad_values = jnp.einsum(
        "nhqk,nqhd->nkhd", probs.astype(half_type), grad_mixed, preferred_element_type=jnp.float32
    )
    grad_probs = jnp.einsum(
        "nqhd,nkhd->nhqk", grad_mixed, kept["value_rows"], preferred_element_type=jnp.float32
    )
    grad_scores = (
        probs * (grad_probs - jnp.sum(probs * grad_probs, axis=-1, keepdims=True))
    ).astype(half_type)
    grad_queries = (
        jnp.einsum(
            "nhqk,nkhd->nqhd", grad_scores, kept["key_rows"], preferred_element_type=jnp.float32
        )
        * inverse_root
    )
    grad_keys = (
        jnp.einsum(
            "nhqk,nqhd->nkhd", grad_scores, kept["queries"], preferred_element_type=jnp.float32
        )
        * inverse_root
    )
    grad_qkv = jnp.concatenate(
        [
            grad_queries.reshape(tokens, D),
            grad_keys.reshape(tokens, D),
            grad_values.reshape(tokens, D),
        ],
        axis=1,
    ).astype(half_type)
    bias_query = column_sums(grad_qkv[:, :D])
    bias_value = column_sums(grad_qkv[:, 2 * D :])
    grad_attend = outer_sum(kept["attn_in"], grad_qkv)
    grad_attn_in = multiply_trans(grad_qkv, attend_weight).reshape(images, SEQ, D)
    grad_shift_attn = jnp.sum(grad_attn_in, axis=1)
    grad_scale_attn = jnp.sum(grad_attn_in * normalize(kept["stream_in"]), axis=1)
    grad_stream = grad_stream + slope(
        normalize, kept["stream_in"], grad_attn_in * (1.0 + scale_attn)
    )
    grad_start = grad_stream.reshape(tokens, D).astype(half_type)
    bias_patch = column_sums(grad_start)
    grad_patch = outer_sum(grad_start, kept["patches"])
    grad_mod = jnp.concatenate(
        [
            grad_shift_attn,
            grad_scale_attn,
            grad_gate_attn,
            grad_shift_mlp,
            grad_scale_mlp,
            grad_gate_mlp,
        ],
        axis=1,
    ).astype(half_type)
    grad_fmod = jnp.concatenate([grad_shift_final, grad_scale_final], axis=1).astype(half_type)
    bias_modulate = column_sums(grad_mod)
    bias_final = column_sums(grad_fmod)
    grad_modulate = outer_sum(kept["active"], grad_mod)
    grad_final_weight = outer_sum(kept["active"], grad_fmod)
    grad_active = multiply_trans(grad_mod, modulate_weight) + multiply_trans(
        grad_fmod, final_weight
    )
    grad_condition = slope(jax.nn.silu, kept["condition"], grad_active)
    grad_embed = grad_condition.astype(half_type)
    bias_second = column_sums(grad_embed)
    grad_second = outer_sum(kept["embed_hidden"], grad_embed)
    grad_embed_hidden = multiply_trans(grad_embed, embed_second)
    grad_embed_pre = slope(jax.nn.silu, kept["embed_pre"], grad_embed_hidden).astype(half_type)
    bias_first = column_sums(grad_embed_pre)
    grad_first = outer_sum(grad_embed_pre, kept["frequency"])
    grad_big = jnp.concatenate(
        [
            grad_attend,
            grad_output_weight,
            grad_up,
            grad_down,
            grad_modulate,
            grad_final_weight,
            grad_second,
            grad_first,
        ],
        axis=1,
    )
    grad_small = (grad_patch, grad_head, grad_condition)
    grad_bias = jnp.concatenate(
        [
            bias_query,
            bias_value,
            bias_output,
            bias_up,
            bias_down,
            bias_modulate,
            bias_final,
            bias_second,
            bias_first,
            bias_patch,
            bias_head,
        ]
    )
    return (grad_big, grad_small, grad_bias)


def on_device(
    noisy_patches,
    targets,
    timesteps,
    labels,
    master_big,
    moment_big,
    error_big,
    factor_right,
    master_small,
    moment_small,
    biases,
    moment_bias,
    step_rates,
):
    shards = lax.axis_size("shard")
    replicas = lax.axis_size("rep")
    gathered = lax.all_gather(master_big.astype(half_type), "shard", axis=1, tiled=True)
    output, kept = forward(gathered, master_small, biases, noisy_patches, timesteps, labels)
    entries = noisy_patches.shape[0] * shards * replicas * SEQ * P_DIM
    error = output - targets.reshape(output.shape)
    loss_part = jnp.sum(error * error) / entries
    grad_output = 2.0 * error / entries
    gathered = lax.all_gather(master_big.astype(half_type), "shard", axis=1, tiled=True)
    grad_big, (grad_patch, grad_head, grad_condition), grad_bias = backward(
        gathered, master_small, kept, grad_output
    )
    grad_table = jnp.einsum("nd,nc->dc", grad_condition, kept["chosen"], precision=highest)
    grad_small = jnp.concatenate([grad_patch, grad_table, grad_head], axis=1)
    owned = lax.psum_scatter(
        grad_big.astype(jnp.bfloat16), "shard", scatter_dimension=1, tiled=True
    ).astype(jnp.float32)
    matrices = owned + error_big[0]
    left_part = jnp.dot(
        matrices, factor_right, precision=highest, preferred_element_type=jnp.float32
    )
    small_sum, bias_sum, total_loss = lax.psum((grad_small, grad_bias, loss_part), ("shard", "rep"))
    left_sum = lax.psum(left_part, "rep")
    basis = orthonormal(left_sum)
    right_sum = lax.psum(exact_outer(matrices, basis).astype(jnp.bfloat16), "rep").astype(
        jnp.float32
    )
    approx = lax.dot_general(
        basis,
        right_sum,
        (((1,), (1,)), ((), ())),
        precision=highest,
        preferred_element_type=jnp.float32,
    )
    new_error = (matrices - approx / replicas)[None]
    new_moment = momentum_decay * moment_big + approx
    new_master = master_big - step_rates[0] * new_moment
    new_moment_small = momentum_decay * moment_small + small_sum
    new_master_small = master_small - step_rates[1] * new_moment_small
    new_moment_bias = momentum_decay * moment_bias + bias_sum
    new_biases = biases - step_rates[1] * new_moment_bias
    return (
        total_loss,
        new_master,
        new_moment,
        new_error,
        right_sum,
        new_master_small,
        new_moment_small,
        new_biases,
        new_moment_bias,
    )


MESH = pl.DeviceIdType.MESH
BLOCK = 512
RANK = 8
LANES = 128
REPS = 16


def sds(shape, dtype=jnp.float32):
    return jax.ShapeDtypeStruct(shape, dtype)


def split_two(values):
    high = values.astype(half_type)
    low = (values - high.astype(jnp.float32)).astype(half_type)
    return high, low


def greet(others):
    barrier = pltpu.get_barrier_semaphore()
    for other in others:
        pl.semaphore_signal(barrier, inc=1, device_id=other, device_id_type=MESH)
    return barrier, len(others)


def small_kernel(
    sums_ref, rows_ref, total_ref, gathered_ref, half_ref, part_ref, mine_ref, send_sem, recv_sem
):
    shard = lax.axis_index("shard")
    rep = lax.axis_index("rep")
    partner = (1 - shard, rep)
    peers = [(shard, lax.rem(rep + step, REPS)) for step in range(1, REPS)]
    barrier, count = greet([partner] + peers)
    pl.semaphore_wait(barrier, count)

    def remote(source, target, where, who):
        return pltpu.make_async_remote_copy(
            src_ref=source,
            dst_ref=target,
            send_sem=send_sem.at[where],
            recv_sem=recv_sem.at[where],
            device_id=who,
            device_id_type=MESH,
        )

    rows_out = [
        pltpu.make_async_remote_copy(
            src_ref=rows_ref,
            dst_ref=gathered_ref.at[shard, rep],
            send_sem=send_sem.at[step],
            recv_sem=recv_sem.at[rep],
            device_id=peers[step - 1],
            device_id_type=MESH,
        )
        for step in range(1, REPS)
    ]
    own_half = remote(sums_ref.at[1 - shard], half_ref, 16, partner)
    own_half.start()
    for copy in rows_out:
        copy.start()
    gathered_ref[shard, rep] = rows_ref[...]
    own_half.wait()
    half_ref[...] = half_ref[...] + sums_ref[shard]
    parts_out = [
        pltpu.make_async_remote_copy(
            src_ref=half_ref.at[lax.rem(rep + step, REPS)],
            dst_ref=part_ref.at[rep],
            send_sem=send_sem.at[17 + step],
            recv_sem=recv_sem.at[17 + rep],
            device_id=peers[step - 1],
            device_id_type=MESH,
        )
        for step in range(1, REPS)
    ]
    for copy in parts_out:
        copy.start()
    part_ref[rep] = half_ref[rep]

    def arrived(slots, base):
        for step in range(1, REPS):
            other = lax.rem(rep + step, REPS)
            pltpu.make_async_remote_copy(
                src_ref=slots.at[other],
                dst_ref=slots.at[other],
                send_sem=send_sem.at[base],
                recv_sem=recv_sem.at[base + other],
                device_id=peers[step - 1],
                device_id_type=MESH,
            ).wait_recv()

    arrived(part_ref, 17)
    mine_ref[...] = jnp.sum(part_ref[...], axis=0)
    whole_out = [
        pltpu.make_async_remote_copy(
            src_ref=mine_ref,
            dst_ref=total_ref.at[shard, rep],
            send_sem=send_sem.at[33 + step],
            recv_sem=recv_sem.at[33 + rep],
            device_id=peers[step - 1],
            device_id_type=MESH,
        )
        for step in range(1, REPS)
    ]
    for copy in whole_out:
        copy.start()
    total_ref[shard, rep] = mine_ref[...]
    arrived(gathered_ref.at[shard], 0)
    rows_across = remote(gathered_ref.at[shard], gathered_ref.at[shard], 49, partner)
    rows_across.start()
    arrived(total_ref.at[shard], 33)
    total_across = remote(total_ref.at[shard], total_ref.at[shard], 50, partner)
    total_across.start()
    for copy in rows_out + parts_out + whole_out:
        copy.wait_send()
    rows_across.wait()
    total_across.wait()


def small_sums(sums, rows):
    return pl.pallas_call(
        small_kernel,
        out_shape=(sds((2, REPS) + sums.shape[2:]), sds((2, REPS) + rows.shape)),
        in_specs=[pl.BlockSpec(memory_space=pltpu.VMEM)] * 2,
        out_specs=[pl.BlockSpec(memory_space=pltpu.VMEM)] * 2,
        scratch_shapes=[
            pltpu.VMEM(sums.shape[1:], jnp.float32),
            pltpu.VMEM((REPS,) + sums.shape[2:], jnp.float32),
            pltpu.VMEM(sums.shape[2:], jnp.float32),
            pltpu.SemaphoreType.DMA((51,)),
            pltpu.SemaphoreType.DMA((51,)),
        ],
        compiler_params=pltpu.CompilerParams(
            collective_id=1, has_side_effects=True, vmem_limit_bytes=16 * 1024 * 1024
        ),
        name="small_sums",
    )(sums, rows)


def tail_kernel(
    rates_ref,
    own_hbm,
    recv_hbm,
    error_hbm,
    factor_ref,
    moment_hbm,
    master_hbm,
    new_master_hbm,
    new_moment_hbm,
    new_error_hbm,
    right_ref,
    m_ref,
    v_ref,
    own_ref,
    recv_ref,
    master_ref,
    stack_ref,
    left_acc,
    left_ref,
    plane_ref,
    column_ref,
    basis_rows,
    basis_cols,
    send_ref,
    part_ref,
    mine_ref,
    whole_ref,
    load_sem,
    own_sem,
    recv_sem,
    moment_sem,
    master_sem,
    out_sem,
    left_send,
    left_recv,
    right_send,
    right_recv,
):
    blocks = m_ref.shape[0]
    shard = lax.axis_index("shard")
    rep = lax.axis_index("rep")
    peers = [(shard, lax.rem(rep + step, REPS)) for step in range(1, REPS)]
    barrier, count = greet(peers)

    def columns(block):
        return pl.ds(pl.multiple_of(block * BLOCK, BLOCK), BLOCK)

    def load_error(block):
        return pltpu.make_async_copy(
            error_hbm.at[0, :, columns(block)], m_ref.at[block], load_sem.at[block]
        )

    def load_own(block, slot):
        return pltpu.make_async_copy(
            own_hbm.at[:, columns(block)], own_ref.at[slot], own_sem.at[slot]
        )

    def load_recv(block, slot):
        return pltpu.make_async_copy(
            recv_hbm.at[:, columns(block)], recv_ref.at[slot], recv_sem.at[slot]
        )

    def load_moment(block):
        return pltpu.make_async_copy(
            moment_hbm.at[:, columns(block)], v_ref.at[block], moment_sem.at[block]
        )

    depth = own_ref.shape[0]

    for block in range(depth):
        load_error(block).start()
        load_own(block, block).start()
        load_recv(block, block).start()

    high, low = split_two(factor_ref[...])
    stack_ref[...] = jnp.zeros_like(stack_ref)
    stack_ref[0:RANK] = high
    stack_ref[RANK : 2 * RANK] = low
    left_acc[...] = jnp.zeros_like(left_acc)

    def gather_block(block, carry):
        slot = lax.rem(block, depth)
        load_error(block).wait()
        load_own(block, slot).wait()
        load_recv(block, slot).wait()
        matrix = (
            own_ref[slot].astype(jnp.float32) + recv_ref[slot].astype(jnp.float32) + m_ref[block]
        )
        m_ref[block] = matrix
        high, low = split_two(matrix)
        factor = stack_ref[:, columns(block)]
        left_acc[...] += multiply_trans(high, factor) + multiply_trans(low, factor)

        @pl.when(block + depth < blocks)
        def _():
            load_error(block + depth).start()
            load_own(block + depth, slot).start()
            load_recv(block + depth, slot).start()

        return carry

    lax.fori_loop(0, blocks, gather_block, 0)
    for block in range(blocks):
        load_moment(block).start()

    def load_master(block, slot):
        return pltpu.make_async_copy(
            master_hbm.at[:, columns(block)], master_ref.at[slot], master_sem.at[slot]
        )

    slots = master_ref.shape[0]
    for block in range(slots):
        load_master(block, block).start()

    turned = left_acc[...].T
    left_ref[...] = turned[0:RANK] + turned[RANK : 2 * RANK]
    pl.semaphore_wait(barrier, count)

    place = lax.rem(rep, 4)
    level = lax.div(rep, 4)
    plane_out = []
    for step in range(1, 4):
        other = lax.rem(place + step, 4)
        plane_out.append(
            pltpu.make_async_remote_copy(
                src_ref=left_ref,
                dst_ref=plane_ref.at[place],
                send_sem=left_send.at[step],
                recv_sem=left_recv.at[place],
                device_id=(shard, level * 4 + other),
                device_id_type=MESH,
            )
        )
    for copy in plane_out:
        copy.start()
    plane_ref[place] = left_ref[...]
    for step in range(1, 4):
        other = lax.rem(place + step, 4)
        pltpu.make_async_remote_copy(
            src_ref=left_ref,
            dst_ref=plane_ref.at[other],
            send_sem=left_send.at[step],
            recv_sem=left_recv.at[other],
            device_id=(shard, level * 4 + other),
            device_id_type=MESH,
        ).wait_recv()
    plane_sum = (plane_ref[0] + plane_ref[1]) + (plane_ref[2] + plane_ref[3])
    for copy in plane_out:
        copy.wait_send()
    left_ref[...] = plane_sum
    column_out = []
    for step in range(1, 4):
        other = lax.rem(level + step, 4)
        column_out.append(
            pltpu.make_async_remote_copy(
                src_ref=left_ref,
                dst_ref=column_ref.at[level],
                send_sem=left_send.at[4 + step],
                recv_sem=left_recv.at[4 + level],
                device_id=(shard, other * 4 + place),
                device_id_type=MESH,
            )
        )
    for copy in column_out:
        copy.start()
    column_ref[level] = plane_sum
    for step in range(1, 4):
        other = lax.rem(level + step, 4)
        pltpu.make_async_remote_copy(
            src_ref=left_ref,
            dst_ref=column_ref.at[other],
            send_sem=left_send.at[4 + step],
            recv_sem=left_recv.at[4 + other],
            device_id=(shard, other * 4 + place),
            device_id_type=MESH,
        ).wait_recv()
    vectors = (column_ref[0] + column_ref[1]) + (column_ref[2] + column_ref[3])

    row_index = lax.broadcasted_iota(jnp.int32, (RANK, 1), 0)
    for place_of in range(RANK):
        row = vectors[place_of : place_of + 1]
        unit = row * lax.rsqrt(jnp.sum(row * row, axis=1, keepdims=True) + tiny_value)
        dots = jnp.sum(vectors * unit, axis=1, keepdims=True)
        vectors = jnp.where(
            row_index > place_of,
            vectors - dots * unit,
            jnp.where(row_index == place_of, unit, vectors),
        )
    high, low = split_two(vectors)
    basis_rows[...] = jnp.concatenate([high, low], axis=0)
    padded = jnp.concatenate(
        [
            high.astype(jnp.float32),
            low.astype(jnp.float32),
            jnp.zeros((LANES - 2 * RANK, vectors.shape[1]), jnp.float32),
        ],
        axis=0,
    )
    basis_cols[...] = padded.T.astype(half_type)
    for copy in column_out:
        copy.wait_send()

    def right_block(block, carry):
        high, low = split_two(m_ref[block])
        first = multiply(basis_rows[...], high)
        second = multiply(basis_rows[...], low)
        both = first + second
        send_ref[block] = (both[0:RANK] + both[RANK : 2 * RANK]).astype(half_type)
        return carry

    lax.fori_loop(0, blocks, right_block, 0)

    def right_copy(source, target, base, step, sender):
        return pltpu.make_async_remote_copy(
            src_ref=source,
            dst_ref=target,
            send_sem=right_send.at[base + step],
            recv_sem=right_recv.at[base + sender],
            device_id=peers[step - 1],
            device_id_type=MESH,
        )

    scatter = [
        right_copy(send_ref.at[lax.rem(rep + step, REPS)], part_ref.at[rep], 0, step, rep)
        for step in range(1, REPS)
    ]
    for copy in scatter:
        copy.start()
    part_ref[rep] = send_ref[rep]
    for step in range(1, REPS):
        other = lax.rem(rep + step, REPS)
        right_copy(send_ref.at[other], part_ref.at[other], 0, step, other).wait_recv()
    mine_ref[...] = jnp.sum(part_ref[...].astype(jnp.float32), axis=0).astype(half_type)
    spread = [
        right_copy(mine_ref, whole_ref.at[rep], REPS, step, rep) for step in range(1, REPS)
    ]
    for copy in spread:
        copy.start()
    whole_ref[rep] = mine_ref[...]
    for step in range(1, REPS):
        other = lax.rem(rep + step, REPS)
        right_copy(mine_ref, whole_ref.at[other], REPS, step, other).wait_recv()

    def out_error(block):
        return pltpu.make_async_copy(
            m_ref.at[block], new_error_hbm.at[0, :, columns(block)], load_sem.at[block]
        )

    def out_moment(block):
        return pltpu.make_async_copy(
            v_ref.at[block], new_moment_hbm.at[:, columns(block)], moment_sem.at[block]
        )

    def out_master(block, slot):
        return pltpu.make_async_copy(
            master_ref.at[slot], new_master_hbm.at[:, columns(block)], out_sem.at[slot]
        )

    rate = rates_ref[0]

    def update_block(block, carry):
        slot = lax.rem(block, slots)

        @pl.when(jnp.logical_and(block >= 1, block - 1 + slots < blocks))
        def _():
            earlier = lax.rem(block - 1, slots)
            out_master(block - 1, earlier).wait()
            load_master(block - 1 + slots, earlier).start()

        right = whole_ref[block]
        right_ref[:, columns(block)] = right.astype(jnp.float32)
        approx = multiply(
            basis_cols[:, 0 : 2 * RANK], jnp.concatenate([right, right], axis=0)
        )
        m_ref[block] = m_ref[block] - approx * (1.0 / REPS)
        out_error(block).start()
        load_moment(block).wait()
        moment = momentum_decay * v_ref[block] + approx
        v_ref[block] = moment
        out_moment(block).start()
        load_master(block, slot).wait()
        master_ref[slot] = master_ref[slot] - rate * moment
        out_master(block, slot).start()
        return carry

    lax.fori_loop(0, blocks, update_block, 0)
    for block in range(blocks):
        out_error(block).wait()
        out_moment(block).wait()
    for block in range(blocks - slots, blocks):
        out_master(block, block % slots).wait()
    for copy in scatter + spread:
        copy.wait_send()


def compress(rates, own, received, error, factor_rows, moment, master):
    rows, cols = own.shape
    blocks = cols // BLOCK
    depth = 3
    slots = 3
    hbm = pl.BlockSpec(memory_space=pl.ANY)
    vmem = pl.BlockSpec(memory_space=pltpu.VMEM)
    return pl.pallas_call(
        tail_kernel,
        out_shape=(
            sds(master.shape),
            sds(moment.shape),
            sds(error.shape),
            sds((RANK, cols)),
        ),
        in_specs=[pl.BlockSpec(memory_space=pltpu.SMEM), hbm, hbm, hbm, vmem, hbm, hbm],
        out_specs=[hbm, hbm, hbm, vmem],
        scratch_shapes=[
            pltpu.VMEM((blocks, rows, BLOCK), jnp.float32),
            pltpu.VMEM((blocks, rows, BLOCK), jnp.float32),
            pltpu.VMEM((depth, rows, BLOCK), half_type),
            pltpu.VMEM((depth, rows, BLOCK), half_type),
            pltpu.VMEM((slots, rows, BLOCK), jnp.float32),
            pltpu.VMEM((LANES, cols), half_type),
            pltpu.VMEM((rows, LANES), jnp.float32),
            pltpu.VMEM((RANK, rows), jnp.float32),
            pltpu.VMEM((4, RANK, rows), jnp.float32),
            pltpu.VMEM((4, RANK, rows), jnp.float32),
            pltpu.VMEM((2 * RANK, rows), half_type),
            pltpu.VMEM((rows, LANES), half_type),
            pltpu.VMEM((blocks, RANK, BLOCK), half_type),
            pltpu.VMEM((blocks, RANK, BLOCK), half_type),
            pltpu.VMEM((RANK, BLOCK), half_type),
            pltpu.VMEM((blocks, RANK, BLOCK), half_type),
            pltpu.SemaphoreType.DMA((blocks,)),
            pltpu.SemaphoreType.DMA((depth,)),
            pltpu.SemaphoreType.DMA((depth,)),
            pltpu.SemaphoreType.DMA((blocks,)),
            pltpu.SemaphoreType.DMA((slots,)),
            pltpu.SemaphoreType.DMA((slots,)),
            pltpu.SemaphoreType.DMA((8,)),
            pltpu.SemaphoreType.DMA((8,)),
            pltpu.SemaphoreType.DMA((2 * REPS,)),
            pltpu.SemaphoreType.DMA((2 * REPS,)),
        ],
        compiler_params=pltpu.CompilerParams(
            collective_id=2, has_side_effects=True, vmem_limit_bytes=67_000_000
        ),
        name="compress",
    )(rates, own, received, error, factor_rows, moment, master)


def on_pair(
    noisy_patches,
    targets,
    timesteps,
    labels,
    master_big,
    moment_big,
    error_big,
    factor_right,
    master_small,
    moment_small,
    biases,
    moment_bias,
    step_rates,
):
    shards = lax.axis_size("shard")
    replicas = lax.axis_size("rep")
    gathered = lax.all_gather(master_big.astype(half_type), "shard", axis=1, tiled=True)
    output, kept = forward(gathered, master_small, biases, noisy_patches, timesteps, labels)
    entries = noisy_patches.shape[0] * shards * replicas * SEQ * P_DIM
    error = output - targets.reshape(output.shape)
    loss_part = jnp.sum(error * error) / entries
    grad_output = 2.0 * error / entries
    grad_big, (grad_patch, grad_head, grad_condition), grad_bias = backward(
        gathered, master_small, kept, grad_output
    )
    shard = lax.axis_index("shard")
    cols = master_big.shape[1]
    low_grad = grad_big.astype(half_type)
    own = lax.dynamic_slice_in_dim(low_grad, shard * cols, cols, axis=1)
    received = lax.ppermute(
        lax.dynamic_slice_in_dim(low_grad, (1 - shard) * cols, cols, axis=1),
        "shard",
        [(0, 1), (1, 0)],
    )
    images = labels.shape[0]
    flat = jnp.concatenate(
        [
            grad_patch.T.reshape(-1),
            grad_head.T.reshape(-1),
            grad_bias,
            loss_part[None],
        ]
    )
    width = shards * replicas * 16 * LANES
    sums = jnp.pad(flat, (0, width - flat.shape[0])).reshape(shards, replicas, 16, LANES)
    lines = images * D // LANES
    rows = jnp.concatenate(
        [
            grad_condition.reshape(lines, LANES),
            jnp.pad(labels.astype(jnp.float32)[None], ((0, 7), (0, LANES - images))),
        ]
    )
    total, all_rows = small_sums(sums, rows)
    new_master, new_moment, new_error, right_rows = compress(
        step_rates, own, received, error_big, factor_right.T, moment_big, master_big
    )
    total = total.reshape(-1)
    all_labels = all_rows[:, :, lines, :images].reshape(-1).astype(jnp.int32)
    conditions = all_rows[:, :, :lines, :].reshape(-1, D)
    chosen = (jnp.arange(NCLASS, dtype=jnp.int32)[:, None] == all_labels[None, :]).astype(
        jnp.float32
    )
    table_rows = jnp.dot(chosen, conditions, precision=highest, preferred_element_type=jnp.float32)
    strip = P_DIM * D
    small_sum = jnp.concatenate(
        [total[:strip].reshape(P_DIM, D), table_rows, total[strip : 2 * strip].reshape(P_DIM, D)]
    ).T
    bias_count = biases.shape[0]
    bias_sum = total[2 * strip : 2 * strip + bias_count]
    total_loss = total[2 * strip + bias_count]
    new_moment_small = momentum_decay * moment_small + small_sum
    new_master_small = master_small - step_rates[1] * new_moment_small
    new_moment_bias = momentum_decay * moment_bias + bias_sum
    new_biases = biases - step_rates[1] * new_moment_bias
    return (
        total_loss,
        new_master,
        new_moment,
        new_error,
        right_rows.T,
        new_master_small,
        new_moment_small,
        new_biases,
        new_moment_bias,
    )


def solution(mesh):
    in_specs = (
        P(("shard", "rep"), None),
        P(("shard", "rep"), None),
        P(("shard", "rep")),
        P(("shard", "rep")),
        P(None, "shard"),
        P(None, "shard"),
        P("rep", None, "shard"),
        P("shard", None),
        P(),
        P(),
        P(),
        P(),
        P(),
    )
    out_specs = (
        P(),
        P(None, "shard"),
        P(None, "shard"),
        P("rep", None, "shard"),
        P("shard", None),
        P(),
        P(),
        P(),
        P(),
    )
    fits = mesh.shape["shard"] == 2 and mesh.shape["rep"] == 16
    return jax.shard_map(
        on_pair if fits else on_device, mesh=mesh, in_specs=in_specs, out_specs=out_specs, check_vma=False
    )
```

```python
import functools
import math

import jax
import jax.numpy as jnp
from jax import lax
from jax.experimental import pallas as pl
from jax.experimental.pallas import tpu as pltpu
from jax.sharding import PartitionSpec as P

D = 768
HEADS = 12
HEAD_DIM = 64
FF = 3072
GRID = 16
FREQ = 256
NCLASS = 1000
P_DIM = 16
SEQ = 256


highest = lax.Precision.HIGHEST
epsilon = 1e-06
tiny_value = 1e-30
momentum_decay = 0.9
half_type = jnp.bfloat16


def multiply(left_side, right_side):
    return jnp.dot(left_side, right_side, preferred_element_type=jnp.float32)


def multiply_trans(left_side, right_side):
    return lax.dot_general(
        left_side, right_side, (((1,), (1,)), ((), ())), preferred_element_type=jnp.float32
    )


def outer_sum(left_side, right_side):
    return lax.dot_general(
        left_side, right_side, (((0,), (0,)), ((), ())), preferred_element_type=jnp.float32
    )


def exact_outer(left_side, right_side):
    return lax.dot_general(
        left_side,
        right_side,
        (((0,), (0,)), ((), ())),
        precision=highest,
        preferred_element_type=jnp.float32,
    )


def normalize(values):
    center = values - jnp.mean(values, axis=-1, keepdims=True)
    return center * lax.rsqrt(jnp.mean(center * center, axis=-1, keepdims=True) + epsilon)


def gelu_tanh(values):
    return jax.nn.gelu(values, approximate=True)


def slope(function, values, grad):
    unused, pullback = jax.vjp(function, values)
    return pullback(grad)[0]


def timestep_features(steps):
    half_count = FREQ // 2
    freqs = jnp.exp(-math.log(10000.0) * jnp.arange(half_count, dtype=jnp.float32) / half_count)
    angles = steps.astype(jnp.float32)[:, None] * freqs[None, :]
    return jnp.concatenate([jnp.cos(angles), jnp.sin(angles)], axis=1)


def position_table():
    quarter = D // 4
    omega = 1.0 / 10000.0 ** (jnp.arange(quarter, dtype=jnp.float32) / quarter)
    cells = jnp.arange(SEQ, dtype=jnp.int32)
    across = (cells % GRID).astype(jnp.float32)[:, None] * omega[None, :]
    downward = (cells // GRID).astype(jnp.float32)[:, None] * omega[None, :]
    return jnp.concatenate(
        [jnp.sin(across), jnp.cos(across), jnp.sin(downward), jnp.cos(downward)], axis=1
    )


def split_at(matrix, edges):
    return tuple((matrix[..., edges[place] : edges[place + 1]] for place in range(len(edges) - 1)))


def split_big(matrix):
    return split_at(
        matrix,
        [
            0,
            3 * D,
            4 * D,
            4 * D + FF,
            4 * D + 2 * FF,
            10 * D + 2 * FF,
            12 * D + 2 * FF,
            13 * D + 2 * FF,
            13 * D + 2 * FF + FREQ,
        ],
    )


def split_small(matrix):
    return split_at(matrix, [0, P_DIM, P_DIM + NCLASS, 2 * P_DIM + NCLASS])


def split_bias(vector):
    return split_at(
        vector,
        [
            0,
            D,
            2 * D,
            3 * D,
            3 * D + FF,
            4 * D + FF,
            10 * D + FF,
            12 * D + FF,
            13 * D + FF,
            14 * D + FF,
            15 * D + FF,
            15 * D + FF + P_DIM,
        ],
    )


def orthonormal(factor):
    columns = []
    for place in range(factor.shape[-1]):
        vector = factor[..., place]
        for earlier in columns:
            vector = vector - jnp.sum(earlier * vector, axis=-1, keepdims=True) * earlier
        vector = vector * lax.rsqrt(jnp.sum(vector * vector, axis=-1, keepdims=True) + tiny_value)
        columns.append(vector)
    return jnp.stack(columns, axis=-1)


def column_sums(grad):
    return jnp.sum(grad.astype(jnp.float32), axis=0)


def forward(gathered, master_small, biases, noisy_patches, timesteps, labels):
    (
        attend_weight,
        output_weight,
        up_weight,
        down_weight,
        modulate_weight,
        final_weight,
        embed_second,
        embed_first,
    ) = split_big(gathered)
    patch_weight, unused_table, head_weight = split_small(master_small.astype(half_type))
    class_table = split_small(master_small)[1]
    (
        query_bias,
        value_bias,
        output_bias,
        up_bias,
        down_bias,
        modulate_bias,
        final_bias,
        second_bias,
        first_bias,
        patch_bias,
        head_bias,
    ) = split_bias(biases)
    images = noisy_patches.shape[0]
    tokens = images * SEQ
    frequency = timestep_features(timesteps).astype(half_type)
    embed_pre = multiply_trans(frequency, embed_first) + first_bias
    embed_hidden = jax.nn.silu(embed_pre).astype(half_type)
    time_embed = multiply(embed_hidden, embed_second) + second_bias
    chosen = (labels[:, None] == jnp.arange(NCLASS, dtype=jnp.int32)[None, :]).astype(jnp.float32)
    condition = time_embed + lax.dot_general(
        chosen,
        class_table,
        (((1,), (1,)), ((), ())),
        precision=highest,
        preferred_element_type=jnp.float32,
    )
    active = jax.nn.silu(condition).astype(half_type)
    modulation = multiply(active, modulate_weight) + modulate_bias
    final_mod = multiply(active, final_weight) + final_bias
    patches = noisy_patches.reshape(tokens, P_DIM)
    stream_in = (multiply_trans(patches, patch_weight) + patch_bias).reshape(
        images, SEQ, D
    ) + position_table()[None]
    shift_attn, scale_attn, gate_attn, shift_mlp, scale_mlp, gate_mlp = jnp.split(
        modulation[:, None, :], 6, axis=2
    )
    shift_final, scale_final = jnp.split(final_mod[:, None, :], 2, axis=2)
    attn_in = (
        (normalize(stream_in) * (1.0 + scale_attn) + shift_attn)
        .astype(half_type)
        .reshape(tokens, D)
    )
    qkv_bias = jnp.concatenate([query_bias, jnp.zeros_like(query_bias), value_bias])
    projected = (multiply(attn_in, attend_weight) + qkv_bias).astype(half_type)
    queries, key_rows, value_rows = [
        piece.reshape(images, SEQ, HEADS, HEAD_DIM) for piece in jnp.split(projected, 3, axis=1)
    ]
    scores = jnp.einsum(
        "nqhd,nkhd->nhqk", queries, key_rows, preferred_element_type=jnp.float32
    ) / math.sqrt(HEAD_DIM)
    highest_score = jnp.max(scores, axis=-1, keepdims=True)
    logsum = highest_score + jnp.log(
        jnp.sum(jnp.exp(scores - highest_score), axis=-1, keepdims=True)
    )
    probs_low = jnp.exp(scores - logsum).astype(half_type)
    mixed_rows = (
        jnp.einsum("nhqk,nkhd->nqhd", probs_low, value_rows, preferred_element_type=jnp.float32)
        .astype(half_type)
        .reshape(tokens, D)
    )
    attended = (multiply(mixed_rows, output_weight) + output_bias).reshape(images, SEQ, D)
    stream_mid = stream_in + gate_attn * attended
    mlp_in = (
        (normalize(stream_mid) * (1.0 + scale_mlp) + shift_mlp).astype(half_type).reshape(tokens, D)
    )
    hidden_pre = multiply(mlp_in, up_weight) + up_bias
    hidden = gelu_tanh(hidden_pre).astype(half_type)
    mlp_out = (multiply_trans(hidden, down_weight) + down_bias).reshape(images, SEQ, D)
    stream_out = stream_mid + gate_mlp * mlp_out
    final_in = (
        (normalize(stream_out) * (1.0 + scale_final) + shift_final)
        .astype(half_type)
        .reshape(tokens, D)
    )
    output = multiply(final_in, head_weight) + head_bias
    kept = dict(
        frequency=frequency,
        embed_pre=embed_pre,
        embed_hidden=embed_hidden,
        chosen=chosen,
        condition=condition,
        active=active,
        modulation=modulation,
        final_mod=final_mod,
        patches=patches,
        stream_in=stream_in,
        attn_in=attn_in,
        queries=queries,
        key_rows=key_rows,
        value_rows=value_rows,
        logsum=logsum,
        mixed_rows=mixed_rows,
        attended=attended,
        stream_mid=stream_mid,
        mlp_in=mlp_in,
        hidden_pre=hidden_pre,
        hidden=hidden,
        mlp_out=mlp_out,
        stream_out=stream_out,
        final_in=final_in,
    )
    return (output, kept)


def backward(gathered, master_small, kept, grad_output):
    (
        attend_weight,
        output_weight,
        up_weight,
        down_weight,
        modulate_weight,
        final_weight,
        embed_second,
        embed_first,
    ) = split_big(gathered)
    patch_weight, unused_table, head_weight = split_small(master_small.astype(half_type))
    images = kept["stream_in"].shape[0]
    tokens = images * SEQ
    shift_attn, scale_attn, gate_attn, shift_mlp, scale_mlp, gate_mlp = jnp.split(
        kept["modulation"][:, None, :], 6, axis=2
    )
    shift_final, scale_final = jnp.split(kept["final_mod"][:, None, :], 2, axis=2)
    grad_out = grad_output.astype(half_type)
    grad_head = outer_sum(kept["final_in"], grad_out)
    bias_head = column_sums(grad_out)
    grad_final = multiply_trans(grad_out, head_weight).reshape(images, SEQ, D)
    grad_shift_final = jnp.sum(grad_final, axis=1)
    grad_scale_final = jnp.sum(grad_final * normalize(kept["stream_out"]), axis=1)
    grad_stream = slope(normalize, kept["stream_out"], grad_final * (1.0 + scale_final))
    grad_gate_mlp = jnp.sum(grad_stream * kept["mlp_out"], axis=1)
    grad_mlp = (grad_stream * gate_mlp).reshape(tokens, D).astype(half_type)
    bias_down = column_sums(grad_mlp)
    grad_down = outer_sum(grad_mlp, kept["hidden"])
    grad_hidden = multiply(grad_mlp, down_weight)
    grad_pre = slope(gelu_tanh, kept["hidden_pre"], grad_hidden).astype(half_type)
    bias_up = column_sums(grad_pre)
    grad_up = outer_sum(kept["mlp_in"], grad_pre)
    grad_mlp_in = multiply_trans(grad_pre, up_weight).reshape(images, SEQ, D)
    grad_shift_mlp = jnp.sum(grad_mlp_in, axis=1)
    grad_scale_mlp = jnp.sum(grad_mlp_in * normalize(kept["stream_mid"]), axis=1)
    grad_stream = grad_stream + slope(
        normalize, kept["stream_mid"], grad_mlp_in * (1.0 + scale_mlp)
    )
    grad_gate_attn = jnp.sum(grad_stream * kept["attended"], axis=1)
    grad_attn = (grad_stream * gate_attn).reshape(tokens, D).astype(half_type)
    bias_output = column_sums(grad_attn)
    grad_output_weight = outer_sum(kept["mixed_rows"], grad_attn)
    grad_mixed = (
        multiply_trans(grad_attn, output_weight)
        .astype(half_type)
        .reshape(images, SEQ, HEADS, HEAD_DIM)
    )
    inverse_root = 1.0 / math.sqrt(HEAD_DIM)
    scores = (
        jnp.einsum(
            "nqhd,nkhd->nhqk", kept["queries"], kept["key_rows"], preferred_element_type=jnp.float32
        )
        * inverse_root
    )
    probs = jnp.exp(scores - kept["logsum"])
    grad_values = jnp.einsum(
        "nhqk,nqhd->nkhd", probs.astype(half_type), grad_mixed, preferred_element_type=jnp.float32
    )
    grad_probs = jnp.einsum(
        "nqhd,nkhd->nhqk", grad_mixed, kept["value_rows"], preferred_element_type=jnp.float32
    )
    grad_scores = (
        probs * (grad_probs - jnp.sum(probs * grad_probs, axis=-1, keepdims=True))
    ).astype(half_type)
    grad_queries = (
        jnp.einsum(
            "nhqk,nkhd->nqhd", grad_scores, kept["key_rows"], preferred_element_type=jnp.float32
        )
        * inverse_root
    )
    grad_keys = (
        jnp.einsum(
            "nhqk,nqhd->nkhd", grad_scores, kept["queries"], preferred_element_type=jnp.float32
        )
        * inverse_root
    )
    grad_qkv = jnp.concatenate(
        [
            grad_queries.reshape(tokens, D),
            grad_keys.reshape(tokens, D),
            grad_values.reshape(tokens, D),
        ],
        axis=1,
    ).astype(half_type)
    bias_query = column_sums(grad_qkv[:, :D])
    bias_value = column_sums(grad_qkv[:, 2 * D :])
    grad_attend = outer_sum(kept["attn_in"], grad_qkv)
    grad_attn_in = multiply_trans(grad_qkv, attend_weight).reshape(images, SEQ, D)
    grad_shift_attn = jnp.sum(grad_attn_in, axis=1)
    grad_scale_attn = jnp.sum(grad_attn_in * normalize(kept["stream_in"]), axis=1)
    grad_stream = grad_stream + slope(
        normalize, kept["stream_in"], grad_attn_in * (1.0 + scale_attn)
    )
    grad_start = grad_stream.reshape(tokens, D).astype(half_type)
    bias_patch = column_sums(grad_start)
    grad_patch = outer_sum(grad_start, kept["patches"])
    grad_mod = jnp.concatenate(
        [
            grad_shift_attn,
            grad_scale_attn,
            grad_gate_attn,
            grad_shift_mlp,
            grad_scale_mlp,
            grad_gate_mlp,
        ],
        axis=1,
    ).astype(half_type)
    grad_fmod = jnp.concatenate([grad_shift_final, grad_scale_final], axis=1).astype(half_type)
    bias_modulate = column_sums(grad_mod)
    bias_final = column_sums(grad_fmod)
    grad_modulate = outer_sum(kept["active"], grad_mod)
    grad_final_weight = outer_sum(kept["active"], grad_fmod)
    grad_active = multiply_trans(grad_mod, modulate_weight) + multiply_trans(
        grad_fmod, final_weight
    )
    grad_condition = slope(jax.nn.silu, kept["condition"], grad_active)
    grad_embed = grad_condition.astype(half_type)
    bias_second = column_sums(grad_embed)
    grad_second = outer_sum(kept["embed_hidden"], grad_embed)
    grad_embed_hidden = multiply_trans(grad_embed, embed_second)
    grad_embed_pre = slope(jax.nn.silu, kept["embed_pre"], grad_embed_hidden).astype(half_type)
    bias_first = column_sums(grad_embed_pre)
    grad_first = outer_sum(grad_embed_pre, kept["frequency"])
    grad_big = jnp.concatenate(
        [
            grad_attend,
            grad_output_weight,
            grad_up,
            grad_down,
            grad_modulate,
            grad_final_weight,
            grad_second,
            grad_first,
        ],
        axis=1,
    )
    grad_small = (grad_patch, grad_head, grad_condition)
    grad_bias = jnp.concatenate(
        [
            bias_query,
            bias_value,
            bias_output,
            bias_up,
            bias_down,
            bias_modulate,
            bias_final,
            bias_second,
            bias_first,
            bias_patch,
            bias_head,
        ]
    )
    return (grad_big, grad_small, grad_bias)


def on_device(
    noisy_patches,
    targets,
    timesteps,
    labels,
    master_big,
    moment_big,
    error_big,
    factor_right,
    master_small,
    moment_small,
    biases,
    moment_bias,
    step_rates,
):
    shards = lax.axis_size("shard")
    replicas = lax.axis_size("rep")
    gathered = lax.all_gather(master_big.astype(half_type), "shard", axis=1, tiled=True)
    output, kept = forward(gathered, master_small, biases, noisy_patches, timesteps, labels)
    entries = noisy_patches.shape[0] * shards * replicas * SEQ * P_DIM
    error = output - targets.reshape(output.shape)
    loss_part = jnp.sum(error * error) / entries
    grad_output = 2.0 * error / entries
    gathered = lax.all_gather(master_big.astype(half_type), "shard", axis=1, tiled=True)
    grad_big, (grad_patch, grad_head, grad_condition), grad_bias = backward(
        gathered, master_small, kept, grad_output
    )
    grad_table = jnp.einsum("nd,nc->dc", grad_condition, kept["chosen"], precision=highest)
    grad_small = jnp.concatenate([grad_patch, grad_table, grad_head], axis=1)
    owned = lax.psum_scatter(
        grad_big.astype(jnp.bfloat16), "shard", scatter_dimension=1, tiled=True
    ).astype(jnp.float32)
    matrices = owned + error_big[0]
    left_part = jnp.dot(
        matrices, factor_right, precision=highest, preferred_element_type=jnp.float32
    )
    small_sum, bias_sum, total_loss = lax.psum((grad_small, grad_bias, loss_part), ("shard", "rep"))
    left_sum = lax.psum(left_part, "rep")
    basis = orthonormal(left_sum)
    right_sum = lax.psum(exact_outer(matrices, basis).astype(jnp.bfloat16), "rep").astype(
        jnp.float32
    )
    approx = lax.dot_general(
        basis,
        right_sum,
        (((1,), (1,)), ((), ())),
        precision=highest,
        preferred_element_type=jnp.float32,
    )
    new_error = (matrices - approx / replicas)[None]
    new_moment = momentum_decay * moment_big + approx
    new_master = master_big - step_rates[0] * new_moment
    new_moment_small = momentum_decay * moment_small + small_sum
    new_master_small = master_small - step_rates[1] * new_moment_small
    new_moment_bias = momentum_decay * moment_bias + bias_sum
    new_biases = biases - step_rates[1] * new_moment_bias
    return (
        total_loss,
        new_master,
        new_moment,
        new_error,
        right_sum,
        new_master_small,
        new_moment_small,
        new_biases,
        new_moment_bias,
    )


MESH = pl.DeviceIdType.MESH
BLOCK = 512
RANK = 8
LANES = 128
REPS = 16


def sds(shape, dtype=jnp.float32):
    return jax.ShapeDtypeStruct(shape, dtype)


def split_two(values):
    high = values.astype(half_type)
    low = (values - high.astype(jnp.float32)).astype(half_type)
    return high, low


def greet(others):
    barrier = pltpu.get_barrier_semaphore()
    for other in others:
        pl.semaphore_signal(barrier, inc=1, device_id=other, device_id_type=MESH)
    return barrier, len(others)


def small_kernel(
    sums_ref, rows_ref, total_ref, gathered_ref, half_ref, part_ref, mine_ref, send_sem, recv_sem
):
    shard = lax.axis_index("shard")
    rep = lax.axis_index("rep")
    partner = (1 - shard, rep)
    peers = [(shard, lax.rem(rep + step, REPS)) for step in range(1, REPS)]
    barrier, count = greet([partner] + peers)
    pl.semaphore_wait(barrier, count)

    def remote(source, target, where, who):
        return pltpu.make_async_remote_copy(
            src_ref=source,
            dst_ref=target,
            send_sem=send_sem.at[where],
            recv_sem=recv_sem.at[where],
            device_id=who,
            device_id_type=MESH,
        )

    rows_out = [
        pltpu.make_async_remote_copy(
            src_ref=rows_ref,
            dst_ref=gathered_ref.at[shard, rep],
            send_sem=send_sem.at[step],
            recv_sem=recv_sem.at[rep],
            device_id=peers[step - 1],
            device_id_type=MESH,
        )
        for step in range(1, REPS)
    ]
    own_half = remote(sums_ref.at[1 - shard], half_ref, 16, partner)
    own_half.start()
    for copy in rows_out:
        copy.start()
    gathered_ref[shard, rep] = rows_ref[...]
    own_half.wait()
    half_ref[...] = half_ref[...] + sums_ref[shard]
    parts_out = [
        pltpu.make_async_remote_copy(
            src_ref=half_ref.at[lax.rem(rep + step, REPS)],
            dst_ref=part_ref.at[rep],
            send_sem=send_sem.at[17 + step],
            recv_sem=recv_sem.at[17 + rep],
            device_id=peers[step - 1],
            device_id_type=MESH,
        )
        for step in range(1, REPS)
    ]
    for copy in parts_out:
        copy.start()
    part_ref[rep] = half_ref[rep]

    def arrived(slots, base):
        for step in range(1, REPS):
            other = lax.rem(rep + step, REPS)
            pltpu.make_async_remote_copy(
                src_ref=slots.at[other],
                dst_ref=slots.at[other],
                send_sem=send_sem.at[base],
                recv_sem=recv_sem.at[base + other],
                device_id=peers[step - 1],
                device_id_type=MESH,
            ).wait_recv()

    arrived(part_ref, 17)
    mine_ref[...] = jnp.sum(part_ref[...], axis=0)
    whole_out = [
        pltpu.make_async_remote_copy(
            src_ref=mine_ref,
            dst_ref=total_ref.at[shard, rep],
            send_sem=send_sem.at[33 + step],
            recv_sem=recv_sem.at[33 + rep],
            device_id=peers[step - 1],
            device_id_type=MESH,
        )
        for step in range(1, REPS)
    ]
    for copy in whole_out:
        copy.start()
    total_ref[shard, rep] = mine_ref[...]
    arrived(gathered_ref.at[shard], 0)
    rows_across = remote(gathered_ref.at[shard], gathered_ref.at[shard], 49, partner)
    rows_across.start()
    arrived(total_ref.at[shard], 33)
    total_across = remote(total_ref.at[shard], total_ref.at[shard], 50, partner)
    total_across.start()
    for copy in rows_out + parts_out + whole_out:
        copy.wait_send()
    rows_across.wait()
    total_across.wait()


def small_sums(sums, rows):
    return pl.pallas_call(
        small_kernel,
        out_shape=(sds((2, REPS) + sums.shape[2:]), sds((2, REPS) + rows.shape)),
        in_specs=[pl.BlockSpec(memory_space=pltpu.VMEM)] * 2,
        out_specs=[pl.BlockSpec(memory_space=pltpu.VMEM)] * 2,
        scratch_shapes=[
            pltpu.VMEM(sums.shape[1:], jnp.float32),
            pltpu.VMEM((REPS,) + sums.shape[2:], jnp.float32),
            pltpu.VMEM(sums.shape[2:], jnp.float32),
            pltpu.SemaphoreType.DMA((51,)),
            pltpu.SemaphoreType.DMA((51,)),
        ],
        compiler_params=pltpu.CompilerParams(
            collective_id=1, has_side_effects=True, vmem_limit_bytes=16 * 1024 * 1024
        ),
        name="small_sums",
    )(sums, rows)


def tail_kernel(
    own_hbm,
    recv_hbm,
    error_hbm,
    factor_ref,
    moment_hbm,
    m_ref,
    v_ref,
    whole_ref,
    basis_cols,
    own_ref,
    recv_ref,
    stack_ref,
    left_acc,
    left_ref,
    plane_ref,
    column_ref,
    basis_rows,
    send_ref,
    part_ref,
    mine_ref,
    load_sem,
    own_sem,
    recv_sem,
    moment_sem,
    left_send,
    left_recv,
    right_send,
    right_recv,
):
    blocks = m_ref.shape[0]
    shard = lax.axis_index("shard")
    rep = lax.axis_index("rep")
    peers = [(shard, lax.rem(rep + step, REPS)) for step in range(1, REPS)]
    barrier, count = greet(peers)

    def columns(block):
        return pl.ds(pl.multiple_of(block * BLOCK, BLOCK), BLOCK)

    def load_error(block):
        return pltpu.make_async_copy(
            error_hbm.at[0, :, columns(block)], m_ref.at[block], load_sem.at[block]
        )

    def load_own(block, slot):
        return pltpu.make_async_copy(
            own_hbm.at[:, columns(block)], own_ref.at[slot], own_sem.at[slot]
        )

    def load_recv(block, slot):
        return pltpu.make_async_copy(
            recv_hbm.at[:, columns(block)], recv_ref.at[slot], recv_sem.at[slot]
        )

    def load_moment(block):
        return pltpu.make_async_copy(
            moment_hbm.at[:, columns(block)], v_ref.at[block], moment_sem.at[block]
        )

    depth = own_ref.shape[0]

    for block in range(depth):
        load_error(block).start()
        load_own(block, block).start()
        load_recv(block, block).start()

    high, low = split_two(factor_ref[...])
    stack_ref[...] = jnp.zeros_like(stack_ref)
    stack_ref[0:RANK] = high
    stack_ref[RANK : 2 * RANK] = low
    left_acc[...] = jnp.zeros_like(left_acc)

    def gather_block(block, carry):
        slot = lax.rem(block, depth)
        load_error(block).wait()
        load_own(block, slot).wait()
        load_recv(block, slot).wait()
        matrix = (
            own_ref[slot].astype(jnp.float32) + recv_ref[slot].astype(jnp.float32) + m_ref[block]
        )
        m_ref[block] = matrix
        high, low = split_two(matrix)
        factor = stack_ref[:, columns(block)]
        left_acc[...] += multiply_trans(high, factor) + multiply_trans(low, factor)

        @pl.when(block + depth < blocks)
        def _():
            load_error(block + depth).start()
            load_own(block + depth, slot).start()
            load_recv(block + depth, slot).start()

        return carry

    lax.fori_loop(0, blocks, gather_block, 0)
    for block in range(v_ref.shape[0]):
        load_moment(block).start()

    turned = left_acc[...].T
    left_ref[...] = turned[0:RANK] + turned[RANK : 2 * RANK]
    pl.semaphore_wait(barrier, count)

    place = lax.rem(rep, 4)
    level = lax.div(rep, 4)
    plane_out = []
    for step in range(1, 4):
        other = lax.rem(place + step, 4)
        plane_out.append(
            pltpu.make_async_remote_copy(
                src_ref=left_ref,
                dst_ref=plane_ref.at[place],
                send_sem=left_send.at[step],
                recv_sem=left_recv.at[place],
                device_id=(shard, level * 4 + other),
                device_id_type=MESH,
            )
        )
    for copy in plane_out:
        copy.start()
    plane_ref[place] = left_ref[...]
    for step in range(1, 4):
        other = lax.rem(place + step, 4)
        pltpu.make_async_remote_copy(
            src_ref=left_ref,
            dst_ref=plane_ref.at[other],
            send_sem=left_send.at[step],
            recv_sem=left_recv.at[other],
            device_id=(shard, level * 4 + other),
            device_id_type=MESH,
        ).wait_recv()
    plane_sum = (plane_ref[0] + plane_ref[1]) + (plane_ref[2] + plane_ref[3])
    for copy in plane_out:
        copy.wait_send()
    left_ref[...] = plane_sum
    column_out = []
    for step in range(1, 4):
        other = lax.rem(level + step, 4)
        column_out.append(
            pltpu.make_async_remote_copy(
                src_ref=left_ref,
                dst_ref=column_ref.at[level],
                send_sem=left_send.at[4 + step],
                recv_sem=left_recv.at[4 + level],
                device_id=(shard, other * 4 + place),
                device_id_type=MESH,
            )
        )
    for copy in column_out:
        copy.start()
    column_ref[level] = plane_sum
    for step in range(1, 4):
        other = lax.rem(level + step, 4)
        pltpu.make_async_remote_copy(
            src_ref=left_ref,
            dst_ref=column_ref.at[other],
            send_sem=left_send.at[4 + step],
            recv_sem=left_recv.at[4 + other],
            device_id=(shard, other * 4 + place),
            device_id_type=MESH,
        ).wait_recv()
    vectors = (column_ref[0] + column_ref[1]) + (column_ref[2] + column_ref[3])

    row_index = lax.broadcasted_iota(jnp.int32, (RANK, 1), 0)
    for place_of in range(RANK):
        row = vectors[place_of : place_of + 1]
        unit = row * lax.rsqrt(jnp.sum(row * row, axis=1, keepdims=True) + tiny_value)
        dots = jnp.sum(vectors * unit, axis=1, keepdims=True)
        vectors = jnp.where(
            row_index > place_of,
            vectors - dots * unit,
            jnp.where(row_index == place_of, unit, vectors),
        )
    high, low = split_two(vectors)
    basis_rows[...] = jnp.concatenate([high, low], axis=0)
    padded = jnp.concatenate(
        [
            high.astype(jnp.float32),
            low.astype(jnp.float32),
            jnp.zeros((LANES - 2 * RANK, vectors.shape[1]), jnp.float32),
        ],
        axis=0,
    )
    basis_cols[...] = padded.T.astype(half_type)
    for copy in column_out:
        copy.wait_send()

    def right_block(block, carry):
        high, low = split_two(m_ref[block])
        first = multiply(basis_rows[...], high)
        second = multiply(basis_rows[...], low)
        both = first + second
        send_ref[block] = (both[0:RANK] + both[RANK : 2 * RANK]).astype(half_type)
        return carry

    lax.fori_loop(0, blocks, right_block, 0)

    def right_copy(source, target, base, step, sender):
        return pltpu.make_async_remote_copy(
            src_ref=source,
            dst_ref=target,
            send_sem=right_send.at[base + step],
            recv_sem=right_recv.at[base + sender],
            device_id=peers[step - 1],
            device_id_type=MESH,
        )

    scatter = [
        right_copy(send_ref.at[lax.rem(rep + step, REPS)], part_ref.at[rep], 0, step, rep)
        for step in range(1, REPS)
    ]
    for copy in scatter:
        copy.start()
    part_ref[rep] = send_ref[rep]
    for step in range(1, REPS):
        other = lax.rem(rep + step, REPS)
        right_copy(send_ref.at[other], part_ref.at[other], 0, step, other).wait_recv()
    mine_ref[...] = jnp.sum(part_ref[...].astype(jnp.float32), axis=0).astype(half_type)
    spread = [
        right_copy(mine_ref, whole_ref.at[rep], REPS, step, rep) for step in range(1, REPS)
    ]
    for copy in spread:
        copy.start()
    whole_ref[rep] = mine_ref[...]
    for step in range(1, REPS):
        other = lax.rem(rep + step, REPS)
        right_copy(mine_ref, whole_ref.at[other], REPS, step, other).wait_recv()
    for copy in scatter + spread:
        copy.wait_send()
    for block in range(v_ref.shape[0]):
        load_moment(block).wait()


def update_kernel(
    rates_ref,
    m_ref,
    v_ref,
    whole_ref,
    basis_cols,
    moment_hbm,
    master_hbm,
    new_master_hbm,
    new_moment_hbm,
    new_error_hbm,
    right_ref,
    error_ref,
    moment_ref,
    master_ref,
    moment_sem,
    master_sem,
    error_out,
    moment_out,
    master_out,
):
    blocks = m_ref.shape[0]
    early = v_ref.shape[0]
    slots = master_ref.shape[0]
    rate = rates_ref[0]

    def columns(block):
        return pl.ds(pl.multiple_of(block * BLOCK, BLOCK), BLOCK)

    def load_master(block, slot):
        return pltpu.make_async_copy(
            master_hbm.at[:, columns(block)], master_ref.at[slot], master_sem.at[slot]
        )

    def load_moment(block, slot):
        return pltpu.make_async_copy(
            moment_hbm.at[:, columns(block)], moment_ref.at[slot], moment_sem.at[slot]
        )

    def out_error(block, slot):
        return pltpu.make_async_copy(
            error_ref.at[slot], new_error_hbm.at[0, :, columns(block)], error_out.at[slot]
        )

    def out_moment(block, slot):
        return pltpu.make_async_copy(
            moment_ref.at[slot], new_moment_hbm.at[:, columns(block)], moment_out.at[slot]
        )

    def out_master(block, slot):
        return pltpu.make_async_copy(
            master_ref.at[slot], new_master_hbm.at[:, columns(block)], master_out.at[slot]
        )

    ahead = slots - 2
    for block in range(ahead):
        load_master(block, block).start()

    def update_block(block, carry):
        slot = lax.rem(block, slots)
        next_slot = lax.rem(block + ahead, slots)

        @pl.when(block >= 2)
        def _():
            out_error(block - 2, next_slot).wait()
            out_moment(block - 2, next_slot).wait()
            out_master(block - 2, next_slot).wait()

        @pl.when(block + ahead < blocks)
        def _():
            load_master(block + ahead, next_slot).start()

            @pl.when(block + ahead >= early)
            def _():
                load_moment(block + ahead, next_slot).start()

        right = whole_ref[block]
        right_ref[:, columns(block)] = right.astype(jnp.float32)
        approx = multiply(basis_cols[:, 0 : 2 * RANK], jnp.concatenate([right, right], axis=0))
        error_ref[slot] = m_ref[block] - approx * (1.0 / REPS)
        out_error(block, slot).start()

        @pl.when(block < early)
        def _():
            moment_ref[slot] = momentum_decay * v_ref[jnp.minimum(block, early - 1)] + approx

        @pl.when(block >= early)
        def _():
            load_moment(block, slot).wait()
            moment_ref[slot] = momentum_decay * moment_ref[slot] + approx

        out_moment(block, slot).start()
        load_master(block, slot).wait()
        master_ref[slot] = master_ref[slot] - rate * moment_ref[slot]
        out_master(block, slot).start()
        return carry

    lax.fori_loop(0, blocks, update_block, 0)
    for block in range(blocks - 2, blocks):
        out_error(block, block % slots).wait()
        out_moment(block, block % slots).wait()
        out_master(block, block % slots).wait()


def compress(rates, own, received, error, factor_rows, moment, master):
    rows, cols = own.shape
    blocks = cols // BLOCK
    depth = 3
    slots = 4
    hbm = pl.BlockSpec(memory_space=pl.ANY)
    vmem = pl.BlockSpec(memory_space=pltpu.VMEM)
    matrices, moments, whole, basis = pl.pallas_call(
        tail_kernel,
        out_shape=(
            pltpu.VMEM((blocks, rows, BLOCK), jnp.float32),
            pltpu.VMEM((4, rows, BLOCK), jnp.float32),
            pltpu.VMEM((blocks, RANK, BLOCK), half_type),
            pltpu.VMEM((rows, LANES), half_type),
        ),
        in_specs=[hbm, hbm, hbm, vmem, hbm],
        out_specs=[vmem] * 4,
        scratch_shapes=[
            pltpu.VMEM((depth, rows, BLOCK), half_type),
            pltpu.VMEM((depth, rows, BLOCK), half_type),
            pltpu.VMEM((LANES, cols), half_type),
            pltpu.VMEM((rows, LANES), jnp.float32),
            pltpu.VMEM((RANK, rows), jnp.float32),
            pltpu.VMEM((4, RANK, rows), jnp.float32),
            pltpu.VMEM((4, RANK, rows), jnp.float32),
            pltpu.VMEM((2 * RANK, rows), half_type),
            pltpu.VMEM((blocks, RANK, BLOCK), half_type),
            pltpu.VMEM((blocks, RANK, BLOCK), half_type),
            pltpu.VMEM((RANK, BLOCK), half_type),
            pltpu.SemaphoreType.DMA((blocks,)),
            pltpu.SemaphoreType.DMA((depth,)),
            pltpu.SemaphoreType.DMA((depth,)),
            pltpu.SemaphoreType.DMA((blocks,)),
            pltpu.SemaphoreType.DMA((8,)),
            pltpu.SemaphoreType.DMA((8,)),
            pltpu.SemaphoreType.DMA((2 * REPS,)),
            pltpu.SemaphoreType.DMA((2 * REPS,)),
        ],
        compiler_params=pltpu.CompilerParams(
            collective_id=2, has_side_effects=True, vmem_limit_bytes=14_000_000
        ),
        name="compress",
    )(own, received, error, factor_rows, moment)
    return pl.pallas_call(
        update_kernel,
        out_shape=(
            sds(master.shape),
            sds(moment.shape),
            sds(error.shape),
            sds((RANK, cols)),
        ),
        in_specs=[pl.BlockSpec(memory_space=pltpu.SMEM), vmem, vmem, vmem, vmem, hbm, hbm],
        out_specs=[hbm, hbm, hbm, vmem],
        scratch_shapes=[
            pltpu.VMEM((slots, rows, BLOCK), jnp.float32),
            pltpu.VMEM((slots, rows, BLOCK), jnp.float32),
            pltpu.VMEM((slots, rows, BLOCK), jnp.float32),
            pltpu.SemaphoreType.DMA((slots,)),
            pltpu.SemaphoreType.DMA((slots,)),
            pltpu.SemaphoreType.DMA((slots,)),
            pltpu.SemaphoreType.DMA((slots,)),
            pltpu.SemaphoreType.DMA((slots,)),
        ],
        compiler_params=pltpu.CompilerParams(vmem_limit_bytes=24500000),
        name="update",
    )(rates, matrices, moments, whole, basis, moment, master)


GROUP = 2 * HEAD_DIM
CHUNK = 768


def unit_rows(values):
    center = values - jnp.mean(values, axis=-1, keepdims=True)
    inverse = lax.rsqrt(jnp.mean(center * center, axis=-1, keepdims=True) + epsilon)
    return center * inverse, inverse


def unit_back(unit, inverse, grad):
    return inverse * (
        grad
        - jnp.mean(grad, axis=-1, keepdims=True)
        - unit * jnp.mean(grad * unit, axis=-1, keepdims=True)
    )


def gelu_both(values):
    scale = math.sqrt(2.0 / math.pi)
    square = values * values
    bent = jnp.tanh(scale * (values + 0.044715 * (values * square)))
    half = 0.5 * (1.0 + bent)
    slope = half + 0.5 * values * (1.0 - bent * bent) * (scale * (1.0 + 0.134145 * square))
    return values * half, slope


def token_sum(values):
    return jnp.sum(values, axis=0, keepdims=True)


def image_kernel(
    entries,
    patches_ref,
    targets_ref,
    mods_ref,
    place_ref,
    patch_weight_ref,
    head_weight_ref,
    qkv_bias_ref,
    output_bias_ref,
    up_bias_ref,
    down_bias_ref,
    patch_bias_ref,
    head_bias_ref,
    weights_hbm,
    attn_in_ref,
    mixed_ref,
    mlp_in_ref,
    hidden_ref,
    grad_qkv_ref,
    grad_attn_ref,
    grad_pre_ref,
    grad_mlp_ref,
    mod_grad_ref,
    grad_patch_ref,
    grad_head_ref,
    bias_qkv_ref,
    bias_output_ref,
    bias_up_ref,
    bias_down_ref,
    bias_patch_ref,
    bias_head_ref,
    loss_ref,
    weight_ref,
    qkv_ref,
    probs_ref,
    slope_ref,
    unit_start_ref,
    unit_mid_ref,
    stream_ref,
    attended_ref,
    mlp_out_ref,
    grad_mixed_ref,
    total_ref,
    sem,
):
    image = pl.program_id(0)
    edges = [0, 3 * D, 4 * D, 4 * D + FF, 4 * D + 2 * FF]

    def load(part):
        span = slice(edges[part], edges[part + 1])
        return pltpu.make_async_copy(weights_hbm.at[:, span], weight_ref.at[:, span], sem.at[part])

    sums = [
        grad_patch_ref,
        grad_head_ref,
        bias_qkv_ref,
        bias_output_ref,
        bias_up_ref,
        bias_down_ref,
        bias_patch_ref,
        bias_head_ref,
        loss_ref,
    ]

    @pl.when(image == 0)
    def _():
        for part in range(4):
            load(part).start()
        for total in sums:
            total[...] = jnp.zeros_like(total)

    def arrived(part):
        @pl.when(image == 0)
        def _():
            load(part).wait()

    def modulation(place):
        return mods_ref[0, place : place + 1, :]

    def weight(first, width):
        return weight_ref[:, pl.ds(first, width)]

    patches = patches_ref[...]
    start = multiply(patches, patch_weight_ref[...]) + patch_bias_ref[...] + place_ref[...]
    stream_ref[...] = start
    unit, inverse_start = unit_rows(start)
    unit_start_ref[...] = unit
    attn_in_ref[...] = (unit * (1.0 + modulation(1)) + modulation(0)).astype(half_type)
    arrived(0)
    for part in range(3):
        span = slice(part * D, (part + 1) * D)
        qkv_ref[:, span] = (
            multiply(attn_in_ref[...], weight_ref[:, span]) + qkv_bias_ref[:, span]
        ).astype(half_type)

    scale = 1.0 / math.sqrt(HEAD_DIM)
    first_half = lax.broadcasted_iota(jnp.int32, (1, GROUP), 1) < HEAD_DIM

    def pair_slice(ref, part, pair):
        return ref[:, pl.ds(pl.multiple_of(part * D + pair * GROUP, GROUP), GROUP)]

    def halves(values):
        nothing = jnp.zeros_like(values)
        return jnp.where(first_half, values, nothing), jnp.where(first_half, nothing, values)

    def attend(pair, carry):
        queries = pair_slice(qkv_ref, 0, pair)
        keys = halves(pair_slice(qkv_ref, 1, pair))
        turned = pair_slice(qkv_ref, 2, pair).T
        rows = []
        for half in range(2):
            scores = multiply_trans(keys[half], queries) * scale
            weights = jnp.exp(scores - jnp.max(scores, axis=0, keepdims=True))
            probs = weights * (1.0 / jnp.sum(weights, axis=0, keepdims=True))
            probs_ref[2 * pair + half] = probs
            rows.append(
                multiply(
                    turned[half * HEAD_DIM : (half + 1) * HEAD_DIM], probs.astype(half_type)
                )
            )
        mixed_ref[:, pl.ds(pl.multiple_of(pair * GROUP, GROUP), GROUP)] = (
            jnp.concatenate(rows, axis=0).T.astype(half_type)
        )
        return carry

    lax.fori_loop(0, HEADS // 2, attend, 0)
    arrived(1)
    attended = multiply(mixed_ref[...], weight_ref[:, edges[1] : edges[2]]) + output_bias_ref[...]
    attended_ref[...] = attended
    middle = stream_ref[...] + modulation(2) * attended
    stream_ref[...] = middle
    unit, inverse_mid = unit_rows(middle)
    unit_mid_ref[...] = unit
    mlp_in_ref[...] = (unit * (1.0 + modulation(4)) + modulation(3)).astype(half_type)
    arrived(2)
    arrived(3)
    total_ref[...] = jnp.zeros_like(total_ref) + down_bias_ref[...]
    for part in range(FF // CHUNK):
        span = slice(part * CHUNK, (part + 1) * CHUNK)
        before = (
            multiply(mlp_in_ref[...], weight(edges[2] + part * CHUNK, CHUNK)) + up_bias_ref[:, span]
        )
        after, slope_part = gelu_both(before)
        slope_ref[:, span] = slope_part
        after = after.astype(half_type)
        hidden_ref[:, span] = after
        total_ref[...] += multiply_trans(after, weight(edges[3] + part * CHUNK, CHUNK))
    mlp_out_ref[...] = total_ref[...]
    unit, inverse_end = unit_rows(stream_ref[...] + modulation(5) * total_ref[...])
    final_in = (unit * (1.0 + modulation(7)) + modulation(6)).astype(half_type)
    error = (
        multiply_trans(final_in, head_weight_ref[...]) + head_bias_ref[...] - targets_ref[...]
    )
    loss_ref[...] += token_sum(error * error)
    grad_out = (error * (2.0 / entries)).astype(half_type)
    bias_head_ref[...] += token_sum(grad_out.astype(jnp.float32))
    grad_head_ref[...] += outer_sum(grad_out, final_in)

    grad_final = multiply(grad_out, head_weight_ref[...])
    mod_grad_ref[0, 6:7] = token_sum(grad_final)
    mod_grad_ref[0, 7:8] = token_sum(grad_final * unit)
    grad_stream = unit_back(unit, inverse_end, grad_final * (1.0 + modulation(7)))
    stream_ref[...] = grad_stream
    mod_grad_ref[0, 5:6] = token_sum(grad_stream * mlp_out_ref[...])
    grad_mlp = (grad_stream * modulation(5)).astype(half_type)
    grad_mlp_ref[...] = grad_mlp
    bias_down_ref[...] += token_sum(grad_mlp.astype(jnp.float32))
    total_ref[...] = jnp.zeros_like(total_ref)
    for part in range(FF // CHUNK):
        span = slice(part * CHUNK, (part + 1) * CHUNK)
        grad_pre = (
            multiply(grad_mlp_ref[...], weight(edges[3] + part * CHUNK, CHUNK)) * slope_ref[:, span]
        ).astype(half_type)
        grad_pre_ref[:, span] = grad_pre
        bias_up_ref[:, span] += token_sum(grad_pre.astype(jnp.float32))
        total_ref[...] += multiply_trans(grad_pre, weight(edges[2] + part * CHUNK, CHUNK))
    grad_in = total_ref[...]
    unit = unit_mid_ref[...]
    mod_grad_ref[0, 3:4] = token_sum(grad_in)
    mod_grad_ref[0, 4:5] = token_sum(grad_in * unit)
    grad_stream = stream_ref[...] + unit_back(unit, inverse_mid, grad_in * (1.0 + modulation(4)))
    stream_ref[...] = grad_stream
    mod_grad_ref[0, 2:3] = token_sum(grad_stream * attended_ref[...])
    grad_attn = (grad_stream * modulation(2)).astype(half_type)
    grad_attn_ref[...] = grad_attn
    bias_output_ref[...] += token_sum(grad_attn.astype(jnp.float32))
    grad_mixed_ref[...] = multiply_trans(grad_attn, weight_ref[:, edges[1] : edges[2]]).astype(
        half_type
    )

    def attend_back(pair, carry):
        queries = pair_slice(qkv_ref, 0, pair)
        keys_turned = pair_slice(qkv_ref, 1, pair).T
        values = halves(pair_slice(qkv_ref, 2, pair))
        grads = pair_slice(grad_mixed_ref, 0, pair)
        rows, key_grads, value_grads = [], [], []
        for half in range(2):
            probs = probs_ref[2 * pair + half]
            grad_probs = multiply_trans(values[half], grads)
            value_grads.append(multiply(probs.astype(half_type), grads))
            product = probs * grad_probs
            grad_scores = (product - probs * token_sum(product)).astype(half_type)
            key_grads.append(multiply(grad_scores, queries))
            rows.append(
                multiply(keys_turned[half * HEAD_DIM : (half + 1) * HEAD_DIM], grad_scores)
            )

        def put(part, values):
            grad_qkv_ref[:, pl.ds(pl.multiple_of(part * D + pair * GROUP, GROUP), GROUP)] = (
                values.astype(half_type)
            )

        put(0, jnp.concatenate(rows, axis=0).T * scale)
        put(1, jnp.where(first_half, key_grads[0], key_grads[1]) * scale)
        put(2, jnp.where(first_half, value_grads[0], value_grads[1]))
        return carry

    lax.fori_loop(0, HEADS // 2, attend_back, 0)
    bias_qkv_ref[...] += token_sum(grad_qkv_ref[...].astype(jnp.float32))
    grad_in = multiply_trans(grad_qkv_ref[...], weight_ref[:, : edges[1]])
    unit = unit_start_ref[...]
    mod_grad_ref[0, 0:1] = token_sum(grad_in)
    mod_grad_ref[0, 1:2] = token_sum(grad_in * unit)
    grad_start = (
        stream_ref[...] + unit_back(unit, inverse_start, grad_in * (1.0 + modulation(1)))
    ).astype(half_type)
    bias_patch_ref[...] += token_sum(grad_start.astype(jnp.float32))
    grad_patch_ref[...] += outer_sum(patches, grad_start)


def run_images(
    patches, targets, mods, places, patch_weight, head_weight, biases, gathered, entries
):
    images = mods.shape[0]
    tokens = images * SEQ
    wide = 4 * D + 2 * FF

    def rows(width):
        return pl.BlockSpec((SEQ, width), lambda image: (image, 0))

    def fixed(array):
        return pl.BlockSpec(array.shape, lambda image: (0,) * len(array.shape))

    vector = [(P_DIM, D), (P_DIM, D), (1, 3 * D), (1, D), (1, FF), (1, D), (1, D), (1, P_DIM)]
    vector = [sds(shape) for shape in vector + [(1, P_DIM)]]
    saved = [D, D, D, FF, 3 * D, D, FF, D]
    per_image = pl.BlockSpec((1, 8, D), lambda image: (image, 0, 0))
    return pl.pallas_call(
        functools.partial(image_kernel, entries),
        grid=(images,),
        out_shape=[sds((tokens, width), half_type) for width in saved]
        + [sds((images, 8, D))]
        + vector,
        in_specs=[rows(P_DIM), rows(P_DIM), per_image, fixed(places)]
        + [fixed(patch_weight), fixed(head_weight)]
        + [fixed(bias) for bias in biases]
        + [pl.BlockSpec(memory_space=pl.ANY)],
        out_specs=[rows(width) for width in saved] + [per_image] + [fixed(item) for item in vector],
        scratch_shapes=[
            pltpu.VMEM((D, wide), half_type),
            pltpu.VMEM((SEQ, 3 * D), half_type),
            pltpu.VMEM((HEADS, SEQ, SEQ), jnp.float32),
            pltpu.VMEM((SEQ, FF), jnp.float32),
            pltpu.VMEM((SEQ, D), jnp.float32),
            pltpu.VMEM((SEQ, D), jnp.float32),
            pltpu.VMEM((SEQ, D), jnp.float32),
            pltpu.VMEM((SEQ, D), jnp.float32),
            pltpu.VMEM((SEQ, D), jnp.float32),
            pltpu.VMEM((SEQ, D), half_type),
            pltpu.VMEM((SEQ, D), jnp.float32),
            pltpu.SemaphoreType.DMA((4,)),
        ],
        compiler_params=pltpu.CompilerParams(vmem_limit_bytes=60_000_000),
        name="images",
    )(patches, targets, mods, places, patch_weight, head_weight, *biases, gathered)


def train_gradients(gathered, master_small, biases, noisy_patches, targets, timesteps, labels, entries):
    edges = [0, 3 * D, 4 * D, 4 * D + FF, 4 * D + 2 * FF]
    pieces = split_big(gathered)
    modulate_weight, final_weight, embed_second, embed_first = pieces[4:]
    patch_weight, class_table, head_weight = split_small(master_small)
    (
        query_bias,
        value_bias,
        output_bias,
        up_bias,
        down_bias,
        modulate_bias,
        final_bias,
        second_bias,
        first_bias,
        patch_bias,
        head_bias,
    ) = split_bias(biases)
    images = noisy_patches.shape[0]
    frequency = timestep_features(timesteps).astype(half_type)
    embed_pre = multiply_trans(frequency, embed_first) + first_bias
    embed_hidden = jax.nn.silu(embed_pre).astype(half_type)
    time_embed = multiply(embed_hidden, embed_second) + second_bias
    chosen = (labels[:, None] == jnp.arange(NCLASS, dtype=jnp.int32)[None, :]).astype(jnp.float32)
    condition = time_embed + lax.dot_general(
        chosen,
        class_table,
        (((1,), (1,)), ((), ())),
        precision=highest,
        preferred_element_type=jnp.float32,
    )
    active = jax.nn.silu(condition).astype(half_type)
    both_weight = gathered[:, edges[4] : edges[4] + 8 * D]
    mods = multiply(active, both_weight) + jnp.concatenate([modulate_bias, final_bias])
    qkv_bias = jnp.concatenate([query_bias, jnp.zeros_like(query_bias), value_bias])
    (
        attn_in,
        mixed,
        mlp_in,
        hidden,
        grad_qkv,
        grad_attn,
        grad_pre,
        grad_mlp,
        mod_grads,
        grad_patch,
        grad_head,
        bias_qkv,
        bias_output,
        bias_up,
        bias_down,
        bias_patch,
        bias_head,
        losses,
    ) = run_images(
        noisy_patches.reshape(-1, P_DIM),
        targets.reshape(-1, P_DIM),
        mods.reshape(images, 8, D),
        position_table(),
        patch_weight.T.astype(half_type),
        head_weight.T.astype(half_type),
        [item[None] for item in (qkv_bias, output_bias, up_bias, down_bias, patch_bias, head_bias)],
        gathered,
        entries,
    )
    grad_mods = mod_grads.reshape(images, 8 * D).astype(half_type)
    bias_mods = column_sums(grad_mods)
    grad_active = multiply_trans(grad_mods, both_weight)
    grad_condition = slope(jax.nn.silu, condition, grad_active)
    grad_embed = grad_condition.astype(half_type)
    grad_embed_hidden = multiply_trans(grad_embed, embed_second)
    grad_embed_pre = slope(jax.nn.silu, embed_pre, grad_embed_hidden).astype(half_type)
    grad_big = jnp.concatenate(
        [
            outer_sum(attn_in, grad_qkv),
            outer_sum(mixed, grad_attn),
            outer_sum(mlp_in, grad_pre),
            outer_sum(grad_mlp, hidden),
            outer_sum(active, grad_mods),
            outer_sum(embed_hidden, grad_embed),
            outer_sum(grad_embed_pre, frequency),
        ],
        axis=1,
    )
    grad_bias = jnp.concatenate(
        [
            bias_qkv[0, :D],
            bias_qkv[0, 2 * D :],
            bias_output[0],
            bias_up[0],
            bias_down[0],
            bias_mods,
            column_sums(grad_embed),
            column_sums(grad_embed_pre),
            bias_patch[0],
            bias_head[0],
        ]
    )
    loss_part = jnp.sum(losses) / entries
    return grad_big, grad_patch, grad_head, grad_condition, grad_bias, loss_part


def on_pair(
    noisy_patches,
    targets,
    timesteps,
    labels,
    master_big,
    moment_big,
    error_big,
    factor_right,
    master_small,
    moment_small,
    biases,
    moment_bias,
    step_rates,
):
    shards = lax.axis_size("shard")
    replicas = lax.axis_size("rep")
    gathered = lax.all_gather(master_big.astype(half_type), "shard", axis=1, tiled=True)
    entries = noisy_patches.shape[0] * shards * replicas * SEQ * P_DIM
    grad_big, grad_patch, grad_head, grad_condition, grad_bias, loss_part = train_gradients(
        gathered, master_small, biases, noisy_patches, targets, timesteps, labels, entries
    )
    shard = lax.axis_index("shard")
    cols = master_big.shape[1]
    low_grad = grad_big.astype(half_type)
    own = lax.dynamic_slice_in_dim(low_grad, shard * cols, cols, axis=1)
    received = lax.ppermute(
        lax.dynamic_slice_in_dim(low_grad, (1 - shard) * cols, cols, axis=1),
        "shard",
        [(0, 1), (1, 0)],
    )
    images = labels.shape[0]
    flat = jnp.concatenate(
        [
            grad_patch.reshape(-1),
            grad_head.reshape(-1),
            grad_bias,
            loss_part[None],
        ]
    )
    width = shards * replicas * 16 * LANES
    sums = jnp.pad(flat, (0, width - flat.shape[0])).reshape(shards, replicas, 16, LANES)
    lines = images * D // LANES
    rows = jnp.concatenate(
        [
            grad_condition.reshape(lines, LANES),
            jnp.pad(labels.astype(jnp.float32)[None], ((0, 7), (0, LANES - images))),
        ]
    )
    total, all_rows = small_sums(sums, rows)
    total = total.reshape(-1)
    all_labels = all_rows[:, :, lines, :images].reshape(-1).astype(jnp.int32)
    conditions = all_rows[:, :, :lines, :].reshape(-1, D)
    chosen = (jnp.arange(NCLASS, dtype=jnp.int32)[:, None] == all_labels[None, :]).astype(
        jnp.float32
    )
    table_rows = jnp.dot(chosen, conditions, precision=highest, preferred_element_type=jnp.float32)
    strip = P_DIM * D
    small_sum = jnp.concatenate(
        [total[:strip].reshape(P_DIM, D), table_rows, total[strip : 2 * strip].reshape(P_DIM, D)]
    ).T
    bias_count = biases.shape[0]
    bias_sum = total[2 * strip : 2 * strip + bias_count]
    total_loss = total[2 * strip + bias_count]
    new_moment_small = momentum_decay * moment_small + small_sum
    new_master_small = master_small - step_rates[1] * new_moment_small
    new_moment_bias = momentum_decay * moment_bias + bias_sum
    new_biases = biases - step_rates[1] * new_moment_bias
    factor_rows, *small = lax.optimization_barrier(
        (
            factor_right.T,
            total_loss,
            new_master_small,
            new_moment_small,
            new_biases,
            new_moment_bias,
        )
    )
    total_loss, new_master_small, new_moment_small, new_biases, new_moment_bias = small
    new_master, new_moment, new_error, right_rows = compress(
        step_rates, own, received, error_big, factor_rows, moment_big, master_big
    )
    return (
        total_loss,
        new_master,
        new_moment,
        new_error,
        right_rows.T,
        new_master_small,
        new_moment_small,
        new_biases,
        new_moment_bias,
    )


def solution(mesh):
    in_specs = (
        P(("shard", "rep"), None),
        P(("shard", "rep"), None),
        P(("shard", "rep")),
        P(("shard", "rep")),
        P(None, "shard"),
        P(None, "shard"),
        P("rep", None, "shard"),
        P("shard", None),
        P(),
        P(),
        P(),
        P(),
        P(),
    )
    out_specs = (
        P(),
        P(None, "shard"),
        P(None, "shard"),
        P("rep", None, "shard"),
        P("shard", None),
        P(),
        P(),
        P(),
        P(),
    )
    fits = mesh.shape["shard"] == 2 and mesh.shape["rep"] == 16
    return jax.shard_map(
        on_pair if fits else on_device, mesh=mesh, in_specs=in_specs, out_specs=out_specs, check_vma=False
    )
```

```python
import functools
import math

import jax
import jax.numpy as jnp
from jax import lax
from jax.experimental import pallas as pl
from jax.experimental.pallas import tpu as pltpu
from jax.sharding import PartitionSpec as P

D = 768
HEADS = 12
HEAD_DIM = 64
FF = 3072
GRID = 16
FREQ = 256
NCLASS = 1000
P_DIM = 16
SEQ = 256


highest = lax.Precision.HIGHEST
epsilon = 1e-06
tiny_value = 1e-30
momentum_decay = 0.9
half_type = jnp.bfloat16


def multiply(left_side, right_side):
    return jnp.dot(left_side, right_side, preferred_element_type=jnp.float32)


def multiply_trans(left_side, right_side):
    return lax.dot_general(
        left_side, right_side, (((1,), (1,)), ((), ())), preferred_element_type=jnp.float32
    )


def outer_sum(left_side, right_side):
    return lax.dot_general(
        left_side, right_side, (((0,), (0,)), ((), ())), preferred_element_type=jnp.float32
    )


def exact_outer(left_side, right_side):
    return lax.dot_general(
        left_side,
        right_side,
        (((0,), (0,)), ((), ())),
        precision=highest,
        preferred_element_type=jnp.float32,
    )


def normalize(values):
    center = values - jnp.mean(values, axis=-1, keepdims=True)
    return center * lax.rsqrt(jnp.mean(center * center, axis=-1, keepdims=True) + epsilon)


def gelu_tanh(values):
    return jax.nn.gelu(values, approximate=True)


def slope(function, values, grad):
    unused, pullback = jax.vjp(function, values)
    return pullback(grad)[0]


def timestep_features(steps):
    half_count = FREQ // 2
    freqs = jnp.exp(-math.log(10000.0) * jnp.arange(half_count, dtype=jnp.float32) / half_count)
    angles = steps.astype(jnp.float32)[:, None] * freqs[None, :]
    return jnp.concatenate([jnp.cos(angles), jnp.sin(angles)], axis=1)


def position_table():
    quarter = D // 4
    omega = 1.0 / 10000.0 ** (jnp.arange(quarter, dtype=jnp.float32) / quarter)
    cells = jnp.arange(SEQ, dtype=jnp.int32)
    across = (cells % GRID).astype(jnp.float32)[:, None] * omega[None, :]
    downward = (cells // GRID).astype(jnp.float32)[:, None] * omega[None, :]
    return jnp.concatenate(
        [jnp.sin(across), jnp.cos(across), jnp.sin(downward), jnp.cos(downward)], axis=1
    )


def split_at(matrix, edges):
    return tuple((matrix[..., edges[place] : edges[place + 1]] for place in range(len(edges) - 1)))


def split_big(matrix):
    return split_at(
        matrix,
        [
            0,
            3 * D,
            4 * D,
            4 * D + FF,
            4 * D + 2 * FF,
            10 * D + 2 * FF,
            12 * D + 2 * FF,
            13 * D + 2 * FF,
            13 * D + 2 * FF + FREQ,
        ],
    )


def split_small(matrix):
    return split_at(matrix, [0, P_DIM, P_DIM + NCLASS, 2 * P_DIM + NCLASS])


def split_bias(vector):
    return split_at(
        vector,
        [
            0,
            D,
            2 * D,
            3 * D,
            3 * D + FF,
            4 * D + FF,
            10 * D + FF,
            12 * D + FF,
            13 * D + FF,
            14 * D + FF,
            15 * D + FF,
            15 * D + FF + P_DIM,
        ],
    )


def orthonormal(factor):
    columns = []
    for place in range(factor.shape[-1]):
        vector = factor[..., place]
        for earlier in columns:
            vector = vector - jnp.sum(earlier * vector, axis=-1, keepdims=True) * earlier
        vector = vector * lax.rsqrt(jnp.sum(vector * vector, axis=-1, keepdims=True) + tiny_value)
        columns.append(vector)
    return jnp.stack(columns, axis=-1)


def column_sums(grad):
    return jnp.sum(grad.astype(jnp.float32), axis=0)


def forward(gathered, master_small, biases, noisy_patches, timesteps, labels):
    (
        attend_weight,
        output_weight,
        up_weight,
        down_weight,
        modulate_weight,
        final_weight,
        embed_second,
        embed_first,
    ) = split_big(gathered)
    patch_weight, unused_table, head_weight = split_small(master_small.astype(half_type))
    class_table = split_small(master_small)[1]
    (
        query_bias,
        value_bias,
        output_bias,
        up_bias,
        down_bias,
        modulate_bias,
        final_bias,
        second_bias,
        first_bias,
        patch_bias,
        head_bias,
    ) = split_bias(biases)
    images = noisy_patches.shape[0]
    tokens = images * SEQ
    frequency = timestep_features(timesteps).astype(half_type)
    embed_pre = multiply_trans(frequency, embed_first) + first_bias
    embed_hidden = jax.nn.silu(embed_pre).astype(half_type)
    time_embed = multiply(embed_hidden, embed_second) + second_bias
    chosen = (labels[:, None] == jnp.arange(NCLASS, dtype=jnp.int32)[None, :]).astype(jnp.float32)
    condition = time_embed + lax.dot_general(
        chosen,
        class_table,
        (((1,), (1,)), ((), ())),
        precision=highest,
        preferred_element_type=jnp.float32,
    )
    active = jax.nn.silu(condition).astype(half_type)
    modulation = multiply(active, modulate_weight) + modulate_bias
    final_mod = multiply(active, final_weight) + final_bias
    patches = noisy_patches.reshape(tokens, P_DIM)
    stream_in = (multiply_trans(patches, patch_weight) + patch_bias).reshape(
        images, SEQ, D
    ) + position_table()[None]
    shift_attn, scale_attn, gate_attn, shift_mlp, scale_mlp, gate_mlp = jnp.split(
        modulation[:, None, :], 6, axis=2
    )
    shift_final, scale_final = jnp.split(final_mod[:, None, :], 2, axis=2)
    attn_in = (
        (normalize(stream_in) * (1.0 + scale_attn) + shift_attn)
        .astype(half_type)
        .reshape(tokens, D)
    )
    qkv_bias = jnp.concatenate([query_bias, jnp.zeros_like(query_bias), value_bias])
    projected = (multiply(attn_in, attend_weight) + qkv_bias).astype(half_type)
    queries, key_rows, value_rows = [
        piece.reshape(images, SEQ, HEADS, HEAD_DIM) for piece in jnp.split(projected, 3, axis=1)
    ]
    scores = jnp.einsum(
        "nqhd,nkhd->nhqk", queries, key_rows, preferred_element_type=jnp.float32
    ) / math.sqrt(HEAD_DIM)
    highest_score = jnp.max(scores, axis=-1, keepdims=True)
    logsum = highest_score + jnp.log(
        jnp.sum(jnp.exp(scores - highest_score), axis=-1, keepdims=True)
    )
    probs_low = jnp.exp(scores - logsum).astype(half_type)
    mixed_rows = (
        jnp.einsum("nhqk,nkhd->nqhd", probs_low, value_rows, preferred_element_type=jnp.float32)
        .astype(half_type)
        .reshape(tokens, D)
    )
    attended = (multiply(mixed_rows, output_weight) + output_bias).reshape(images, SEQ, D)
    stream_mid = stream_in + gate_attn * attended
    mlp_in = (
        (normalize(stream_mid) * (1.0 + scale_mlp) + shift_mlp).astype(half_type).reshape(tokens, D)
    )
    hidden_pre = multiply(mlp_in, up_weight) + up_bias
    hidden = gelu_tanh(hidden_pre).astype(half_type)
    mlp_out = (multiply_trans(hidden, down_weight) + down_bias).reshape(images, SEQ, D)
    stream_out = stream_mid + gate_mlp * mlp_out
    final_in = (
        (normalize(stream_out) * (1.0 + scale_final) + shift_final)
        .astype(half_type)
        .reshape(tokens, D)
    )
    output = multiply(final_in, head_weight) + head_bias
    kept = dict(
        frequency=frequency,
        embed_pre=embed_pre,
        embed_hidden=embed_hidden,
        chosen=chosen,
        condition=condition,
        active=active,
        modulation=modulation,
        final_mod=final_mod,
        patches=patches,
        stream_in=stream_in,
        attn_in=attn_in,
        queries=queries,
        key_rows=key_rows,
        value_rows=value_rows,
        logsum=logsum,
        mixed_rows=mixed_rows,
        attended=attended,
        stream_mid=stream_mid,
        mlp_in=mlp_in,
        hidden_pre=hidden_pre,
        hidden=hidden,
        mlp_out=mlp_out,
        stream_out=stream_out,
        final_in=final_in,
    )
    return (output, kept)


def backward(gathered, master_small, kept, grad_output):
    (
        attend_weight,
        output_weight,
        up_weight,
        down_weight,
        modulate_weight,
        final_weight,
        embed_second,
        embed_first,
    ) = split_big(gathered)
    patch_weight, unused_table, head_weight = split_small(master_small.astype(half_type))
    images = kept["stream_in"].shape[0]
    tokens = images * SEQ
    shift_attn, scale_attn, gate_attn, shift_mlp, scale_mlp, gate_mlp = jnp.split(
        kept["modulation"][:, None, :], 6, axis=2
    )
    shift_final, scale_final = jnp.split(kept["final_mod"][:, None, :], 2, axis=2)
    grad_out = grad_output.astype(half_type)
    grad_head = outer_sum(kept["final_in"], grad_out)
    bias_head = column_sums(grad_out)
    grad_final = multiply_trans(grad_out, head_weight).reshape(images, SEQ, D)
    grad_shift_final = jnp.sum(grad_final, axis=1)
    grad_scale_final = jnp.sum(grad_final * normalize(kept["stream_out"]), axis=1)
    grad_stream = slope(normalize, kept["stream_out"], grad_final * (1.0 + scale_final))
    grad_gate_mlp = jnp.sum(grad_stream * kept["mlp_out"], axis=1)
    grad_mlp = (grad_stream * gate_mlp).reshape(tokens, D).astype(half_type)
    bias_down = column_sums(grad_mlp)
    grad_down = outer_sum(grad_mlp, kept["hidden"])
    grad_hidden = multiply(grad_mlp, down_weight)
    grad_pre = slope(gelu_tanh, kept["hidden_pre"], grad_hidden).astype(half_type)
    bias_up = column_sums(grad_pre)
    grad_up = outer_sum(kept["mlp_in"], grad_pre)
    grad_mlp_in = multiply_trans(grad_pre, up_weight).reshape(images, SEQ, D)
    grad_shift_mlp = jnp.sum(grad_mlp_in, axis=1)
    grad_scale_mlp = jnp.sum(grad_mlp_in * normalize(kept["stream_mid"]), axis=1)
    grad_stream = grad_stream + slope(
        normalize, kept["stream_mid"], grad_mlp_in * (1.0 + scale_mlp)
    )
    grad_gate_attn = jnp.sum(grad_stream * kept["attended"], axis=1)
    grad_attn = (grad_stream * gate_attn).reshape(tokens, D).astype(half_type)
    bias_output = column_sums(grad_attn)
    grad_output_weight = outer_sum(kept["mixed_rows"], grad_attn)
    grad_mixed = (
        multiply_trans(grad_attn, output_weight)
        .astype(half_type)
        .reshape(images, SEQ, HEADS, HEAD_DIM)
    )
    inverse_root = 1.0 / math.sqrt(HEAD_DIM)
    scores = (
        jnp.einsum(
            "nqhd,nkhd->nhqk", kept["queries"], kept["key_rows"], preferred_element_type=jnp.float32
        )
        * inverse_root
    )
    probs = jnp.exp(scores - kept["logsum"])
    grad_values = jnp.einsum(
        "nhqk,nqhd->nkhd", probs.astype(half_type), grad_mixed, preferred_element_type=jnp.float32
    )
    grad_probs = jnp.einsum(
        "nqhd,nkhd->nhqk", grad_mixed, kept["value_rows"], preferred_element_type=jnp.float32
    )
    grad_scores = (
        probs * (grad_probs - jnp.sum(probs * grad_probs, axis=-1, keepdims=True))
    ).astype(half_type)
    grad_queries = (
        jnp.einsum(
            "nhqk,nkhd->nqhd", grad_scores, kept["key_rows"], preferred_element_type=jnp.float32
        )
        * inverse_root
    )
    grad_keys = (
        jnp.einsum(
            "nhqk,nqhd->nkhd", grad_scores, kept["queries"], preferred_element_type=jnp.float32
        )
        * inverse_root
    )
    grad_qkv = jnp.concatenate(
        [
            grad_queries.reshape(tokens, D),
            grad_keys.reshape(tokens, D),
            grad_values.reshape(tokens, D),
        ],
        axis=1,
    ).astype(half_type)
    bias_query = column_sums(grad_qkv[:, :D])
    bias_value = column_sums(grad_qkv[:, 2 * D :])
    grad_attend = outer_sum(kept["attn_in"], grad_qkv)
    grad_attn_in = multiply_trans(grad_qkv, attend_weight).reshape(images, SEQ, D)
    grad_shift_attn = jnp.sum(grad_attn_in, axis=1)
    grad_scale_attn = jnp.sum(grad_attn_in * normalize(kept["stream_in"]), axis=1)
    grad_stream = grad_stream + slope(
        normalize, kept["stream_in"], grad_attn_in * (1.0 + scale_attn)
    )
    grad_start = grad_stream.reshape(tokens, D).astype(half_type)
    bias_patch = column_sums(grad_start)
    grad_patch = outer_sum(grad_start, kept["patches"])
    grad_mod = jnp.concatenate(
        [
            grad_shift_attn,
            grad_scale_attn,
            grad_gate_attn,
            grad_shift_mlp,
            grad_scale_mlp,
            grad_gate_mlp,
        ],
        axis=1,
    ).astype(half_type)
    grad_fmod = jnp.concatenate([grad_shift_final, grad_scale_final], axis=1).astype(half_type)
    bias_modulate = column_sums(grad_mod)
    bias_final = column_sums(grad_fmod)
    grad_modulate = outer_sum(kept["active"], grad_mod)
    grad_final_weight = outer_sum(kept["active"], grad_fmod)
    grad_active = multiply_trans(grad_mod, modulate_weight) + multiply_trans(
        grad_fmod, final_weight
    )
    grad_condition = slope(jax.nn.silu, kept["condition"], grad_active)
    grad_embed = grad_condition.astype(half_type)
    bias_second = column_sums(grad_embed)
    grad_second = outer_sum(kept["embed_hidden"], grad_embed)
    grad_embed_hidden = multiply_trans(grad_embed, embed_second)
    grad_embed_pre = slope(jax.nn.silu, kept["embed_pre"], grad_embed_hidden).astype(half_type)
    bias_first = column_sums(grad_embed_pre)
    grad_first = outer_sum(grad_embed_pre, kept["frequency"])
    grad_big = jnp.concatenate(
        [
            grad_attend,
            grad_output_weight,
            grad_up,
            grad_down,
            grad_modulate,
            grad_final_weight,
            grad_second,
            grad_first,
        ],
        axis=1,
    )
    grad_small = (grad_patch, grad_head, grad_condition)
    grad_bias = jnp.concatenate(
        [
            bias_query,
            bias_value,
            bias_output,
            bias_up,
            bias_down,
            bias_modulate,
            bias_final,
            bias_second,
            bias_first,
            bias_patch,
            bias_head,
        ]
    )
    return (grad_big, grad_small, grad_bias)


def on_device(
    noisy_patches,
    targets,
    timesteps,
    labels,
    master_big,
    moment_big,
    error_big,
    factor_right,
    master_small,
    moment_small,
    biases,
    moment_bias,
    step_rates,
):
    shards = lax.axis_size("shard")
    replicas = lax.axis_size("rep")
    gathered = lax.all_gather(master_big.astype(half_type), "shard", axis=1, tiled=True)
    output, kept = forward(gathered, master_small, biases, noisy_patches, timesteps, labels)
    entries = noisy_patches.shape[0] * shards * replicas * SEQ * P_DIM
    error = output - targets.reshape(output.shape)
    loss_part = jnp.sum(error * error) / entries
    grad_output = 2.0 * error / entries
    gathered = lax.all_gather(master_big.astype(half_type), "shard", axis=1, tiled=True)
    grad_big, (grad_patch, grad_head, grad_condition), grad_bias = backward(
        gathered, master_small, kept, grad_output
    )
    grad_table = jnp.einsum("nd,nc->dc", grad_condition, kept["chosen"], precision=highest)
    grad_small = jnp.concatenate([grad_patch, grad_table, grad_head], axis=1)
    owned = lax.psum_scatter(
        grad_big.astype(jnp.bfloat16), "shard", scatter_dimension=1, tiled=True
    ).astype(jnp.float32)
    matrices = owned + error_big[0]
    left_part = jnp.dot(
        matrices, factor_right, precision=highest, preferred_element_type=jnp.float32
    )
    small_sum, bias_sum, total_loss = lax.psum((grad_small, grad_bias, loss_part), ("shard", "rep"))
    left_sum = lax.psum(left_part, "rep")
    basis = orthonormal(left_sum)
    right_sum = lax.psum(exact_outer(matrices, basis).astype(jnp.bfloat16), "rep").astype(
        jnp.float32
    )
    approx = lax.dot_general(
        basis,
        right_sum,
        (((1,), (1,)), ((), ())),
        precision=highest,
        preferred_element_type=jnp.float32,
    )
    new_error = (matrices - approx / replicas)[None]
    new_moment = momentum_decay * moment_big + approx
    new_master = master_big - step_rates[0] * new_moment
    new_moment_small = momentum_decay * moment_small + small_sum
    new_master_small = master_small - step_rates[1] * new_moment_small
    new_moment_bias = momentum_decay * moment_bias + bias_sum
    new_biases = biases - step_rates[1] * new_moment_bias
    return (
        total_loss,
        new_master,
        new_moment,
        new_error,
        right_sum,
        new_master_small,
        new_moment_small,
        new_biases,
        new_moment_bias,
    )


MESH = pl.DeviceIdType.MESH
BLOCK = 512
PIECE = 256
EARLY = 10
KERNEL_BYTES = 18_000_000
EXCHANGE_BYTES = 36_000_000
RANK = 8
LANES = 128
REPS = 16


def sds(shape, dtype=jnp.float32):
    return jax.ShapeDtypeStruct(shape, dtype)


def split_two(values):
    high = values.astype(half_type)
    low = (values - high.astype(jnp.float32)).astype(half_type)
    return high, low


def greet(others):
    barrier = pltpu.get_barrier_semaphore()
    for other in others:
        pl.semaphore_signal(barrier, inc=1, device_id=other, device_id_type=MESH)
    return barrier, len(others)


def tail_kernel(
    grad_hbm,
    error_hbm,
    factor_ref,
    moment_hbm,
    sums_ref,
    rows_ref,
    v_ref,
    whole_ref,
    basis_cols,
    total_ref,
    gathered_ref,
    recv_hbm,
    m_hbm,
    m_ref,
    own_ref,
    recv_ref,
    stack_ref,
    left_acc,
    left_ref,
    plane_ref,
    column_ref,
    basis_rows,
    send_ref,
    part_ref,
    mine_ref,
    half_ref,
    share_ref,
    small_ref,
    load_sem,
    own_sem,
    recv_sem,
    moment_sem,
    left_send,
    left_recv,
    right_send,
    right_recv,
    grad_send,
    grad_recv,
    small_send,
    small_recv,
    m_sem,
):
    blocks = m_ref.shape[0]
    cols = recv_hbm.shape[1]
    shard = lax.axis_index("shard")
    rep = lax.axis_index("rep")
    partner = (1 - shard, rep)
    peers = [(shard, lax.rem(rep + step, REPS)) for step in range(1, REPS)]
    barrier, count = greet([partner] + peers)

    def columns(block):
        return pl.ds(pl.multiple_of(block * BLOCK, BLOCK), BLOCK)

    def part_columns(part, block):
        return pl.ds(pl.multiple_of(part * cols + block * BLOCK, BLOCK), BLOCK)

    def send_grad(block):
        return pltpu.make_async_remote_copy(
            src_ref=grad_hbm.at[:, part_columns(1 - shard, block)],
            dst_ref=recv_hbm.at[:, columns(block)],
            send_sem=grad_send.at[block],
            recv_sem=grad_recv.at[block],
            device_id=partner,
            device_id_type=MESH,
        )

    def small_copy(source, target, sent, got, who):
        return pltpu.make_async_remote_copy(
            src_ref=source,
            dst_ref=target,
            send_sem=small_send.at[sent],
            recv_sem=small_recv.at[got],
            device_id=who,
            device_id_type=MESH,
        )

    def arrived(slots, base):
        for step in range(1, REPS):
            other = lax.rem(rep + step, REPS)
            small_copy(
                slots.at[other], slots.at[other], base, base + other, peers[step - 1]
            ).wait_recv()

    def load_error(block):
        return pltpu.make_async_copy(
            error_hbm.at[0, :, columns(block)], m_ref.at[block], load_sem.at[block]
        )

    def load_own(block, slot):
        return pltpu.make_async_copy(
            grad_hbm.at[:, part_columns(shard, block)], own_ref.at[slot], own_sem.at[slot]
        )

    def load_recv(block, slot):
        return pltpu.make_async_copy(
            recv_hbm.at[:, columns(block)], recv_ref.at[slot], recv_sem.at[slot]
        )

    def save_matrix(block):
        return pltpu.make_async_copy(m_ref.at[block], m_hbm.at[block], m_sem.at[block])

    def load_moment(block):
        return pltpu.make_async_copy(
            moment_hbm.at[:, columns(block)], v_ref.at[block], moment_sem.at[block]
        )

    depth = own_ref.shape[0]

    for block in range(depth):
        load_error(block).start()
        load_own(block, block).start()
    pl.semaphore_wait(barrier, count)
    own_half = small_copy(sums_ref.at[1 - shard], half_ref, 16, 16, partner)
    own_half.start()
    for block in range(blocks):
        send_grad(block).start()
    rows_out = [
        small_copy(rows_ref, gathered_ref.at[shard, rep], step, rep, peers[step - 1])
        for step in range(1, REPS)
    ]
    for copy in rows_out:
        copy.start()
    gathered_ref[shard, rep] = rows_ref[...]

    high, low = split_two(factor_ref[...])
    stack_ref[...] = jnp.zeros_like(stack_ref)
    stack_ref[0:RANK] = high
    stack_ref[RANK : 2 * RANK] = low
    left_acc[...] = jnp.zeros_like(left_acc)
    for block in range(depth):
        send_grad(block).wait_recv()
        load_recv(block, block).start()

    def gather_block(block, carry):
        slot = lax.rem(block, depth)
        load_error(block).wait()
        load_own(block, slot).wait()
        load_recv(block, slot).wait()
        matrix = (
            own_ref[slot].astype(jnp.float32) + recv_ref[slot].astype(jnp.float32) + m_ref[block]
        )
        m_ref[block] = matrix
        save_matrix(block).start()
        high, low = split_two(matrix)
        factor = stack_ref[:, columns(block)]
        left_acc[...] += multiply_trans(high, factor) + multiply_trans(low, factor)

        @pl.when(block + depth < blocks)
        def _():
            load_error(block + depth).start()
            load_own(block + depth, slot).start()
            send_grad(block + depth).wait_recv()
            load_recv(block + depth, slot).start()

        return carry

    lax.fori_loop(0, blocks // 2, gather_block, 0)
    own_half.wait()
    half_ref[...] = half_ref[...] + sums_ref[shard]
    shares_out = [
        small_copy(
            half_ref.at[lax.rem(rep + step, REPS)],
            share_ref.at[rep],
            17 + step,
            17 + rep,
            peers[step - 1],
        )
        for step in range(1, REPS)
    ]
    for copy in shares_out:
        copy.start()
    share_ref[rep] = half_ref[rep]
    lax.fori_loop(blocks // 2, blocks, gather_block, 0)
    for block in range(v_ref.shape[0]):
        load_moment(block).start()

    turned = left_acc[...].T
    left_ref[...] = turned[0:RANK] + turned[RANK : 2 * RANK]

    place = lax.rem(rep, 4)
    level = lax.div(rep, 4)
    plane_out = []
    for step in range(1, 4):
        other = lax.rem(place + step, 4)
        plane_out.append(
            pltpu.make_async_remote_copy(
                src_ref=left_ref,
                dst_ref=plane_ref.at[place],
                send_sem=left_send.at[step],
                recv_sem=left_recv.at[place],
                device_id=(shard, level * 4 + other),
                device_id_type=MESH,
            )
        )
    for copy in plane_out:
        copy.start()
    plane_ref[place] = left_ref[...]
    arrived(share_ref, 17)
    small_ref[...] = jnp.sum(share_ref[...], axis=0)
    whole_out = [
        small_copy(small_ref, total_ref.at[shard, rep], 33 + step, 33 + rep, peers[step - 1])
        for step in range(1, REPS)
    ]
    for copy in whole_out:
        copy.start()
    total_ref[shard, rep] = small_ref[...]
    for step in range(1, 4):
        other = lax.rem(place + step, 4)
        pltpu.make_async_remote_copy(
            src_ref=left_ref,
            dst_ref=plane_ref.at[other],
            send_sem=left_send.at[step],
            recv_sem=left_recv.at[other],
            device_id=(shard, level * 4 + other),
            device_id_type=MESH,
        ).wait_recv()
    plane_sum = (plane_ref[0] + plane_ref[1]) + (plane_ref[2] + plane_ref[3])
    for copy in plane_out:
        copy.wait_send()
    left_ref[...] = plane_sum
    column_out = []
    for step in range(1, 4):
        other = lax.rem(level + step, 4)
        column_out.append(
            pltpu.make_async_remote_copy(
                src_ref=left_ref,
                dst_ref=column_ref.at[level],
                send_sem=left_send.at[4 + step],
                recv_sem=left_recv.at[4 + level],
                device_id=(shard, other * 4 + place),
                device_id_type=MESH,
            )
        )
    for copy in column_out:
        copy.start()
    column_ref[level] = plane_sum
    for step in range(1, 4):
        other = lax.rem(level + step, 4)
        pltpu.make_async_remote_copy(
            src_ref=left_ref,
            dst_ref=column_ref.at[other],
            send_sem=left_send.at[4 + step],
            recv_sem=left_recv.at[4 + other],
            device_id=(shard, other * 4 + place),
            device_id_type=MESH,
        ).wait_recv()
    vectors = (column_ref[0] + column_ref[1]) + (column_ref[2] + column_ref[3])

    row_index = lax.broadcasted_iota(jnp.int32, (RANK, 1), 0)
    for place_of in range(RANK):
        row = vectors[place_of : place_of + 1]
        unit = row * lax.rsqrt(jnp.sum(row * row, axis=1, keepdims=True) + tiny_value)
        dots = jnp.sum(vectors * unit, axis=1, keepdims=True)
        vectors = jnp.where(
            row_index > place_of,
            vectors - dots * unit,
            jnp.where(row_index == place_of, unit, vectors),
        )
    high, low = split_two(vectors)
    basis_rows[...] = jnp.concatenate([high, low], axis=0)
    padded = jnp.concatenate(
        [
            high.astype(jnp.float32),
            low.astype(jnp.float32),
            jnp.zeros((LANES - 2 * RANK, vectors.shape[1]), jnp.float32),
        ],
        axis=0,
    )
    basis_cols[...] = padded.T.astype(half_type)
    for copy in column_out:
        copy.wait_send()
    arrived(gathered_ref.at[shard], 0)
    rows_across = small_copy(gathered_ref.at[shard], gathered_ref.at[shard], 49, 49, partner)
    rows_across.start()
    arrived(total_ref.at[shard], 33)
    total_across = small_copy(total_ref.at[shard], total_ref.at[shard], 50, 50, partner)
    total_across.start()

    def right_block(block, carry):
        high, low = split_two(m_ref[block])
        first = multiply(basis_rows[...], high)
        second = multiply(basis_rows[...], low)
        both = first + second
        send_ref[block] = (both[0:RANK] + both[RANK : 2 * RANK]).astype(half_type)
        return carry

    lax.fori_loop(0, blocks, right_block, 0)

    def right_copy(source, target, base, step, sender):
        return pltpu.make_async_remote_copy(
            src_ref=source,
            dst_ref=target,
            send_sem=right_send.at[base + step],
            recv_sem=right_recv.at[base + sender],
            device_id=peers[step - 1],
            device_id_type=MESH,
        )

    scatter = [
        right_copy(send_ref.at[lax.rem(rep + step, REPS)], part_ref.at[rep], 0, step, rep)
        for step in range(1, REPS)
    ]
    for copy in scatter:
        copy.start()
    part_ref[rep] = send_ref[rep]
    for step in range(1, REPS):
        other = lax.rem(rep + step, REPS)
        right_copy(send_ref.at[other], part_ref.at[other], 0, step, other).wait_recv()
    mine_ref[...] = jnp.sum(part_ref[...].astype(jnp.float32), axis=0).astype(half_type)
    spread = [
        right_copy(mine_ref, whole_ref.at[rep], REPS, step, rep) for step in range(1, REPS)
    ]
    for copy in spread:
        copy.start()
    whole_ref[rep] = mine_ref[...]
    for step in range(1, REPS):
        other = lax.rem(rep + step, REPS)
        right_copy(mine_ref, whole_ref.at[other], REPS, step, other).wait_recv()
    for copy in scatter + spread + rows_out + shares_out + whole_out:
        copy.wait_send()
    for block in range(blocks):
        send_grad(block).wait_send()
        save_matrix(block).wait()
    rows_across.wait()
    total_across.wait()
    for block in range(v_ref.shape[0]):
        load_moment(block).wait()


def update_kernel(
    rates_ref,
    m_hbm,
    v_ref,
    whole_ref,
    basis_cols,
    moment_hbm,
    master_hbm,
    new_master_hbm,
    new_moment_hbm,
    new_error_hbm,
    right_ref,
    error_ref,
    moment_ref,
    master_ref,
    moment_sem,
    master_sem,
    matrix_sem,
    error_out,
    moment_out,
    master_out,
):
    pieces = BLOCK // PIECE
    blocks = m_hbm.shape[0] * pieces
    early = v_ref.shape[0] * pieces
    slots = master_ref.shape[0]
    rate = rates_ref[0]

    def columns(block):
        return pl.ds(pl.multiple_of(block * PIECE, PIECE), PIECE)

    def load_master(block, slot):
        return pltpu.make_async_copy(
            master_hbm.at[:, columns(block)], master_ref.at[slot], master_sem.at[slot]
        )

    def load_matrix(block, slot):
        return pltpu.make_async_copy(
            m_hbm.at[
                lax.div(block, pieces),
                :,
                pl.ds(pl.multiple_of(lax.rem(block, pieces) * PIECE, PIECE), PIECE),
            ],
            error_ref.at[slot],
            matrix_sem.at[slot],
        )

    def load_moment(block, slot):
        return pltpu.make_async_copy(
            moment_hbm.at[:, columns(block)], moment_ref.at[slot], moment_sem.at[slot]
        )

    def out_error(block, slot):
        return pltpu.make_async_copy(
            error_ref.at[slot], new_error_hbm.at[0, :, columns(block)], error_out.at[slot]
        )

    def out_moment(block, slot):
        return pltpu.make_async_copy(
            moment_ref.at[slot], new_moment_hbm.at[:, columns(block)], moment_out.at[slot]
        )

    def out_master(block, slot):
        return pltpu.make_async_copy(
            master_ref.at[slot], new_master_hbm.at[:, columns(block)], master_out.at[slot]
        )

    ahead = slots - 2
    for block in range(ahead):
        load_matrix(block, block).start()
        load_master(block, block).start()

    def update_piece(whole, piece):
        block = whole * pieces + piece
        span = slice(piece * PIECE, (piece + 1) * PIECE)
        slot = lax.rem(block, slots)
        next_slot = lax.rem(block + ahead, slots)

        @pl.when(block >= 2)
        def _():
            out_error(block - 2, next_slot).wait()
            out_moment(block - 2, next_slot).wait()
            out_master(block - 2, next_slot).wait()

        @pl.when(block + ahead < blocks)
        def _():
            load_matrix(block + ahead, next_slot).start()
            load_master(block + ahead, next_slot).start()

            @pl.when(block + ahead >= early)
            def _():
                load_moment(block + ahead, next_slot).start()

        right = whole_ref[whole, :, span]
        right_ref[:, columns(block)] = right.astype(jnp.float32)
        approx = multiply(basis_cols[:, 0 : 2 * RANK], jnp.concatenate([right, right], axis=0))
        load_matrix(block, slot).wait()
        error_ref[slot] = error_ref[slot] - approx * (1.0 / REPS)
        out_error(block, slot).start()

        @pl.when(block < early)
        def _():
            moment_ref[slot] = (
                momentum_decay * v_ref[jnp.minimum(whole, v_ref.shape[0] - 1), :, span] + approx
            )

        @pl.when(block >= early)
        def _():
            load_moment(block, slot).wait()
            moment_ref[slot] = momentum_decay * moment_ref[slot] + approx

        out_moment(block, slot).start()
        load_master(block, slot).wait()
        master_ref[slot] = master_ref[slot] - rate * moment_ref[slot]
        out_master(block, slot).start()

    def update_block(whole, carry):
        for piece in range(pieces):
            update_piece(whole, piece)
        return carry

    lax.fori_loop(0, m_hbm.shape[0], update_block, 0)
    for block in range(blocks - 2, blocks):
        out_error(block, block % slots).wait()
        out_moment(block, block % slots).wait()
        out_master(block, block % slots).wait()


def compress(rates, grads, error, factor_rows, moment, master, sums, lines):
    rows, cols = master.shape
    blocks = cols // BLOCK
    depth = 3
    slots = 6
    hbm = pl.BlockSpec(memory_space=pltpu.HBM)
    vmem = pl.BlockSpec(memory_space=pltpu.VMEM)
    moments, whole, basis, total, gathered, unused, matrices = pl.pallas_call(
        tail_kernel,
        out_shape=(
            pltpu.VMEM((EARLY, rows, BLOCK), jnp.float32),
            pltpu.VMEM((blocks, RANK, BLOCK), half_type),
            pltpu.VMEM((rows, LANES), half_type),
            sds((2, REPS) + sums.shape[2:]),
            sds((2, REPS) + lines.shape),
            pltpu.HBM((rows, cols), half_type),
            pltpu.HBM((blocks, rows, BLOCK), jnp.float32),
        ),
        in_specs=[hbm, hbm, vmem, hbm, vmem, vmem],
        out_specs=[vmem] * 5 + [pl.BlockSpec(memory_space=pltpu.HBM)] * 2,
        scratch_shapes=[
            pltpu.VMEM((blocks, rows, BLOCK), jnp.float32),
            pltpu.VMEM((depth, rows, BLOCK), half_type),
            pltpu.VMEM((depth, rows, BLOCK), half_type),
            pltpu.VMEM((LANES, cols), half_type),
            pltpu.VMEM((rows, LANES), jnp.float32),
            pltpu.VMEM((RANK, rows), jnp.float32),
            pltpu.VMEM((4, RANK, rows), jnp.float32),
            pltpu.VMEM((4, RANK, rows), jnp.float32),
            pltpu.VMEM((2 * RANK, rows), half_type),
            pltpu.VMEM((blocks, RANK, BLOCK), half_type),
            pltpu.VMEM((blocks, RANK, BLOCK), half_type),
            pltpu.VMEM((RANK, BLOCK), half_type),
            pltpu.VMEM(sums.shape[1:], jnp.float32),
            pltpu.VMEM(sums.shape[1:], jnp.float32),
            pltpu.VMEM(sums.shape[2:], jnp.float32),
            pltpu.SemaphoreType.DMA((blocks,)),
            pltpu.SemaphoreType.DMA((depth,)),
            pltpu.SemaphoreType.DMA((depth,)),
            pltpu.SemaphoreType.DMA((blocks,)),
            pltpu.SemaphoreType.DMA((8,)),
            pltpu.SemaphoreType.DMA((8,)),
            pltpu.SemaphoreType.DMA((2 * REPS,)),
            pltpu.SemaphoreType.DMA((2 * REPS,)),
            pltpu.SemaphoreType.DMA((blocks,)),
            pltpu.SemaphoreType.DMA((blocks,)),
            pltpu.SemaphoreType.DMA((51,)),
            pltpu.SemaphoreType.DMA((51,)),
            pltpu.SemaphoreType.DMA((blocks,)),
        ],
        compiler_params=pltpu.CompilerParams(
            collective_id=2, has_side_effects=True, vmem_limit_bytes=EXCHANGE_BYTES
        ),
        name="compress",
    )(grads, error, factor_rows, moment, sums, lines)
    updated = pl.pallas_call(
        update_kernel,
        out_shape=(
            sds(master.shape),
            sds(moment.shape),
            sds(error.shape),
            sds((RANK, cols)),
        ),
        in_specs=[pl.BlockSpec(memory_space=pltpu.SMEM), hbm, vmem, vmem, vmem, hbm, hbm],
        out_specs=[hbm, hbm, hbm, vmem],
        scratch_shapes=[
            pltpu.VMEM((slots, rows, PIECE), jnp.float32),
            pltpu.VMEM((slots, rows, PIECE), jnp.float32),
            pltpu.VMEM((slots, rows, PIECE), jnp.float32),
            pltpu.SemaphoreType.DMA((slots,)),
            pltpu.SemaphoreType.DMA((slots,)),
            pltpu.SemaphoreType.DMA((slots,)),
            pltpu.SemaphoreType.DMA((slots,)),
            pltpu.SemaphoreType.DMA((slots,)),
            pltpu.SemaphoreType.DMA((slots,)),
        ],
        compiler_params=pltpu.CompilerParams(vmem_limit_bytes=KERNEL_BYTES),
        name="update",
    )(rates, matrices, moments, whole, basis, moment, master)
    return lax.optimization_barrier((tuple(updated), total, gathered))


def small_kernel(
    rates_ref, sums_ref, lines_ref, moment_ref, master_ref, new_moment_ref, new_master_ref
):
    step = pl.program_id(0)
    height = moment_ref.shape[0]
    images = lines_ref.shape[0] * lines_ref.shape[1] * 8
    strips = D // LANES

    def piece(place):
        return lines_ref[:, :, place * 8 : (place + 1) * 8, :].reshape(images, LANES)

    labels = piece(strips)[:, 0:1]
    place = lax.broadcasted_iota(jnp.int32, (images, height), 1) + (step * height - P_DIM)
    chosen = (place.astype(jnp.float32) == labels).astype(half_type)
    for strip in range(strips):
        span = slice(strip * LANES, (strip + 1) * LANES)
        high, low = split_two(piece(strip))
        new_moment_ref[:, span] = (
            momentum_decay * moment_ref[:, span] + outer_sum(chosen, high) + outer_sum(chosen, low)
        )

    def add(first, base):
        for strip in range(strips):
            span = slice(strip * LANES, (strip + 1) * LANES)
            new_moment_ref[first : first + P_DIM, span] += sums_ref[
                base + strip * P_DIM : base + (strip + 1) * P_DIM, :
            ]

    @pl.when(step == 0)
    def _():
        add(0, 0)

    @pl.when(step == pl.num_programs(0) - 1)
    def _():
        add(height - P_DIM, strips * P_DIM)

    new_master_ref[...] = master_ref[...] - rates_ref[1] * new_moment_ref[...]


def update_small(rates, total, gathered, moment, master):
    rows = moment.shape[0]
    steps = 3
    vmem = pl.BlockSpec(memory_space=pltpu.VMEM)
    block = pl.BlockSpec((rows // steps, D), lambda step: (step, 0))
    return pl.pallas_call(
        small_kernel,
        grid=(steps,),
        out_shape=(sds(moment.shape), sds(master.shape)),
        in_specs=[pl.BlockSpec(memory_space=pltpu.SMEM), vmem, vmem, block, block],
        out_specs=[block, block],
        name="update_small",
    )(rates, total.reshape(-1, LANES), gathered, moment, master)


GROUP = 2 * HEAD_DIM
CHUNK = 768


def unit_rows(values):
    center = values - jnp.mean(values, axis=-1, keepdims=True)
    inverse = lax.rsqrt(jnp.mean(center * center, axis=-1, keepdims=True) + epsilon)
    return center * inverse, inverse


def unit_back(unit, inverse, grad):
    return inverse * (
        grad
        - jnp.mean(grad, axis=-1, keepdims=True)
        - unit * jnp.mean(grad * unit, axis=-1, keepdims=True)
    )


def gelu_both(values):
    scale = math.sqrt(2.0 / math.pi)
    square = values * values
    bent = jnp.tanh(scale * (values + 0.044715 * (values * square)))
    half = 0.5 * (1.0 + bent)
    slope = half + 0.5 * values * (1.0 - bent * bent) * (scale * (1.0 + 0.134145 * square))
    return values * half, slope


def token_sum(values):
    return jnp.sum(values, axis=0, keepdims=True)


def image_kernel(
    entries,
    patches_ref,
    targets_ref,
    mods_ref,
    place_ref,
    patch_weight_ref,
    head_weight_ref,
    qkv_bias_ref,
    output_bias_ref,
    up_bias_ref,
    down_bias_ref,
    patch_bias_ref,
    head_bias_ref,
    weights_hbm,
    attn_in_ref,
    mixed_ref,
    mlp_in_ref,
    hidden_ref,
    grad_qkv_ref,
    grad_attn_ref,
    grad_pre_ref,
    grad_mlp_ref,
    mod_grad_ref,
    grad_patch_ref,
    grad_head_ref,
    bias_qkv_ref,
    bias_output_ref,
    bias_up_ref,
    bias_down_ref,
    bias_patch_ref,
    bias_head_ref,
    loss_ref,
    weight_ref,
    qkv_ref,
    probs_ref,
    slope_ref,
    unit_start_ref,
    unit_mid_ref,
    stream_ref,
    attended_ref,
    mlp_out_ref,
    grad_mixed_ref,
    total_ref,
    sem,
):
    image = pl.program_id(0)
    edges = [0, 3 * D, 4 * D, 4 * D + FF, 4 * D + 2 * FF]

    def load(part):
        span = slice(edges[part], edges[part + 1])
        return pltpu.make_async_copy(weights_hbm.at[:, span], weight_ref.at[:, span], sem.at[part])

    sums = [
        grad_patch_ref,
        grad_head_ref,
        bias_qkv_ref,
        bias_output_ref,
        bias_up_ref,
        bias_down_ref,
        bias_patch_ref,
        bias_head_ref,
        loss_ref,
    ]

    @pl.when(image == 0)
    def _():
        for part in range(4):
            load(part).start()
        for total in sums:
            total[...] = jnp.zeros_like(total)

    def arrived(part):
        @pl.when(image == 0)
        def _():
            load(part).wait()

    def modulation(place):
        return mods_ref[0, place : place + 1, :]

    def weight(first, width):
        return weight_ref[:, pl.ds(first, width)]

    patches = patches_ref[...]
    start = multiply(patches, patch_weight_ref[...]) + patch_bias_ref[...] + place_ref[...]
    stream_ref[...] = start
    unit, inverse_start = unit_rows(start)
    unit_start_ref[...] = unit
    attn_in_ref[...] = (unit * (1.0 + modulation(1)) + modulation(0)).astype(half_type)
    arrived(0)
    for part in range(3):
        span = slice(part * D, (part + 1) * D)
        qkv_ref[:, span] = (
            multiply(attn_in_ref[...], weight_ref[:, span]) + qkv_bias_ref[:, span]
        ).astype(half_type)

    scale = 1.0 / math.sqrt(HEAD_DIM)
    first_half = lax.broadcasted_iota(jnp.int32, (1, GROUP), 1) < HEAD_DIM

    def pair_slice(ref, part, pair):
        return ref[:, pl.ds(pl.multiple_of(part * D + pair * GROUP, GROUP), GROUP)]

    def halves(values):
        nothing = jnp.zeros_like(values)
        return jnp.where(first_half, values, nothing), jnp.where(first_half, nothing, values)

    def attend(pair, carry):
        queries = pair_slice(qkv_ref, 0, pair)
        keys = halves(pair_slice(qkv_ref, 1, pair))
        turned = pair_slice(qkv_ref, 2, pair).T
        rows = []
        for half in range(2):
            scores = multiply_trans(keys[half], queries) * scale
            weights = jnp.exp(scores - jnp.max(scores, axis=0, keepdims=True))
            probs = weights * (1.0 / jnp.sum(weights, axis=0, keepdims=True))
            probs_ref[2 * pair + half] = probs
            rows.append(
                multiply(
                    turned[half * HEAD_DIM : (half + 1) * HEAD_DIM], probs.astype(half_type)
                )
            )
        mixed_ref[:, pl.ds(pl.multiple_of(pair * GROUP, GROUP), GROUP)] = (
            jnp.concatenate(rows, axis=0).T.astype(half_type)
        )
        return carry

    lax.fori_loop(0, HEADS // 2, attend, 0)
    arrived(1)
    attended = multiply(mixed_ref[...], weight_ref[:, edges[1] : edges[2]]) + output_bias_ref[...]
    attended_ref[...] = attended
    middle = stream_ref[...] + modulation(2) * attended
    stream_ref[...] = middle
    unit, inverse_mid = unit_rows(middle)
    unit_mid_ref[...] = unit
    mlp_in_ref[...] = (unit * (1.0 + modulation(4)) + modulation(3)).astype(half_type)
    arrived(2)
    arrived(3)
    total_ref[...] = jnp.zeros_like(total_ref) + down_bias_ref[...]
    for part in range(FF // CHUNK):
        span = slice(part * CHUNK, (part + 1) * CHUNK)
        before = (
            multiply(mlp_in_ref[...], weight(edges[2] + part * CHUNK, CHUNK)) + up_bias_ref[:, span]
        )
        after, slope_part = gelu_both(before)
        slope_ref[:, span] = slope_part
        after = after.astype(half_type)
        hidden_ref[:, span] = after
        total_ref[...] += multiply_trans(after, weight(edges[3] + part * CHUNK, CHUNK))
    mlp_out_ref[...] = total_ref[...]
    unit, inverse_end = unit_rows(stream_ref[...] + modulation(5) * total_ref[...])
    final_in = (unit * (1.0 + modulation(7)) + modulation(6)).astype(half_type)
    error = (
        multiply_trans(final_in, head_weight_ref[...]) + head_bias_ref[...] - targets_ref[...]
    )
    loss_ref[...] += token_sum(error * error)
    grad_out = (error * (2.0 / entries)).astype(half_type)
    bias_head_ref[...] += token_sum(grad_out.astype(jnp.float32))
    grad_head_ref[...] += outer_sum(grad_out, final_in)

    grad_final = multiply(grad_out, head_weight_ref[...])
    mod_grad_ref[0, 6:7] = token_sum(grad_final)
    mod_grad_ref[0, 7:8] = token_sum(grad_final * unit)
    grad_stream = unit_back(unit, inverse_end, grad_final * (1.0 + modulation(7)))
    stream_ref[...] = grad_stream
    mod_grad_ref[0, 5:6] = token_sum(grad_stream * mlp_out_ref[...])
    grad_mlp = (grad_stream * modulation(5)).astype(half_type)
    grad_mlp_ref[...] = grad_mlp
    bias_down_ref[...] += token_sum(grad_mlp.astype(jnp.float32))
    total_ref[...] = jnp.zeros_like(total_ref)
    for part in range(FF // CHUNK):
        span = slice(part * CHUNK, (part + 1) * CHUNK)
        grad_pre = (
            multiply(grad_mlp_ref[...], weight(edges[3] + part * CHUNK, CHUNK)) * slope_ref[:, span]
        ).astype(half_type)
        grad_pre_ref[:, span] = grad_pre
        bias_up_ref[:, span] += token_sum(grad_pre.astype(jnp.float32))
        total_ref[...] += multiply_trans(grad_pre, weight(edges[2] + part * CHUNK, CHUNK))
    grad_in = total_ref[...]
    unit = unit_mid_ref[...]
    mod_grad_ref[0, 3:4] = token_sum(grad_in)
    mod_grad_ref[0, 4:5] = token_sum(grad_in * unit)
    grad_stream = stream_ref[...] + unit_back(unit, inverse_mid, grad_in * (1.0 + modulation(4)))
    stream_ref[...] = grad_stream
    mod_grad_ref[0, 2:3] = token_sum(grad_stream * attended_ref[...])
    grad_attn = (grad_stream * modulation(2)).astype(half_type)
    grad_attn_ref[...] = grad_attn
    bias_output_ref[...] += token_sum(grad_attn.astype(jnp.float32))
    grad_mixed_ref[...] = multiply_trans(grad_attn, weight_ref[:, edges[1] : edges[2]]).astype(
        half_type
    )

    def attend_back(pair, carry):
        queries = pair_slice(qkv_ref, 0, pair)
        keys_turned = pair_slice(qkv_ref, 1, pair).T
        values = halves(pair_slice(qkv_ref, 2, pair))
        grads = pair_slice(grad_mixed_ref, 0, pair)
        rows, key_grads, value_grads = [], [], []
        for half in range(2):
            probs = probs_ref[2 * pair + half]
            grad_probs = multiply_trans(values[half], grads)
            value_grads.append(multiply(probs.astype(half_type), grads))
            product = probs * grad_probs
            grad_scores = (product - probs * token_sum(product)).astype(half_type)
            key_grads.append(multiply(grad_scores, queries))
            rows.append(
                multiply(keys_turned[half * HEAD_DIM : (half + 1) * HEAD_DIM], grad_scores)
            )

        def put(part, values):
            grad_qkv_ref[:, pl.ds(pl.multiple_of(part * D + pair * GROUP, GROUP), GROUP)] = (
                values.astype(half_type)
            )

        put(0, jnp.concatenate(rows, axis=0).T * scale)
        put(1, jnp.where(first_half, key_grads[0], key_grads[1]) * scale)
        put(2, jnp.where(first_half, value_grads[0], value_grads[1]))
        return carry

    lax.fori_loop(0, HEADS // 2, attend_back, 0)
    bias_qkv_ref[...] += token_sum(grad_qkv_ref[...].astype(jnp.float32))
    grad_in = multiply_trans(grad_qkv_ref[...], weight_ref[:, : edges[1]])
    unit = unit_start_ref[...]
    mod_grad_ref[0, 0:1] = token_sum(grad_in)
    mod_grad_ref[0, 1:2] = token_sum(grad_in * unit)
    grad_start = (
        stream_ref[...] + unit_back(unit, inverse_start, grad_in * (1.0 + modulation(1)))
    ).astype(half_type)
    bias_patch_ref[...] += token_sum(grad_start.astype(jnp.float32))
    grad_patch_ref[...] += outer_sum(patches, grad_start)


def run_images(
    patches, targets, mods, places, patch_weight, head_weight, biases, gathered, entries
):
    images = mods.shape[0]
    tokens = images * SEQ
    wide = 4 * D + 2 * FF

    def rows(width):
        return pl.BlockSpec((SEQ, width), lambda image: (image, 0))

    def fixed(array):
        return pl.BlockSpec(array.shape, lambda image: (0,) * len(array.shape))

    vector = [(P_DIM, D), (P_DIM, D), (1, 3 * D), (1, D), (1, FF), (1, D), (1, D), (1, P_DIM)]
    vector = [sds(shape) for shape in vector + [(1, P_DIM)]]
    saved = [D, D, D, FF, 3 * D, D, FF, D]
    per_image = pl.BlockSpec((1, 8, D), lambda image: (image, 0, 0))
    return pl.pallas_call(
        functools.partial(image_kernel, entries),
        grid=(images,),
        out_shape=[sds((tokens, width), half_type) for width in saved]
        + [sds((images, 8, D))]
        + vector,
        in_specs=[rows(P_DIM), rows(P_DIM), per_image, fixed(places)]
        + [fixed(patch_weight), fixed(head_weight)]
        + [fixed(bias) for bias in biases]
        + [pl.BlockSpec(memory_space=pl.ANY)],
        out_specs=[rows(width) for width in saved] + [per_image] + [fixed(item) for item in vector],
        scratch_shapes=[
            pltpu.VMEM((D, wide), half_type),
            pltpu.VMEM((SEQ, 3 * D), half_type),
            pltpu.VMEM((HEADS, SEQ, SEQ), jnp.float32),
            pltpu.VMEM((SEQ, FF), jnp.float32),
            pltpu.VMEM((SEQ, D), jnp.float32),
            pltpu.VMEM((SEQ, D), jnp.float32),
            pltpu.VMEM((SEQ, D), jnp.float32),
            pltpu.VMEM((SEQ, D), jnp.float32),
            pltpu.VMEM((SEQ, D), jnp.float32),
            pltpu.VMEM((SEQ, D), half_type),
            pltpu.VMEM((SEQ, D), jnp.float32),
            pltpu.SemaphoreType.DMA((4,)),
        ],
        compiler_params=pltpu.CompilerParams(vmem_limit_bytes=60_000_000),
        name="images",
    )(patches, targets, mods, places, patch_weight, head_weight, *biases, gathered)


def train_gradients(gathered, master_small, biases, noisy_patches, targets, timesteps, labels, entries):
    edges = [0, 3 * D, 4 * D, 4 * D + FF, 4 * D + 2 * FF]
    pieces = split_big(gathered)
    modulate_weight, final_weight, embed_second, embed_first = pieces[4:]
    patch_weight, class_table, head_weight = split_small(master_small)
    (
        query_bias,
        value_bias,
        output_bias,
        up_bias,
        down_bias,
        modulate_bias,
        final_bias,
        second_bias,
        first_bias,
        patch_bias,
        head_bias,
    ) = split_bias(biases)
    images = noisy_patches.shape[0]
    frequency = timestep_features(timesteps).astype(half_type)
    embed_pre = multiply_trans(frequency, embed_first) + first_bias
    embed_hidden = jax.nn.silu(embed_pre).astype(half_type)
    time_embed = multiply(embed_hidden, embed_second) + second_bias
    chosen = (labels[:, None] == jnp.arange(NCLASS, dtype=jnp.int32)[None, :]).astype(jnp.float32)
    condition = time_embed + lax.dot_general(
        chosen,
        class_table,
        (((1,), (1,)), ((), ())),
        precision=highest,
        preferred_element_type=jnp.float32,
    )
    active = jax.nn.silu(condition).astype(half_type)
    both_weight = gathered[:, edges[4] : edges[4] + 8 * D]
    mods = multiply(active, both_weight) + jnp.concatenate([modulate_bias, final_bias])
    qkv_bias = jnp.concatenate([query_bias, jnp.zeros_like(query_bias), value_bias])
    (
        attn_in,
        mixed,
        mlp_in,
        hidden,
        grad_qkv,
        grad_attn,
        grad_pre,
        grad_mlp,
        mod_grads,
        grad_patch,
        grad_head,
        bias_qkv,
        bias_output,
        bias_up,
        bias_down,
        bias_patch,
        bias_head,
        losses,
    ) = run_images(
        noisy_patches.reshape(-1, P_DIM),
        targets.reshape(-1, P_DIM),
        mods.reshape(images, 8, D),
        position_table(),
        patch_weight.T.astype(half_type),
        head_weight.T.astype(half_type),
        [item[None] for item in (qkv_bias, output_bias, up_bias, down_bias, patch_bias, head_bias)],
        gathered,
        entries,
    )
    grad_mods = mod_grads.reshape(images, 8 * D).astype(half_type)
    bias_mods = column_sums(grad_mods)
    grad_active = multiply_trans(grad_mods, both_weight)
    grad_condition = slope(jax.nn.silu, condition, grad_active)
    grad_embed = grad_condition.astype(half_type)
    grad_embed_hidden = multiply_trans(grad_embed, embed_second)
    grad_embed_pre = slope(jax.nn.silu, embed_pre, grad_embed_hidden).astype(half_type)
    grad_big = jnp.concatenate(
        [
            outer_sum(attn_in, grad_qkv),
            outer_sum(mixed, grad_attn),
            outer_sum(mlp_in, grad_pre),
            outer_sum(grad_mlp, hidden),
            outer_sum(active, grad_mods),
            outer_sum(embed_hidden, grad_embed),
            outer_sum(grad_embed_pre, frequency),
        ],
        axis=1,
    )
    grad_bias = jnp.concatenate(
        [
            bias_qkv[0, :D],
            bias_qkv[0, 2 * D :],
            bias_output[0],
            bias_up[0],
            bias_down[0],
            bias_mods,
            column_sums(grad_embed),
            column_sums(grad_embed_pre),
            bias_patch[0],
            bias_head[0],
        ]
    )
    loss_part = jnp.sum(losses) / entries
    return grad_big, grad_patch, grad_head, grad_condition, grad_bias, loss_part


def on_pair(
    noisy_patches,
    targets,
    timesteps,
    labels,
    master_big,
    moment_big,
    error_big,
    factor_right,
    master_small,
    moment_small,
    biases,
    moment_bias,
    step_rates,
):
    shards = lax.axis_size("shard")
    replicas = lax.axis_size("rep")
    gathered = lax.all_gather(master_big.astype(half_type), "shard", axis=1, tiled=True)
    entries = noisy_patches.shape[0] * shards * replicas * SEQ * P_DIM
    grad_big, grad_patch, grad_head, grad_condition, grad_bias, loss_part = train_gradients(
        gathered, master_small, biases, noisy_patches, targets, timesteps, labels, entries
    )
    images = labels.shape[0]
    strips = D // LANES

    def lines_of(matrix):
        return matrix.reshape(-1, strips, LANES).transpose(1, 0, 2)

    flat = jnp.concatenate(
        [
            lines_of(grad_patch).reshape(-1),
            lines_of(grad_head).reshape(-1),
            grad_bias,
            loss_part[None],
        ]
    )
    width = shards * replicas * 16 * LANES
    sums = jnp.pad(flat, (0, width - flat.shape[0])).reshape(shards, replicas, 16, LANES)
    label_lines = jnp.broadcast_to(labels.astype(jnp.float32)[None, :, None], (1, images, LANES))
    lines = jnp.concatenate(
        [
            jnp.pad(lines_of(grad_condition), ((0, 0), (0, 8 - images), (0, 0))),
            jnp.pad(label_lines, ((0, 0), (0, 8 - images), (0, 0)), constant_values=-100000.0),
        ]
    ).reshape(-1, LANES)
    (new_master, new_moment, new_error, right_rows), total, gathered_lines = compress(
        step_rates,
        grad_big.astype(half_type),
        error_big,
        factor_right.T,
        moment_big,
        master_big,
        sums,
        lines,
    )
    new_moment_small, new_master_small = update_small(
        step_rates, total, gathered_lines, moment_small.T, master_small.T
    )
    total = total.reshape(-1)
    bias_count = biases.shape[0]
    base = 2 * P_DIM * D
    total_loss = total[base + bias_count]
    new_moment_bias = momentum_decay * moment_bias + total[base : base + bias_count]
    new_biases = biases - step_rates[1] * new_moment_bias
    return (
        total_loss,
        new_master,
        new_moment,
        new_error,
        right_rows.T,
        new_master_small.T,
        new_moment_small.T,
        new_biases,
        new_moment_bias,
    )


def solution(mesh):
    in_specs = (
        P(("shard", "rep"), None),
        P(("shard", "rep"), None),
        P(("shard", "rep")),
        P(("shard", "rep")),
        P(None, "shard"),
        P(None, "shard"),
        P("rep", None, "shard"),
        P("shard", None),
        P(),
        P(),
        P(),
        P(),
        P(),
    )
    out_specs = (
        P(),
        P(None, "shard"),
        P(None, "shard"),
        P("rep", None, "shard"),
        P("shard", None),
        P(),
        P(),
        P(),
        P(),
    )
    fits = mesh.shape["shard"] == 2 and mesh.shape["rep"] == 16
    return jax.shard_map(
        on_pair if fits else on_device, mesh=mesh, in_specs=in_specs, out_specs=out_specs, check_vma=False
    )
```

```python
import functools
import math

import jax
import jax.numpy as jnp
from jax import lax
from jax.experimental import pallas as pl
from jax.experimental.pallas import tpu as pltpu
from jax.sharding import PartitionSpec as P

D = 768
HEADS = 12
HEAD_DIM = 64
FF = 3072
GRID = 16
FREQ = 256
NCLASS = 1000
P_DIM = 16
SEQ = 256


highest = lax.Precision.HIGHEST
epsilon = 1e-06
tiny_value = 1e-30
momentum_decay = 0.9
half_type = jnp.bfloat16


def multiply(left_side, right_side):
    return jnp.dot(left_side, right_side, preferred_element_type=jnp.float32)


def multiply_trans(left_side, right_side):
    return lax.dot_general(
        left_side, right_side, (((1,), (1,)), ((), ())), preferred_element_type=jnp.float32
    )


def outer_sum(left_side, right_side):
    return lax.dot_general(
        left_side, right_side, (((0,), (0,)), ((), ())), preferred_element_type=jnp.float32
    )


def exact_outer(left_side, right_side):
    return lax.dot_general(
        left_side,
        right_side,
        (((0,), (0,)), ((), ())),
        precision=highest,
        preferred_element_type=jnp.float32,
    )


def normalize(values):
    center = values - jnp.mean(values, axis=-1, keepdims=True)
    return center * lax.rsqrt(jnp.mean(center * center, axis=-1, keepdims=True) + epsilon)


def gelu_tanh(values):
    return jax.nn.gelu(values, approximate=True)


def slope(function, values, grad):
    unused, pullback = jax.vjp(function, values)
    return pullback(grad)[0]


def timestep_features(steps):
    half_count = FREQ // 2
    freqs = jnp.exp(-math.log(10000.0) * jnp.arange(half_count, dtype=jnp.float32) / half_count)
    angles = steps.astype(jnp.float32)[:, None] * freqs[None, :]
    return jnp.concatenate([jnp.cos(angles), jnp.sin(angles)], axis=1)


def position_table():
    quarter = D // 4
    omega = 1.0 / 10000.0 ** (jnp.arange(quarter, dtype=jnp.float32) / quarter)
    cells = jnp.arange(SEQ, dtype=jnp.int32)
    across = (cells % GRID).astype(jnp.float32)[:, None] * omega[None, :]
    downward = (cells // GRID).astype(jnp.float32)[:, None] * omega[None, :]
    return jnp.concatenate(
        [jnp.sin(across), jnp.cos(across), jnp.sin(downward), jnp.cos(downward)], axis=1
    )


def split_at(matrix, edges):
    return tuple((matrix[..., edges[place] : edges[place + 1]] for place in range(len(edges) - 1)))


def split_big(matrix):
    return split_at(
        matrix,
        [
            0,
            3 * D,
            4 * D,
            4 * D + FF,
            4 * D + 2 * FF,
            10 * D + 2 * FF,
            12 * D + 2 * FF,
            13 * D + 2 * FF,
            13 * D + 2 * FF + FREQ,
        ],
    )


def split_small(matrix):
    return split_at(matrix, [0, P_DIM, P_DIM + NCLASS, 2 * P_DIM + NCLASS])


def split_bias(vector):
    return split_at(
        vector,
        [
            0,
            D,
            2 * D,
            3 * D,
            3 * D + FF,
            4 * D + FF,
            10 * D + FF,
            12 * D + FF,
            13 * D + FF,
            14 * D + FF,
            15 * D + FF,
            15 * D + FF + P_DIM,
        ],
    )


def orthonormal(factor):
    columns = []
    for place in range(factor.shape[-1]):
        vector = factor[..., place]
        for earlier in columns:
            vector = vector - jnp.sum(earlier * vector, axis=-1, keepdims=True) * earlier
        vector = vector * lax.rsqrt(jnp.sum(vector * vector, axis=-1, keepdims=True) + tiny_value)
        columns.append(vector)
    return jnp.stack(columns, axis=-1)


def column_sums(grad):
    return jnp.sum(grad.astype(jnp.float32), axis=0)


def forward(gathered, master_small, biases, noisy_patches, timesteps, labels):
    (
        attend_weight,
        output_weight,
        up_weight,
        down_weight,
        modulate_weight,
        final_weight,
        embed_second,
        embed_first,
    ) = split_big(gathered)
    patch_weight, unused_table, head_weight = split_small(master_small.astype(half_type))
    class_table = split_small(master_small)[1]
    (
        query_bias,
        value_bias,
        output_bias,
        up_bias,
        down_bias,
        modulate_bias,
        final_bias,
        second_bias,
        first_bias,
        patch_bias,
        head_bias,
    ) = split_bias(biases)
    images = noisy_patches.shape[0]
    tokens = images * SEQ
    frequency = timestep_features(timesteps).astype(half_type)
    embed_pre = multiply_trans(frequency, embed_first) + first_bias
    embed_hidden = jax.nn.silu(embed_pre).astype(half_type)
    time_embed = multiply(embed_hidden, embed_second) + second_bias
    chosen = (labels[:, None] == jnp.arange(NCLASS, dtype=jnp.int32)[None, :]).astype(jnp.float32)
    condition = time_embed + lax.dot_general(
        chosen,
        class_table,
        (((1,), (1,)), ((), ())),
        precision=highest,
        preferred_element_type=jnp.float32,
    )
    active = jax.nn.silu(condition).astype(half_type)
    modulation = multiply(active, modulate_weight) + modulate_bias
    final_mod = multiply(active, final_weight) + final_bias
    patches = noisy_patches.reshape(tokens, P_DIM)
    stream_in = (multiply_trans(patches, patch_weight) + patch_bias).reshape(
        images, SEQ, D
    ) + position_table()[None]
    shift_attn, scale_attn, gate_attn, shift_mlp, scale_mlp, gate_mlp = jnp.split(
        modulation[:, None, :], 6, axis=2
    )
    shift_final, scale_final = jnp.split(final_mod[:, None, :], 2, axis=2)
    attn_in = (
        (normalize(stream_in) * (1.0 + scale_attn) + shift_attn)
        .astype(half_type)
        .reshape(tokens, D)
    )
    qkv_bias = jnp.concatenate([query_bias, jnp.zeros_like(query_bias), value_bias])
    projected = (multiply(attn_in, attend_weight) + qkv_bias).astype(half_type)
    queries, key_rows, value_rows = [
        piece.reshape(images, SEQ, HEADS, HEAD_DIM) for piece in jnp.split(projected, 3, axis=1)
    ]
    scores = jnp.einsum(
        "nqhd,nkhd->nhqk", queries, key_rows, preferred_element_type=jnp.float32
    ) / math.sqrt(HEAD_DIM)
    highest_score = jnp.max(scores, axis=-1, keepdims=True)
    logsum = highest_score + jnp.log(
        jnp.sum(jnp.exp(scores - highest_score), axis=-1, keepdims=True)
    )
    probs_low = jnp.exp(scores - logsum).astype(half_type)
    mixed_rows = (
        jnp.einsum("nhqk,nkhd->nqhd", probs_low, value_rows, preferred_element_type=jnp.float32)
        .astype(half_type)
        .reshape(tokens, D)
    )
    attended = (multiply(mixed_rows, output_weight) + output_bias).reshape(images, SEQ, D)
    stream_mid = stream_in + gate_attn * attended
    mlp_in = (
        (normalize(stream_mid) * (1.0 + scale_mlp) + shift_mlp).astype(half_type).reshape(tokens, D)
    )
    hidden_pre = multiply(mlp_in, up_weight) + up_bias
    hidden = gelu_tanh(hidden_pre).astype(half_type)
    mlp_out = (multiply_trans(hidden, down_weight) + down_bias).reshape(images, SEQ, D)
    stream_out = stream_mid + gate_mlp * mlp_out
    final_in = (
        (normalize(stream_out) * (1.0 + scale_final) + shift_final)
        .astype(half_type)
        .reshape(tokens, D)
    )
    output = multiply(final_in, head_weight) + head_bias
    kept = dict(
        frequency=frequency,
        embed_pre=embed_pre,
        embed_hidden=embed_hidden,
        chosen=chosen,
        condition=condition,
        active=active,
        modulation=modulation,
        final_mod=final_mod,
        patches=patches,
        stream_in=stream_in,
        attn_in=attn_in,
        queries=queries,
        key_rows=key_rows,
        value_rows=value_rows,
        logsum=logsum,
        mixed_rows=mixed_rows,
        attended=attended,
        stream_mid=stream_mid,
        mlp_in=mlp_in,
        hidden_pre=hidden_pre,
        hidden=hidden,
        mlp_out=mlp_out,
        stream_out=stream_out,
        final_in=final_in,
    )
    return (output, kept)


def backward(gathered, master_small, kept, grad_output):
    (
        attend_weight,
        output_weight,
        up_weight,
        down_weight,
        modulate_weight,
        final_weight,
        embed_second,
        embed_first,
    ) = split_big(gathered)
    patch_weight, unused_table, head_weight = split_small(master_small.astype(half_type))
    images = kept["stream_in"].shape[0]
    tokens = images * SEQ
    shift_attn, scale_attn, gate_attn, shift_mlp, scale_mlp, gate_mlp = jnp.split(
        kept["modulation"][:, None, :], 6, axis=2
    )
    shift_final, scale_final = jnp.split(kept["final_mod"][:, None, :], 2, axis=2)
    grad_out = grad_output.astype(half_type)
    grad_head = outer_sum(kept["final_in"], grad_out)
    bias_head = column_sums(grad_out)
    grad_final = multiply_trans(grad_out, head_weight).reshape(images, SEQ, D)
    grad_shift_final = jnp.sum(grad_final, axis=1)
    grad_scale_final = jnp.sum(grad_final * normalize(kept["stream_out"]), axis=1)
    grad_stream = slope(normalize, kept["stream_out"], grad_final * (1.0 + scale_final))
    grad_gate_mlp = jnp.sum(grad_stream * kept["mlp_out"], axis=1)
    grad_mlp = (grad_stream * gate_mlp).reshape(tokens, D).astype(half_type)
    bias_down = column_sums(grad_mlp)
    grad_down = outer_sum(grad_mlp, kept["hidden"])
    grad_hidden = multiply(grad_mlp, down_weight)
    grad_pre = slope(gelu_tanh, kept["hidden_pre"], grad_hidden).astype(half_type)
    bias_up = column_sums(grad_pre)
    grad_up = outer_sum(kept["mlp_in"], grad_pre)
    grad_mlp_in = multiply_trans(grad_pre, up_weight).reshape(images, SEQ, D)
    grad_shift_mlp = jnp.sum(grad_mlp_in, axis=1)
    grad_scale_mlp = jnp.sum(grad_mlp_in * normalize(kept["stream_mid"]), axis=1)
    grad_stream = grad_stream + slope(
        normalize, kept["stream_mid"], grad_mlp_in * (1.0 + scale_mlp)
    )
    grad_gate_attn = jnp.sum(grad_stream * kept["attended"], axis=1)
    grad_attn = (grad_stream * gate_attn).reshape(tokens, D).astype(half_type)
    bias_output = column_sums(grad_attn)
    grad_output_weight = outer_sum(kept["mixed_rows"], grad_attn)
    grad_mixed = (
        multiply_trans(grad_attn, output_weight)
        .astype(half_type)
        .reshape(images, SEQ, HEADS, HEAD_DIM)
    )
    inverse_root = 1.0 / math.sqrt(HEAD_DIM)
    scores = (
        jnp.einsum(
            "nqhd,nkhd->nhqk", kept["queries"], kept["key_rows"], preferred_element_type=jnp.float32
        )
        * inverse_root
    )
    probs = jnp.exp(scores - kept["logsum"])
    grad_values = jnp.einsum(
        "nhqk,nqhd->nkhd", probs.astype(half_type), grad_mixed, preferred_element_type=jnp.float32
    )
    grad_probs = jnp.einsum(
        "nqhd,nkhd->nhqk", grad_mixed, kept["value_rows"], preferred_element_type=jnp.float32
    )
    grad_scores = (
        probs * (grad_probs - jnp.sum(probs * grad_probs, axis=-1, keepdims=True))
    ).astype(half_type)
    grad_queries = (
        jnp.einsum(
            "nhqk,nkhd->nqhd", grad_scores, kept["key_rows"], preferred_element_type=jnp.float32
        )
        * inverse_root
    )
    grad_keys = (
        jnp.einsum(
            "nhqk,nqhd->nkhd", grad_scores, kept["queries"], preferred_element_type=jnp.float32
        )
        * inverse_root
    )
    grad_qkv = jnp.concatenate(
        [
            grad_queries.reshape(tokens, D),
            grad_keys.reshape(tokens, D),
            grad_values.reshape(tokens, D),
        ],
        axis=1,
    ).astype(half_type)
    bias_query = column_sums(grad_qkv[:, :D])
    bias_value = column_sums(grad_qkv[:, 2 * D :])
    grad_attend = outer_sum(kept["attn_in"], grad_qkv)
    grad_attn_in = multiply_trans(grad_qkv, attend_weight).reshape(images, SEQ, D)
    grad_shift_attn = jnp.sum(grad_attn_in, axis=1)
    grad_scale_attn = jnp.sum(grad_attn_in * normalize(kept["stream_in"]), axis=1)
    grad_stream = grad_stream + slope(
        normalize, kept["stream_in"], grad_attn_in * (1.0 + scale_attn)
    )
    grad_start = grad_stream.reshape(tokens, D).astype(half_type)
    bias_patch = column_sums(grad_start)
    grad_patch = outer_sum(grad_start, kept["patches"])
    grad_mod = jnp.concatenate(
        [
            grad_shift_attn,
            grad_scale_attn,
            grad_gate_attn,
            grad_shift_mlp,
            grad_scale_mlp,
            grad_gate_mlp,
        ],
        axis=1,
    ).astype(half_type)
    grad_fmod = jnp.concatenate([grad_shift_final, grad_scale_final], axis=1).astype(half_type)
    bias_modulate = column_sums(grad_mod)
    bias_final = column_sums(grad_fmod)
    grad_modulate = outer_sum(kept["active"], grad_mod)
    grad_final_weight = outer_sum(kept["active"], grad_fmod)
    grad_active = multiply_trans(grad_mod, modulate_weight) + multiply_trans(
        grad_fmod, final_weight
    )
    grad_condition = slope(jax.nn.silu, kept["condition"], grad_active)
    grad_embed = grad_condition.astype(half_type)
    bias_second = column_sums(grad_embed)
    grad_second = outer_sum(kept["embed_hidden"], grad_embed)
    grad_embed_hidden = multiply_trans(grad_embed, embed_second)
    grad_embed_pre = slope(jax.nn.silu, kept["embed_pre"], grad_embed_hidden).astype(half_type)
    bias_first = column_sums(grad_embed_pre)
    grad_first = outer_sum(grad_embed_pre, kept["frequency"])
    grad_big = jnp.concatenate(
        [
            grad_attend,
            grad_output_weight,
            grad_up,
            grad_down,
            grad_modulate,
            grad_final_weight,
            grad_second,
            grad_first,
        ],
        axis=1,
    )
    grad_small = (grad_patch, grad_head, grad_condition)
    grad_bias = jnp.concatenate(
        [
            bias_query,
            bias_value,
            bias_output,
            bias_up,
            bias_down,
            bias_modulate,
            bias_final,
            bias_second,
            bias_first,
            bias_patch,
            bias_head,
        ]
    )
    return (grad_big, grad_small, grad_bias)


def on_device(
    noisy_patches,
    targets,
    timesteps,
    labels,
    master_big,
    moment_big,
    error_big,
    factor_right,
    master_small,
    moment_small,
    biases,
    moment_bias,
    step_rates,
):
    shards = lax.axis_size("shard")
    replicas = lax.axis_size("rep")
    gathered = lax.all_gather(master_big.astype(half_type), "shard", axis=1, tiled=True)
    output, kept = forward(gathered, master_small, biases, noisy_patches, timesteps, labels)
    entries = noisy_patches.shape[0] * shards * replicas * SEQ * P_DIM
    error = output - targets.reshape(output.shape)
    loss_part = jnp.sum(error * error) / entries
    grad_output = 2.0 * error / entries
    gathered = lax.all_gather(master_big.astype(half_type), "shard", axis=1, tiled=True)
    grad_big, (grad_patch, grad_head, grad_condition), grad_bias = backward(
        gathered, master_small, kept, grad_output
    )
    grad_table = jnp.einsum("nd,nc->dc", grad_condition, kept["chosen"], precision=highest)
    grad_small = jnp.concatenate([grad_patch, grad_table, grad_head], axis=1)
    owned = lax.psum_scatter(
        grad_big.astype(jnp.bfloat16), "shard", scatter_dimension=1, tiled=True
    ).astype(jnp.float32)
    matrices = owned + error_big[0]
    left_part = jnp.dot(
        matrices, factor_right, precision=highest, preferred_element_type=jnp.float32
    )
    small_sum, bias_sum, total_loss = lax.psum((grad_small, grad_bias, loss_part), ("shard", "rep"))
    left_sum = lax.psum(left_part, "rep")
    basis = orthonormal(left_sum)
    right_sum = lax.psum(exact_outer(matrices, basis).astype(jnp.bfloat16), "rep").astype(
        jnp.float32
    )
    approx = lax.dot_general(
        basis,
        right_sum,
        (((1,), (1,)), ((), ())),
        precision=highest,
        preferred_element_type=jnp.float32,
    )
    new_error = (matrices - approx / replicas)[None]
    new_moment = momentum_decay * moment_big + approx
    new_master = master_big - step_rates[0] * new_moment
    new_moment_small = momentum_decay * moment_small + small_sum
    new_master_small = master_small - step_rates[1] * new_moment_small
    new_moment_bias = momentum_decay * moment_bias + bias_sum
    new_biases = biases - step_rates[1] * new_moment_bias
    return (
        total_loss,
        new_master,
        new_moment,
        new_error,
        right_sum,
        new_master_small,
        new_moment_small,
        new_biases,
        new_moment_bias,
    )


MESH = pl.DeviceIdType.MESH
BLOCK = 512
PIECE = 256
EARLY = 5
KERNEL_BYTES = 34_000_000
EXCHANGE_BYTES = 50_000_000
RANK = 8
LANES = 128
REPS = 16


def sds(shape, dtype=jnp.float32):
    return jax.ShapeDtypeStruct(shape, dtype)


def split_two(values):
    high = values.astype(half_type)
    low = (values - high.astype(jnp.float32)).astype(half_type)
    return high, low


def greet(others):
    barrier = pltpu.get_barrier_semaphore()
    for other in others:
        pl.semaphore_signal(barrier, inc=1, device_id=other, device_id_type=MESH)
    return barrier, len(others)


def tail_kernel(
    attn_in_hbm,
    mixed_hbm,
    mlp_in_hbm,
    grad_mlp_hbm,
    grad_qkv_hbm,
    grad_attn_hbm,
    grad_pre_hbm,
    hidden_hbm,
    tail_left_ref,
    tail_right_ref,
    error_hbm,
    factor_ref,
    moment_hbm,
    sums_ref,
    rows_ref,
    v_ref,
    whole_ref,
    basis_cols,
    total_ref,
    gathered_ref,
    recv_hbm,
    m_hbm,
    m_ref,
    error_ref,
    recv_ref,
    left_stage,
    turned_ref,
    right_ref,
    ring_ref,
    stack_ref,
    left_acc,
    left_ref,
    plane_ref,
    column_ref,
    basis_rows,
    send_ref,
    part_ref,
    mine_ref,
    half_ref,
    share_ref,
    small_ref,
    load_sem,
    stage_sem,
    right_sem,
    recv_sem,
    moment_sem,
    left_send,
    left_recv,
    right_send,
    right_recv,
    grad_send,
    grad_recv,
    small_send,
    small_recv,
    m_sem,
):
    blocks = m_ref.shape[0]
    shard = lax.axis_index("shard")
    rep = lax.axis_index("rep")
    partner = (1 - shard, rep)
    shared = blocks - 14 * shard
    shared_there = 2 + 14 * shard
    peers = [(shard, lax.rem(rep + step, REPS)) for step in range(1, REPS)]
    barrier, count = greet([partner] + peers)

    def columns(block):
        return pl.ds(pl.multiple_of(block * BLOCK, BLOCK), BLOCK)

    ring = ring_ref.shape[0]

    def send_piece(local):
        slot = lax.rem(local, ring)
        return pltpu.make_async_remote_copy(
            src_ref=ring_ref.at[slot],
            dst_ref=recv_hbm.at[:, pl.ds(pl.multiple_of(local * PIECE, PIECE), PIECE)],
            send_sem=grad_send.at[slot],
            recv_sem=grad_recv.at[local],
            device_id=partner,
            device_id_type=MESH,
        )

    def small_copy(source, target, sent, got, who):
        return pltpu.make_async_remote_copy(
            src_ref=source,
            dst_ref=target,
            send_sem=small_send.at[sent],
            recv_sem=small_recv.at[got],
            device_id=who,
            device_id_type=MESH,
        )

    def arrived(slots, base):
        for step in range(1, REPS):
            other = lax.rem(rep + step, REPS)
            small_copy(
                slots.at[other], slots.at[other], base, base + other, peers[step - 1]
            ).wait_recv()

    def load_error(block, slot):
        return pltpu.make_async_copy(
            error_hbm.at[0, :, columns(block)], error_ref.at[slot], load_sem.at[slot]
        )

    def block_of(step):
        return lax.rem(step + 2 * shard, blocks)

    def start_loads(step):
        block, slot = block_of(step), lax.rem(step, depth)
        load_error(block, slot).start()

        @pl.when(block < shared)
        def _():
            send_piece(2 * block).wait_recv()
            send_piece(2 * block + 1).wait_recv()
            load_recv(block, slot).start()

    def load_recv(block, slot):
        return pltpu.make_async_copy(
            recv_hbm.at[:, columns(block)], recv_ref.at[slot], recv_sem.at[slot]
        )

    def save_matrix(block):
        return pltpu.make_async_copy(m_ref.at[block], m_hbm.at[block], m_sem.at[block])

    def load_moment(block):
        return pltpu.make_async_copy(
            moment_hbm.at[:, columns(block)], v_ref.at[block], moment_sem.at[block]
        )

    depth = error_ref.shape[0]
    lefts = [attn_in_hbm, mixed_hbm, mlp_in_hbm, grad_mlp_hbm]
    rights = [grad_qkv_hbm, grad_attn_hbm, grad_pre_hbm, hidden_hbm]
    window = right_ref.shape[0]
    halves = 2 * blocks

    def load_left(part):
        return pltpu.make_async_copy(lefts[part], left_stage, stage_sem.at[0])

    def load_right(part, index):
        slot = lax.rem(index, window)
        return pltpu.make_async_copy(
            rights[part].at[:, pl.ds(pl.multiple_of(index * PIECE, PIECE), PIECE)],
            right_ref.at[slot],
            right_sem.at[slot],
        )

    load_left(0).start()
    for index in range(window):
        load_right(0, index).start()
    pl.semaphore_wait(barrier, count)
    own_half = small_copy(sums_ref.at[1 - shard], half_ref, 16, 16, partner)
    own_half.start()
    rows_out = [
        small_copy(rows_ref, gathered_ref.at[shard, rep], step, rep, peers[step - 1])
        for step in range(1, REPS)
    ]
    for copy in rows_out:
        copy.start()
    gathered_ref[shard, rep] = rows_ref[...]

    high, low = split_two(factor_ref[...])
    stack_ref[...] = jnp.zeros_like(stack_ref)
    stack_ref[0:RANK] = high
    stack_ref[RANK : 2 * RANK] = low
    left_acc[...] = jnp.zeros_like(left_acc)
    edge = 0
    for part in range(4):
        number = rights[part].shape[1] // PIECE
        load_left(part).wait()
        turned_ref[...] = left_stage[...].T
        if part < 3:
            load_left(part + 1).start()

        def grad_piece(index, carry):
            load_right(part, index).wait()
            grad = multiply(turned_ref[...], right_ref[lax.rem(index, window)])

            @pl.when(index + window < number)
            def _():
                load_right(part, index + window).start()

            place = edge + index
            low_half = place < halves
            local = lax.rem(place, halves)
            mine = jnp.logical_xor(low_half, shard == 1)

            @pl.when(mine)
            def _():
                span = pl.ds(pl.multiple_of(lax.rem(local, 2) * PIECE, PIECE), PIECE)
                m_ref[lax.div(local, 2), :, span] = grad

            @pl.when(jnp.logical_not(mine))
            def _():
                @pl.when(local >= ring)
                def _():
                    send_piece(local - ring).wait_send()

                ring_ref[lax.rem(local, ring)] = grad.astype(half_type)
                send_piece(local).start()

            return carry

        lax.fori_loop(0, number, grad_piece, 0)
        edge += number
        if part < 3:
            for index in range(min(window, rights[part + 1].shape[1] // PIECE)):
                load_right(part + 1, index).start()
    for step in range(depth):
        start_loads(step)

    def gather_block(step, carry):
        block, slot = block_of(step), lax.rem(step, depth)
        load_error(block, slot).wait()

        @pl.when(block < shared)
        def _():
            load_recv(block, slot).wait()
            m_ref[block] = m_ref[block] + recv_ref[slot].astype(jnp.float32) + error_ref[slot]

        @pl.when(block >= shared)
        def _():
            m_ref[block] = error_ref[slot] + multiply(
                tail_left_ref[...], tail_right_ref[:, columns(block - shared)]
            )

        save_matrix(block).start()
        high, low = split_two(m_ref[block])
        factor = stack_ref[:, columns(block)]
        left_acc[...] += multiply_trans(high, factor) + multiply_trans(low, factor)

        @pl.when(step + depth < blocks)
        def _():
            start_loads(step + depth)

        return carry

    own_half.wait()
    half_ref[...] = half_ref[...] + sums_ref[shard]
    shares_out = [
        small_copy(
            half_ref.at[lax.rem(rep + step, REPS)],
            share_ref.at[rep],
            17 + step,
            17 + rep,
            peers[step - 1],
        )
        for step in range(1, REPS)
    ]
    for copy in shares_out:
        copy.start()
    share_ref[rep] = half_ref[rep]
    lax.fori_loop(0, blocks, gather_block, 0)
    for block in range(v_ref.shape[0]):
        load_moment(block).start()

    turned = left_acc[...].T
    left_ref[...] = turned[0:RANK] + turned[RANK : 2 * RANK]

    place = lax.rem(rep, 4)
    level = lax.div(rep, 4)
    plane_out = []
    for step in range(1, 4):
        other = lax.rem(place + step, 4)
        plane_out.append(
            pltpu.make_async_remote_copy(
                src_ref=left_ref,
                dst_ref=plane_ref.at[place],
                send_sem=left_send.at[step],
                recv_sem=left_recv.at[place],
                device_id=(shard, level * 4 + other),
                device_id_type=MESH,
            )
        )
    for copy in plane_out:
        copy.start()
    plane_ref[place] = left_ref[...]
    arrived(share_ref, 17)
    small_ref[...] = jnp.sum(share_ref[...], axis=0)
    whole_out = [
        small_copy(small_ref, total_ref.at[shard, rep], 33 + step, 33 + rep, peers[step - 1])
        for step in range(1, REPS)
    ]
    for copy in whole_out:
        copy.start()
    total_ref[shard, rep] = small_ref[...]
    for step in range(1, 4):
        other = lax.rem(place + step, 4)
        pltpu.make_async_remote_copy(
            src_ref=left_ref,
            dst_ref=plane_ref.at[other],
            send_sem=left_send.at[step],
            recv_sem=left_recv.at[other],
            device_id=(shard, level * 4 + other),
            device_id_type=MESH,
        ).wait_recv()
    plane_sum = (plane_ref[0] + plane_ref[1]) + (plane_ref[2] + plane_ref[3])
    for copy in plane_out:
        copy.wait_send()
    left_ref[...] = plane_sum
    column_out = []
    for step in range(1, 4):
        other = lax.rem(level + step, 4)
        column_out.append(
            pltpu.make_async_remote_copy(
                src_ref=left_ref,
                dst_ref=column_ref.at[level],
                send_sem=left_send.at[4 + step],
                recv_sem=left_recv.at[4 + level],
                device_id=(shard, other * 4 + place),
                device_id_type=MESH,
            )
        )
    for copy in column_out:
        copy.start()
    column_ref[level] = plane_sum
    for step in range(1, 4):
        other = lax.rem(level + step, 4)
        pltpu.make_async_remote_copy(
            src_ref=left_ref,
            dst_ref=column_ref.at[other],
            send_sem=left_send.at[4 + step],
            recv_sem=left_recv.at[4 + other],
            device_id=(shard, other * 4 + place),
            device_id_type=MESH,
        ).wait_recv()
    vectors = (column_ref[0] + column_ref[1]) + (column_ref[2] + column_ref[3])

    row_index = lax.broadcasted_iota(jnp.int32, (RANK, 1), 0)
    for place_of in range(RANK):
        row = vectors[place_of : place_of + 1]
        unit = row * lax.rsqrt(jnp.sum(row * row, axis=1, keepdims=True) + tiny_value)
        dots = jnp.sum(vectors * unit, axis=1, keepdims=True)
        vectors = jnp.where(
            row_index > place_of,
            vectors - dots * unit,
            jnp.where(row_index == place_of, unit, vectors),
        )
    high, low = split_two(vectors)
    basis_rows[...] = jnp.concatenate([high, low], axis=0)
    padded = jnp.concatenate(
        [
            high.astype(jnp.float32),
            low.astype(jnp.float32),
            jnp.zeros((LANES - 2 * RANK, vectors.shape[1]), jnp.float32),
        ],
        axis=0,
    )
    basis_cols[...] = padded.T.astype(half_type)
    for copy in column_out:
        copy.wait_send()
    arrived(gathered_ref.at[shard], 0)
    rows_across = small_copy(gathered_ref.at[shard], gathered_ref.at[shard], 49, 49, partner)
    rows_across.start()
    arrived(total_ref.at[shard], 33)
    total_across = small_copy(total_ref.at[shard], total_ref.at[shard], 50, 50, partner)
    total_across.start()

    def right_block(block, carry):
        high, low = split_two(m_ref[block])
        first = multiply(basis_rows[...], high)
        second = multiply(basis_rows[...], low)
        both = first + second
        send_ref[block] = (both[0:RANK] + both[RANK : 2 * RANK]).astype(half_type)
        return carry

    lax.fori_loop(0, blocks, right_block, 0)

    def right_copy(source, target, base, step, sender):
        return pltpu.make_async_remote_copy(
            src_ref=source,
            dst_ref=target,
            send_sem=right_send.at[base + step],
            recv_sem=right_recv.at[base + sender],
            device_id=peers[step - 1],
            device_id_type=MESH,
        )

    scatter = [
        right_copy(send_ref.at[lax.rem(rep + step, REPS)], part_ref.at[rep], 0, step, rep)
        for step in range(1, REPS)
    ]
    for copy in scatter:
        copy.start()
    part_ref[rep] = send_ref[rep]
    for step in range(1, REPS):
        other = lax.rem(rep + step, REPS)
        right_copy(send_ref.at[other], part_ref.at[other], 0, step, other).wait_recv()
    mine_ref[...] = jnp.sum(part_ref[...].astype(jnp.float32), axis=0).astype(half_type)
    spread = [
        right_copy(mine_ref, whole_ref.at[rep], REPS, step, rep) for step in range(1, REPS)
    ]
    for copy in spread:
        copy.start()
    whole_ref[rep] = mine_ref[...]
    for step in range(1, REPS):
        other = lax.rem(rep + step, REPS)
        right_copy(mine_ref, whole_ref.at[other], REPS, step, other).wait_recv()
    for copy in scatter + spread + rows_out + shares_out + whole_out:
        copy.wait_send()

    def sent_piece(local, carry):
        send_piece(local).wait_send()
        return carry

    sent = 2 * shared_there
    lax.fori_loop((halves - ring) * shard, sent, sent_piece, 0)
    for block in range(blocks):
        save_matrix(block).wait()
    rows_across.wait()
    total_across.wait()
    for block in range(v_ref.shape[0]):
        load_moment(block).wait()


def update_kernel(
    rates_ref,
    m_hbm,
    v_ref,
    whole_ref,
    basis_cols,
    moment_hbm,
    master_hbm,
    new_master_hbm,
    new_moment_hbm,
    new_error_hbm,
    right_ref,
    error_ref,
    moment_ref,
    master_ref,
    moment_sem,
    master_sem,
    matrix_sem,
    error_out,
    moment_out,
    master_out,
):
    pieces = BLOCK // PIECE
    blocks = m_hbm.shape[0] * pieces
    early = v_ref.shape[0] * pieces
    slots = master_ref.shape[0]
    rate = rates_ref[0]

    def columns(block):
        return pl.ds(pl.multiple_of(block * PIECE, PIECE), PIECE)

    def load_master(block, slot):
        return pltpu.make_async_copy(
            master_hbm.at[:, columns(block)], master_ref.at[slot], master_sem.at[slot]
        )

    def load_matrix(block, slot):
        return pltpu.make_async_copy(
            m_hbm.at[
                lax.div(block, pieces),
                :,
                pl.ds(pl.multiple_of(lax.rem(block, pieces) * PIECE, PIECE), PIECE),
            ],
            error_ref.at[slot],
            matrix_sem.at[slot],
        )

    def load_moment(block, slot):
        return pltpu.make_async_copy(
            moment_hbm.at[:, columns(block)], moment_ref.at[slot], moment_sem.at[slot]
        )

    def out_error(block, slot):
        return pltpu.make_async_copy(
            error_ref.at[slot], new_error_hbm.at[0, :, columns(block)], error_out.at[slot]
        )

    def out_moment(block, slot):
        return pltpu.make_async_copy(
            moment_ref.at[slot], new_moment_hbm.at[:, columns(block)], moment_out.at[slot]
        )

    def out_master(block, slot):
        return pltpu.make_async_copy(
            master_ref.at[slot], new_master_hbm.at[:, columns(block)], master_out.at[slot]
        )

    ahead = slots - 2
    for block in range(ahead):
        load_matrix(block, block).start()
        load_master(block, block).start()

    def update_piece(whole, piece):
        block = whole * pieces + piece
        span = slice(piece * PIECE, (piece + 1) * PIECE)
        slot = lax.rem(block, slots)
        next_slot = lax.rem(block + ahead, slots)

        @pl.when(block >= 2)
        def _():
            out_error(block - 2, next_slot).wait()
            out_moment(block - 2, next_slot).wait()
            out_master(block - 2, next_slot).wait()

        @pl.when(block + ahead < blocks)
        def _():
            load_matrix(block + ahead, next_slot).start()
            load_master(block + ahead, next_slot).start()

            @pl.when(block + ahead >= early)
            def _():
                load_moment(block + ahead, next_slot).start()

        right = whole_ref[whole, :, span]
        right_ref[:, columns(block)] = right.astype(jnp.float32)
        approx = multiply(basis_cols[:, 0 : 2 * RANK], jnp.concatenate([right, right], axis=0))
        load_matrix(block, slot).wait()
        error_ref[slot] = error_ref[slot] - approx * (1.0 / REPS)
        out_error(block, slot).start()

        @pl.when(block < early)
        def _():
            moment_ref[slot] = (
                momentum_decay * v_ref[jnp.minimum(whole, v_ref.shape[0] - 1), :, span] + approx
            )

        @pl.when(block >= early)
        def _():
            load_moment(block, slot).wait()
            moment_ref[slot] = momentum_decay * moment_ref[slot] + approx

        out_moment(block, slot).start()
        load_master(block, slot).wait()
        master_ref[slot] = master_ref[slot] - rate * moment_ref[slot]
        out_master(block, slot).start()

    def update_block(whole, carry):
        for piece in range(pieces):
            update_piece(whole, piece)
        return carry

    lax.fori_loop(0, m_hbm.shape[0], update_block, 0)
    for block in range(blocks - 2, blocks):
        out_error(block, block % slots).wait()
        out_moment(block, block % slots).wait()
        out_master(block, block % slots).wait()


def compress(rates, sides, tail_left, tail_right, error, factor_rows, moment, master, sums, lines):
    rows, cols = master.shape
    blocks = cols // BLOCK
    depth = 3
    slots = 8
    hbm = pl.BlockSpec(memory_space=pltpu.HBM)
    vmem = pl.BlockSpec(memory_space=pltpu.VMEM)
    moments, whole, basis, total, gathered, unused, matrices = pl.pallas_call(
        tail_kernel,
        out_shape=(
            pltpu.VMEM((EARLY, rows, BLOCK), jnp.float32),
            pltpu.VMEM((blocks, RANK, BLOCK), half_type),
            pltpu.VMEM((rows, LANES), half_type),
            sds((2, REPS) + sums.shape[2:]),
            sds((2, REPS) + lines.shape),
            pltpu.HBM((rows, cols), half_type),
            pltpu.HBM((blocks, rows, BLOCK), jnp.float32),
        ),
        in_specs=[hbm] * 8 + [vmem, vmem, hbm, vmem, hbm, vmem, vmem],
        out_specs=[vmem] * 5 + [pl.BlockSpec(memory_space=pltpu.HBM)] * 2,
        scratch_shapes=[
            pltpu.VMEM((blocks, rows, BLOCK), jnp.float32),
            pltpu.VMEM((depth, rows, BLOCK), jnp.float32),
            pltpu.VMEM((depth, rows, BLOCK), half_type),
            pltpu.VMEM(sides[0].shape, half_type),
            pltpu.VMEM(sides[0].shape[::-1], half_type),
            pltpu.VMEM((4, sides[0].shape[0], PIECE), half_type),
            pltpu.VMEM((4, rows, PIECE), half_type),
            pltpu.VMEM((LANES, cols), half_type),
            pltpu.VMEM((rows, LANES), jnp.float32),
            pltpu.VMEM((RANK, rows), jnp.float32),
            pltpu.VMEM((4, RANK, rows), jnp.float32),
            pltpu.VMEM((4, RANK, rows), jnp.float32),
            pltpu.VMEM((2 * RANK, rows), half_type),
            pltpu.VMEM((blocks, RANK, BLOCK), half_type),
            pltpu.VMEM((blocks, RANK, BLOCK), half_type),
            pltpu.VMEM((RANK, BLOCK), half_type),
            pltpu.VMEM(sums.shape[1:], jnp.float32),
            pltpu.VMEM(sums.shape[1:], jnp.float32),
            pltpu.VMEM(sums.shape[2:], jnp.float32),
            pltpu.SemaphoreType.DMA((depth,)),
            pltpu.SemaphoreType.DMA((1,)),
            pltpu.SemaphoreType.DMA((4,)),
            pltpu.SemaphoreType.DMA((depth,)),
            pltpu.SemaphoreType.DMA((blocks,)),
            pltpu.SemaphoreType.DMA((8,)),
            pltpu.SemaphoreType.DMA((8,)),
            pltpu.SemaphoreType.DMA((2 * REPS,)),
            pltpu.SemaphoreType.DMA((2 * REPS,)),
            pltpu.SemaphoreType.DMA((4,)),
            pltpu.SemaphoreType.DMA((2 * blocks,)),
            pltpu.SemaphoreType.DMA((51,)),
            pltpu.SemaphoreType.DMA((51,)),
            pltpu.SemaphoreType.DMA((blocks,)),
        ],
        compiler_params=pltpu.CompilerParams(
            collective_id=2, has_side_effects=True, vmem_limit_bytes=EXCHANGE_BYTES
        ),
        name="compress",
    )(*sides, tail_left, tail_right, error, factor_rows, moment, sums, lines)
    updated = pl.pallas_call(
        update_kernel,
        out_shape=(
            sds(master.shape),
            sds(moment.shape),
            sds(error.shape),
            sds((RANK, cols)),
        ),
        in_specs=[pl.BlockSpec(memory_space=pltpu.SMEM), hbm, vmem, vmem, vmem, hbm, hbm],
        out_specs=[hbm, hbm, hbm, vmem],
        scratch_shapes=[
            pltpu.VMEM((slots, rows, PIECE), jnp.float32),
            pltpu.VMEM((slots, rows, PIECE), jnp.float32),
            pltpu.VMEM((slots, rows, PIECE), jnp.float32),
            pltpu.SemaphoreType.DMA((slots,)),
            pltpu.SemaphoreType.DMA((slots,)),
            pltpu.SemaphoreType.DMA((slots,)),
            pltpu.SemaphoreType.DMA((slots,)),
            pltpu.SemaphoreType.DMA((slots,)),
            pltpu.SemaphoreType.DMA((slots,)),
        ],
        compiler_params=pltpu.CompilerParams(vmem_limit_bytes=KERNEL_BYTES),
        name="update",
    )(rates, matrices, moments, whole, basis, moment, master)
    return lax.optimization_barrier((tuple(updated), total, gathered))


def small_kernel(
    rates_ref, sums_ref, lines_ref, moment_ref, master_ref, new_moment_ref, new_master_ref
):
    step = pl.program_id(0)
    height = moment_ref.shape[0]
    images = lines_ref.shape[1] * 8
    strips = D // LANES

    def piece(place):
        return lines_ref[1, :, place * 8 : (place + 1) * 8, :].reshape(images, LANES)

    labels = piece(strips)[:, 0:1]
    place = lax.broadcasted_iota(jnp.int32, (images, height), 1) + (step * height - P_DIM)
    chosen = (place.astype(jnp.float32) == labels).astype(half_type)
    for strip in range(strips):
        span = slice(strip * LANES, (strip + 1) * LANES)
        high, low = split_two(piece(strip))
        new_moment_ref[:, span] = (
            momentum_decay * moment_ref[:, span] + outer_sum(chosen, high) + outer_sum(chosen, low)
        )

    def add(first, base):
        for strip in range(strips):
            span = slice(strip * LANES, (strip + 1) * LANES)
            new_moment_ref[first : first + P_DIM, span] += sums_ref[
                base + strip * P_DIM : base + (strip + 1) * P_DIM, :
            ]

    @pl.when(step == 0)
    def _():
        add(0, 0)

    @pl.when(step == pl.num_programs(0) - 1)
    def _():
        add(height - P_DIM, strips * P_DIM)

    new_master_ref[...] = master_ref[...] - rates_ref[1] * new_moment_ref[...]


def update_small(rates, total, gathered, moment, master):
    rows = moment.shape[0]
    steps = 3
    vmem = pl.BlockSpec(memory_space=pltpu.VMEM)
    block = pl.BlockSpec((rows // steps, D), lambda step: (step, 0))
    return pl.pallas_call(
        small_kernel,
        grid=(steps,),
        out_shape=(sds(moment.shape), sds(master.shape)),
        in_specs=[pl.BlockSpec(memory_space=pltpu.SMEM), vmem, vmem, block, block],
        out_specs=[block, block],
        name="update_small",
    )(rates, total.reshape(-1, LANES), gathered, moment, master)


GROUP = 2 * HEAD_DIM
CHUNK = 768


def unit_rows(values):
    center = values - jnp.mean(values, axis=-1, keepdims=True)
    inverse = lax.rsqrt(jnp.mean(center * center, axis=-1, keepdims=True) + epsilon)
    return center * inverse, inverse


def unit_back(unit, inverse, grad):
    return inverse * (
        grad
        - jnp.mean(grad, axis=-1, keepdims=True)
        - unit * jnp.mean(grad * unit, axis=-1, keepdims=True)
    )


def gelu_both(values):
    scale = math.sqrt(2.0 / math.pi)
    square = values * values
    bent = jnp.tanh(scale * (values + 0.044715 * (values * square)))
    half = 0.5 * (1.0 + bent)
    slope = half + 0.5 * values * (1.0 - bent * bent) * (scale * (1.0 + 0.134145 * square))
    return values * half, slope


def token_sum(values):
    return jnp.sum(values, axis=0, keepdims=True)


def image_kernel(
    entries,
    patches_ref,
    targets_ref,
    both_mods_ref,
    place_ref,
    patch_weight_ref,
    head_weight_ref,
    qkv_bias_ref,
    output_bias_ref,
    up_bias_ref,
    down_bias_ref,
    patch_bias_ref,
    head_bias_ref,
    master_hbm,
    attn_in_ref,
    mixed_ref,
    mlp_in_ref,
    hidden_ref,
    grad_qkv_ref,
    grad_attn_ref,
    grad_pre_ref,
    grad_mlp_ref,
    both_grads_ref,
    grad_patch_ref,
    grad_head_ref,
    bias_qkv_ref,
    bias_output_ref,
    bias_up_ref,
    bias_down_ref,
    bias_patch_ref,
    bias_head_ref,
    loss_ref,
    weight_ref,
    qkv_ref,
    probs_ref,
    slope_ref,
    unit_start_ref,
    unit_mid_ref,
    stream_ref,
    attended_ref,
    mlp_out_ref,
    grad_mixed_ref,
    total_ref,
    stage_ref,
    mods_ref,
    got_mods_ref,
    mod_grad_ref,
    got_grads_ref,
    stage_sem,
    weight_send,
    weight_recv,
    mod_send,
    mod_recv,
):
    image = pl.program_id(0)
    last = pl.num_programs(0) - 1
    images = mods_ref.shape[0]
    edges = [0, 3 * D, 4 * D, 4 * D + FF, 4 * D + 2 * FF]
    shard = lax.axis_index("shard")
    partner = (1 - shard, lax.axis_index("rep"))
    cols = master_hbm.shape[1]
    first_count = cols // BLOCK
    all_count = edges[4] // BLOCK
    count = first_count - (2 * first_count - all_count) * shard
    depth = stage_ref.shape[0]

    def load(block):
        slot = lax.rem(block, depth)
        return pltpu.make_async_copy(
            master_hbm.at[:, pl.ds(pl.multiple_of(block * BLOCK, BLOCK), BLOCK)],
            stage_ref.at[slot],
            stage_sem.at[slot],
        )

    def weight_copy(block):
        span = pl.ds(pl.multiple_of(block * BLOCK, BLOCK), BLOCK)
        return pltpu.make_async_remote_copy(
            src_ref=weight_ref.at[:, span],
            dst_ref=weight_ref.at[:, span],
            send_sem=weight_send.at[block],
            recv_sem=weight_recv.at[block],
            device_id=partner,
            device_id_type=MESH,
        )

    def mod_copy(source, target, place):
        return pltpu.make_async_remote_copy(
            src_ref=source,
            dst_ref=target,
            send_sem=mod_send.at[place],
            recv_sem=mod_recv.at[place],
            device_id=partner,
            device_id_type=MESH,
        )

    mods_across = mod_copy(both_mods_ref.at[pl.ds(images, images)], got_mods_ref, 0)
    grads_across = mod_copy(mod_grad_ref, got_grads_ref, 1)

    sums = [
        grad_patch_ref,
        grad_head_ref,
        bias_qkv_ref,
        bias_output_ref,
        bias_up_ref,
        bias_down_ref,
        bias_patch_ref,
        bias_head_ref,
        loss_ref,
    ]

    @pl.when(image == 0)
    def _():
        for block in range(2):
            load(block).start()
        barrier, greeted = greet([partner])
        pl.semaphore_wait(barrier, greeted)
        mods_across.start()
        for total in sums:
            total[...] = jnp.zeros_like(total)

        def cast(block, carry):
            @pl.when(block + 2 < count)
            def _():
                load(block + 2).start()

            load(block).wait()
            place = shard * first_count + block
            weight_ref[:, pl.ds(pl.multiple_of(place * BLOCK, BLOCK), BLOCK)] = stage_ref[
                lax.rem(block, depth)
            ].astype(half_type)
            weight_copy(place).start()
            return carry

        lax.fori_loop(0, count, cast, 0)
        mods_across.wait_recv()
        mods_ref[...] = jnp.where(shard == 1, both_mods_ref[0:images], got_mods_ref[...])

    stops = [-(-edge // BLOCK) for edge in edges]

    def arrived(part):
        @pl.when(jnp.logical_and(image == 0, shard == 1))
        def _():
            for block in range(stops[part], min(stops[part + 1], first_count)):
                weight_copy(block).wait_recv()

        if stops[part + 1] > first_count:

            @pl.when(jnp.logical_and(image == 0, shard == 0))
            def _():
                for block in range(first_count, all_count):
                    weight_copy(block).wait_recv()

    def modulation(place):
        return mods_ref[image, place : place + 1, :]

    def weight(first, width):
        return weight_ref[:, pl.ds(first, width)]

    patches = patches_ref[...]
    start = multiply(patches, patch_weight_ref[...]) + patch_bias_ref[...] + place_ref[...]
    stream_ref[...] = start
    unit, inverse_start = unit_rows(start)
    unit_start_ref[...] = unit
    attn_in_ref[...] = (unit * (1.0 + modulation(1)) + modulation(0)).astype(half_type)
    arrived(0)
    for part in range(3):
        span = slice(part * D, (part + 1) * D)
        qkv_ref[:, span] = (
            multiply(attn_in_ref[...], weight_ref[:, span]) + qkv_bias_ref[:, span]
        ).astype(half_type)

    scale = 1.0 / math.sqrt(HEAD_DIM)
    first_half = lax.broadcasted_iota(jnp.int32, (1, GROUP), 1) < HEAD_DIM

    def pair_slice(ref, part, pair):
        return ref[:, pl.ds(pl.multiple_of(part * D + pair * GROUP, GROUP), GROUP)]

    def halves(values):
        nothing = jnp.zeros_like(values)
        return jnp.where(first_half, values, nothing), jnp.where(first_half, nothing, values)

    def attend(pair, carry):
        queries = pair_slice(qkv_ref, 0, pair)
        keys = halves(pair_slice(qkv_ref, 1, pair))
        turned = pair_slice(qkv_ref, 2, pair).T
        rows = []
        for half in range(2):
            scores = multiply_trans(keys[half], queries) * scale
            weights = jnp.exp(scores - jnp.max(scores, axis=0, keepdims=True))
            probs = weights * (1.0 / jnp.sum(weights, axis=0, keepdims=True))
            probs_ref[2 * pair + half] = probs
            rows.append(
                multiply(
                    turned[half * HEAD_DIM : (half + 1) * HEAD_DIM], probs.astype(half_type)
                )
            )
        mixed_ref[:, pl.ds(pl.multiple_of(pair * GROUP, GROUP), GROUP)] = (
            jnp.concatenate(rows, axis=0).T.astype(half_type)
        )
        return carry

    lax.fori_loop(0, HEADS // 2, attend, 0)
    arrived(1)
    attended = multiply(mixed_ref[...], weight_ref[:, edges[1] : edges[2]]) + output_bias_ref[...]
    attended_ref[...] = attended
    middle = stream_ref[...] + modulation(2) * attended
    stream_ref[...] = middle
    unit, inverse_mid = unit_rows(middle)
    unit_mid_ref[...] = unit
    mlp_in_ref[...] = (unit * (1.0 + modulation(4)) + modulation(3)).astype(half_type)
    arrived(2)
    arrived(3)
    total_ref[...] = jnp.zeros_like(total_ref) + down_bias_ref[...]
    for part in range(FF // CHUNK):
        span = slice(part * CHUNK, (part + 1) * CHUNK)
        before = (
            multiply(mlp_in_ref[...], weight(edges[2] + part * CHUNK, CHUNK)) + up_bias_ref[:, span]
        )
        after, slope_part = gelu_both(before)
        slope_ref[:, span] = slope_part
        after = after.astype(half_type)
        hidden_ref[:, span] = after
        total_ref[...] += multiply_trans(after, weight(edges[3] + part * CHUNK, CHUNK))
    mlp_out_ref[...] = total_ref[...]
    unit, inverse_end = unit_rows(stream_ref[...] + modulation(5) * total_ref[...])
    final_in = (unit * (1.0 + modulation(7)) + modulation(6)).astype(half_type)
    error = (
        multiply_trans(final_in, head_weight_ref[...]) + head_bias_ref[...] - targets_ref[...]
    )
    loss_ref[...] += token_sum(error * error)
    grad_out = (error * (2.0 / entries)).astype(half_type)
    bias_head_ref[...] += token_sum(grad_out.astype(jnp.float32))
    grad_head_ref[...] += outer_sum(grad_out, final_in)

    grad_final = multiply(grad_out, head_weight_ref[...])
    mod_grad_ref[image, 6:7] = token_sum(grad_final)
    mod_grad_ref[image, 7:8] = token_sum(grad_final * unit)
    grad_stream = unit_back(unit, inverse_end, grad_final * (1.0 + modulation(7)))
    stream_ref[...] = grad_stream
    mod_grad_ref[image, 5:6] = token_sum(grad_stream * mlp_out_ref[...])
    grad_mlp = (grad_stream * modulation(5)).astype(half_type)
    grad_mlp_ref[...] = grad_mlp
    bias_down_ref[...] += token_sum(grad_mlp.astype(jnp.float32))
    total_ref[...] = jnp.zeros_like(total_ref)
    for part in range(FF // CHUNK):
        span = slice(part * CHUNK, (part + 1) * CHUNK)
        grad_pre = (
            multiply(grad_mlp_ref[...], weight(edges[3] + part * CHUNK, CHUNK)) * slope_ref[:, span]
        ).astype(half_type)
        grad_pre_ref[:, span] = grad_pre
        bias_up_ref[:, span] += token_sum(grad_pre.astype(jnp.float32))
        total_ref[...] += multiply_trans(grad_pre, weight(edges[2] + part * CHUNK, CHUNK))
    grad_in = total_ref[...]
    unit = unit_mid_ref[...]
    mod_grad_ref[image, 3:4] = token_sum(grad_in)
    mod_grad_ref[image, 4:5] = token_sum(grad_in * unit)
    grad_stream = stream_ref[...] + unit_back(unit, inverse_mid, grad_in * (1.0 + modulation(4)))
    stream_ref[...] = grad_stream
    mod_grad_ref[image, 2:3] = token_sum(grad_stream * attended_ref[...])
    grad_attn = (grad_stream * modulation(2)).astype(half_type)
    grad_attn_ref[...] = grad_attn
    bias_output_ref[...] += token_sum(grad_attn.astype(jnp.float32))
    grad_mixed_ref[...] = multiply_trans(grad_attn, weight_ref[:, edges[1] : edges[2]]).astype(
        half_type
    )

    def attend_back(pair, carry):
        queries = pair_slice(qkv_ref, 0, pair)
        keys_turned = pair_slice(qkv_ref, 1, pair).T
        values = halves(pair_slice(qkv_ref, 2, pair))
        grads = pair_slice(grad_mixed_ref, 0, pair)
        rows, key_grads, value_grads = [], [], []
        for half in range(2):
            probs = probs_ref[2 * pair + half]
            grad_probs = multiply_trans(values[half], grads)
            value_grads.append(multiply(probs.astype(half_type), grads))
            product = probs * grad_probs
            grad_scores = (product - probs * token_sum(product)).astype(half_type)
            key_grads.append(multiply(grad_scores, queries))
            rows.append(
                multiply(keys_turned[half * HEAD_DIM : (half + 1) * HEAD_DIM], grad_scores)
            )

        def put(part, values):
            grad_qkv_ref[:, pl.ds(pl.multiple_of(part * D + pair * GROUP, GROUP), GROUP)] = (
                values.astype(half_type)
            )

        put(0, jnp.concatenate(rows, axis=0).T * scale)
        put(1, jnp.where(first_half, key_grads[0], key_grads[1]) * scale)
        put(2, jnp.where(first_half, value_grads[0], value_grads[1]))
        return carry

    lax.fori_loop(0, HEADS // 2, attend_back, 0)
    bias_qkv_ref[...] += token_sum(grad_qkv_ref[...].astype(jnp.float32))
    grad_in = multiply_trans(grad_qkv_ref[...], weight_ref[:, : edges[1]])
    unit = unit_start_ref[...]
    mod_grad_ref[image, 0:1] = token_sum(grad_in)
    mod_grad_ref[image, 1:2] = token_sum(grad_in * unit)
    grad_start = (
        stream_ref[...] + unit_back(unit, inverse_start, grad_in * (1.0 + modulation(1)))
    ).astype(half_type)
    bias_patch_ref[...] += token_sum(grad_start.astype(jnp.float32))
    grad_patch_ref[...] += outer_sum(patches, grad_start)

    @pl.when(image == last)
    def _():
        grads_across.start()

        def sent(block, carry):
            weight_copy(shard * first_count + block).wait_send()
            return carry

        lax.fori_loop(0, count, sent, 0)
        mods_across.wait_send()
        both_grads_ref[0:images] = mod_grad_ref[...]
        grads_across.wait()
        both_grads_ref[images : 2 * images] = got_grads_ref[...]


def run_images(
    patches, targets, mods, places, patch_weight, head_weight, biases, master, entries
):
    images = mods.shape[0] // 2
    tokens = images * SEQ
    wide = 4 * D + 2 * FF

    def rows(width):
        return pl.BlockSpec((SEQ, width), lambda image: (image, 0))

    def fixed(array):
        return pl.BlockSpec(array.shape, lambda image: (0,) * len(array.shape))

    vector = [(P_DIM, D), (P_DIM, D), (1, 3 * D), (1, D), (1, FF), (1, D), (1, D), (1, P_DIM)]
    vector = [sds(shape) for shape in vector + [(1, P_DIM)]]
    saved = [D, D, D, FF, 3 * D, D, FF, D]
    return pl.pallas_call(
        functools.partial(image_kernel, entries),
        grid=(images,),
        out_shape=[sds((tokens, width), half_type) for width in saved]
        + [sds(mods.shape)]
        + vector,
        in_specs=[rows(P_DIM), rows(P_DIM), fixed(mods), fixed(places)]
        + [fixed(patch_weight), fixed(head_weight)]
        + [fixed(bias) for bias in biases]
        + [pl.BlockSpec(memory_space=pltpu.HBM)],
        out_specs=[rows(width) for width in saved] + [fixed(mods)] + [fixed(item) for item in vector],
        scratch_shapes=[
            pltpu.VMEM((D, wide), half_type),
            pltpu.VMEM((SEQ, 3 * D), half_type),
            pltpu.VMEM((HEADS, SEQ, SEQ), jnp.float32),
            pltpu.VMEM((SEQ, FF), jnp.float32),
            pltpu.VMEM((SEQ, D), jnp.float32),
            pltpu.VMEM((SEQ, D), jnp.float32),
            pltpu.VMEM((SEQ, D), jnp.float32),
            pltpu.VMEM((SEQ, D), jnp.float32),
            pltpu.VMEM((SEQ, D), jnp.float32),
            pltpu.VMEM((SEQ, D), half_type),
            pltpu.VMEM((SEQ, D), jnp.float32),
            pltpu.VMEM((3, D, BLOCK), jnp.float32),
            pltpu.VMEM((images, 8, D), jnp.float32),
            pltpu.VMEM((images, 8, D), jnp.float32),
            pltpu.VMEM((images, 8, D), jnp.float32),
            pltpu.VMEM((images, 8, D), jnp.float32),
            pltpu.SemaphoreType.DMA((3,)),
            pltpu.SemaphoreType.DMA((wide // BLOCK,)),
            pltpu.SemaphoreType.DMA((wide // BLOCK,)),
            pltpu.SemaphoreType.DMA((2,)),
            pltpu.SemaphoreType.DMA((2,)),
        ],
        compiler_params=pltpu.CompilerParams(
            collective_id=1, has_side_effects=True, vmem_limit_bytes=60_000_000
        ),
        name="images",
    )(patches, targets, mods, places, patch_weight, head_weight, *biases, master)


def train_gradients(master, master_small, biases, noisy_patches, targets, timesteps, labels, entries):
    owner = lax.axis_index("shard") == 1
    last = master.shape[1]
    first_edge = last - 9 * D - FREQ
    both_weight, embed_second, embed_first = split_at(
        master, [first_edge, last - D - FREQ, last - FREQ, last]
    )
    patch_weight, class_table, head_weight = split_small(master_small)
    (
        query_bias,
        value_bias,
        output_bias,
        up_bias,
        down_bias,
        modulate_bias,
        final_bias,
        second_bias,
        first_bias,
        patch_bias,
        head_bias,
    ) = split_bias(biases)
    images = noisy_patches.shape[0]
    frequency = timestep_features(timesteps).astype(half_type)
    embed_pre = multiply_trans(frequency.astype(jnp.float32), embed_first) + first_bias
    embed_hidden = jax.nn.silu(embed_pre).astype(half_type)
    time_embed = multiply(embed_hidden.astype(jnp.float32), embed_second) + second_bias
    chosen = (labels[:, None] == jnp.arange(NCLASS, dtype=jnp.int32)[None, :]).astype(jnp.float32)
    condition = time_embed + lax.dot_general(
        chosen,
        class_table,
        (((1,), (1,)), ((), ())),
        precision=highest,
        preferred_element_type=jnp.float32,
    )
    active = jax.nn.silu(condition).astype(half_type)
    mods = multiply(active.astype(jnp.float32), both_weight) + jnp.concatenate([modulate_bias, final_bias])
    qkv_bias = jnp.concatenate([query_bias, jnp.zeros_like(query_bias), value_bias])
    (
        attn_in,
        mixed,
        mlp_in,
        hidden,
        grad_qkv,
        grad_attn,
        grad_pre,
        grad_mlp,
        mod_grads,
        grad_patch,
        grad_head,
        bias_qkv,
        bias_output,
        bias_up,
        bias_down,
        bias_patch,
        bias_head,
        losses,
    ) = run_images(
        noisy_patches.reshape(-1, P_DIM),
        targets.reshape(-1, P_DIM),
        mods.reshape(-1, 8, D),
        position_table(),
        patch_weight.T.astype(half_type),
        head_weight.T.astype(half_type),
        [item[None] for item in (qkv_bias, output_bias, up_bias, down_bias, patch_bias, head_bias)],
        master,
        entries,
    )
    grad_mods = mod_grads.reshape(-1, 8 * D).astype(half_type)
    bias_mods = column_sums(grad_mods)
    grad_active = multiply_trans(grad_mods.astype(jnp.float32), both_weight)
    grad_condition = slope(jax.nn.silu, condition, grad_active)
    grad_embed = grad_condition.astype(half_type)
    grad_embed_hidden = multiply_trans(grad_embed.astype(jnp.float32), embed_second)
    grad_embed_pre = slope(jax.nn.silu, embed_pre, grad_embed_hidden).astype(half_type)
    tail_left = jnp.pad(
        jnp.concatenate([active, embed_hidden, grad_embed_pre]), ((0, 8), (0, 0))
    ).T
    tail_right = jnp.concatenate(
        [
            jnp.pad(grad_mods, ((0, 0), (0, D + FREQ))),
            jnp.pad(grad_embed, ((0, 0), (8 * D, FREQ))),
            jnp.pad(frequency, ((0, 16 - frequency.shape[0]), (9 * D, 0))),
        ]
    )
    sides = (attn_in, mixed, mlp_in, grad_mlp, grad_qkv, grad_attn, grad_pre, hidden)
    grad_bias = jnp.concatenate(
        [
            bias_qkv[0, :D],
            bias_qkv[0, 2 * D :],
            bias_output[0],
            bias_up[0],
            bias_down[0],
            jnp.where(
                owner,
                jnp.concatenate([bias_mods, column_sums(grad_embed), column_sums(grad_embed_pre)]),
                0.0,
            ),
            bias_patch[0],
            bias_head[0],
        ]
    )
    loss_part = jnp.sum(losses) / entries
    return sides, tail_left, tail_right, grad_patch, grad_head, grad_condition, grad_bias, loss_part


def on_pair(
    noisy_patches,
    targets,
    timesteps,
    labels,
    master_big,
    moment_big,
    error_big,
    factor_right,
    master_small,
    moment_small,
    biases,
    moment_bias,
    step_rates,
):
    shards = lax.axis_size("shard")
    replicas = lax.axis_size("rep")
    entries = noisy_patches.shape[0] * shards * replicas * SEQ * P_DIM
    own = jnp.stack([timesteps, labels])
    timesteps, labels = jnp.concatenate(
        [own, lax.ppermute(own, "shard", [(0, 1), (1, 0)])], axis=1
    )
    sides, tail_left, tail_right, grad_patch, grad_head, grad_condition, grad_bias, loss_part = (
        train_gradients(
            master_big, master_small, biases, noisy_patches, targets, timesteps, labels, entries
        )
    )
    images = labels.shape[0]
    strips = D // LANES

    def lines_of(matrix):
        return matrix.reshape(-1, strips, LANES).transpose(1, 0, 2)

    flat = jnp.concatenate(
        [
            lines_of(grad_patch).reshape(-1),
            lines_of(grad_head).reshape(-1),
            grad_bias,
            loss_part[None],
        ]
    )
    width = shards * replicas * 16 * LANES
    sums = jnp.pad(flat, (0, width - flat.shape[0])).reshape(shards, replicas, 16, LANES)
    label_lines = jnp.broadcast_to(labels.astype(jnp.float32)[None, :, None], (1, images, LANES))
    lines = jnp.concatenate(
        [
            lines_of(grad_condition),
            label_lines,
        ]
    ).reshape(-1, LANES)
    (new_master, new_moment, new_error, right_rows), total, gathered_lines = compress(
        step_rates,
        sides,
        tail_left,
        tail_right,
        error_big,
        factor_right.T,
        moment_big,
        master_big,
        sums,
        lines,
    )
    new_moment_small, new_master_small = update_small(
        step_rates, total, gathered_lines, moment_small.T, master_small.T
    )
    total = total.reshape(-1)
    bias_count = biases.shape[0]
    base = 2 * P_DIM * D
    total_loss = total[base + bias_count]
    new_moment_bias = momentum_decay * moment_bias + total[base : base + bias_count]
    new_biases = biases - step_rates[1] * new_moment_bias
    return (
        total_loss,
        new_master,
        new_moment,
        new_error,
        right_rows.T,
        new_master_small.T,
        new_moment_small.T,
        new_biases,
        new_moment_bias,
    )


def solution(mesh):
    in_specs = (
        P(("shard", "rep"), None),
        P(("shard", "rep"), None),
        P(("shard", "rep")),
        P(("shard", "rep")),
        P(None, "shard"),
        P(None, "shard"),
        P("rep", None, "shard"),
        P("shard", None),
        P(),
        P(),
        P(),
        P(),
        P(),
    )
    out_specs = (
        P(),
        P(None, "shard"),
        P(None, "shard"),
        P("rep", None, "shard"),
        P("shard", None),
        P(),
        P(),
        P(),
        P(),
    )
    fits = mesh.shape["shard"] == 2 and mesh.shape["rep"] == 16
    return jax.shard_map(
        on_pair if fits else on_device, mesh=mesh, in_specs=in_specs, out_specs=out_specs, check_vma=False
    )
```

```python
import functools
import math

import jax
import jax.numpy as jnp
import numpy as np
from jax import lax
from jax.experimental import pallas as pl
from jax.experimental.pallas import tpu as pltpu
from jax.sharding import PartitionSpec as P

D = 768
HEADS = 12
HEAD_DIM = 64
FF = 3072
GRID = 16
FREQ = 256
NCLASS = 1000
P_DIM = 16
SEQ = 256


highest = lax.Precision.HIGHEST
epsilon = 1e-06
tiny_value = 1e-30
momentum_decay = 0.9
half_type = jnp.bfloat16


def multiply(left_side, right_side):
    return jnp.dot(left_side, right_side, preferred_element_type=jnp.float32)


def multiply_trans(left_side, right_side):
    return lax.dot_general(
        left_side, right_side, (((1,), (1,)), ((), ())), preferred_element_type=jnp.float32
    )


def outer_sum(left_side, right_side):
    return lax.dot_general(
        left_side, right_side, (((0,), (0,)), ((), ())), preferred_element_type=jnp.float32
    )


def exact_outer(left_side, right_side):
    return lax.dot_general(
        left_side,
        right_side,
        (((0,), (0,)), ((), ())),
        precision=highest,
        preferred_element_type=jnp.float32,
    )


def normalize(values):
    center = values - jnp.mean(values, axis=-1, keepdims=True)
    return center * lax.rsqrt(jnp.mean(center * center, axis=-1, keepdims=True) + epsilon)


def gelu_tanh(values):
    return jax.nn.gelu(values, approximate=True)


def slope(function, values, grad):
    unused, pullback = jax.vjp(function, values)
    return pullback(grad)[0]


def timestep_features(steps):
    half_count = FREQ // 2
    freqs = jnp.exp(-math.log(10000.0) * jnp.arange(half_count, dtype=jnp.float32) / half_count)
    angles = steps.astype(jnp.float32)[:, None] * freqs[None, :]
    return jnp.concatenate([jnp.cos(angles), jnp.sin(angles)], axis=1)


def position_table():
    quarter = D // 4
    omega = 1.0 / 10000.0 ** (jnp.arange(quarter, dtype=jnp.float32) / quarter)
    cells = jnp.arange(SEQ, dtype=jnp.int32)
    across = (cells % GRID).astype(jnp.float32)[:, None] * omega[None, :]
    downward = (cells // GRID).astype(jnp.float32)[:, None] * omega[None, :]
    return jnp.concatenate(
        [jnp.sin(across), jnp.cos(across), jnp.sin(downward), jnp.cos(downward)], axis=1
    )


def position_constant():
    quarter = D // 4
    omega = 1.0 / 10000.0 ** (np.arange(quarter, dtype=np.float32) / np.float32(quarter))
    cells = np.arange(SEQ)
    across = (cells % GRID).astype(np.float32)[:, None] * omega[None, :].astype(np.float32)
    downward = (cells // GRID).astype(np.float32)[:, None] * omega[None, :].astype(np.float32)
    return np.concatenate(
        [np.sin(across), np.cos(across), np.sin(downward), np.cos(downward)], axis=1
    ).astype(np.float32)


def split_at(matrix, edges):
    return tuple((matrix[..., edges[place] : edges[place + 1]] for place in range(len(edges) - 1)))


def split_big(matrix):
    return split_at(
        matrix,
        [
            0,
            3 * D,
            4 * D,
            4 * D + FF,
            4 * D + 2 * FF,
            10 * D + 2 * FF,
            12 * D + 2 * FF,
            13 * D + 2 * FF,
            13 * D + 2 * FF + FREQ,
        ],
    )


def split_small(matrix):
    return split_at(matrix, [0, P_DIM, P_DIM + NCLASS, 2 * P_DIM + NCLASS])


def split_bias(vector):
    return split_at(
        vector,
        [
            0,
            D,
            2 * D,
            3 * D,
            3 * D + FF,
            4 * D + FF,
            10 * D + FF,
            12 * D + FF,
            13 * D + FF,
            14 * D + FF,
            15 * D + FF,
            15 * D + FF + P_DIM,
        ],
    )


def orthonormal(factor):
    columns = []
    for place in range(factor.shape[-1]):
        vector = factor[..., place]
        for earlier in columns:
            vector = vector - jnp.sum(earlier * vector, axis=-1, keepdims=True) * earlier
        vector = vector * lax.rsqrt(jnp.sum(vector * vector, axis=-1, keepdims=True) + tiny_value)
        columns.append(vector)
    return jnp.stack(columns, axis=-1)


def column_sums(grad):
    return jnp.sum(grad.astype(jnp.float32), axis=0)


def forward(gathered, master_small, biases, noisy_patches, timesteps, labels):
    (
        attend_weight,
        output_weight,
        up_weight,
        down_weight,
        modulate_weight,
        final_weight,
        embed_second,
        embed_first,
    ) = split_big(gathered)
    patch_weight, unused_table, head_weight = split_small(master_small.astype(half_type))
    class_table = split_small(master_small)[1]
    (
        query_bias,
        value_bias,
        output_bias,
        up_bias,
        down_bias,
        modulate_bias,
        final_bias,
        second_bias,
        first_bias,
        patch_bias,
        head_bias,
    ) = split_bias(biases)
    images = noisy_patches.shape[0]
    tokens = images * SEQ
    frequency = timestep_features(timesteps).astype(half_type)
    embed_pre = multiply_trans(frequency, embed_first) + first_bias
    embed_hidden = jax.nn.silu(embed_pre).astype(half_type)
    time_embed = multiply(embed_hidden, embed_second) + second_bias
    chosen = (labels[:, None] == jnp.arange(NCLASS, dtype=jnp.int32)[None, :]).astype(jnp.float32)
    condition = time_embed + lax.dot_general(
        chosen,
        class_table,
        (((1,), (1,)), ((), ())),
        precision=highest,
        preferred_element_type=jnp.float32,
    )
    active = jax.nn.silu(condition).astype(half_type)
    modulation = multiply(active, modulate_weight) + modulate_bias
    final_mod = multiply(active, final_weight) + final_bias
    patches = noisy_patches.reshape(tokens, P_DIM)
    stream_in = (multiply_trans(patches, patch_weight) + patch_bias).reshape(
        images, SEQ, D
    ) + position_table()[None]
    shift_attn, scale_attn, gate_attn, shift_mlp, scale_mlp, gate_mlp = jnp.split(
        modulation[:, None, :], 6, axis=2
    )
    shift_final, scale_final = jnp.split(final_mod[:, None, :], 2, axis=2)
    attn_in = (
        (normalize(stream_in) * (1.0 + scale_attn) + shift_attn)
        .astype(half_type)
        .reshape(tokens, D)
    )
    qkv_bias = jnp.concatenate([query_bias, jnp.zeros_like(query_bias), value_bias])
    projected = (multiply(attn_in, attend_weight) + qkv_bias).astype(half_type)
    queries, key_rows, value_rows = [
        piece.reshape(images, SEQ, HEADS, HEAD_DIM) for piece in jnp.split(projected, 3, axis=1)
    ]
    scores = jnp.einsum(
        "nqhd,nkhd->nhqk", queries, key_rows, preferred_element_type=jnp.float32
    ) / math.sqrt(HEAD_DIM)
    highest_score = jnp.max(scores, axis=-1, keepdims=True)
    logsum = highest_score + jnp.log(
        jnp.sum(jnp.exp(scores - highest_score), axis=-1, keepdims=True)
    )
    probs_low = jnp.exp(scores - logsum).astype(half_type)
    mixed_rows = (
        jnp.einsum("nhqk,nkhd->nqhd", probs_low, value_rows, preferred_element_type=jnp.float32)
        .astype(half_type)
        .reshape(tokens, D)
    )
    attended = (multiply(mixed_rows, output_weight) + output_bias).reshape(images, SEQ, D)
    stream_mid = stream_in + gate_attn * attended
    mlp_in = (
        (normalize(stream_mid) * (1.0 + scale_mlp) + shift_mlp).astype(half_type).reshape(tokens, D)
    )
    hidden_pre = multiply(mlp_in, up_weight) + up_bias
    hidden = gelu_tanh(hidden_pre).astype(half_type)
    mlp_out = (multiply_trans(hidden, down_weight) + down_bias).reshape(images, SEQ, D)
    stream_out = stream_mid + gate_mlp * mlp_out
    final_in = (
        (normalize(stream_out) * (1.0 + scale_final) + shift_final)
        .astype(half_type)
        .reshape(tokens, D)
    )
    output = multiply(final_in, head_weight) + head_bias
    kept = dict(
        frequency=frequency,
        embed_pre=embed_pre,
        embed_hidden=embed_hidden,
        chosen=chosen,
        condition=condition,
        active=active,
        modulation=modulation,
        final_mod=final_mod,
        patches=patches,
        stream_in=stream_in,
        attn_in=attn_in,
        queries=queries,
        key_rows=key_rows,
        value_rows=value_rows,
        logsum=logsum,
        mixed_rows=mixed_rows,
        attended=attended,
        stream_mid=stream_mid,
        mlp_in=mlp_in,
        hidden_pre=hidden_pre,
        hidden=hidden,
        mlp_out=mlp_out,
        stream_out=stream_out,
        final_in=final_in,
    )
    return (output, kept)


def backward(gathered, master_small, kept, grad_output):
    (
        attend_weight,
        output_weight,
        up_weight,
        down_weight,
        modulate_weight,
        final_weight,
        embed_second,
        embed_first,
    ) = split_big(gathered)
    patch_weight, unused_table, head_weight = split_small(master_small.astype(half_type))
    images = kept["stream_in"].shape[0]
    tokens = images * SEQ
    shift_attn, scale_attn, gate_attn, shift_mlp, scale_mlp, gate_mlp = jnp.split(
        kept["modulation"][:, None, :], 6, axis=2
    )
    shift_final, scale_final = jnp.split(kept["final_mod"][:, None, :], 2, axis=2)
    grad_out = grad_output.astype(half_type)
    grad_head = outer_sum(kept["final_in"], grad_out)
    bias_head = column_sums(grad_out)
    grad_final = multiply_trans(grad_out, head_weight).reshape(images, SEQ, D)
    grad_shift_final = jnp.sum(grad_final, axis=1)
    grad_scale_final = jnp.sum(grad_final * normalize(kept["stream_out"]), axis=1)
    grad_stream = slope(normalize, kept["stream_out"], grad_final * (1.0 + scale_final))
    grad_gate_mlp = jnp.sum(grad_stream * kept["mlp_out"], axis=1)
    grad_mlp = (grad_stream * gate_mlp).reshape(tokens, D).astype(half_type)
    bias_down = column_sums(grad_mlp)
    grad_down = outer_sum(grad_mlp, kept["hidden"])
    grad_hidden = multiply(grad_mlp, down_weight)
    grad_pre = slope(gelu_tanh, kept["hidden_pre"], grad_hidden).astype(half_type)
    bias_up = column_sums(grad_pre)
    grad_up = outer_sum(kept["mlp_in"], grad_pre)
    grad_mlp_in = multiply_trans(grad_pre, up_weight).reshape(images, SEQ, D)
    grad_shift_mlp = jnp.sum(grad_mlp_in, axis=1)
    grad_scale_mlp = jnp.sum(grad_mlp_in * normalize(kept["stream_mid"]), axis=1)
    grad_stream = grad_stream + slope(
        normalize, kept["stream_mid"], grad_mlp_in * (1.0 + scale_mlp)
    )
    grad_gate_attn = jnp.sum(grad_stream * kept["attended"], axis=1)
    grad_attn = (grad_stream * gate_attn).reshape(tokens, D).astype(half_type)
    bias_output = column_sums(grad_attn)
    grad_output_weight = outer_sum(kept["mixed_rows"], grad_attn)
    grad_mixed = (
        multiply_trans(grad_attn, output_weight)
        .astype(half_type)
        .reshape(images, SEQ, HEADS, HEAD_DIM)
    )
    inverse_root = 1.0 / math.sqrt(HEAD_DIM)
    scores = (
        jnp.einsum(
            "nqhd,nkhd->nhqk", kept["queries"], kept["key_rows"], preferred_element_type=jnp.float32
        )
        * inverse_root
    )
    probs = jnp.exp(scores - kept["logsum"])
    grad_values = jnp.einsum(
        "nhqk,nqhd->nkhd", probs.astype(half_type), grad_mixed, preferred_element_type=jnp.float32
    )
    grad_probs = jnp.einsum(
        "nqhd,nkhd->nhqk", grad_mixed, kept["value_rows"], preferred_element_type=jnp.float32
    )
    grad_scores = (
        probs * (grad_probs - jnp.sum(probs * grad_probs, axis=-1, keepdims=True))
    ).astype(half_type)
    grad_queries = (
        jnp.einsum(
            "nhqk,nkhd->nqhd", grad_scores, kept["key_rows"], preferred_element_type=jnp.float32
        )
        * inverse_root
    )
    grad_keys = (
        jnp.einsum(
            "nhqk,nqhd->nkhd", grad_scores, kept["queries"], preferred_element_type=jnp.float32
        )
        * inverse_root
    )
    grad_qkv = jnp.concatenate(
        [
            grad_queries.reshape(tokens, D),
            grad_keys.reshape(tokens, D),
            grad_values.reshape(tokens, D),
        ],
        axis=1,
    ).astype(half_type)
    bias_query = column_sums(grad_qkv[:, :D])
    bias_value = column_sums(grad_qkv[:, 2 * D :])
    grad_attend = outer_sum(kept["attn_in"], grad_qkv)
    grad_attn_in = multiply_trans(grad_qkv, attend_weight).reshape(images, SEQ, D)
    grad_shift_attn = jnp.sum(grad_attn_in, axis=1)
    grad_scale_attn = jnp.sum(grad_attn_in * normalize(kept["stream_in"]), axis=1)
    grad_stream = grad_stream + slope(
        normalize, kept["stream_in"], grad_attn_in * (1.0 + scale_attn)
    )
    grad_start = grad_stream.reshape(tokens, D).astype(half_type)
    bias_patch = column_sums(grad_start)
    grad_patch = outer_sum(grad_start, kept["patches"])
    grad_mod = jnp.concatenate(
        [
            grad_shift_attn,
            grad_scale_attn,
            grad_gate_attn,
            grad_shift_mlp,
            grad_scale_mlp,
            grad_gate_mlp,
        ],
        axis=1,
    ).astype(half_type)
    grad_fmod = jnp.concatenate([grad_shift_final, grad_scale_final], axis=1).astype(half_type)
    bias_modulate = column_sums(grad_mod)
    bias_final = column_sums(grad_fmod)
    grad_modulate = outer_sum(kept["active"], grad_mod)
    grad_final_weight = outer_sum(kept["active"], grad_fmod)
    grad_active = multiply_trans(grad_mod, modulate_weight) + multiply_trans(
        grad_fmod, final_weight
    )
    grad_condition = slope(jax.nn.silu, kept["condition"], grad_active)
    grad_embed = grad_condition.astype(half_type)
    bias_second = column_sums(grad_embed)
    grad_second = outer_sum(kept["embed_hidden"], grad_embed)
    grad_embed_hidden = multiply_trans(grad_embed, embed_second)
    grad_embed_pre = slope(jax.nn.silu, kept["embed_pre"], grad_embed_hidden).astype(half_type)
    bias_first = column_sums(grad_embed_pre)
    grad_first = outer_sum(grad_embed_pre, kept["frequency"])
    grad_big = jnp.concatenate(
        [
            grad_attend,
            grad_output_weight,
            grad_up,
            grad_down,
            grad_modulate,
            grad_final_weight,
            grad_second,
            grad_first,
        ],
        axis=1,
    )
    grad_small = (grad_patch, grad_head, grad_condition)
    grad_bias = jnp.concatenate(
        [
            bias_query,
            bias_value,
            bias_output,
            bias_up,
            bias_down,
            bias_modulate,
            bias_final,
            bias_second,
            bias_first,
            bias_patch,
            bias_head,
        ]
    )
    return (grad_big, grad_small, grad_bias)


def on_device(
    noisy_patches,
    targets,
    timesteps,
    labels,
    master_big,
    moment_big,
    error_big,
    factor_right,
    master_small,
    moment_small,
    biases,
    moment_bias,
    step_rates,
):
    shards = lax.axis_size("shard")
    replicas = lax.axis_size("rep")
    gathered = lax.all_gather(master_big.astype(half_type), "shard", axis=1, tiled=True)
    output, kept = forward(gathered, master_small, biases, noisy_patches, timesteps, labels)
    entries = noisy_patches.shape[0] * shards * replicas * SEQ * P_DIM
    error = output - targets.reshape(output.shape)
    loss_part = jnp.sum(error * error) / entries
    grad_output = 2.0 * error / entries
    gathered = lax.all_gather(master_big.astype(half_type), "shard", axis=1, tiled=True)
    grad_big, (grad_patch, grad_head, grad_condition), grad_bias = backward(
        gathered, master_small, kept, grad_output
    )
    grad_table = jnp.einsum("nd,nc->dc", grad_condition, kept["chosen"], precision=highest)
    grad_small = jnp.concatenate([grad_patch, grad_table, grad_head], axis=1)
    owned = lax.psum_scatter(
        grad_big.astype(jnp.bfloat16), "shard", scatter_dimension=1, tiled=True
    ).astype(jnp.float32)
    matrices = owned + error_big[0]
    left_part = jnp.dot(
        matrices, factor_right, precision=highest, preferred_element_type=jnp.float32
    )
    small_sum, bias_sum, total_loss = lax.psum((grad_small, grad_bias, loss_part), ("shard", "rep"))
    left_sum = lax.psum(left_part, "rep")
    basis = orthonormal(left_sum)
    right_sum = lax.psum(exact_outer(matrices, basis).astype(jnp.bfloat16), "rep").astype(
        jnp.float32
    )
    approx = lax.dot_general(
        basis,
        right_sum,
        (((1,), (1,)), ((), ())),
        precision=highest,
        preferred_element_type=jnp.float32,
    )
    new_error = (matrices - approx / replicas)[None]
    new_moment = momentum_decay * moment_big + approx
    new_master = master_big - step_rates[0] * new_moment
    new_moment_small = momentum_decay * moment_small + small_sum
    new_master_small = master_small - step_rates[1] * new_moment_small
    new_moment_bias = momentum_decay * moment_bias + bias_sum
    new_biases = biases - step_rates[1] * new_moment_bias
    return (
        total_loss,
        new_master,
        new_moment,
        new_error,
        right_sum,
        new_master_small,
        new_moment_small,
        new_biases,
        new_moment_bias,
    )


MESH = pl.DeviceIdType.MESH
BLOCK = 512
PIECE = 256
EARLY = 5
KERNEL_BYTES = 34_000_000
EXCHANGE_BYTES = 50_000_000
RANK = 8
LANES = 128
REPS = 16


def sds(shape, dtype=jnp.float32):
    return jax.ShapeDtypeStruct(shape, dtype)


def split_two(values):
    high = values.astype(half_type)
    low = (values - high.astype(jnp.float32)).astype(half_type)
    return high, low


def greet(others):
    barrier = pltpu.get_barrier_semaphore()
    for other in others:
        pl.semaphore_signal(barrier, inc=1, device_id=other, device_id_type=MESH)
    return barrier, len(others)


def tail_kernel(
    attn_in_hbm,
    mixed_hbm,
    mlp_in_hbm,
    grad_mlp_hbm,
    grad_qkv_hbm,
    grad_attn_hbm,
    grad_pre_hbm,
    hidden_hbm,
    tail_left_ref,
    tail_right_ref,
    error_hbm,
    factor_ref,
    moment_hbm,
    sums_ref,
    rows_ref,
    v_ref,
    whole_ref,
    basis_cols,
    total_ref,
    gathered_ref,
    recv_hbm,
    m_hbm,
    m_ref,
    error_ref,
    recv_ref,
    left_stage,
    turned_ref,
    right_ref,
    ring_ref,
    stack_ref,
    left_acc,
    left_ref,
    plane_ref,
    column_ref,
    basis_rows,
    send_ref,
    part_ref,
    mine_ref,
    half_ref,
    share_ref,
    small_ref,
    load_sem,
    stage_sem,
    right_sem,
    recv_sem,
    moment_sem,
    left_send,
    left_recv,
    right_send,
    right_recv,
    grad_send,
    grad_recv,
    small_send,
    small_recv,
    m_sem,
):
    blocks = m_ref.shape[0]
    shard = lax.axis_index("shard")
    rep = lax.axis_index("rep")
    partner = (1 - shard, rep)
    shared = blocks - 14 * shard
    shared_there = 2 + 14 * shard
    peers = [(shard, lax.rem(rep + step, REPS)) for step in range(1, REPS)]
    barrier, count = greet([partner] + peers)

    def columns(block):
        return pl.ds(pl.multiple_of(block * BLOCK, BLOCK), BLOCK)

    ring = ring_ref.shape[0]

    def send_piece(local):
        slot = lax.rem(local, ring)
        return pltpu.make_async_remote_copy(
            src_ref=ring_ref.at[slot],
            dst_ref=recv_hbm.at[:, pl.ds(pl.multiple_of(local * PIECE, PIECE), PIECE)],
            send_sem=grad_send.at[slot],
            recv_sem=grad_recv.at[local],
            device_id=partner,
            device_id_type=MESH,
        )

    def small_copy(source, target, sent, got, who):
        return pltpu.make_async_remote_copy(
            src_ref=source,
            dst_ref=target,
            send_sem=small_send.at[sent],
            recv_sem=small_recv.at[got],
            device_id=who,
            device_id_type=MESH,
        )

    def arrived(slots, base):
        for step in range(1, REPS):
            other = lax.rem(rep + step, REPS)
            small_copy(
                slots.at[other], slots.at[other], base, base + other, peers[step - 1]
            ).wait_recv()

    def load_error(block, slot):
        return pltpu.make_async_copy(
            error_hbm.at[0, :, columns(block)], error_ref.at[slot], load_sem.at[slot]
        )

    def block_of(step):
        return lax.rem(step + 2 * shard, blocks)

    def start_loads(step):
        block, slot = block_of(step), lax.rem(step, depth)
        load_error(block, slot).start()

        @pl.when(block < shared)
        def _():
            send_piece(2 * block).wait_recv()
            send_piece(2 * block + 1).wait_recv()
            load_recv(block, slot).start()

    def load_recv(block, slot):
        return pltpu.make_async_copy(
            recv_hbm.at[:, columns(block)], recv_ref.at[slot], recv_sem.at[slot]
        )

    def save_matrix(block):
        return pltpu.make_async_copy(m_ref.at[block], m_hbm.at[block], m_sem.at[block])

    def load_moment(block):
        return pltpu.make_async_copy(
            moment_hbm.at[:, columns(block)], v_ref.at[block], moment_sem.at[block]
        )

    depth = error_ref.shape[0]
    lefts = [attn_in_hbm, mixed_hbm, mlp_in_hbm, grad_mlp_hbm]
    rights = [grad_qkv_hbm, grad_attn_hbm, grad_pre_hbm, hidden_hbm]
    window = right_ref.shape[0]
    halves = 2 * blocks

    def load_left(part):
        return pltpu.make_async_copy(lefts[part], left_stage, stage_sem.at[0])

    def load_right(part, index):
        slot = lax.rem(index, window)
        return pltpu.make_async_copy(
            rights[part].at[:, pl.ds(pl.multiple_of(index * PIECE, PIECE), PIECE)],
            right_ref.at[slot],
            right_sem.at[slot],
        )

    load_left(0).start()
    for index in range(window):
        load_right(0, index).start()
    pl.semaphore_wait(barrier, count)
    own_half = small_copy(sums_ref.at[1 - shard], half_ref, 16, 16, partner)
    own_half.start()
    rows_out = [
        small_copy(rows_ref, gathered_ref.at[shard, rep], step, rep, peers[step - 1])
        for step in range(1, REPS)
    ]
    for copy in rows_out:
        copy.start()
    gathered_ref[shard, rep] = rows_ref[...]

    high, low = split_two(factor_ref[...])
    stack_ref[...] = jnp.zeros_like(stack_ref)
    stack_ref[0:RANK] = high
    stack_ref[RANK : 2 * RANK] = low
    left_acc[...] = jnp.zeros_like(left_acc)
    edge = 0
    for part in range(4):
        number = rights[part].shape[1] // PIECE
        load_left(part).wait()
        turned_ref[...] = left_stage[...].T
        if part < 3:
            load_left(part + 1).start()

        def grad_piece(index, carry):
            load_right(part, index).wait()
            grad = multiply(turned_ref[...], right_ref[lax.rem(index, window)])

            @pl.when(index + window < number)
            def _():
                load_right(part, index + window).start()

            place = edge + index
            low_half = place < halves
            local = lax.rem(place, halves)
            mine = jnp.logical_xor(low_half, shard == 1)

            @pl.when(mine)
            def _():
                span = pl.ds(pl.multiple_of(lax.rem(local, 2) * PIECE, PIECE), PIECE)
                m_ref[lax.div(local, 2), :, span] = grad

            @pl.when(jnp.logical_not(mine))
            def _():
                @pl.when(local >= ring)
                def _():
                    send_piece(local - ring).wait_send()

                ring_ref[lax.rem(local, ring)] = grad.astype(half_type)
                send_piece(local).start()

            return carry

        lax.fori_loop(0, number, grad_piece, 0)
        edge += number
        if part < 3:
            for index in range(min(window, rights[part + 1].shape[1] // PIECE)):
                load_right(part + 1, index).start()
    for step in range(depth):
        start_loads(step)

    def gather_block(step, carry):
        block, slot = block_of(step), lax.rem(step, depth)
        load_error(block, slot).wait()

        @pl.when(block < shared)
        def _():
            load_recv(block, slot).wait()
            m_ref[block] = m_ref[block] + recv_ref[slot].astype(jnp.float32) + error_ref[slot]

        @pl.when(block >= shared)
        def _():
            m_ref[block] = error_ref[slot] + multiply(
                tail_left_ref[...], tail_right_ref[:, columns(block - shared)]
            )

        save_matrix(block).start()
        high, low = split_two(m_ref[block])
        factor = stack_ref[:, columns(block)]
        left_acc[...] += multiply_trans(high, factor) + multiply_trans(low, factor)

        @pl.when(step + depth < blocks)
        def _():
            start_loads(step + depth)

        return carry

    own_half.wait()
    half_ref[...] = half_ref[...] + sums_ref[shard]
    shares_out = [
        small_copy(
            half_ref.at[lax.rem(rep + step, REPS)],
            share_ref.at[rep],
            17 + step,
            17 + rep,
            peers[step - 1],
        )
        for step in range(1, REPS)
    ]
    for copy in shares_out:
        copy.start()
    share_ref[rep] = half_ref[rep]
    lax.fori_loop(0, blocks, gather_block, 0)
    for block in range(v_ref.shape[0]):
        load_moment(block).start()

    turned = left_acc[...].T
    left_ref[...] = turned[0:RANK] + turned[RANK : 2 * RANK]

    place = lax.rem(rep, 4)
    level = lax.div(rep, 4)
    plane_out = []
    for step in range(1, 4):
        other = lax.rem(place + step, 4)
        plane_out.append(
            pltpu.make_async_remote_copy(
                src_ref=left_ref,
                dst_ref=plane_ref.at[place],
                send_sem=left_send.at[step],
                recv_sem=left_recv.at[place],
                device_id=(shard, level * 4 + other),
                device_id_type=MESH,
            )
        )
    for copy in plane_out:
        copy.start()
    plane_ref[place] = left_ref[...]
    arrived(share_ref, 17)
    small_ref[...] = jnp.sum(share_ref[...], axis=0)
    whole_out = [
        small_copy(small_ref, total_ref.at[shard, rep], 33 + step, 33 + rep, peers[step - 1])
        for step in range(1, REPS)
    ]
    for copy in whole_out:
        copy.start()
    total_ref[shard, rep] = small_ref[...]
    for step in range(1, 4):
        other = lax.rem(place + step, 4)
        pltpu.make_async_remote_copy(
            src_ref=left_ref,
            dst_ref=plane_ref.at[other],
            send_sem=left_send.at[step],
            recv_sem=left_recv.at[other],
            device_id=(shard, level * 4 + other),
            device_id_type=MESH,
        ).wait_recv()
    plane_sum = (plane_ref[0] + plane_ref[1]) + (plane_ref[2] + plane_ref[3])
    for copy in plane_out:
        copy.wait_send()
    left_ref[...] = plane_sum
    column_out = []
    for step in range(1, 4):
        other = lax.rem(level + step, 4)
        column_out.append(
            pltpu.make_async_remote_copy(
                src_ref=left_ref,
                dst_ref=column_ref.at[level],
                send_sem=left_send.at[4 + step],
                recv_sem=left_recv.at[4 + level],
                device_id=(shard, other * 4 + place),
                device_id_type=MESH,
            )
        )
    for copy in column_out:
        copy.start()
    column_ref[level] = plane_sum
    for step in range(1, 4):
        other = lax.rem(level + step, 4)
        pltpu.make_async_remote_copy(
            src_ref=left_ref,
            dst_ref=column_ref.at[other],
            send_sem=left_send.at[4 + step],
            recv_sem=left_recv.at[4 + other],
            device_id=(shard, other * 4 + place),
            device_id_type=MESH,
        ).wait_recv()
    vectors = (column_ref[0] + column_ref[1]) + (column_ref[2] + column_ref[3])

    row_index = lax.broadcasted_iota(jnp.int32, (RANK, 1), 0)
    for place_of in range(RANK):
        row = vectors[place_of : place_of + 1]
        unit = row * lax.rsqrt(jnp.sum(row * row, axis=1, keepdims=True) + tiny_value)
        dots = jnp.sum(vectors * unit, axis=1, keepdims=True)
        vectors = jnp.where(
            row_index > place_of,
            vectors - dots * unit,
            jnp.where(row_index == place_of, unit, vectors),
        )
    high, low = split_two(vectors)
    basis_rows[...] = jnp.concatenate([high, low], axis=0)
    padded = jnp.concatenate(
        [
            high.astype(jnp.float32),
            low.astype(jnp.float32),
            jnp.zeros((LANES - 2 * RANK, vectors.shape[1]), jnp.float32),
        ],
        axis=0,
    )
    basis_cols[...] = padded.T.astype(half_type)
    for copy in column_out:
        copy.wait_send()
    arrived(gathered_ref.at[shard], 0)
    rows_across = small_copy(gathered_ref.at[shard], gathered_ref.at[shard], 49, 49, partner)
    rows_across.start()
    arrived(total_ref.at[shard], 33)
    total_across = small_copy(total_ref.at[shard], total_ref.at[shard], 50, 50, partner)
    total_across.start()

    def right_block(block, carry):
        both = multiply(basis_rows[...], m_ref[block].astype(half_type))
        send_ref[block] = (both[0:RANK] + both[RANK : 2 * RANK]).astype(half_type)
        return carry

    lax.fori_loop(0, blocks, right_block, 0)

    def right_copy(source, target, base, step, sender):
        return pltpu.make_async_remote_copy(
            src_ref=source,
            dst_ref=target,
            send_sem=right_send.at[base + step],
            recv_sem=right_recv.at[base + sender],
            device_id=peers[step - 1],
            device_id_type=MESH,
        )

    scatter = [
        right_copy(send_ref.at[lax.rem(rep + step, REPS)], part_ref.at[rep], 0, step, rep)
        for step in range(1, REPS)
    ]
    for copy in scatter:
        copy.start()
    part_ref[rep] = send_ref[rep]
    for step in range(1, REPS):
        other = lax.rem(rep + step, REPS)
        right_copy(send_ref.at[other], part_ref.at[other], 0, step, other).wait_recv()
    mine_ref[...] = jnp.sum(part_ref[...].astype(jnp.float32), axis=0).astype(half_type)
    spread = [
        right_copy(mine_ref, whole_ref.at[rep], REPS, step, rep) for step in range(1, REPS)
    ]
    for copy in spread:
        copy.start()
    whole_ref[rep] = mine_ref[...]
    for step in range(1, REPS):
        other = lax.rem(rep + step, REPS)
        right_copy(mine_ref, whole_ref.at[other], REPS, step, other).wait_recv()
    for copy in scatter + spread + rows_out + shares_out + whole_out:
        copy.wait_send()

    def sent_piece(local, carry):
        send_piece(local).wait_send()
        return carry

    sent = 2 * shared_there
    lax.fori_loop((halves - ring) * shard, sent, sent_piece, 0)
    for block in range(blocks):
        save_matrix(block).wait()
    rows_across.wait()
    total_across.wait()
    for block in range(v_ref.shape[0]):
        load_moment(block).wait()


def update_kernel(
    rates_ref,
    m_hbm,
    v_ref,
    whole_ref,
    basis_cols,
    moment_hbm,
    master_hbm,
    new_master_hbm,
    new_moment_hbm,
    new_error_hbm,
    right_ref,
    error_ref,
    moment_ref,
    master_ref,
    moment_sem,
    master_sem,
    matrix_sem,
    error_out,
    moment_out,
    master_out,
):
    pieces = BLOCK // PIECE
    blocks = m_hbm.shape[0] * pieces
    early = v_ref.shape[0] * pieces
    slots = master_ref.shape[0]
    rate = rates_ref[0]

    def columns(block):
        return pl.ds(pl.multiple_of(block * PIECE, PIECE), PIECE)

    def load_master(block, slot):
        return pltpu.make_async_copy(
            master_hbm.at[:, columns(block)], master_ref.at[slot], master_sem.at[slot]
        )

    def load_matrix(block, slot):
        return pltpu.make_async_copy(
            m_hbm.at[
                lax.div(block, pieces),
                :,
                pl.ds(pl.multiple_of(lax.rem(block, pieces) * PIECE, PIECE), PIECE),
            ],
            error_ref.at[slot],
            matrix_sem.at[slot],
        )

    def load_moment(block, slot):
        return pltpu.make_async_copy(
            moment_hbm.at[:, columns(block)], moment_ref.at[slot], moment_sem.at[slot]
        )

    def out_error(block, slot):
        return pltpu.make_async_copy(
            error_ref.at[slot], new_error_hbm.at[0, :, columns(block)], error_out.at[slot]
        )

    def out_moment(block, slot):
        return pltpu.make_async_copy(
            moment_ref.at[slot], new_moment_hbm.at[:, columns(block)], moment_out.at[slot]
        )

    def out_master(block, slot):
        return pltpu.make_async_copy(
            master_ref.at[slot], new_master_hbm.at[:, columns(block)], master_out.at[slot]
        )

    ahead = slots - 2
    for block in range(ahead):
        load_matrix(block, block).start()
        load_master(block, block).start()

    def update_piece(whole, piece):
        block = whole * pieces + piece
        span = slice(piece * PIECE, (piece + 1) * PIECE)
        slot = lax.rem(block, slots)
        next_slot = lax.rem(block + ahead, slots)

        @pl.when(block >= 2)
        def _():
            out_error(block - 2, next_slot).wait()
            out_moment(block - 2, next_slot).wait()
            out_master(block - 2, next_slot).wait()

        @pl.when(block + ahead < blocks)
        def _():
            load_matrix(block + ahead, next_slot).start()
            load_master(block + ahead, next_slot).start()

            @pl.when(block + ahead >= early)
            def _():
                load_moment(block + ahead, next_slot).start()

        right = whole_ref[whole, :, span]
        right_ref[:, columns(block)] = right.astype(jnp.float32)
        approx = multiply(basis_cols[:, 0 : 2 * RANK], jnp.concatenate([right, right], axis=0))
        load_matrix(block, slot).wait()
        error_ref[slot] = error_ref[slot] - approx * (1.0 / REPS)
        out_error(block, slot).start()

        @pl.when(block < early)
        def _():
            moment_ref[slot] = (
                momentum_decay * v_ref[jnp.minimum(whole, v_ref.shape[0] - 1), :, span] + approx
            )

        @pl.when(block >= early)
        def _():
            load_moment(block, slot).wait()
            moment_ref[slot] = momentum_decay * moment_ref[slot] + approx

        out_moment(block, slot).start()
        load_master(block, slot).wait()
        master_ref[slot] = master_ref[slot] - rate * moment_ref[slot]
        out_master(block, slot).start()

    def update_block(whole, carry):
        for piece in range(pieces):
            update_piece(whole, piece)
        return carry

    lax.fori_loop(0, m_hbm.shape[0], update_block, 0)
    for block in range(blocks - 2, blocks):
        out_error(block, block % slots).wait()
        out_moment(block, block % slots).wait()
        out_master(block, block % slots).wait()


def compress(rates, sides, tail_left, tail_right, error, factor_rows, moment, master, sums, lines):
    rows, cols = master.shape
    blocks = cols // BLOCK
    depth = 3
    slots = 8
    hbm = pl.BlockSpec(memory_space=pltpu.HBM)
    vmem = pl.BlockSpec(memory_space=pltpu.VMEM)
    moments, whole, basis, total, gathered, unused, matrices = pl.pallas_call(
        tail_kernel,
        out_shape=(
            pltpu.VMEM((EARLY, rows, BLOCK), jnp.float32),
            pltpu.VMEM((blocks, RANK, BLOCK), half_type),
            pltpu.VMEM((rows, LANES), half_type),
            sds((2, REPS) + sums.shape[2:]),
            sds((2, REPS) + lines.shape),
            pltpu.HBM((rows, cols), half_type),
            pltpu.HBM((blocks, rows, BLOCK), jnp.float32),
        ),
        in_specs=[hbm] * 8 + [vmem, vmem, hbm, vmem, hbm, vmem, vmem],
        out_specs=[vmem] * 5 + [pl.BlockSpec(memory_space=pltpu.HBM)] * 2,
        scratch_shapes=[
            pltpu.VMEM((blocks, rows, BLOCK), jnp.float32),
            pltpu.VMEM((depth, rows, BLOCK), jnp.float32),
            pltpu.VMEM((depth, rows, BLOCK), half_type),
            pltpu.VMEM(sides[0].shape, half_type),
            pltpu.VMEM(sides[0].shape[::-1], half_type),
            pltpu.VMEM((4, sides[0].shape[0], PIECE), half_type),
            pltpu.VMEM((4, rows, PIECE), half_type),
            pltpu.VMEM((LANES, cols), half_type),
            pltpu.VMEM((rows, LANES), jnp.float32),
            pltpu.VMEM((RANK, rows), jnp.float32),
            pltpu.VMEM((4, RANK, rows), jnp.float32),
            pltpu.VMEM((4, RANK, rows), jnp.float32),
            pltpu.VMEM((2 * RANK, rows), half_type),
            pltpu.VMEM((blocks, RANK, BLOCK), half_type),
            pltpu.VMEM((blocks, RANK, BLOCK), half_type),
            pltpu.VMEM((RANK, BLOCK), half_type),
            pltpu.VMEM(sums.shape[1:], jnp.float32),
            pltpu.VMEM(sums.shape[1:], jnp.float32),
            pltpu.VMEM(sums.shape[2:], jnp.float32),
            pltpu.SemaphoreType.DMA((depth,)),
            pltpu.SemaphoreType.DMA((1,)),
            pltpu.SemaphoreType.DMA((4,)),
            pltpu.SemaphoreType.DMA((depth,)),
            pltpu.SemaphoreType.DMA((blocks,)),
            pltpu.SemaphoreType.DMA((8,)),
            pltpu.SemaphoreType.DMA((8,)),
            pltpu.SemaphoreType.DMA((2 * REPS,)),
            pltpu.SemaphoreType.DMA((2 * REPS,)),
            pltpu.SemaphoreType.DMA((4,)),
            pltpu.SemaphoreType.DMA((2 * blocks,)),
            pltpu.SemaphoreType.DMA((51,)),
            pltpu.SemaphoreType.DMA((51,)),
            pltpu.SemaphoreType.DMA((blocks,)),
        ],
        compiler_params=pltpu.CompilerParams(
            collective_id=2, has_side_effects=True, vmem_limit_bytes=EXCHANGE_BYTES
        ),
        name="compress",
    )(*sides, tail_left, tail_right, error, factor_rows, moment, sums, lines)
    updated = pl.pallas_call(
        update_kernel,
        out_shape=(
            sds(master.shape),
            sds(moment.shape),
            sds(error.shape),
            sds((RANK, cols)),
        ),
        in_specs=[pl.BlockSpec(memory_space=pltpu.SMEM), hbm, vmem, vmem, vmem, hbm, hbm],
        out_specs=[hbm, hbm, hbm, vmem],
        scratch_shapes=[
            pltpu.VMEM((slots, rows, PIECE), jnp.float32),
            pltpu.VMEM((slots, rows, PIECE), jnp.float32),
            pltpu.VMEM((slots, rows, PIECE), jnp.float32),
            pltpu.SemaphoreType.DMA((slots,)),
            pltpu.SemaphoreType.DMA((slots,)),
            pltpu.SemaphoreType.DMA((slots,)),
            pltpu.SemaphoreType.DMA((slots,)),
            pltpu.SemaphoreType.DMA((slots,)),
            pltpu.SemaphoreType.DMA((slots,)),
        ],
        compiler_params=pltpu.CompilerParams(vmem_limit_bytes=KERNEL_BYTES),
        name="update",
    )(rates, matrices, moments, whole, basis, moment, master)
    return lax.optimization_barrier((tuple(updated), total, gathered))


def small_kernel(
    rates_ref, sums_ref, lines_ref, moment_ref, master_ref, new_moment_ref, new_master_ref
):
    step = pl.program_id(0)
    height = moment_ref.shape[0]
    images = lines_ref.shape[1] * 8
    strips = D // LANES

    def piece(place):
        return lines_ref[1, :, place * 8 : (place + 1) * 8, :].reshape(images, LANES)

    labels = piece(strips)[:, 0:1]
    place = lax.broadcasted_iota(jnp.int32, (images, height), 1) + (step * height - P_DIM)
    chosen = (place.astype(jnp.float32) == labels).astype(half_type)
    for strip in range(strips):
        span = slice(strip * LANES, (strip + 1) * LANES)
        high, low = split_two(piece(strip))
        new_moment_ref[:, span] = (
            momentum_decay * moment_ref[:, span] + outer_sum(chosen, high) + outer_sum(chosen, low)
        )

    def add(first, base):
        for strip in range(strips):
            span = slice(strip * LANES, (strip + 1) * LANES)
            new_moment_ref[first : first + P_DIM, span] += sums_ref[
                base + strip * P_DIM : base + (strip + 1) * P_DIM, :
            ]

    @pl.when(step == 0)
    def _():
        add(0, 0)

    @pl.when(step == pl.num_programs(0) - 1)
    def _():
        add(height - P_DIM, strips * P_DIM)

    new_master_ref[...] = master_ref[...] - rates_ref[1] * new_moment_ref[...]


def update_small(rates, total, gathered, moment, master):
    rows = moment.shape[0]
    steps = 3
    vmem = pl.BlockSpec(memory_space=pltpu.VMEM)
    block = pl.BlockSpec((rows // steps, D), lambda step: (step, 0))
    return pl.pallas_call(
        small_kernel,
        grid=(steps,),
        out_shape=(sds(moment.shape), sds(master.shape)),
        in_specs=[pl.BlockSpec(memory_space=pltpu.SMEM), vmem, vmem, block, block],
        out_specs=[block, block],
        name="update_small",
    )(rates, total.reshape(-1, LANES), gathered, moment, master)


GROUP = 2 * HEAD_DIM
CHUNK = 768
UNROLL = 6


def unit_rows(values):
    center = values - jnp.mean(values, axis=-1, keepdims=True)
    inverse = lax.rsqrt(jnp.mean(center * center, axis=-1, keepdims=True) + epsilon)
    return center * inverse, inverse


def unit_back(unit, inverse, grad):
    return inverse * (
        grad
        - jnp.mean(grad, axis=-1, keepdims=True)
        - unit * jnp.mean(grad * unit, axis=-1, keepdims=True)
    )


def gelu_both(values):
    scale = math.sqrt(2.0 / math.pi)
    square = values * values
    bent = jnp.tanh(scale * (values + 0.044715 * (values * square)))
    half = 0.5 * (1.0 + bent)
    slope = half + 0.5 * values * (1.0 - bent * bent) * (scale * (1.0 + 0.134145 * square))
    return values * half, slope


def token_sum(values):
    return jnp.sum(values, axis=0, keepdims=True)


def image_kernel(
    entries,
    patches_ref,
    targets_ref,
    active_ref,
    mod_bias_ref,
    place_ref,
    patch_weight_ref,
    head_weight_ref,
    qkv_bias_ref,
    output_bias_ref,
    up_bias_ref,
    down_bias_ref,
    patch_bias_ref,
    head_bias_ref,
    master_hbm,
    attn_in_ref,
    mixed_ref,
    mlp_in_ref,
    hidden_ref,
    grad_qkv_ref,
    grad_attn_ref,
    grad_pre_ref,
    grad_mlp_ref,
    both_grads_ref,
    grad_patch_ref,
    grad_head_ref,
    bias_qkv_ref,
    bias_output_ref,
    bias_up_ref,
    bias_down_ref,
    bias_patch_ref,
    bias_head_ref,
    loss_ref,
    weight_ref,
    qkv_ref,
    probs_ref,
    slope_ref,
    unit_start_ref,
    unit_mid_ref,
    stream_ref,
    attended_ref,
    mlp_out_ref,
    grad_mixed_ref,
    total_ref,
    stage_ref,
    flat_mods_ref,
    mods_ref,
    got_mods_ref,
    mod_grad_ref,
    got_grads_ref,
    stage_sem,
    weight_send,
    weight_recv,
    mod_send,
    mod_recv,
):
    image = pl.program_id(0)
    last = pl.num_programs(0) - 1
    images = mods_ref.shape[0]
    edges = [0, 3 * D, 4 * D, 4 * D + FF, 4 * D + 2 * FF]
    shard = lax.axis_index("shard")
    partner = (1 - shard, lax.axis_index("rep"))
    cols = master_hbm.shape[1]
    first_count = cols // BLOCK
    all_count = edges[4] // BLOCK
    count = first_count - (2 * first_count - all_count) * shard
    depth = stage_ref.shape[0]
    loads = first_count - 2 * shard

    def load(block):
        slot = lax.rem(block, depth)
        return pltpu.make_async_copy(
            master_hbm.at[:, pl.ds(pl.multiple_of(block * BLOCK, BLOCK), BLOCK)],
            stage_ref.at[slot],
            stage_sem.at[slot],
        )

    def weight_copy(block):
        span = pl.ds(pl.multiple_of(block * BLOCK, BLOCK), BLOCK)
        return pltpu.make_async_remote_copy(
            src_ref=weight_ref.at[:, span],
            dst_ref=weight_ref.at[:, span],
            send_sem=weight_send.at[block],
            recv_sem=weight_recv.at[block],
            device_id=partner,
            device_id_type=MESH,
        )

    def mod_copy(source, target, place):
        return pltpu.make_async_remote_copy(
            src_ref=source,
            dst_ref=target,
            send_sem=mod_send.at[place],
            recv_sem=mod_recv.at[place],
            device_id=partner,
            device_id_type=MESH,
        )

    mods_across = mod_copy(flat_mods_ref, got_mods_ref, 0)
    grads_across = mod_copy(mod_grad_ref, got_grads_ref, 1)

    sums = [
        grad_patch_ref,
        grad_head_ref,
        bias_qkv_ref,
        bias_output_ref,
        bias_up_ref,
        bias_down_ref,
        bias_patch_ref,
        bias_head_ref,
        loss_ref,
    ]

    @pl.when(image == 0)
    def _():
        for block in range(2):
            load(block).start()
        barrier, greeted = greet([partner])
        pl.semaphore_wait(barrier, greeted)
        for total in sums:
            total[...] = jnp.zeros_like(total)

        def cast(block, carry):
            @pl.when(block + 2 < loads)
            def _():
                load(block + 2).start()

            load(block).wait()
            low_weight = stage_ref[lax.rem(block, depth)].astype(half_type)

            @pl.when(block < count)
            def _():
                place = shard * first_count + block
                weight_ref[:, pl.ds(pl.multiple_of(place * BLOCK, BLOCK), BLOCK)] = low_weight
                weight_copy(place).start()

            @pl.when(block >= count)
            def _():
                span = pl.ds(pl.multiple_of((block - count) * BLOCK, BLOCK), BLOCK)
                flat_mods_ref[:, span] = (
                    multiply(active_ref[...], low_weight) + mod_bias_ref[:, span]
                )
            return carry

        lax.fori_loop(0, loads, cast, 0)

        @pl.when(shard == 1)
        def _():
            mods_across.start()
            for place in range(8):
                mods_ref[:, place, :] = flat_mods_ref[0:images, place * D : (place + 1) * D]

        @pl.when(shard == 0)
        def _():
            mods_across.wait_recv()
            for place in range(8):
                mods_ref[:, place, :] = got_mods_ref[
                    images : 2 * images, place * D : (place + 1) * D
                ]

    stops = [-(-edge // BLOCK) for edge in edges]

    def arrived(part):
        @pl.when(jnp.logical_and(image == 0, shard == 1))
        def _():
            for block in range(stops[part], min(stops[part + 1], first_count)):
                weight_copy(block).wait_recv()

        if stops[part + 1] > first_count:

            @pl.when(jnp.logical_and(image == 0, shard == 0))
            def _():
                for block in range(first_count, all_count):
                    weight_copy(block).wait_recv()

    def modulation(place):
        return mods_ref[image, place : place + 1, :]

    def weight(first, width):
        return weight_ref[:, pl.ds(first, width)]

    patches = patches_ref[...]
    start = multiply(patches, patch_weight_ref[...]) + patch_bias_ref[...] + place_ref[...]
    stream_ref[...] = start
    unit, inverse_start = unit_rows(start)
    unit_start_ref[...] = unit
    attn_in_ref[...] = (unit * (1.0 + modulation(1)) + modulation(0)).astype(half_type)
    arrived(0)
    for part in range(3):
        span = slice(part * D, (part + 1) * D)
        qkv_ref[:, span] = (
            multiply(attn_in_ref[...], weight_ref[:, span]) + qkv_bias_ref[:, span]
        ).astype(half_type)

    scale = 1.0 / math.sqrt(HEAD_DIM)
    first_half = lax.broadcasted_iota(jnp.int32, (1, GROUP), 1) < HEAD_DIM

    def pair_slice(ref, part, pair):
        return ref[:, pl.ds(pl.multiple_of(part * D + pair * GROUP, GROUP), GROUP)]

    def halves(values):
        nothing = jnp.zeros_like(values)
        return jnp.where(first_half, values, nothing), jnp.where(first_half, nothing, values)

    def attend(pair, carry):
        queries = pair_slice(qkv_ref, 0, pair)
        keys = halves(pair_slice(qkv_ref, 1, pair))
        turned = pair_slice(qkv_ref, 2, pair).T
        rows = []
        for half in range(2):
            scores = multiply_trans(keys[half], queries) * scale
            weights = jnp.exp(scores - jnp.max(scores, axis=0, keepdims=True))
            probs = weights * (1.0 / jnp.sum(weights, axis=0, keepdims=True))
            probs_ref[2 * pair + half] = probs
            rows.append(
                multiply(
                    turned[half * HEAD_DIM : (half + 1) * HEAD_DIM], probs.astype(half_type)
                )
            )
        mixed_ref[:, pl.ds(pl.multiple_of(pair * GROUP, GROUP), GROUP)] = (
            jnp.concatenate(rows, axis=0).T.astype(half_type)
        )
        return carry

    lax.fori_loop(0, HEADS // 2, attend, 0, unroll=UNROLL)
    arrived(1)
    attended = multiply(mixed_ref[...], weight_ref[:, edges[1] : edges[2]]) + output_bias_ref[...]
    attended_ref[...] = attended
    middle = stream_ref[...] + modulation(2) * attended
    stream_ref[...] = middle
    unit, inverse_mid = unit_rows(middle)
    unit_mid_ref[...] = unit
    mlp_in_ref[...] = (unit * (1.0 + modulation(4)) + modulation(3)).astype(half_type)
    arrived(2)
    arrived(3)
    total_ref[...] = jnp.zeros_like(total_ref) + down_bias_ref[...]
    for part in range(FF // CHUNK):
        span = slice(part * CHUNK, (part + 1) * CHUNK)
        before = (
            multiply(mlp_in_ref[...], weight(edges[2] + part * CHUNK, CHUNK)) + up_bias_ref[:, span]
        )
        after, slope_part = gelu_both(before)
        slope_ref[:, span] = slope_part
        after = after.astype(half_type)
        hidden_ref[:, span] = after
        total_ref[...] += multiply_trans(after, weight(edges[3] + part * CHUNK, CHUNK))
    mlp_out_ref[...] = total_ref[...]
    unit, inverse_end = unit_rows(stream_ref[...] + modulation(5) * total_ref[...])
    final_in = (unit * (1.0 + modulation(7)) + modulation(6)).astype(half_type)
    error = (
        multiply_trans(final_in, head_weight_ref[...]) + head_bias_ref[...] - targets_ref[...]
    )
    loss_ref[...] += token_sum(error * error)
    grad_out = (error * (2.0 / entries)).astype(half_type)
    bias_head_ref[...] += token_sum(grad_out.astype(jnp.float32))
    grad_head_ref[...] += outer_sum(grad_out, final_in)

    grad_final = multiply(grad_out, head_weight_ref[...])
    mod_grad_ref[image, 6:7] = token_sum(grad_final)
    mod_grad_ref[image, 7:8] = token_sum(grad_final * unit)
    grad_stream = unit_back(unit, inverse_end, grad_final * (1.0 + modulation(7)))
    stream_ref[...] = grad_stream
    mod_grad_ref[image, 5:6] = token_sum(grad_stream * mlp_out_ref[...])
    grad_mlp = (grad_stream * modulation(5)).astype(half_type)
    grad_mlp_ref[...] = grad_mlp
    bias_down_ref[...] += token_sum(grad_mlp.astype(jnp.float32))
    total_ref[...] = jnp.zeros_like(total_ref)
    for part in range(FF // CHUNK):
        span = slice(part * CHUNK, (part + 1) * CHUNK)
        grad_pre = (
            multiply(grad_mlp_ref[...], weight(edges[3] + part * CHUNK, CHUNK)) * slope_ref[:, span]
        ).astype(half_type)
        grad_pre_ref[:, span] = grad_pre
        bias_up_ref[:, span] += token_sum(grad_pre.astype(jnp.float32))
        total_ref[...] += multiply_trans(grad_pre, weight(edges[2] + part * CHUNK, CHUNK))
    grad_in = total_ref[...]
    unit = unit_mid_ref[...]
    mod_grad_ref[image, 3:4] = token_sum(grad_in)
    mod_grad_ref[image, 4:5] = token_sum(grad_in * unit)
    grad_stream = stream_ref[...] + unit_back(unit, inverse_mid, grad_in * (1.0 + modulation(4)))
    stream_ref[...] = grad_stream
    mod_grad_ref[image, 2:3] = token_sum(grad_stream * attended_ref[...])
    grad_attn = (grad_stream * modulation(2)).astype(half_type)
    grad_attn_ref[...] = grad_attn
    bias_output_ref[...] += token_sum(grad_attn.astype(jnp.float32))
    grad_mixed_ref[...] = multiply_trans(grad_attn, weight_ref[:, edges[1] : edges[2]]).astype(
        half_type
    )

    def attend_back(pair, carry):
        queries = pair_slice(qkv_ref, 0, pair)
        keys_turned = pair_slice(qkv_ref, 1, pair).T
        values = halves(pair_slice(qkv_ref, 2, pair))
        grads = pair_slice(grad_mixed_ref, 0, pair)
        rows, key_grads, value_grads = [], [], []
        for half in range(2):
            probs = probs_ref[2 * pair + half]
            grad_probs = multiply_trans(values[half], grads)
            value_grads.append(multiply(probs.astype(half_type), grads))
            product = probs * grad_probs
            grad_scores = (product - probs * token_sum(product)).astype(half_type)
            key_grads.append(multiply(grad_scores, queries))
            rows.append(
                multiply(keys_turned[half * HEAD_DIM : (half + 1) * HEAD_DIM], grad_scores)
            )

        def put(part, values):
            grad_qkv_ref[:, pl.ds(pl.multiple_of(part * D + pair * GROUP, GROUP), GROUP)] = (
                values.astype(half_type)
            )

        put(0, jnp.concatenate(rows, axis=0).T * scale)
        put(1, jnp.where(first_half, key_grads[0], key_grads[1]) * scale)
        put(2, jnp.where(first_half, value_grads[0], value_grads[1]))
        return carry

    lax.fori_loop(0, HEADS // 2, attend_back, 0, unroll=UNROLL)
    bias_qkv_ref[...] += token_sum(grad_qkv_ref[...].astype(jnp.float32))
    grad_in = multiply_trans(grad_qkv_ref[...], weight_ref[:, : edges[1]])
    unit = unit_start_ref[...]
    mod_grad_ref[image, 0:1] = token_sum(grad_in)
    mod_grad_ref[image, 1:2] = token_sum(grad_in * unit)
    grad_start = (
        stream_ref[...] + unit_back(unit, inverse_start, grad_in * (1.0 + modulation(1)))
    ).astype(half_type)
    bias_patch_ref[...] += token_sum(grad_start.astype(jnp.float32))
    grad_patch_ref[...] += outer_sum(patches, grad_start)

    @pl.when(image == last)
    def _():
        grads_across.start()

        def sent(block, carry):
            weight_copy(shard * first_count + block).wait_send()
            return carry

        lax.fori_loop(0, count, sent, 0)
        @pl.when(shard == 1)
        def _():
            mods_across.wait_send()

        both_grads_ref[0:images] = mod_grad_ref[...]
        grads_across.wait()
        both_grads_ref[images : 2 * images] = got_grads_ref[...]


def run_images(
    patches, targets, active, mod_bias, places, patch_weight, head_weight, biases, master, entries
):
    images = active.shape[0] // 2
    tokens = images * SEQ
    wide = 4 * D + 2 * FF

    def rows(width):
        return pl.BlockSpec((SEQ, width), lambda image: (image, 0))

    def fixed(array):
        return pl.BlockSpec(array.shape, lambda image: (0,) * len(array.shape))

    vector = [(P_DIM, D), (P_DIM, D), (1, 3 * D), (1, D), (1, FF), (1, D), (1, D), (1, P_DIM)]
    vector = [sds(shape) for shape in vector + [(1, P_DIM)]]
    saved = [D, D, D, FF, 3 * D, D, FF, D]
    return pl.pallas_call(
        functools.partial(image_kernel, entries),
        grid=(images,),
        out_shape=[sds((tokens, width), half_type) for width in saved]
        + [sds((2 * images, 8, D))]
        + vector,
        in_specs=[rows(P_DIM), rows(P_DIM), fixed(active), fixed(mod_bias), fixed(places)]
        + [fixed(patch_weight), fixed(head_weight)]
        + [fixed(bias) for bias in biases]
        + [pl.BlockSpec(memory_space=pltpu.HBM)],
        out_specs=[rows(width) for width in saved] + [fixed(sds((2 * images, 8, D)))] + [fixed(item) for item in vector],
        scratch_shapes=[
            pltpu.VMEM((D, wide), half_type),
            pltpu.VMEM((SEQ, 3 * D), half_type),
            pltpu.VMEM((HEADS, SEQ, SEQ), jnp.float32),
            pltpu.VMEM((SEQ, FF), jnp.float32),
            pltpu.VMEM((SEQ, D), jnp.float32),
            pltpu.VMEM((SEQ, D), jnp.float32),
            pltpu.VMEM((SEQ, D), jnp.float32),
            pltpu.VMEM((SEQ, D), jnp.float32),
            pltpu.VMEM((SEQ, D), jnp.float32),
            pltpu.VMEM((SEQ, D), half_type),
            pltpu.VMEM((SEQ, D), jnp.float32),
            pltpu.VMEM((3, D, BLOCK), jnp.float32),
            pltpu.VMEM((2 * images, 8 * D), jnp.float32),
            pltpu.VMEM((images, 8, D), jnp.float32),
            pltpu.VMEM((2 * images, 8 * D), jnp.float32),
            pltpu.VMEM((images, 8, D), jnp.float32),
            pltpu.VMEM((images, 8, D), jnp.float32),
            pltpu.SemaphoreType.DMA((3,)),
            pltpu.SemaphoreType.DMA((wide // BLOCK,)),
            pltpu.SemaphoreType.DMA((wide // BLOCK,)),
            pltpu.SemaphoreType.DMA((2,)),
            pltpu.SemaphoreType.DMA((2,)),
        ],
        compiler_params=pltpu.CompilerParams(
            collective_id=1, has_side_effects=True, vmem_limit_bytes=60_000_000
        ),
        name="images",
    )(patches, targets, active, mod_bias, places, patch_weight, head_weight, *biases, master)


def train_gradients(master, master_small, biases, noisy_patches, targets, timesteps, labels, entries):
    owner = lax.axis_index("shard") == 1
    last = master.shape[1]
    first_edge = last - 9 * D - FREQ
    both_weight, embed_second, embed_first = split_at(
        master, [first_edge, last - D - FREQ, last - FREQ, last]
    )
    patch_weight, class_table, head_weight = split_small(master_small)
    (
        query_bias,
        value_bias,
        output_bias,
        up_bias,
        down_bias,
        modulate_bias,
        final_bias,
        second_bias,
        first_bias,
        patch_bias,
        head_bias,
    ) = split_bias(biases)
    images = noisy_patches.shape[0]
    frequency = timestep_features(timesteps).astype(half_type)
    embed_pre = multiply_trans(frequency.astype(jnp.float32), embed_first) + first_bias
    embed_hidden = jax.nn.silu(embed_pre).astype(half_type)
    time_embed = multiply(embed_hidden.astype(jnp.float32), embed_second) + second_bias
    chosen = (labels[:, None] == jnp.arange(NCLASS, dtype=jnp.int32)[None, :]).astype(jnp.float32)
    condition = time_embed + lax.dot_general(
        chosen,
        class_table,
        (((1,), (1,)), ((), ())),
        precision=highest,
        preferred_element_type=jnp.float32,
    )
    active = jax.nn.silu(condition).astype(half_type)
    mod_bias = jnp.concatenate([modulate_bias, final_bias]).reshape(1, 8 * D)
    qkv_bias = jnp.concatenate([query_bias, jnp.zeros_like(query_bias), value_bias])
    (
        attn_in,
        mixed,
        mlp_in,
        hidden,
        grad_qkv,
        grad_attn,
        grad_pre,
        grad_mlp,
        mod_grads,
        grad_patch,
        grad_head,
        bias_qkv,
        bias_output,
        bias_up,
        bias_down,
        bias_patch,
        bias_head,
        losses,
    ) = run_images(
        noisy_patches.reshape(-1, P_DIM),
        targets.reshape(-1, P_DIM),
        active,
        mod_bias,
        jnp.asarray(position_constant()),
        patch_weight.T.astype(half_type),
        head_weight.T.astype(half_type),
        [item[None] for item in (qkv_bias, output_bias, up_bias, down_bias, patch_bias, head_bias)],
        master,
        entries,
    )
    grad_mods = mod_grads.reshape(-1, 8 * D).astype(half_type)
    bias_mods = column_sums(grad_mods)
    grad_active = multiply_trans(grad_mods.astype(jnp.float32), both_weight)
    grad_condition = slope(jax.nn.silu, condition, grad_active)
    grad_embed = grad_condition.astype(half_type)
    grad_embed_hidden = multiply_trans(grad_embed.astype(jnp.float32), embed_second)
    grad_embed_pre = slope(jax.nn.silu, embed_pre, grad_embed_hidden).astype(half_type)
    tail_left = jnp.pad(
        jnp.concatenate([active, embed_hidden, grad_embed_pre]), ((0, 8), (0, 0))
    ).T
    tail_right = jnp.concatenate(
        [
            jnp.pad(grad_mods, ((0, 0), (0, D + FREQ))),
            jnp.pad(grad_embed, ((0, 0), (8 * D, FREQ))),
            jnp.pad(frequency, ((0, 16 - frequency.shape[0]), (9 * D, 0))),
        ]
    )
    sides = (attn_in, mixed, mlp_in, grad_mlp, grad_qkv, grad_attn, grad_pre, hidden)
    grad_bias = jnp.concatenate(
        [
            bias_qkv[0, :D],
            bias_qkv[0, 2 * D :],
            bias_output[0],
            bias_up[0],
            bias_down[0],
            jnp.where(
                owner,
                jnp.concatenate([bias_mods, column_sums(grad_embed), column_sums(grad_embed_pre)]),
                0.0,
            ),
            bias_patch[0],
            bias_head[0],
        ]
    )
    loss_part = jnp.sum(losses) / entries
    return sides, tail_left, tail_right, grad_patch, grad_head, grad_condition, grad_bias, loss_part


def on_pair(
    noisy_patches,
    targets,
    timesteps,
    labels,
    master_big,
    moment_big,
    error_big,
    factor_right,
    master_small,
    moment_small,
    biases,
    moment_bias,
    step_rates,
):
    shards = lax.axis_size("shard")
    replicas = lax.axis_size("rep")
    entries = noisy_patches.shape[0] * shards * replicas * SEQ * P_DIM
    own = jnp.stack([timesteps, labels])
    timesteps, labels = jnp.concatenate(
        [own, lax.ppermute(own, "shard", [(0, 1), (1, 0)])], axis=1
    )
    sides, tail_left, tail_right, grad_patch, grad_head, grad_condition, grad_bias, loss_part = (
        train_gradients(
            master_big, master_small, biases, noisy_patches, targets, timesteps, labels, entries
        )
    )
    images = labels.shape[0]
    strips = D // LANES

    def lines_of(matrix):
        return matrix.reshape(-1, strips, LANES).transpose(1, 0, 2)

    flat = jnp.concatenate(
        [
            lines_of(grad_patch).reshape(-1),
            lines_of(grad_head).reshape(-1),
            grad_bias,
            loss_part[None],
        ]
    )
    width = shards * replicas * 16 * LANES
    sums = jnp.pad(flat, (0, width - flat.shape[0])).reshape(shards, replicas, 16, LANES)
    label_lines = jnp.broadcast_to(labels.astype(jnp.float32)[None, :, None], (1, images, LANES))
    lines = jnp.concatenate(
        [
            lines_of(grad_condition),
            label_lines,
        ]
    ).reshape(-1, LANES)
    (new_master, new_moment, new_error, right_rows), total, gathered_lines = compress(
        step_rates,
        sides,
        tail_left,
        tail_right,
        error_big,
        factor_right.T,
        moment_big,
        master_big,
        sums,
        lines,
    )
    new_moment_small, new_master_small = update_small(
        step_rates, total, gathered_lines, moment_small.T, master_small.T
    )
    total = total.reshape(-1)
    bias_count = biases.shape[0]
    base = 2 * P_DIM * D
    total_loss = total[base + bias_count]
    new_moment_bias = momentum_decay * moment_bias + total[base : base + bias_count]
    new_biases = biases - step_rates[1] * new_moment_bias
    return (
        total_loss,
        new_master,
        new_moment,
        new_error,
        right_rows.T,
        new_master_small.T,
        new_moment_small.T,
        new_biases,
        new_moment_bias,
    )


def solution(mesh):
    in_specs = (
        P(("shard", "rep"), None),
        P(("shard", "rep"), None),
        P(("shard", "rep")),
        P(("shard", "rep")),
        P(None, "shard"),
        P(None, "shard"),
        P("rep", None, "shard"),
        P("shard", None),
        P(),
        P(),
        P(),
        P(),
        P(),
    )
    out_specs = (
        P(),
        P(None, "shard"),
        P(None, "shard"),
        P("rep", None, "shard"),
        P("shard", None),
        P(),
        P(),
        P(),
        P(),
    )
    fits = mesh.shape["shard"] == 2 and mesh.shape["rep"] == 16
    return jax.shard_map(
        on_pair if fits else on_device, mesh=mesh, in_specs=in_specs, out_specs=out_specs, check_vma=False
    )
```

```python
import functools
import math

import jax
import jax.numpy as jnp
import numpy as np
from jax import lax
from jax.experimental import pallas as pl
from jax.experimental.pallas import tpu as pltpu
from jax.sharding import PartitionSpec as P

D = 768
HEADS = 12
HEAD_DIM = 64
FF = 3072
GRID = 16
FREQ = 256
NCLASS = 1000
P_DIM = 16
SEQ = 256


highest = lax.Precision.HIGHEST
epsilon = 1e-06
tiny_value = 1e-30
momentum_decay = 0.9
half_type = jnp.bfloat16


def multiply(left_side, right_side):
    return jnp.dot(left_side, right_side, preferred_element_type=jnp.float32)


def multiply_trans(left_side, right_side):
    return lax.dot_general(
        left_side, right_side, (((1,), (1,)), ((), ())), preferred_element_type=jnp.float32
    )


def outer_sum(left_side, right_side):
    return lax.dot_general(
        left_side, right_side, (((0,), (0,)), ((), ())), preferred_element_type=jnp.float32
    )


def exact_outer(left_side, right_side):
    return lax.dot_general(
        left_side,
        right_side,
        (((0,), (0,)), ((), ())),
        precision=highest,
        preferred_element_type=jnp.float32,
    )


def normalize(values):
    center = values - jnp.mean(values, axis=-1, keepdims=True)
    return center * lax.rsqrt(jnp.mean(center * center, axis=-1, keepdims=True) + epsilon)


def gelu_tanh(values):
    return jax.nn.gelu(values, approximate=True)


def slope(function, values, grad):
    unused, pullback = jax.vjp(function, values)
    return pullback(grad)[0]


def timestep_features(steps):
    half_count = FREQ // 2
    freqs = jnp.exp(-math.log(10000.0) * jnp.arange(half_count, dtype=jnp.float32) / half_count)
    angles = steps.astype(jnp.float32)[:, None] * freqs[None, :]
    return jnp.concatenate([jnp.cos(angles), jnp.sin(angles)], axis=1)


def position_table():
    quarter = D // 4
    omega = 1.0 / 10000.0 ** (jnp.arange(quarter, dtype=jnp.float32) / quarter)
    cells = jnp.arange(SEQ, dtype=jnp.int32)
    across = (cells % GRID).astype(jnp.float32)[:, None] * omega[None, :]
    downward = (cells // GRID).astype(jnp.float32)[:, None] * omega[None, :]
    return jnp.concatenate(
        [jnp.sin(across), jnp.cos(across), jnp.sin(downward), jnp.cos(downward)], axis=1
    )


def position_constant():
    quarter = D // 4
    omega = 1.0 / 10000.0 ** (np.arange(quarter, dtype=np.float32) / np.float32(quarter))
    cells = np.arange(SEQ)
    across = (cells % GRID).astype(np.float32)[:, None] * omega[None, :].astype(np.float32)
    downward = (cells // GRID).astype(np.float32)[:, None] * omega[None, :].astype(np.float32)
    return np.concatenate(
        [np.sin(across), np.cos(across), np.sin(downward), np.cos(downward)], axis=1
    ).astype(np.float32)


def split_at(matrix, edges):
    return tuple((matrix[..., edges[place] : edges[place + 1]] for place in range(len(edges) - 1)))


def split_big(matrix):
    return split_at(
        matrix,
        [
            0,
            3 * D,
            4 * D,
            4 * D + FF,
            4 * D + 2 * FF,
            10 * D + 2 * FF,
            12 * D + 2 * FF,
            13 * D + 2 * FF,
            13 * D + 2 * FF + FREQ,
        ],
    )


def split_small(matrix):
    return split_at(matrix, [0, P_DIM, P_DIM + NCLASS, 2 * P_DIM + NCLASS])


def split_bias(vector):
    return split_at(
        vector,
        [
            0,
            D,
            2 * D,
            3 * D,
            3 * D + FF,
            4 * D + FF,
            10 * D + FF,
            12 * D + FF,
            13 * D + FF,
            14 * D + FF,
            15 * D + FF,
            15 * D + FF + P_DIM,
        ],
    )


def orthonormal(factor):
    columns = []
    for place in range(factor.shape[-1]):
        vector = factor[..., place]
        for earlier in columns:
            vector = vector - jnp.sum(earlier * vector, axis=-1, keepdims=True) * earlier
        vector = vector * lax.rsqrt(jnp.sum(vector * vector, axis=-1, keepdims=True) + tiny_value)
        columns.append(vector)
    return jnp.stack(columns, axis=-1)


def column_sums(grad):
    return jnp.sum(grad.astype(jnp.float32), axis=0)


def forward(gathered, master_small, biases, noisy_patches, timesteps, labels):
    (
        attend_weight,
        output_weight,
        up_weight,
        down_weight,
        modulate_weight,
        final_weight,
        embed_second,
        embed_first,
    ) = split_big(gathered)
    patch_weight, unused_table, head_weight = split_small(master_small.astype(half_type))
    class_table = split_small(master_small)[1]
    (
        query_bias,
        value_bias,
        output_bias,
        up_bias,
        down_bias,
        modulate_bias,
        final_bias,
        second_bias,
        first_bias,
        patch_bias,
        head_bias,
    ) = split_bias(biases)
    images = noisy_patches.shape[0]
    tokens = images * SEQ
    frequency = timestep_features(timesteps).astype(half_type)
    embed_pre = multiply_trans(frequency, embed_first) + first_bias
    embed_hidden = jax.nn.silu(embed_pre).astype(half_type)
    time_embed = multiply(embed_hidden, embed_second) + second_bias
    chosen = (labels[:, None] == jnp.arange(NCLASS, dtype=jnp.int32)[None, :]).astype(jnp.float32)
    condition = time_embed + lax.dot_general(
        chosen,
        class_table,
        (((1,), (1,)), ((), ())),
        precision=highest,
        preferred_element_type=jnp.float32,
    )
    active = jax.nn.silu(condition).astype(half_type)
    modulation = multiply(active, modulate_weight) + modulate_bias
    final_mod = multiply(active, final_weight) + final_bias
    patches = noisy_patches.reshape(tokens, P_DIM)
    stream_in = (multiply_trans(patches, patch_weight) + patch_bias).reshape(
        images, SEQ, D
    ) + position_table()[None]
    shift_attn, scale_attn, gate_attn, shift_mlp, scale_mlp, gate_mlp = jnp.split(
        modulation[:, None, :], 6, axis=2
    )
    shift_final, scale_final = jnp.split(final_mod[:, None, :], 2, axis=2)
    attn_in = (
        (normalize(stream_in) * (1.0 + scale_attn) + shift_attn)
        .astype(half_type)
        .reshape(tokens, D)
    )
    qkv_bias = jnp.concatenate([query_bias, jnp.zeros_like(query_bias), value_bias])
    projected = (multiply(attn_in, attend_weight) + qkv_bias).astype(half_type)
    queries, key_rows, value_rows = [
        piece.reshape(images, SEQ, HEADS, HEAD_DIM) for piece in jnp.split(projected, 3, axis=1)
    ]
    scores = jnp.einsum(
        "nqhd,nkhd->nhqk", queries, key_rows, preferred_element_type=jnp.float32
    ) / math.sqrt(HEAD_DIM)
    highest_score = jnp.max(scores, axis=-1, keepdims=True)
    logsum = highest_score + jnp.log(
        jnp.sum(jnp.exp(scores - highest_score), axis=-1, keepdims=True)
    )
    probs_low = jnp.exp(scores - logsum).astype(half_type)
    mixed_rows = (
        jnp.einsum("nhqk,nkhd->nqhd", probs_low, value_rows, preferred_element_type=jnp.float32)
        .astype(half_type)
        .reshape(tokens, D)
    )
    attended = (multiply(mixed_rows, output_weight) + output_bias).reshape(images, SEQ, D)
    stream_mid = stream_in + gate_attn * attended
    mlp_in = (
        (normalize(stream_mid) * (1.0 + scale_mlp) + shift_mlp).astype(half_type).reshape(tokens, D)
    )
    hidden_pre = multiply(mlp_in, up_weight) + up_bias
    hidden = gelu_tanh(hidden_pre).astype(half_type)
    mlp_out = (multiply_trans(hidden, down_weight) + down_bias).reshape(images, SEQ, D)
    stream_out = stream_mid + gate_mlp * mlp_out
    final_in = (
        (normalize(stream_out) * (1.0 + scale_final) + shift_final)
        .astype(half_type)
        .reshape(tokens, D)
    )
    output = multiply(final_in, head_weight) + head_bias
    kept = dict(
        frequency=frequency,
        embed_pre=embed_pre,
        embed_hidden=embed_hidden,
        chosen=chosen,
        condition=condition,
        active=active,
        modulation=modulation,
        final_mod=final_mod,
        patches=patches,
        stream_in=stream_in,
        attn_in=attn_in,
        queries=queries,
        key_rows=key_rows,
        value_rows=value_rows,
        logsum=logsum,
        mixed_rows=mixed_rows,
        attended=attended,
        stream_mid=stream_mid,
        mlp_in=mlp_in,
        hidden_pre=hidden_pre,
        hidden=hidden,
        mlp_out=mlp_out,
        stream_out=stream_out,
        final_in=final_in,
    )
    return (output, kept)


def backward(gathered, master_small, kept, grad_output):
    (
        attend_weight,
        output_weight,
        up_weight,
        down_weight,
        modulate_weight,
        final_weight,
        embed_second,
        embed_first,
    ) = split_big(gathered)
    patch_weight, unused_table, head_weight = split_small(master_small.astype(half_type))
    images = kept["stream_in"].shape[0]
    tokens = images * SEQ
    shift_attn, scale_attn, gate_attn, shift_mlp, scale_mlp, gate_mlp = jnp.split(
        kept["modulation"][:, None, :], 6, axis=2
    )
    shift_final, scale_final = jnp.split(kept["final_mod"][:, None, :], 2, axis=2)
    grad_out = grad_output.astype(half_type)
    grad_head = outer_sum(kept["final_in"], grad_out)
    bias_head = column_sums(grad_out)
    grad_final = multiply_trans(grad_out, head_weight).reshape(images, SEQ, D)
    grad_shift_final = jnp.sum(grad_final, axis=1)
    grad_scale_final = jnp.sum(grad_final * normalize(kept["stream_out"]), axis=1)
    grad_stream = slope(normalize, kept["stream_out"], grad_final * (1.0 + scale_final))
    grad_gate_mlp = jnp.sum(grad_stream * kept["mlp_out"], axis=1)
    grad_mlp = (grad_stream * gate_mlp).reshape(tokens, D).astype(half_type)
    bias_down = column_sums(grad_mlp)
    grad_down = outer_sum(grad_mlp, kept["hidden"])
    grad_hidden = multiply(grad_mlp, down_weight)
    grad_pre = slope(gelu_tanh, kept["hidden_pre"], grad_hidden).astype(half_type)
    bias_up = column_sums(grad_pre)
    grad_up = outer_sum(kept["mlp_in"], grad_pre)
    grad_mlp_in = multiply_trans(grad_pre, up_weight).reshape(images, SEQ, D)
    grad_shift_mlp = jnp.sum(grad_mlp_in, axis=1)
    grad_scale_mlp = jnp.sum(grad_mlp_in * normalize(kept["stream_mid"]), axis=1)
    grad_stream = grad_stream + slope(
        normalize, kept["stream_mid"], grad_mlp_in * (1.0 + scale_mlp)
    )
    grad_gate_attn = jnp.sum(grad_stream * kept["attended"], axis=1)
    grad_attn = (grad_stream * gate_attn).reshape(tokens, D).astype(half_type)
    bias_output = column_sums(grad_attn)
    grad_output_weight = outer_sum(kept["mixed_rows"], grad_attn)
    grad_mixed = (
        multiply_trans(grad_attn, output_weight)
        .astype(half_type)
        .reshape(images, SEQ, HEADS, HEAD_DIM)
    )
    inverse_root = 1.0 / math.sqrt(HEAD_DIM)
    scores = (
        jnp.einsum(
            "nqhd,nkhd->nhqk", kept["queries"], kept["key_rows"], preferred_element_type=jnp.float32
        )
        * inverse_root
    )
    probs = jnp.exp(scores - kept["logsum"])
    grad_values = jnp.einsum(
        "nhqk,nqhd->nkhd", probs.astype(half_type), grad_mixed, preferred_element_type=jnp.float32
    )
    grad_probs = jnp.einsum(
        "nqhd,nkhd->nhqk", grad_mixed, kept["value_rows"], preferred_element_type=jnp.float32
    )
    grad_scores = (
        probs * (grad_probs - jnp.sum(probs * grad_probs, axis=-1, keepdims=True))
    ).astype(half_type)
    grad_queries = (
        jnp.einsum(
            "nhqk,nkhd->nqhd", grad_scores, kept["key_rows"], preferred_element_type=jnp.float32
        )
        * inverse_root
    )
    grad_keys = (
        jnp.einsum(
            "nhqk,nqhd->nkhd", grad_scores, kept["queries"], preferred_element_type=jnp.float32
        )
        * inverse_root
    )
    grad_qkv = jnp.concatenate(
        [
            grad_queries.reshape(tokens, D),
            grad_keys.reshape(tokens, D),
            grad_values.reshape(tokens, D),
        ],
        axis=1,
    ).astype(half_type)
    bias_query = column_sums(grad_qkv[:, :D])
    bias_value = column_sums(grad_qkv[:, 2 * D :])
    grad_attend = outer_sum(kept["attn_in"], grad_qkv)
    grad_attn_in = multiply_trans(grad_qkv, attend_weight).reshape(images, SEQ, D)
    grad_shift_attn = jnp.sum(grad_attn_in, axis=1)
    grad_scale_attn = jnp.sum(grad_attn_in * normalize(kept["stream_in"]), axis=1)
    grad_stream = grad_stream + slope(
        normalize, kept["stream_in"], grad_attn_in * (1.0 + scale_attn)
    )
    grad_start = grad_stream.reshape(tokens, D).astype(half_type)
    bias_patch = column_sums(grad_start)
    grad_patch = outer_sum(grad_start, kept["patches"])
    grad_mod = jnp.concatenate(
        [
            grad_shift_attn,
            grad_scale_attn,
            grad_gate_attn,
            grad_shift_mlp,
            grad_scale_mlp,
            grad_gate_mlp,
        ],
        axis=1,
    ).astype(half_type)
    grad_fmod = jnp.concatenate([grad_shift_final, grad_scale_final], axis=1).astype(half_type)
    bias_modulate = column_sums(grad_mod)
    bias_final = column_sums(grad_fmod)
    grad_modulate = outer_sum(kept["active"], grad_mod)
    grad_final_weight = outer_sum(kept["active"], grad_fmod)
    grad_active = multiply_trans(grad_mod, modulate_weight) + multiply_trans(
        grad_fmod, final_weight
    )
    grad_condition = slope(jax.nn.silu, kept["condition"], grad_active)
    grad_embed = grad_condition.astype(half_type)
    bias_second = column_sums(grad_embed)
    grad_second = outer_sum(kept["embed_hidden"], grad_embed)
    grad_embed_hidden = multiply_trans(grad_embed, embed_second)
    grad_embed_pre = slope(jax.nn.silu, kept["embed_pre"], grad_embed_hidden).astype(half_type)
    bias_first = column_sums(grad_embed_pre)
    grad_first = outer_sum(grad_embed_pre, kept["frequency"])
    grad_big = jnp.concatenate(
        [
            grad_attend,
            grad_output_weight,
            grad_up,
            grad_down,
            grad_modulate,
            grad_final_weight,
            grad_second,
            grad_first,
        ],
        axis=1,
    )
    grad_small = (grad_patch, grad_head, grad_condition)
    grad_bias = jnp.concatenate(
        [
            bias_query,
            bias_value,
            bias_output,
            bias_up,
            bias_down,
            bias_modulate,
            bias_final,
            bias_second,
            bias_first,
            bias_patch,
            bias_head,
        ]
    )
    return (grad_big, grad_small, grad_bias)


def on_device(
    noisy_patches,
    targets,
    timesteps,
    labels,
    master_big,
    moment_big,
    error_big,
    factor_right,
    master_small,
    moment_small,
    biases,
    moment_bias,
    step_rates,
):
    shards = lax.axis_size("shard")
    replicas = lax.axis_size("rep")
    gathered = lax.all_gather(master_big.astype(half_type), "shard", axis=1, tiled=True)
    output, kept = forward(gathered, master_small, biases, noisy_patches, timesteps, labels)
    entries = noisy_patches.shape[0] * shards * replicas * SEQ * P_DIM
    error = output - targets.reshape(output.shape)
    loss_part = jnp.sum(error * error) / entries
    grad_output = 2.0 * error / entries
    gathered = lax.all_gather(master_big.astype(half_type), "shard", axis=1, tiled=True)
    grad_big, (grad_patch, grad_head, grad_condition), grad_bias = backward(
        gathered, master_small, kept, grad_output
    )
    grad_table = jnp.einsum("nd,nc->dc", grad_condition, kept["chosen"], precision=highest)
    grad_small = jnp.concatenate([grad_patch, grad_table, grad_head], axis=1)
    owned = lax.psum_scatter(
        grad_big.astype(jnp.bfloat16), "shard", scatter_dimension=1, tiled=True
    ).astype(jnp.float32)
    matrices = owned + error_big[0]
    left_part = jnp.dot(
        matrices, factor_right, precision=highest, preferred_element_type=jnp.float32
    )
    small_sum, bias_sum, total_loss = lax.psum((grad_small, grad_bias, loss_part), ("shard", "rep"))
    left_sum = lax.psum(left_part, "rep")
    basis = orthonormal(left_sum)
    right_sum = lax.psum(exact_outer(matrices, basis).astype(jnp.bfloat16), "rep").astype(
        jnp.float32
    )
    approx = lax.dot_general(
        basis,
        right_sum,
        (((1,), (1,)), ((), ())),
        precision=highest,
        preferred_element_type=jnp.float32,
    )
    new_error = (matrices - approx / replicas)[None]
    new_moment = momentum_decay * moment_big + approx
    new_master = master_big - step_rates[0] * new_moment
    new_moment_small = momentum_decay * moment_small + small_sum
    new_master_small = master_small - step_rates[1] * new_moment_small
    new_moment_bias = momentum_decay * moment_bias + bias_sum
    new_biases = biases - step_rates[1] * new_moment_bias
    return (
        total_loss,
        new_master,
        new_moment,
        new_error,
        right_sum,
        new_master_small,
        new_moment_small,
        new_biases,
        new_moment_bias,
    )


MESH = pl.DeviceIdType.MESH
BLOCK = 512
PIECE = 256
EARLY = 7
KERNEL_BYTES = 34_000_000
EXCHANGE_BYTES = 50_000_000
RANK = 8
LANES = 128
REPS = 16


def sds(shape, dtype=jnp.float32):
    return jax.ShapeDtypeStruct(shape, dtype)


def split_two(values):
    high = values.astype(half_type)
    low = (values - high.astype(jnp.float32)).astype(half_type)
    return high, low


def greet(others):
    barrier = pltpu.get_barrier_semaphore()
    for other in others:
        pl.semaphore_signal(barrier, inc=1, device_id=other, device_id_type=MESH)
    return barrier, len(others)


def tail_kernel(
    attn_in_hbm,
    mixed_hbm,
    mlp_in_hbm,
    grad_mlp_hbm,
    grad_qkv_hbm,
    grad_attn_hbm,
    grad_pre_hbm,
    hidden_hbm,
    tail_left_ref,
    tail_right_ref,
    error_hbm,
    factor_ref,
    moment_hbm,
    sums_ref,
    rows_ref,
    v_ref,
    whole_ref,
    basis_cols,
    total_ref,
    gathered_ref,
    recv_hbm,
    m_hbm,
    m_ref,
    error_ref,
    recv_ref,
    left_stage,
    turned_ref,
    right_ref,
    ring_ref,
    stack_ref,
    left_acc,
    left_ref,
    plane_ref,
    column_ref,
    basis_rows,
    send_ref,
    part_ref,
    mine_ref,
    half_ref,
    share_ref,
    small_ref,
    load_sem,
    stage_sem,
    right_sem,
    recv_sem,
    moment_sem,
    left_send,
    left_recv,
    right_send,
    right_recv,
    grad_send,
    grad_recv,
    small_send,
    small_recv,
    m_sem,
):
    blocks = m_ref.shape[0]
    shard = lax.axis_index("shard")
    rep = lax.axis_index("rep")
    partner = (1 - shard, rep)
    shared = blocks - 14 * shard
    shared_there = 2 + 14 * shard
    peers = [(shard, lax.rem(rep + step, REPS)) for step in range(1, REPS)]
    barrier, count = greet([partner] + peers)

    def columns(block):
        return pl.ds(pl.multiple_of(block * BLOCK, BLOCK), BLOCK)

    ring = ring_ref.shape[0]

    def send_piece(local):
        slot = lax.rem(local, ring)
        return pltpu.make_async_remote_copy(
            src_ref=ring_ref.at[slot],
            dst_ref=recv_hbm.at[:, pl.ds(pl.multiple_of(local * PIECE, PIECE), PIECE)],
            send_sem=grad_send.at[slot],
            recv_sem=grad_recv.at[local],
            device_id=partner,
            device_id_type=MESH,
        )

    def small_copy(source, target, sent, got, who):
        return pltpu.make_async_remote_copy(
            src_ref=source,
            dst_ref=target,
            send_sem=small_send.at[sent],
            recv_sem=small_recv.at[got],
            device_id=who,
            device_id_type=MESH,
        )

    def arrived(slots, base):
        for step in range(1, REPS):
            other = lax.rem(rep + step, REPS)
            small_copy(
                slots.at[other], slots.at[other], base, base + other, peers[step - 1]
            ).wait_recv()

    def load_error(block, slot):
        return pltpu.make_async_copy(
            error_hbm.at[0, :, columns(block)], error_ref.at[slot], load_sem.at[slot]
        )

    def block_of(step):
        return lax.rem(step + 2 * shard, blocks)

    def start_loads(step):
        block, slot = block_of(step), lax.rem(step, depth)
        load_error(block, slot).start()

        @pl.when(block < shared)
        def _():
            send_piece(2 * block).wait_recv()
            send_piece(2 * block + 1).wait_recv()
            load_recv(block, slot).start()

    def load_recv(block, slot):
        return pltpu.make_async_copy(
            recv_hbm.at[:, columns(block)], recv_ref.at[slot], recv_sem.at[slot]
        )

    def save_matrix(block):
        return pltpu.make_async_copy(m_ref.at[block], m_hbm.at[block], m_sem.at[block])

    def load_moment(block):
        return pltpu.make_async_copy(
            moment_hbm.at[:, columns(block)], v_ref.at[block], moment_sem.at[block]
        )

    depth = error_ref.shape[0]
    lefts = [attn_in_hbm, mixed_hbm, mlp_in_hbm, grad_mlp_hbm]
    rights = [grad_qkv_hbm, grad_attn_hbm, grad_pre_hbm, hidden_hbm]
    window = right_ref.shape[0]
    halves = 2 * blocks

    def load_left(part):
        return pltpu.make_async_copy(lefts[part], left_stage, stage_sem.at[0])

    def load_right(part, index):
        slot = lax.rem(index, window)
        return pltpu.make_async_copy(
            rights[part].at[:, pl.ds(pl.multiple_of(index * PIECE, PIECE), PIECE)],
            right_ref.at[slot],
            right_sem.at[slot],
        )

    load_left(0).start()
    for index in range(window):
        load_right(0, index).start()
    pl.semaphore_wait(barrier, count)
    own_half = small_copy(sums_ref.at[1 - shard], half_ref, 16, 16, partner)
    own_half.start()
    rows_out = [
        small_copy(rows_ref, gathered_ref.at[shard, rep], step, rep, peers[step - 1])
        for step in range(1, REPS)
    ]
    for copy in rows_out:
        copy.start()
    gathered_ref[shard, rep] = rows_ref[...]

    high, low = split_two(factor_ref[...])
    stack_ref[...] = jnp.zeros_like(stack_ref)
    stack_ref[0:RANK] = high
    stack_ref[RANK : 2 * RANK] = low
    left_acc[...] = jnp.zeros_like(left_acc)
    edge = 0
    for part in range(4):
        number = rights[part].shape[1] // PIECE
        load_left(part).wait()
        turned_ref[...] = left_stage[...].T
        if part < 3:
            load_left(part + 1).start()

        def grad_piece(index, carry):
            load_right(part, index).wait()
            grad = multiply(turned_ref[...], right_ref[lax.rem(index, window)])

            @pl.when(index + window < number)
            def _():
                load_right(part, index + window).start()

            place = edge + index
            low_half = place < halves
            local = lax.rem(place, halves)
            mine = jnp.logical_xor(low_half, shard == 1)

            @pl.when(mine)
            def _():
                span = pl.ds(pl.multiple_of(lax.rem(local, 2) * PIECE, PIECE), PIECE)
                m_ref[lax.div(local, 2), :, span] = grad

            @pl.when(jnp.logical_not(mine))
            def _():
                @pl.when(local >= ring)
                def _():
                    send_piece(local - ring).wait_send()

                ring_ref[lax.rem(local, ring)] = grad.astype(half_type)
                send_piece(local).start()

            return carry

        lax.fori_loop(0, number, grad_piece, 0)
        edge += number
        if part < 3:
            for index in range(min(window, rights[part + 1].shape[1] // PIECE)):
                load_right(part + 1, index).start()
    for step in range(depth):
        start_loads(step)

    def gather_block(step, carry):
        block, slot = block_of(step), lax.rem(step, depth)
        load_error(block, slot).wait()

        @pl.when(block < shared)
        def _():
            load_recv(block, slot).wait()
            m_ref[block] = m_ref[block] + recv_ref[slot].astype(jnp.float32) + error_ref[slot]

        @pl.when(block >= shared)
        def _():
            m_ref[block] = error_ref[slot] + multiply(
                tail_left_ref[...], tail_right_ref[:, columns(block - shared)]
            )

        save_matrix(block).start()
        high, low = split_two(m_ref[block])
        factor = stack_ref[:, columns(block)]
        left_acc[...] += multiply_trans(high, factor) + multiply_trans(low, factor)

        @pl.when(step + depth < blocks)
        def _():
            start_loads(step + depth)

        return carry

    own_half.wait()
    half_ref[...] = half_ref[...] + sums_ref[shard]
    shares_out = [
        small_copy(
            half_ref.at[lax.rem(rep + step, REPS)],
            share_ref.at[rep],
            17 + step,
            17 + rep,
            peers[step - 1],
        )
        for step in range(1, REPS)
    ]
    for copy in shares_out:
        copy.start()
    share_ref[rep] = half_ref[rep]
    lax.fori_loop(0, blocks, gather_block, 0)
    for block in range(v_ref.shape[0]):
        load_moment(block).start()

    turned = left_acc[...].T
    left_ref[...] = turned[0:RANK] + turned[RANK : 2 * RANK]

    place = lax.rem(rep, 4)
    level = lax.div(rep, 4)
    plane_out = []
    for step in range(1, 4):
        other = lax.rem(place + step, 4)
        plane_out.append(
            pltpu.make_async_remote_copy(
                src_ref=left_ref,
                dst_ref=plane_ref.at[place],
                send_sem=left_send.at[step],
                recv_sem=left_recv.at[place],
                device_id=(shard, level * 4 + other),
                device_id_type=MESH,
            )
        )
    for copy in plane_out:
        copy.start()
    plane_ref[place] = left_ref[...]
    arrived(share_ref, 17)
    small_ref[...] = jnp.sum(share_ref[...], axis=0)
    whole_out = [
        small_copy(small_ref, total_ref.at[shard, rep], 33 + step, 33 + rep, peers[step - 1])
        for step in range(1, REPS)
    ]
    for copy in whole_out:
        copy.start()
    total_ref[shard, rep] = small_ref[...]
    for step in range(1, 4):
        other = lax.rem(place + step, 4)
        pltpu.make_async_remote_copy(
            src_ref=left_ref,
            dst_ref=plane_ref.at[other],
            send_sem=left_send.at[step],
            recv_sem=left_recv.at[other],
            device_id=(shard, level * 4 + other),
            device_id_type=MESH,
        ).wait_recv()
    plane_sum = (plane_ref[0] + plane_ref[1]) + (plane_ref[2] + plane_ref[3])
    for copy in plane_out:
        copy.wait_send()
    left_ref[...] = plane_sum
    column_out = []
    for step in range(1, 4):
        other = lax.rem(level + step, 4)
        column_out.append(
            pltpu.make_async_remote_copy(
                src_ref=left_ref,
                dst_ref=column_ref.at[level],
                send_sem=left_send.at[4 + step],
                recv_sem=left_recv.at[4 + level],
                device_id=(shard, other * 4 + place),
                device_id_type=MESH,
            )
        )
    for copy in column_out:
        copy.start()
    column_ref[level] = plane_sum
    for step in range(1, 4):
        other = lax.rem(level + step, 4)
        pltpu.make_async_remote_copy(
            src_ref=left_ref,
            dst_ref=column_ref.at[other],
            send_sem=left_send.at[4 + step],
            recv_sem=left_recv.at[4 + other],
            device_id=(shard, other * 4 + place),
            device_id_type=MESH,
        ).wait_recv()
    vectors = (column_ref[0] + column_ref[1]) + (column_ref[2] + column_ref[3])

    row_index = lax.broadcasted_iota(jnp.int32, (RANK, 1), 0)
    for place_of in range(RANK):
        row = vectors[place_of : place_of + 1]
        unit = row * lax.rsqrt(jnp.sum(row * row, axis=1, keepdims=True) + tiny_value)
        dots = jnp.sum(vectors * unit, axis=1, keepdims=True)
        vectors = jnp.where(
            row_index > place_of,
            vectors - dots * unit,
            jnp.where(row_index == place_of, unit, vectors),
        )
    high, low = split_two(vectors)
    basis_rows[...] = jnp.concatenate([high, low], axis=0)
    padded = jnp.concatenate(
        [
            high.astype(jnp.float32),
            low.astype(jnp.float32),
            jnp.zeros((LANES - 2 * RANK, vectors.shape[1]), jnp.float32),
        ],
        axis=0,
    )
    basis_cols[...] = padded.T.astype(half_type)
    for copy in column_out:
        copy.wait_send()
    arrived(gathered_ref.at[shard], 0)
    rows_across = small_copy(gathered_ref.at[shard], gathered_ref.at[shard], 49, 49, partner)
    rows_across.start()
    arrived(total_ref.at[shard], 33)
    total_across = small_copy(total_ref.at[shard], total_ref.at[shard], 50, 50, partner)
    total_across.start()

    def right_block(block, carry):
        both = multiply(basis_rows[...], m_ref[block].astype(half_type))
        send_ref[block] = (both[0:RANK] + both[RANK : 2 * RANK]).astype(half_type)
        return carry

    lax.fori_loop(0, blocks, right_block, 0)

    def right_copy(source, target, base, step, sender):
        return pltpu.make_async_remote_copy(
            src_ref=source,
            dst_ref=target,
            send_sem=right_send.at[base + step],
            recv_sem=right_recv.at[base + sender],
            device_id=peers[step - 1],
            device_id_type=MESH,
        )

    scatter = [
        right_copy(send_ref.at[lax.rem(rep + step, REPS)], part_ref.at[rep], 0, step, rep)
        for step in range(1, REPS)
    ]
    for copy in scatter:
        copy.start()
    part_ref[rep] = send_ref[rep]
    for step in range(1, REPS):
        other = lax.rem(rep + step, REPS)
        right_copy(send_ref.at[other], part_ref.at[other], 0, step, other).wait_recv()
    mine_ref[...] = jnp.sum(part_ref[...].astype(jnp.float32), axis=0).astype(half_type)
    spread = [
        right_copy(mine_ref, whole_ref.at[rep], REPS, step, rep) for step in range(1, REPS)
    ]
    for copy in spread:
        copy.start()
    whole_ref[rep] = mine_ref[...]
    for step in range(1, REPS):
        other = lax.rem(rep + step, REPS)
        right_copy(mine_ref, whole_ref.at[other], REPS, step, other).wait_recv()
    for copy in scatter + spread + rows_out + shares_out + whole_out:
        copy.wait_send()

    def sent_piece(local, carry):
        send_piece(local).wait_send()
        return carry

    sent = 2 * shared_there
    lax.fori_loop((halves - ring) * shard, sent, sent_piece, 0)
    for block in range(blocks):
        save_matrix(block).wait()
    rows_across.wait()
    total_across.wait()
    for block in range(v_ref.shape[0]):
        load_moment(block).wait()


def update_kernel(
    rates_ref,
    m_hbm,
    v_ref,
    whole_ref,
    basis_cols,
    moment_hbm,
    master_hbm,
    new_master_hbm,
    new_moment_hbm,
    new_error_hbm,
    right_ref,
    error_ref,
    moment_ref,
    master_ref,
    moment_sem,
    master_sem,
    matrix_sem,
    error_out,
    moment_out,
    master_out,
):
    pieces = BLOCK // PIECE
    blocks = m_hbm.shape[0] * pieces
    early = v_ref.shape[0] * pieces
    slots = master_ref.shape[0]
    rate = rates_ref[0]

    def columns(block):
        return pl.ds(pl.multiple_of(block * PIECE, PIECE), PIECE)

    def load_master(block, slot):
        return pltpu.make_async_copy(
            master_hbm.at[:, columns(block)], master_ref.at[slot], master_sem.at[slot]
        )

    def load_matrix(block, slot):
        return pltpu.make_async_copy(
            m_hbm.at[
                lax.div(block, pieces),
                :,
                pl.ds(pl.multiple_of(lax.rem(block, pieces) * PIECE, PIECE), PIECE),
            ],
            error_ref.at[slot],
            matrix_sem.at[slot],
        )

    def load_moment(block, slot):
        return pltpu.make_async_copy(
            moment_hbm.at[:, columns(block)], moment_ref.at[slot], moment_sem.at[slot]
        )

    def out_error(block, slot):
        return pltpu.make_async_copy(
            error_ref.at[slot], new_error_hbm.at[0, :, columns(block)], error_out.at[slot]
        )

    def out_moment(block, slot):
        return pltpu.make_async_copy(
            moment_ref.at[slot], new_moment_hbm.at[:, columns(block)], moment_out.at[slot]
        )

    def out_master(block, slot):
        return pltpu.make_async_copy(
            master_ref.at[slot], new_master_hbm.at[:, columns(block)], master_out.at[slot]
        )

    ahead = slots - 2
    for block in range(ahead):
        load_matrix(block, block).start()
        load_master(block, block).start()

    def update_piece(whole, piece):
        block = whole * pieces + piece
        span = slice(piece * PIECE, (piece + 1) * PIECE)
        slot = lax.rem(block, slots)
        next_slot = lax.rem(block + ahead, slots)

        @pl.when(block >= 2)
        def _():
            out_error(block - 2, next_slot).wait()
            out_moment(block - 2, next_slot).wait()
            out_master(block - 2, next_slot).wait()

        @pl.when(block + ahead < blocks)
        def _():
            load_matrix(block + ahead, next_slot).start()
            load_master(block + ahead, next_slot).start()

            @pl.when(block + ahead >= early)
            def _():
                load_moment(block + ahead, next_slot).start()

        right = whole_ref[whole, :, span]
        right_ref[:, columns(block)] = right.astype(jnp.float32)
        approx = multiply(basis_cols[:, 0 : 2 * RANK], jnp.concatenate([right, right], axis=0))
        load_matrix(block, slot).wait()
        error_ref[slot] = error_ref[slot] - approx * (1.0 / REPS)
        out_error(block, slot).start()

        @pl.when(block < early)
        def _():
            moment_ref[slot] = (
                momentum_decay * v_ref[jnp.minimum(whole, v_ref.shape[0] - 1), :, span] + approx
            )

        @pl.when(block >= early)
        def _():
            load_moment(block, slot).wait()
            moment_ref[slot] = momentum_decay * moment_ref[slot] + approx

        out_moment(block, slot).start()
        load_master(block, slot).wait()
        master_ref[slot] = master_ref[slot] - rate * moment_ref[slot]
        out_master(block, slot).start()

    def update_block(whole, carry):
        for piece in range(pieces):
            update_piece(whole, piece)
        return carry

    lax.fori_loop(0, m_hbm.shape[0], update_block, 0)
    for block in range(blocks - 2, blocks):
        out_error(block, block % slots).wait()
        out_moment(block, block % slots).wait()
        out_master(block, block % slots).wait()


def compress(rates, sides, tail_left, tail_right, error, factor_rows, moment, master, sums, lines):
    rows, cols = master.shape
    blocks = cols // BLOCK
    depth = 3
    slots = 8
    hbm = pl.BlockSpec(memory_space=pltpu.HBM)
    vmem = pl.BlockSpec(memory_space=pltpu.VMEM)
    moments, whole, basis, total, gathered, unused, matrices = pl.pallas_call(
        tail_kernel,
        out_shape=(
            pltpu.VMEM((EARLY, rows, BLOCK), jnp.float32),
            pltpu.VMEM((blocks, RANK, BLOCK), half_type),
            pltpu.VMEM((rows, LANES), half_type),
            sds((2, REPS) + sums.shape[2:]),
            sds((2, REPS) + lines.shape),
            pltpu.HBM((rows, cols), half_type),
            pltpu.HBM((blocks, rows, BLOCK), jnp.float32),
        ),
        in_specs=[hbm] * 8 + [vmem, vmem, hbm, vmem, hbm, vmem, vmem],
        out_specs=[vmem] * 5 + [pl.BlockSpec(memory_space=pltpu.HBM)] * 2,
        scratch_shapes=[
            pltpu.VMEM((blocks, rows, BLOCK), jnp.float32),
            pltpu.VMEM((depth, rows, BLOCK), jnp.float32),
            pltpu.VMEM((depth, rows, BLOCK), half_type),
            pltpu.VMEM(sides[0].shape, half_type),
            pltpu.VMEM(sides[0].shape[::-1], half_type),
            pltpu.VMEM((4, sides[0].shape[0], PIECE), half_type),
            pltpu.VMEM((4, rows, PIECE), half_type),
            pltpu.VMEM((LANES, cols), half_type),
            pltpu.VMEM((rows, LANES), jnp.float32),
            pltpu.VMEM((RANK, rows), jnp.float32),
            pltpu.VMEM((4, RANK, rows), jnp.float32),
            pltpu.VMEM((4, RANK, rows), jnp.float32),
            pltpu.VMEM((2 * RANK, rows), half_type),
            pltpu.VMEM((blocks, RANK, BLOCK), half_type),
            pltpu.VMEM((blocks, RANK, BLOCK), half_type),
            pltpu.VMEM((RANK, BLOCK), half_type),
            pltpu.VMEM(sums.shape[1:], jnp.float32),
            pltpu.VMEM(sums.shape[1:], jnp.float32),
            pltpu.VMEM(sums.shape[2:], jnp.float32),
            pltpu.SemaphoreType.DMA((depth,)),
            pltpu.SemaphoreType.DMA((1,)),
            pltpu.SemaphoreType.DMA((4,)),
            pltpu.SemaphoreType.DMA((depth,)),
            pltpu.SemaphoreType.DMA((blocks,)),
            pltpu.SemaphoreType.DMA((8,)),
            pltpu.SemaphoreType.DMA((8,)),
            pltpu.SemaphoreType.DMA((2 * REPS,)),
            pltpu.SemaphoreType.DMA((2 * REPS,)),
            pltpu.SemaphoreType.DMA((4,)),
            pltpu.SemaphoreType.DMA((2 * blocks,)),
            pltpu.SemaphoreType.DMA((51,)),
            pltpu.SemaphoreType.DMA((51,)),
            pltpu.SemaphoreType.DMA((blocks,)),
        ],
        compiler_params=pltpu.CompilerParams(
            collective_id=2, has_side_effects=True, vmem_limit_bytes=EXCHANGE_BYTES
        ),
        name="compress",
    )(*sides, tail_left, tail_right, error, factor_rows, moment, sums, lines)
    updated = pl.pallas_call(
        update_kernel,
        out_shape=(
            sds(master.shape),
            sds(moment.shape),
            sds(error.shape),
            sds((RANK, cols)),
        ),
        in_specs=[pl.BlockSpec(memory_space=pltpu.SMEM), hbm, vmem, vmem, vmem, hbm, hbm],
        out_specs=[hbm, hbm, hbm, vmem],
        scratch_shapes=[
            pltpu.VMEM((slots, rows, PIECE), jnp.float32),
            pltpu.VMEM((slots, rows, PIECE), jnp.float32),
            pltpu.VMEM((slots, rows, PIECE), jnp.float32),
            pltpu.SemaphoreType.DMA((slots,)),
            pltpu.SemaphoreType.DMA((slots,)),
            pltpu.SemaphoreType.DMA((slots,)),
            pltpu.SemaphoreType.DMA((slots,)),
            pltpu.SemaphoreType.DMA((slots,)),
            pltpu.SemaphoreType.DMA((slots,)),
        ],
        compiler_params=pltpu.CompilerParams(vmem_limit_bytes=KERNEL_BYTES),
        name="update",
    )(rates, matrices, moments, whole, basis, moment, master)
    return lax.optimization_barrier((tuple(updated), total, gathered))


def small_kernel(
    rates_ref, sums_ref, lines_ref, moment_ref, master_ref, new_moment_ref, new_master_ref
):
    step = pl.program_id(0)
    height = moment_ref.shape[0]
    images = lines_ref.shape[1] * 8
    strips = D // LANES

    def piece(place):
        return lines_ref[1, :, place * 8 : (place + 1) * 8, :].reshape(images, LANES)

    labels = piece(strips)[:, 0:1]
    place = lax.broadcasted_iota(jnp.int32, (images, height), 1) + (step * height - P_DIM)
    chosen = (place.astype(jnp.float32) == labels).astype(half_type)
    for strip in range(strips):
        span = slice(strip * LANES, (strip + 1) * LANES)
        high, low = split_two(piece(strip))
        new_moment_ref[:, span] = (
            momentum_decay * moment_ref[:, span] + outer_sum(chosen, high) + outer_sum(chosen, low)
        )

    def add(first, base):
        for strip in range(strips):
            span = slice(strip * LANES, (strip + 1) * LANES)
            new_moment_ref[first : first + P_DIM, span] += sums_ref[
                base + strip * P_DIM : base + (strip + 1) * P_DIM, :
            ]

    @pl.when(step == 0)
    def _():
        add(0, 0)

    @pl.when(step == pl.num_programs(0) - 1)
    def _():
        add(height - P_DIM, strips * P_DIM)

    new_master_ref[...] = master_ref[...] - rates_ref[1] * new_moment_ref[...]


def update_small(rates, total, gathered, moment, master):
    rows = moment.shape[0]
    steps = 3
    vmem = pl.BlockSpec(memory_space=pltpu.VMEM)
    block = pl.BlockSpec((rows // steps, D), lambda step: (step, 0))
    return pl.pallas_call(
        small_kernel,
        grid=(steps,),
        out_shape=(sds(moment.shape), sds(master.shape)),
        in_specs=[pl.BlockSpec(memory_space=pltpu.SMEM), vmem, vmem, block, block],
        out_specs=[block, block],
        name="update_small",
    )(rates, total.reshape(-1, LANES), gathered, moment, master)


GROUP = 2 * HEAD_DIM
CHUNK = 768
UNROLL = 6


def unit_rows(values):
    center = values - jnp.mean(values, axis=-1, keepdims=True)
    inverse = lax.rsqrt(jnp.mean(center * center, axis=-1, keepdims=True) + epsilon)
    return center * inverse, inverse


def unit_back(unit, inverse, grad):
    return inverse * (
        grad
        - jnp.mean(grad, axis=-1, keepdims=True)
        - unit * jnp.mean(grad * unit, axis=-1, keepdims=True)
    )


def gelu_both(values):
    scale = math.sqrt(2.0 / math.pi)
    square = values * values
    bent = jnp.tanh(scale * (values + 0.044715 * (values * square)))
    half = 0.5 * (1.0 + bent)
    slope = half + 0.5 * values * (1.0 - bent * bent) * (scale * (1.0 + 0.134145 * square))
    return values * half, slope


def token_sum(values):
    return jnp.sum(values, axis=0, keepdims=True)


def image_kernel(
    entries,
    patches_ref,
    targets_ref,
    active_ref,
    mod_bias_ref,
    place_ref,
    patch_weight_ref,
    head_weight_ref,
    qkv_bias_ref,
    output_bias_ref,
    up_bias_ref,
    down_bias_ref,
    patch_bias_ref,
    head_bias_ref,
    master_hbm,
    attn_in_ref,
    mixed_ref,
    mlp_in_ref,
    hidden_ref,
    grad_qkv_ref,
    grad_attn_ref,
    grad_pre_ref,
    grad_mlp_ref,
    both_grads_ref,
    grad_active_ref,
    grad_patch_ref,
    grad_head_ref,
    bias_qkv_ref,
    bias_output_ref,
    bias_up_ref,
    bias_down_ref,
    bias_patch_ref,
    bias_head_ref,
    loss_ref,
    weight_ref,
    qkv_ref,
    probs_ref,
    slope_ref,
    unit_start_ref,
    unit_mid_ref,
    stream_ref,
    attended_ref,
    mlp_out_ref,
    grad_mixed_ref,
    total_ref,
    stage_ref,
    mod_weight_ref,
    flat_mods_ref,
    mods_ref,
    got_mods_ref,
    mod_grad_ref,
    got_grads_ref,
    stage_sem,
    weight_send,
    weight_recv,
    mod_send,
    mod_recv,
):
    image = pl.program_id(0)
    last = pl.num_programs(0) - 1
    images = mods_ref.shape[0]
    edges = [0, 3 * D, 4 * D, 4 * D + FF, 4 * D + 2 * FF]
    shard = lax.axis_index("shard")
    partner = (1 - shard, lax.axis_index("rep"))
    cols = master_hbm.shape[1]
    first_count = cols // BLOCK
    all_count = edges[4] // BLOCK
    count = first_count - (2 * first_count - all_count) * shard
    depth = stage_ref.shape[0]
    loads = first_count - 2 * shard

    def load(block):
        slot = lax.rem(block, depth)
        return pltpu.make_async_copy(
            master_hbm.at[:, pl.ds(pl.multiple_of(block * BLOCK, BLOCK), BLOCK)],
            stage_ref.at[slot],
            stage_sem.at[slot],
        )

    def weight_copy(block):
        span = pl.ds(pl.multiple_of(block * BLOCK, BLOCK), BLOCK)
        return pltpu.make_async_remote_copy(
            src_ref=weight_ref.at[:, span],
            dst_ref=weight_ref.at[:, span],
            send_sem=weight_send.at[block],
            recv_sem=weight_recv.at[block],
            device_id=partner,
            device_id_type=MESH,
        )

    def mod_copy(source, target, place):
        return pltpu.make_async_remote_copy(
            src_ref=source,
            dst_ref=target,
            send_sem=mod_send.at[place],
            recv_sem=mod_recv.at[place],
            device_id=partner,
            device_id_type=MESH,
        )

    mods_across = mod_copy(flat_mods_ref, got_mods_ref, 0)
    grads_across = mod_copy(mod_grad_ref, got_grads_ref, 1)

    sums = [
        grad_patch_ref,
        grad_head_ref,
        bias_qkv_ref,
        bias_output_ref,
        bias_up_ref,
        bias_down_ref,
        bias_patch_ref,
        bias_head_ref,
        loss_ref,
    ]

    @pl.when(image == 0)
    def _():
        for block in range(2):
            load(block).start()
        barrier, greeted = greet([partner])
        pl.semaphore_wait(barrier, greeted)
        for total in sums:
            total[...] = jnp.zeros_like(total)

        def cast(block, carry):
            @pl.when(block + 2 < loads)
            def _():
                load(block + 2).start()

            load(block).wait()
            low_weight = stage_ref[lax.rem(block, depth)].astype(half_type)

            @pl.when(block < count)
            def _():
                place = shard * first_count + block
                weight_ref[:, pl.ds(pl.multiple_of(place * BLOCK, BLOCK), BLOCK)] = low_weight
                weight_copy(place).start()

            @pl.when(block >= count)
            def _():
                span = pl.ds(pl.multiple_of((block - count) * BLOCK, BLOCK), BLOCK)
                mod_weight_ref[:, span] = low_weight
                flat_mods_ref[:, span] = (
                    multiply(active_ref[...], low_weight) + mod_bias_ref[:, span]
                )
            return carry

        lax.fori_loop(0, loads, cast, 0)

        @pl.when(shard == 1)
        def _():
            mods_across.start()
            for place in range(8):
                mods_ref[:, place, :] = flat_mods_ref[0:images, place * D : (place + 1) * D]

        @pl.when(shard == 0)
        def _():
            mods_across.wait_recv()
            for place in range(8):
                mods_ref[:, place, :] = got_mods_ref[
                    images : 2 * images, place * D : (place + 1) * D
                ]

    stops = [-(-edge // BLOCK) for edge in edges]

    def arrived(part):
        @pl.when(jnp.logical_and(image == 0, shard == 1))
        def _():
            for block in range(stops[part], min(stops[part + 1], first_count)):
                weight_copy(block).wait_recv()

        if stops[part + 1] > first_count:

            @pl.when(jnp.logical_and(image == 0, shard == 0))
            def _():
                for block in range(first_count, all_count):
                    weight_copy(block).wait_recv()

    def modulation(place):
        return mods_ref[image, place : place + 1, :]

    def weight(first, width):
        return weight_ref[:, pl.ds(first, width)]

    patches = patches_ref[...]
    start = multiply(patches, patch_weight_ref[...]) + patch_bias_ref[...] + place_ref[...]
    stream_ref[...] = start
    unit, inverse_start = unit_rows(start)
    unit_start_ref[...] = unit
    attn_in_ref[...] = (unit * (1.0 + modulation(1)) + modulation(0)).astype(half_type)
    arrived(0)
    for part in range(3):
        span = slice(part * D, (part + 1) * D)
        qkv_ref[:, span] = (
            multiply(attn_in_ref[...], weight_ref[:, span]) + qkv_bias_ref[:, span]
        ).astype(half_type)

    scale = 1.0 / math.sqrt(HEAD_DIM)
    first_half = lax.broadcasted_iota(jnp.int32, (1, GROUP), 1) < HEAD_DIM

    def pair_slice(ref, part, pair):
        return ref[:, pl.ds(pl.multiple_of(part * D + pair * GROUP, GROUP), GROUP)]

    def halves(values):
        nothing = jnp.zeros_like(values)
        return jnp.where(first_half, values, nothing), jnp.where(first_half, nothing, values)

    def attend(pair, carry):
        queries = pair_slice(qkv_ref, 0, pair)
        keys = halves(pair_slice(qkv_ref, 1, pair))
        turned = pair_slice(qkv_ref, 2, pair).T
        rows = []
        for half in range(2):
            scores = multiply_trans(keys[half], queries) * scale
            weights = jnp.exp(scores - jnp.max(scores, axis=0, keepdims=True))
            probs = weights * (1.0 / jnp.sum(weights, axis=0, keepdims=True))
            probs_ref[2 * pair + half] = probs
            rows.append(
                multiply(
                    turned[half * HEAD_DIM : (half + 1) * HEAD_DIM], probs.astype(half_type)
                )
            )
        mixed_ref[:, pl.ds(pl.multiple_of(pair * GROUP, GROUP), GROUP)] = (
            jnp.concatenate(rows, axis=0).T.astype(half_type)
        )
        return carry

    lax.fori_loop(0, HEADS // 2, attend, 0, unroll=UNROLL)
    arrived(1)
    attended = multiply(mixed_ref[...], weight_ref[:, edges[1] : edges[2]]) + output_bias_ref[...]
    attended_ref[...] = attended
    middle = stream_ref[...] + modulation(2) * attended
    stream_ref[...] = middle
    unit, inverse_mid = unit_rows(middle)
    unit_mid_ref[...] = unit
    mlp_in_ref[...] = (unit * (1.0 + modulation(4)) + modulation(3)).astype(half_type)
    arrived(2)
    arrived(3)
    total_ref[...] = jnp.zeros_like(total_ref) + down_bias_ref[...]
    for part in range(FF // CHUNK):
        span = slice(part * CHUNK, (part + 1) * CHUNK)
        before = (
            multiply(mlp_in_ref[...], weight(edges[2] + part * CHUNK, CHUNK)) + up_bias_ref[:, span]
        )
        after, slope_part = gelu_both(before)
        slope_ref[:, span] = slope_part
        after = after.astype(half_type)
        hidden_ref[:, span] = after
        total_ref[...] += multiply_trans(after, weight(edges[3] + part * CHUNK, CHUNK))
    mlp_out_ref[...] = total_ref[...]
    unit, inverse_end = unit_rows(stream_ref[...] + modulation(5) * total_ref[...])
    final_in = (unit * (1.0 + modulation(7)) + modulation(6)).astype(half_type)
    error = (
        multiply_trans(final_in, head_weight_ref[...]) + head_bias_ref[...] - targets_ref[...]
    )
    loss_ref[...] += token_sum(error * error)
    grad_out = (error * (2.0 / entries)).astype(half_type)
    bias_head_ref[...] += token_sum(grad_out.astype(jnp.float32))
    grad_head_ref[...] += outer_sum(grad_out, final_in)

    grad_final = multiply(grad_out, head_weight_ref[...])
    mod_grad_ref[image, 6:7] = token_sum(grad_final)
    mod_grad_ref[image, 7:8] = token_sum(grad_final * unit)
    grad_stream = unit_back(unit, inverse_end, grad_final * (1.0 + modulation(7)))
    stream_ref[...] = grad_stream
    mod_grad_ref[image, 5:6] = token_sum(grad_stream * mlp_out_ref[...])
    grad_mlp = (grad_stream * modulation(5)).astype(half_type)
    grad_mlp_ref[...] = grad_mlp
    bias_down_ref[...] += token_sum(grad_mlp.astype(jnp.float32))
    total_ref[...] = jnp.zeros_like(total_ref)
    for part in range(FF // CHUNK):
        span = slice(part * CHUNK, (part + 1) * CHUNK)
        grad_pre = (
            multiply(grad_mlp_ref[...], weight(edges[3] + part * CHUNK, CHUNK)) * slope_ref[:, span]
        ).astype(half_type)
        grad_pre_ref[:, span] = grad_pre
        bias_up_ref[:, span] += token_sum(grad_pre.astype(jnp.float32))
        total_ref[...] += multiply_trans(grad_pre, weight(edges[2] + part * CHUNK, CHUNK))
    grad_in = total_ref[...]
    unit = unit_mid_ref[...]
    mod_grad_ref[image, 3:4] = token_sum(grad_in)
    mod_grad_ref[image, 4:5] = token_sum(grad_in * unit)
    grad_stream = stream_ref[...] + unit_back(unit, inverse_mid, grad_in * (1.0 + modulation(4)))
    stream_ref[...] = grad_stream
    mod_grad_ref[image, 2:3] = token_sum(grad_stream * attended_ref[...])
    grad_attn = (grad_stream * modulation(2)).astype(half_type)
    grad_attn_ref[...] = grad_attn
    bias_output_ref[...] += token_sum(grad_attn.astype(jnp.float32))
    grad_mixed_ref[...] = multiply_trans(grad_attn, weight_ref[:, edges[1] : edges[2]]).astype(
        half_type
    )

    def attend_back(pair, carry):
        queries = pair_slice(qkv_ref, 0, pair)
        keys_turned = pair_slice(qkv_ref, 1, pair).T
        values = halves(pair_slice(qkv_ref, 2, pair))
        grads = pair_slice(grad_mixed_ref, 0, pair)
        rows, key_grads, value_grads = [], [], []
        for half in range(2):
            probs = probs_ref[2 * pair + half]
            grad_probs = multiply_trans(values[half], grads)
            value_grads.append(multiply(probs.astype(half_type), grads))
            product = probs * grad_probs
            grad_scores = (product - probs * token_sum(product)).astype(half_type)
            key_grads.append(multiply(grad_scores, queries))
            rows.append(
                multiply(keys_turned[half * HEAD_DIM : (half + 1) * HEAD_DIM], grad_scores)
            )

        def put(part, values):
            grad_qkv_ref[:, pl.ds(pl.multiple_of(part * D + pair * GROUP, GROUP), GROUP)] = (
                values.astype(half_type)
            )

        put(0, jnp.concatenate(rows, axis=0).T * scale)
        put(1, jnp.where(first_half, key_grads[0], key_grads[1]) * scale)
        put(2, jnp.where(first_half, value_grads[0], value_grads[1]))
        return carry

    lax.fori_loop(0, HEADS // 2, attend_back, 0, unroll=UNROLL)
    bias_qkv_ref[...] += token_sum(grad_qkv_ref[...].astype(jnp.float32))
    grad_in = multiply_trans(grad_qkv_ref[...], weight_ref[:, : edges[1]])
    unit = unit_start_ref[...]
    mod_grad_ref[image, 0:1] = token_sum(grad_in)
    mod_grad_ref[image, 1:2] = token_sum(grad_in * unit)
    grad_start = (
        stream_ref[...] + unit_back(unit, inverse_start, grad_in * (1.0 + modulation(1)))
    ).astype(half_type)
    bias_patch_ref[...] += token_sum(grad_start.astype(jnp.float32))
    grad_patch_ref[...] += outer_sum(patches, grad_start)

    @pl.when(image == last)
    def _():
        grads_across.start()

        def sent(block, carry):
            weight_copy(shard * first_count + block).wait_send()
            return carry

        lax.fori_loop(0, count, sent, 0)
        @pl.when(shard == 1)
        def _():
            mods_across.wait_send()

        both_grads_ref[0:images] = mod_grad_ref[...]
        grads_across.wait()
        both_grads_ref[images : 2 * images] = got_grads_ref[...]
        grad_active_ref[...] = jnp.zeros_like(grad_active_ref)

        @pl.when(shard == 1)
        def _():
            for place in range(8):
                part = jnp.concatenate(
                    [mod_grad_ref[:, place, :], got_grads_ref[:, place, :]], axis=0
                ).astype(half_type)
                grad_active_ref[...] += multiply_trans(
                    part, mod_weight_ref[:, place * D : (place + 1) * D]
                )


def run_images(
    patches, targets, active, mod_bias, places, patch_weight, head_weight, biases, master, entries
):
    images = active.shape[0] // 2
    tokens = images * SEQ
    wide = 4 * D + 2 * FF

    def rows(width):
        return pl.BlockSpec((SEQ, width), lambda image: (image, 0))

    def fixed(array):
        return pl.BlockSpec(array.shape, lambda image: (0,) * len(array.shape))

    vector = [(P_DIM, D), (P_DIM, D), (1, 3 * D), (1, D), (1, FF), (1, D), (1, D), (1, P_DIM)]
    vector = [sds(shape) for shape in vector + [(1, P_DIM)]]
    saved = [D, D, D, FF, 3 * D, D, FF, D]
    return pl.pallas_call(
        functools.partial(image_kernel, entries),
        grid=(images,),
        out_shape=[sds((tokens, width), half_type) for width in saved]
        + [sds((2 * images, 8, D)), sds((2 * images, D))]
        + vector,
        in_specs=[rows(P_DIM), rows(P_DIM), fixed(active), fixed(mod_bias), fixed(places)]
        + [fixed(patch_weight), fixed(head_weight)]
        + [fixed(bias) for bias in biases]
        + [pl.BlockSpec(memory_space=pltpu.HBM)],
        out_specs=[rows(width) for width in saved] + [fixed(sds((2 * images, 8, D))), fixed(sds((2 * images, D)))] + [fixed(item) for item in vector],
        scratch_shapes=[
            pltpu.VMEM((D, wide), half_type),
            pltpu.VMEM((SEQ, 3 * D), half_type),
            pltpu.VMEM((HEADS, SEQ, SEQ), jnp.float32),
            pltpu.VMEM((SEQ, FF), jnp.float32),
            pltpu.VMEM((SEQ, D), jnp.float32),
            pltpu.VMEM((SEQ, D), jnp.float32),
            pltpu.VMEM((SEQ, D), jnp.float32),
            pltpu.VMEM((SEQ, D), jnp.float32),
            pltpu.VMEM((SEQ, D), jnp.float32),
            pltpu.VMEM((SEQ, D), half_type),
            pltpu.VMEM((SEQ, D), jnp.float32),
            pltpu.VMEM((3, D, BLOCK), jnp.float32),
            pltpu.VMEM((D, 8 * D), half_type),
            pltpu.VMEM((2 * images, 8 * D), jnp.float32),
            pltpu.VMEM((images, 8, D), jnp.float32),
            pltpu.VMEM((2 * images, 8 * D), jnp.float32),
            pltpu.VMEM((images, 8, D), jnp.float32),
            pltpu.VMEM((images, 8, D), jnp.float32),
            pltpu.SemaphoreType.DMA((3,)),
            pltpu.SemaphoreType.DMA((wide // BLOCK,)),
            pltpu.SemaphoreType.DMA((wide // BLOCK,)),
            pltpu.SemaphoreType.DMA((2,)),
            pltpu.SemaphoreType.DMA((2,)),
        ],
        compiler_params=pltpu.CompilerParams(
            collective_id=1, has_side_effects=True, vmem_limit_bytes=64_000_000
        ),
        name="images",
    )(patches, targets, active, mod_bias, places, patch_weight, head_weight, *biases, master)


def train_gradients(master, master_small, biases, noisy_patches, targets, timesteps, labels, entries):
    owner = lax.axis_index("shard") == 1
    last = master.shape[1]
    embed_second, embed_first = split_at(
        master, [last - D - FREQ, last - FREQ, last]
    )
    patch_weight, class_table, head_weight = split_small(master_small)
    (
        query_bias,
        value_bias,
        output_bias,
        up_bias,
        down_bias,
        modulate_bias,
        final_bias,
        second_bias,
        first_bias,
        patch_bias,
        head_bias,
    ) = split_bias(biases)
    images = noisy_patches.shape[0]
    frequency = timestep_features(timesteps).astype(half_type)
    embed_pre = multiply_trans(frequency.astype(jnp.float32), embed_first) + first_bias
    embed_hidden = jax.nn.silu(embed_pre).astype(half_type)
    time_embed = multiply(embed_hidden.astype(jnp.float32), embed_second) + second_bias
    chosen = (labels[:, None] == jnp.arange(NCLASS, dtype=jnp.int32)[None, :]).astype(jnp.float32)
    condition = time_embed + lax.dot_general(
        chosen,
        class_table,
        (((1,), (1,)), ((), ())),
        precision=highest,
        preferred_element_type=jnp.float32,
    )
    active = jax.nn.silu(condition).astype(half_type)
    mod_bias = jnp.concatenate([modulate_bias, final_bias]).reshape(1, 8 * D)
    qkv_bias = jnp.concatenate([query_bias, jnp.zeros_like(query_bias), value_bias])
    (
        attn_in,
        mixed,
        mlp_in,
        hidden,
        grad_qkv,
        grad_attn,
        grad_pre,
        grad_mlp,
        mod_grads,
        grad_active,
        grad_patch,
        grad_head,
        bias_qkv,
        bias_output,
        bias_up,
        bias_down,
        bias_patch,
        bias_head,
        losses,
    ) = run_images(
        noisy_patches.reshape(-1, P_DIM),
        targets.reshape(-1, P_DIM),
        active,
        mod_bias,
        jnp.asarray(position_constant()),
        patch_weight.T.astype(half_type),
        head_weight.T.astype(half_type),
        [item[None] for item in (qkv_bias, output_bias, up_bias, down_bias, patch_bias, head_bias)],
        master,
        entries,
    )
    grad_mods = mod_grads.reshape(-1, 8 * D).astype(half_type)
    bias_mods = column_sums(grad_mods)
    grad_condition = slope(jax.nn.silu, condition, grad_active)
    grad_embed = grad_condition.astype(half_type)
    grad_embed_hidden = multiply_trans(grad_embed.astype(jnp.float32), embed_second)
    grad_embed_pre = slope(jax.nn.silu, embed_pre, grad_embed_hidden).astype(half_type)
    tail_left = jnp.pad(
        jnp.concatenate([active, embed_hidden, grad_embed_pre]), ((0, 8), (0, 0))
    ).T
    tail_right = jnp.concatenate(
        [
            jnp.pad(grad_mods, ((0, 0), (0, D + FREQ))),
            jnp.pad(grad_embed, ((0, 0), (8 * D, FREQ))),
            jnp.pad(frequency, ((0, 16 - frequency.shape[0]), (9 * D, 0))),
        ]
    )
    sides = (attn_in, mixed, mlp_in, grad_mlp, grad_qkv, grad_attn, grad_pre, hidden)
    grad_bias = jnp.concatenate(
        [
            bias_qkv[0, :D],
            bias_qkv[0, 2 * D :],
            bias_output[0],
            bias_up[0],
            bias_down[0],
            jnp.where(
                owner,
                jnp.concatenate([bias_mods, column_sums(grad_embed), column_sums(grad_embed_pre)]),
                0.0,
            ),
            bias_patch[0],
            bias_head[0],
        ]
    )
    loss_part = jnp.sum(losses) / entries
    return sides, tail_left, tail_right, grad_patch, grad_head, grad_condition, grad_bias, loss_part


def on_pair(
    noisy_patches,
    targets,
    timesteps,
    labels,
    master_big,
    moment_big,
    error_big,
    factor_right,
    master_small,
    moment_small,
    biases,
    moment_bias,
    step_rates,
):
    shards = lax.axis_size("shard")
    replicas = lax.axis_size("rep")
    entries = noisy_patches.shape[0] * shards * replicas * SEQ * P_DIM
    own = jnp.stack([timesteps, labels])
    timesteps, labels = jnp.concatenate(
        [own, lax.ppermute(own, "shard", [(0, 1), (1, 0)])], axis=1
    )
    sides, tail_left, tail_right, grad_patch, grad_head, grad_condition, grad_bias, loss_part = (
        train_gradients(
            master_big, master_small, biases, noisy_patches, targets, timesteps, labels, entries
        )
    )
    images = labels.shape[0]
    strips = D // LANES

    def lines_of(matrix):
        return matrix.reshape(-1, strips, LANES).transpose(1, 0, 2)

    flat = jnp.concatenate(
        [
            lines_of(grad_patch).reshape(-1),
            lines_of(grad_head).reshape(-1),
            grad_bias,
            loss_part[None],
        ]
    )
    width = shards * replicas * 16 * LANES
    sums = jnp.pad(flat, (0, width - flat.shape[0])).reshape(shards, replicas, 16, LANES)
    label_lines = jnp.broadcast_to(labels.astype(jnp.float32)[None, :, None], (1, images, LANES))
    lines = jnp.concatenate(
        [
            lines_of(grad_condition),
            label_lines,
        ]
    ).reshape(-1, LANES)
    (new_master, new_moment, new_error, right_rows), total, gathered_lines = compress(
        step_rates,
        sides,
        tail_left,
        tail_right,
        error_big,
        factor_right.T,
        moment_big,
        master_big,
        sums,
        lines,
    )
    new_moment_small, new_master_small = update_small(
        step_rates, total, gathered_lines, moment_small.T, master_small.T
    )
    total = total.reshape(-1)
    bias_count = biases.shape[0]
    base = 2 * P_DIM * D
    total_loss = total[base + bias_count]
    new_moment_bias = momentum_decay * moment_bias + total[base : base + bias_count]
    new_biases = biases - step_rates[1] * new_moment_bias
    return (
        total_loss,
        new_master,
        new_moment,
        new_error,
        right_rows.T,
        new_master_small.T,
        new_moment_small.T,
        new_biases,
        new_moment_bias,
    )


def solution(mesh):
    in_specs = (
        P(("shard", "rep"), None),
        P(("shard", "rep"), None),
        P(("shard", "rep")),
        P(("shard", "rep")),
        P(None, "shard"),
        P(None, "shard"),
        P("rep", None, "shard"),
        P("shard", None),
        P(),
        P(),
        P(),
        P(),
        P(),
    )
    out_specs = (
        P(),
        P(None, "shard"),
        P(None, "shard"),
        P("rep", None, "shard"),
        P("shard", None),
        P(),
        P(),
        P(),
        P(),
    )
    fits = mesh.shape["shard"] == 2 and mesh.shape["rep"] == 16
    return jax.shard_map(
        on_pair if fits else on_device, mesh=mesh, in_specs=in_specs, out_specs=out_specs, check_vma=False
    )
```

```python
import functools
import math

import jax
import jax.numpy as jnp
import numpy as np
from jax import lax
from jax.experimental import pallas as pl
from jax.experimental.pallas import tpu as pltpu
from jax.sharding import PartitionSpec as P

D = 768
HEADS = 12
HEAD_DIM = 64
FF = 3072
GRID = 16
FREQ = 256
NCLASS = 1000
P_DIM = 16
SEQ = 256


highest = lax.Precision.HIGHEST
epsilon = 1e-06
tiny_value = 1e-30
momentum_decay = 0.9
half_type = jnp.bfloat16


def multiply(left_side, right_side):
    return jnp.dot(left_side, right_side, preferred_element_type=jnp.float32)


def multiply_trans(left_side, right_side):
    return lax.dot_general(
        left_side, right_side, (((1,), (1,)), ((), ())), preferred_element_type=jnp.float32
    )


def outer_sum(left_side, right_side):
    return lax.dot_general(
        left_side, right_side, (((0,), (0,)), ((), ())), preferred_element_type=jnp.float32
    )


def exact_outer(left_side, right_side):
    return lax.dot_general(
        left_side,
        right_side,
        (((0,), (0,)), ((), ())),
        precision=highest,
        preferred_element_type=jnp.float32,
    )


def normalize(values):
    center = values - jnp.mean(values, axis=-1, keepdims=True)
    return center * lax.rsqrt(jnp.mean(center * center, axis=-1, keepdims=True) + epsilon)


def gelu_tanh(values):
    return jax.nn.gelu(values, approximate=True)


def slope(function, values, grad):
    unused, pullback = jax.vjp(function, values)
    return pullback(grad)[0]


def timestep_features(steps):
    half_count = FREQ // 2
    freqs = jnp.exp(-math.log(10000.0) * jnp.arange(half_count, dtype=jnp.float32) / half_count)
    angles = steps.astype(jnp.float32)[:, None] * freqs[None, :]
    return jnp.concatenate([jnp.cos(angles), jnp.sin(angles)], axis=1)


def position_table():
    quarter = D // 4
    omega = 1.0 / 10000.0 ** (jnp.arange(quarter, dtype=jnp.float32) / quarter)
    cells = jnp.arange(SEQ, dtype=jnp.int32)
    across = (cells % GRID).astype(jnp.float32)[:, None] * omega[None, :]
    downward = (cells // GRID).astype(jnp.float32)[:, None] * omega[None, :]
    return jnp.concatenate(
        [jnp.sin(across), jnp.cos(across), jnp.sin(downward), jnp.cos(downward)], axis=1
    )


def position_constant():
    quarter = D // 4
    omega = 1.0 / 10000.0 ** (np.arange(quarter, dtype=np.float32) / np.float32(quarter))
    cells = np.arange(SEQ)
    across = (cells % GRID).astype(np.float32)[:, None] * omega[None, :].astype(np.float32)
    downward = (cells // GRID).astype(np.float32)[:, None] * omega[None, :].astype(np.float32)
    return np.concatenate(
        [np.sin(across), np.cos(across), np.sin(downward), np.cos(downward)], axis=1
    ).astype(np.float32)


def split_at(matrix, edges):
    return tuple((matrix[..., edges[place] : edges[place + 1]] for place in range(len(edges) - 1)))


def split_big(matrix):
    return split_at(
        matrix,
        [
            0,
            3 * D,
            4 * D,
            4 * D + FF,
            4 * D + 2 * FF,
            10 * D + 2 * FF,
            12 * D + 2 * FF,
            13 * D + 2 * FF,
            13 * D + 2 * FF + FREQ,
        ],
    )


def split_small(matrix):
    return split_at(matrix, [0, P_DIM, P_DIM + NCLASS, 2 * P_DIM + NCLASS])


def split_bias(vector):
    return split_at(
        vector,
        [
            0,
            D,
            2 * D,
            3 * D,
            3 * D + FF,
            4 * D + FF,
            10 * D + FF,
            12 * D + FF,
            13 * D + FF,
            14 * D + FF,
            15 * D + FF,
            15 * D + FF + P_DIM,
        ],
    )


def orthonormal(factor):
    columns = []
    for place in range(factor.shape[-1]):
        vector = factor[..., place]
        for earlier in columns:
            vector = vector - jnp.sum(earlier * vector, axis=-1, keepdims=True) * earlier
        vector = vector * lax.rsqrt(jnp.sum(vector * vector, axis=-1, keepdims=True) + tiny_value)
        columns.append(vector)
    return jnp.stack(columns, axis=-1)


def column_sums(grad):
    return jnp.sum(grad.astype(jnp.float32), axis=0)


def forward(gathered, master_small, biases, noisy_patches, timesteps, labels):
    (
        attend_weight,
        output_weight,
        up_weight,
        down_weight,
        modulate_weight,
        final_weight,
        embed_second,
        embed_first,
    ) = split_big(gathered)
    patch_weight, unused_table, head_weight = split_small(master_small.astype(half_type))
    class_table = split_small(master_small)[1]
    (
        query_bias,
        value_bias,
        output_bias,
        up_bias,
        down_bias,
        modulate_bias,
        final_bias,
        second_bias,
        first_bias,
        patch_bias,
        head_bias,
    ) = split_bias(biases)
    images = noisy_patches.shape[0]
    tokens = images * SEQ
    frequency = timestep_features(timesteps).astype(half_type)
    embed_pre = multiply_trans(frequency, embed_first) + first_bias
    embed_hidden = jax.nn.silu(embed_pre).astype(half_type)
    time_embed = multiply(embed_hidden, embed_second) + second_bias
    chosen = (labels[:, None] == jnp.arange(NCLASS, dtype=jnp.int32)[None, :]).astype(jnp.float32)
    condition = time_embed + lax.dot_general(
        chosen,
        class_table,
        (((1,), (1,)), ((), ())),
        precision=highest,
        preferred_element_type=jnp.float32,
    )
    active = jax.nn.silu(condition).astype(half_type)
    modulation = multiply(active, modulate_weight) + modulate_bias
    final_mod = multiply(active, final_weight) + final_bias
    patches = noisy_patches.reshape(tokens, P_DIM)
    stream_in = (multiply_trans(patches, patch_weight) + patch_bias).reshape(
        images, SEQ, D
    ) + position_table()[None]
    shift_attn, scale_attn, gate_attn, shift_mlp, scale_mlp, gate_mlp = jnp.split(
        modulation[:, None, :], 6, axis=2
    )
    shift_final, scale_final = jnp.split(final_mod[:, None, :], 2, axis=2)
    attn_in = (
        (normalize(stream_in) * (1.0 + scale_attn) + shift_attn)
        .astype(half_type)
        .reshape(tokens, D)
    )
    qkv_bias = jnp.concatenate([query_bias, jnp.zeros_like(query_bias), value_bias])
    projected = (multiply(attn_in, attend_weight) + qkv_bias).astype(half_type)
    queries, key_rows, value_rows = [
        piece.reshape(images, SEQ, HEADS, HEAD_DIM) for piece in jnp.split(projected, 3, axis=1)
    ]
    scores = jnp.einsum(
        "nqhd,nkhd->nhqk", queries, key_rows, preferred_element_type=jnp.float32
    ) / math.sqrt(HEAD_DIM)
    highest_score = jnp.max(scores, axis=-1, keepdims=True)
    logsum = highest_score + jnp.log(
        jnp.sum(jnp.exp(scores - highest_score), axis=-1, keepdims=True)
    )
    probs_low = jnp.exp(scores - logsum).astype(half_type)
    mixed_rows = (
        jnp.einsum("nhqk,nkhd->nqhd", probs_low, value_rows, preferred_element_type=jnp.float32)
        .astype(half_type)
        .reshape(tokens, D)
    )
    attended = (multiply(mixed_rows, output_weight) + output_bias).reshape(images, SEQ, D)
    stream_mid = stream_in + gate_attn * attended
    mlp_in = (
        (normalize(stream_mid) * (1.0 + scale_mlp) + shift_mlp).astype(half_type).reshape(tokens, D)
    )
    hidden_pre = multiply(mlp_in, up_weight) + up_bias
    hidden = gelu_tanh(hidden_pre).astype(half_type)
    mlp_out = (multiply_trans(hidden, down_weight) + down_bias).reshape(images, SEQ, D)
    stream_out = stream_mid + gate_mlp * mlp_out
    final_in = (
        (normalize(stream_out) * (1.0 + scale_final) + shift_final)
        .astype(half_type)
        .reshape(tokens, D)
    )
    output = multiply(final_in, head_weight) + head_bias
    kept = dict(
        frequency=frequency,
        embed_pre=embed_pre,
        embed_hidden=embed_hidden,
        chosen=chosen,
        condition=condition,
        active=active,
        modulation=modulation,
        final_mod=final_mod,
        patches=patches,
        stream_in=stream_in,
        attn_in=attn_in,
        queries=queries,
        key_rows=key_rows,
        value_rows=value_rows,
        logsum=logsum,
        mixed_rows=mixed_rows,
        attended=attended,
        stream_mid=stream_mid,
        mlp_in=mlp_in,
        hidden_pre=hidden_pre,
        hidden=hidden,
        mlp_out=mlp_out,
        stream_out=stream_out,
        final_in=final_in,
    )
    return (output, kept)


def backward(gathered, master_small, kept, grad_output):
    (
        attend_weight,
        output_weight,
        up_weight,
        down_weight,
        modulate_weight,
        final_weight,
        embed_second,
        embed_first,
    ) = split_big(gathered)
    patch_weight, unused_table, head_weight = split_small(master_small.astype(half_type))
    images = kept["stream_in"].shape[0]
    tokens = images * SEQ
    shift_attn, scale_attn, gate_attn, shift_mlp, scale_mlp, gate_mlp = jnp.split(
        kept["modulation"][:, None, :], 6, axis=2
    )
    shift_final, scale_final = jnp.split(kept["final_mod"][:, None, :], 2, axis=2)
    grad_out = grad_output.astype(half_type)
    grad_head = outer_sum(kept["final_in"], grad_out)
    bias_head = column_sums(grad_out)
    grad_final = multiply_trans(grad_out, head_weight).reshape(images, SEQ, D)
    grad_shift_final = jnp.sum(grad_final, axis=1)
    grad_scale_final = jnp.sum(grad_final * normalize(kept["stream_out"]), axis=1)
    grad_stream = slope(normalize, kept["stream_out"], grad_final * (1.0 + scale_final))
    grad_gate_mlp = jnp.sum(grad_stream * kept["mlp_out"], axis=1)
    grad_mlp = (grad_stream * gate_mlp).reshape(tokens, D).astype(half_type)
    bias_down = column_sums(grad_mlp)
    grad_down = outer_sum(grad_mlp, kept["hidden"])
    grad_hidden = multiply(grad_mlp, down_weight)
    grad_pre = slope(gelu_tanh, kept["hidden_pre"], grad_hidden).astype(half_type)
    bias_up = column_sums(grad_pre)
    grad_up = outer_sum(kept["mlp_in"], grad_pre)
    grad_mlp_in = multiply_trans(grad_pre, up_weight).reshape(images, SEQ, D)
    grad_shift_mlp = jnp.sum(grad_mlp_in, axis=1)
    grad_scale_mlp = jnp.sum(grad_mlp_in * normalize(kept["stream_mid"]), axis=1)
    grad_stream = grad_stream + slope(
        normalize, kept["stream_mid"], grad_mlp_in * (1.0 + scale_mlp)
    )
    grad_gate_attn = jnp.sum(grad_stream * kept["attended"], axis=1)
    grad_attn = (grad_stream * gate_attn).reshape(tokens, D).astype(half_type)
    bias_output = column_sums(grad_attn)
    grad_output_weight = outer_sum(kept["mixed_rows"], grad_attn)
    grad_mixed = (
        multiply_trans(grad_attn, output_weight)
        .astype(half_type)
        .reshape(images, SEQ, HEADS, HEAD_DIM)
    )
    inverse_root = 1.0 / math.sqrt(HEAD_DIM)
    scores = (
        jnp.einsum(
            "nqhd,nkhd->nhqk", kept["queries"], kept["key_rows"], preferred_element_type=jnp.float32
        )
        * inverse_root
    )
    probs = jnp.exp(scores - kept["logsum"])
    grad_values = jnp.einsum(
        "nhqk,nqhd->nkhd", probs.astype(half_type), grad_mixed, preferred_element_type=jnp.float32
    )
    grad_probs = jnp.einsum(
        "nqhd,nkhd->nhqk", grad_mixed, kept["value_rows"], preferred_element_type=jnp.float32
    )
    grad_scores = (
        probs * (grad_probs - jnp.sum(probs * grad_probs, axis=-1, keepdims=True))
    ).astype(half_type)
    grad_queries = (
        jnp.einsum(
            "nhqk,nkhd->nqhd", grad_scores, kept["key_rows"], preferred_element_type=jnp.float32
        )
        * inverse_root
    )
    grad_keys = (
        jnp.einsum(
            "nhqk,nqhd->nkhd", grad_scores, kept["queries"], preferred_element_type=jnp.float32
        )
        * inverse_root
    )
    grad_qkv = jnp.concatenate(
        [
            grad_queries.reshape(tokens, D),
            grad_keys.reshape(tokens, D),
            grad_values.reshape(tokens, D),
        ],
        axis=1,
    ).astype(half_type)
    bias_query = column_sums(grad_qkv[:, :D])
    bias_value = column_sums(grad_qkv[:, 2 * D :])
    grad_attend = outer_sum(kept["attn_in"], grad_qkv)
    grad_attn_in = multiply_trans(grad_qkv, attend_weight).reshape(images, SEQ, D)
    grad_shift_attn = jnp.sum(grad_attn_in, axis=1)
    grad_scale_attn = jnp.sum(grad_attn_in * normalize(kept["stream_in"]), axis=1)
    grad_stream = grad_stream + slope(
        normalize, kept["stream_in"], grad_attn_in * (1.0 + scale_attn)
    )
    grad_start = grad_stream.reshape(tokens, D).astype(half_type)
    bias_patch = column_sums(grad_start)
    grad_patch = outer_sum(grad_start, kept["patches"])
    grad_mod = jnp.concatenate(
        [
            grad_shift_attn,
            grad_scale_attn,
            grad_gate_attn,
            grad_shift_mlp,
            grad_scale_mlp,
            grad_gate_mlp,
        ],
        axis=1,
    ).astype(half_type)
    grad_fmod = jnp.concatenate([grad_shift_final, grad_scale_final], axis=1).astype(half_type)
    bias_modulate = column_sums(grad_mod)
    bias_final = column_sums(grad_fmod)
    grad_modulate = outer_sum(kept["active"], grad_mod)
    grad_final_weight = outer_sum(kept["active"], grad_fmod)
    grad_active = multiply_trans(grad_mod, modulate_weight) + multiply_trans(
        grad_fmod, final_weight
    )
    grad_condition = slope(jax.nn.silu, kept["condition"], grad_active)
    grad_embed = grad_condition.astype(half_type)
    bias_second = column_sums(grad_embed)
    grad_second = outer_sum(kept["embed_hidden"], grad_embed)
    grad_embed_hidden = multiply_trans(grad_embed, embed_second)
    grad_embed_pre = slope(jax.nn.silu, kept["embed_pre"], grad_embed_hidden).astype(half_type)
    bias_first = column_sums(grad_embed_pre)
    grad_first = outer_sum(grad_embed_pre, kept["frequency"])
    grad_big = jnp.concatenate(
        [
            grad_attend,
            grad_output_weight,
            grad_up,
            grad_down,
            grad_modulate,
            grad_final_weight,
            grad_second,
            grad_first,
        ],
        axis=1,
    )
    grad_small = (grad_patch, grad_head, grad_condition)
    grad_bias = jnp.concatenate(
        [
            bias_query,
            bias_value,
            bias_output,
            bias_up,
            bias_down,
            bias_modulate,
            bias_final,
            bias_second,
            bias_first,
            bias_patch,
            bias_head,
        ]
    )
    return (grad_big, grad_small, grad_bias)


def on_device(
    noisy_patches,
    targets,
    timesteps,
    labels,
    master_big,
    moment_big,
    error_big,
    factor_right,
    master_small,
    moment_small,
    biases,
    moment_bias,
    step_rates,
):
    shards = lax.axis_size("shard")
    replicas = lax.axis_size("rep")
    gathered = lax.all_gather(master_big.astype(half_type), "shard", axis=1, tiled=True)
    output, kept = forward(gathered, master_small, biases, noisy_patches, timesteps, labels)
    entries = noisy_patches.shape[0] * shards * replicas * SEQ * P_DIM
    error = output - targets.reshape(output.shape)
    loss_part = jnp.sum(error * error) / entries
    grad_output = 2.0 * error / entries
    gathered = lax.all_gather(master_big.astype(half_type), "shard", axis=1, tiled=True)
    grad_big, (grad_patch, grad_head, grad_condition), grad_bias = backward(
        gathered, master_small, kept, grad_output
    )
    grad_table = jnp.einsum("nd,nc->dc", grad_condition, kept["chosen"], precision=highest)
    grad_small = jnp.concatenate([grad_patch, grad_table, grad_head], axis=1)
    owned = lax.psum_scatter(
        grad_big.astype(jnp.bfloat16), "shard", scatter_dimension=1, tiled=True
    ).astype(jnp.float32)
    matrices = owned + error_big[0]
    left_part = jnp.dot(
        matrices, factor_right, precision=highest, preferred_element_type=jnp.float32
    )
    small_sum, bias_sum, total_loss = lax.psum((grad_small, grad_bias, loss_part), ("shard", "rep"))
    left_sum = lax.psum(left_part, "rep")
    basis = orthonormal(left_sum)
    right_sum = lax.psum(exact_outer(matrices, basis).astype(jnp.bfloat16), "rep").astype(
        jnp.float32
    )
    approx = lax.dot_general(
        basis,
        right_sum,
        (((1,), (1,)), ((), ())),
        precision=highest,
        preferred_element_type=jnp.float32,
    )
    new_error = (matrices - approx / replicas)[None]
    new_moment = momentum_decay * moment_big + approx
    new_master = master_big - step_rates[0] * new_moment
    new_moment_small = momentum_decay * moment_small + small_sum
    new_master_small = master_small - step_rates[1] * new_moment_small
    new_moment_bias = momentum_decay * moment_bias + bias_sum
    new_biases = biases - step_rates[1] * new_moment_bias
    return (
        total_loss,
        new_master,
        new_moment,
        new_error,
        right_sum,
        new_master_small,
        new_moment_small,
        new_biases,
        new_moment_bias,
    )


MESH = pl.DeviceIdType.MESH
BLOCK = 512
PIECE = 256
EARLY = 7
KERNEL_BYTES = 34_000_000
EXCHANGE_BYTES = 50_000_000
RANK = 8
LANES = 128
REPS = 16


def sds(shape, dtype=jnp.float32):
    return jax.ShapeDtypeStruct(shape, dtype)


def split_two(values):
    high = values.astype(half_type)
    low = (values - high.astype(jnp.float32)).astype(half_type)
    return high, low


def greet(others):
    barrier = pltpu.get_barrier_semaphore()
    for other in others:
        pl.semaphore_signal(barrier, inc=1, device_id=other, device_id_type=MESH)
    return barrier, len(others)


def tail_kernel(
    attn_in_hbm,
    mixed_hbm,
    mlp_in_hbm,
    grad_mlp_hbm,
    grad_qkv_hbm,
    grad_attn_hbm,
    grad_pre_hbm,
    hidden_hbm,
    tail_left_ref,
    tail_right_ref,
    error_hbm,
    factor_ref,
    moment_hbm,
    sums_ref,
    rows_ref,
    v_ref,
    whole_ref,
    basis_cols,
    total_ref,
    gathered_ref,
    recv_hbm,
    m_hbm,
    m_ref,
    error_ref,
    recv_ref,
    left_stage,
    turned_ref,
    right_ref,
    ring_ref,
    stack_ref,
    left_acc,
    left_ref,
    plane_ref,
    column_ref,
    basis_rows,
    send_ref,
    part_ref,
    mine_ref,
    half_ref,
    share_ref,
    small_ref,
    load_sem,
    stage_sem,
    right_sem,
    recv_sem,
    moment_sem,
    left_send,
    left_recv,
    right_send,
    right_recv,
    grad_send,
    grad_recv,
    small_send,
    small_recv,
    m_sem,
):
    blocks = m_ref.shape[0]
    shard = lax.axis_index("shard")
    rep = lax.axis_index("rep")
    partner = (1 - shard, rep)
    shared = blocks - 14 * shard
    shared_there = 2 + 14 * shard
    peers = [(shard, lax.rem(rep + step, REPS)) for step in range(1, REPS)]
    barrier, count = greet([partner] + peers)

    def columns(block):
        return pl.ds(pl.multiple_of(block * BLOCK, BLOCK), BLOCK)

    ring = ring_ref.shape[0]

    def send_piece(local):
        slot = lax.rem(local, ring)
        return pltpu.make_async_remote_copy(
            src_ref=ring_ref.at[slot],
            dst_ref=recv_hbm.at[:, pl.ds(pl.multiple_of(local * PIECE, PIECE), PIECE)],
            send_sem=grad_send.at[slot],
            recv_sem=grad_recv.at[local],
            device_id=partner,
            device_id_type=MESH,
        )

    def small_copy(source, target, sent, got, who):
        return pltpu.make_async_remote_copy(
            src_ref=source,
            dst_ref=target,
            send_sem=small_send.at[sent],
            recv_sem=small_recv.at[got],
            device_id=who,
            device_id_type=MESH,
        )

    def arrived(slots, base):
        for step in range(1, REPS):
            other = lax.rem(rep + step, REPS)
            small_copy(
                slots.at[other], slots.at[other], base, base + other, peers[step - 1]
            ).wait_recv()

    def load_error(block, slot):
        return pltpu.make_async_copy(
            error_hbm.at[0, :, columns(block)], error_ref.at[slot], load_sem.at[slot]
        )

    def block_of(step):
        return lax.rem(step + 2 * shard, blocks)

    def start_loads(step):
        block, slot = block_of(step), lax.rem(step, depth)
        load_error(block, slot).start()

        @pl.when(block < shared)
        def _():
            send_piece(2 * block).wait_recv()
            send_piece(2 * block + 1).wait_recv()
            load_recv(block, slot).start()

    def load_recv(block, slot):
        return pltpu.make_async_copy(
            recv_hbm.at[:, columns(block)], recv_ref.at[slot], recv_sem.at[slot]
        )

    def save_matrix(block):
        return pltpu.make_async_copy(m_ref.at[block], m_hbm.at[block], m_sem.at[block])

    def load_moment(block):
        return pltpu.make_async_copy(
            moment_hbm.at[:, columns(block)], v_ref.at[block], moment_sem.at[block]
        )

    depth = error_ref.shape[0]
    lefts = [attn_in_hbm, mixed_hbm, mlp_in_hbm, grad_mlp_hbm]
    rights = [grad_qkv_hbm, grad_attn_hbm, grad_pre_hbm, hidden_hbm]
    window = right_ref.shape[0]
    halves = 2 * blocks

    def load_left(part):
        return pltpu.make_async_copy(lefts[part], left_stage, stage_sem.at[0])

    def load_right(part, index):
        slot = lax.rem(index, window)
        return pltpu.make_async_copy(
            rights[part].at[:, pl.ds(pl.multiple_of(index * PIECE, PIECE), PIECE)],
            right_ref.at[slot],
            right_sem.at[slot],
        )

    load_left(0).start()
    for index in range(window):
        load_right(0, index).start()
    pl.semaphore_wait(barrier, count)
    own_half = small_copy(sums_ref.at[1 - shard], half_ref, 16, 16, partner)
    own_half.start()
    rows_out = [
        small_copy(rows_ref, gathered_ref.at[shard, rep], step, rep, peers[step - 1])
        for step in range(1, REPS)
    ]
    for copy in rows_out:
        copy.start()
    gathered_ref[shard, rep] = rows_ref[...]

    high, low = split_two(factor_ref[...])
    stack_ref[...] = jnp.zeros_like(stack_ref)
    stack_ref[0:RANK] = high
    stack_ref[RANK : 2 * RANK] = low
    left_acc[...] = jnp.zeros_like(left_acc)
    edge = 0
    for part in range(4):
        number = rights[part].shape[1] // PIECE
        load_left(part).wait()
        turned_ref[...] = left_stage[...].T
        if part < 3:
            load_left(part + 1).start()

        def grad_piece(index, carry):
            load_right(part, index).wait()
            grad = multiply(turned_ref[...], right_ref[lax.rem(index, window)])

            @pl.when(index + window < number)
            def _():
                load_right(part, index + window).start()

            place = edge + index
            low_half = place < halves
            local = lax.rem(place, halves)
            mine = jnp.logical_xor(low_half, shard == 1)

            @pl.when(mine)
            def _():
                span = pl.ds(pl.multiple_of(lax.rem(local, 2) * PIECE, PIECE), PIECE)
                m_ref[lax.div(local, 2), :, span] = grad

            @pl.when(jnp.logical_not(mine))
            def _():
                @pl.when(local >= ring)
                def _():
                    send_piece(local - ring).wait_send()

                ring_ref[lax.rem(local, ring)] = grad.astype(half_type)
                send_piece(local).start()

            return carry

        lax.fori_loop(0, number, grad_piece, 0)
        edge += number
        if part < 3:
            for index in range(min(window, rights[part + 1].shape[1] // PIECE)):
                load_right(part + 1, index).start()
    for step in range(depth):
        start_loads(step)

    def gather_block(step, carry):
        block, slot = block_of(step), lax.rem(step, depth)
        load_error(block, slot).wait()

        @pl.when(block < shared)
        def _():
            load_recv(block, slot).wait()
            m_ref[block] = m_ref[block] + recv_ref[slot].astype(jnp.float32) + error_ref[slot]

        @pl.when(block >= shared)
        def _():
            m_ref[block] = error_ref[slot] + multiply(
                tail_left_ref[...], tail_right_ref[:, columns(block - shared)]
            )

        save_matrix(block).start()
        high, low = split_two(m_ref[block])
        factor = stack_ref[:, columns(block)]
        left_acc[...] += multiply_trans(high, factor) + multiply_trans(low, factor)

        @pl.when(step + depth < blocks)
        def _():
            start_loads(step + depth)

        return carry

    own_half.wait()
    half_ref[...] = half_ref[...] + sums_ref[shard]
    shares_out = [
        small_copy(
            half_ref.at[lax.rem(rep + step, REPS)],
            share_ref.at[rep],
            17 + step,
            17 + rep,
            peers[step - 1],
        )
        for step in range(1, REPS)
    ]
    for copy in shares_out:
        copy.start()
    share_ref[rep] = half_ref[rep]
    lax.fori_loop(0, blocks, gather_block, 0)
    for block in range(v_ref.shape[0]):
        load_moment(block).start()

    turned = left_acc[...].T
    left_ref[...] = turned[0:RANK] + turned[RANK : 2 * RANK]

    place = lax.rem(rep, 4)
    level = lax.div(rep, 4)
    plane_out = []
    for step in range(1, 4):
        other = lax.rem(place + step, 4)
        plane_out.append(
            pltpu.make_async_remote_copy(
                src_ref=left_ref,
                dst_ref=plane_ref.at[place],
                send_sem=left_send.at[step],
                recv_sem=left_recv.at[place],
                device_id=(shard, level * 4 + other),
                device_id_type=MESH,
            )
        )
    for copy in plane_out:
        copy.start()
    plane_ref[place] = left_ref[...]
    arrived(share_ref, 17)
    small_ref[...] = jnp.sum(share_ref[...], axis=0)
    whole_out = [
        small_copy(small_ref, total_ref.at[shard, rep], 33 + step, 33 + rep, peers[step - 1])
        for step in range(1, REPS)
    ]
    for copy in whole_out:
        copy.start()
    total_ref[shard, rep] = small_ref[...]
    for step in range(1, 4):
        other = lax.rem(place + step, 4)
        pltpu.make_async_remote_copy(
            src_ref=left_ref,
            dst_ref=plane_ref.at[other],
            send_sem=left_send.at[step],
            recv_sem=left_recv.at[other],
            device_id=(shard, level * 4 + other),
            device_id_type=MESH,
        ).wait_recv()
    plane_sum = (plane_ref[0] + plane_ref[1]) + (plane_ref[2] + plane_ref[3])
    for copy in plane_out:
        copy.wait_send()
    left_ref[...] = plane_sum
    column_out = []
    for step in range(1, 4):
        other = lax.rem(level + step, 4)
        column_out.append(
            pltpu.make_async_remote_copy(
                src_ref=left_ref,
                dst_ref=column_ref.at[level],
                send_sem=left_send.at[4 + step],
                recv_sem=left_recv.at[4 + level],
                device_id=(shard, other * 4 + place),
                device_id_type=MESH,
            )
        )
    for copy in column_out:
        copy.start()
    column_ref[level] = plane_sum
    for step in range(1, 4):
        other = lax.rem(level + step, 4)
        pltpu.make_async_remote_copy(
            src_ref=left_ref,
            dst_ref=column_ref.at[other],
            send_sem=left_send.at[4 + step],
            recv_sem=left_recv.at[4 + other],
            device_id=(shard, other * 4 + place),
            device_id_type=MESH,
        ).wait_recv()
    vectors = (column_ref[0] + column_ref[1]) + (column_ref[2] + column_ref[3])

    row_index = lax.broadcasted_iota(jnp.int32, (RANK, 1), 0)
    for place_of in range(RANK):
        row = vectors[place_of : place_of + 1]
        unit = row * lax.rsqrt(jnp.sum(row * row, axis=1, keepdims=True) + tiny_value)
        dots = jnp.sum(vectors * unit, axis=1, keepdims=True)
        vectors = jnp.where(
            row_index > place_of,
            vectors - dots * unit,
            jnp.where(row_index == place_of, unit, vectors),
        )
    high, low = split_two(vectors)
    basis_rows[...] = jnp.concatenate([high, low], axis=0)
    padded = jnp.concatenate(
        [
            high.astype(jnp.float32),
            low.astype(jnp.float32),
            jnp.zeros((LANES - 2 * RANK, vectors.shape[1]), jnp.float32),
        ],
        axis=0,
    )
    basis_cols[...] = padded.T.astype(half_type)
    for copy in column_out:
        copy.wait_send()
    arrived(gathered_ref.at[shard], 0)
    rows_across = small_copy(gathered_ref.at[shard], gathered_ref.at[shard], 49, 49, partner)
    rows_across.start()
    arrived(total_ref.at[shard], 33)
    total_across = small_copy(total_ref.at[shard], total_ref.at[shard], 50, 50, partner)
    total_across.start()

    def right_block(block, carry):
        both = multiply(basis_rows[...], m_ref[block].astype(half_type))
        send_ref[block] = (both[0:RANK] + both[RANK : 2 * RANK]).astype(half_type)
        return carry

    lax.fori_loop(0, blocks, right_block, 0)

    def right_copy(source, target, base, step, sender):
        return pltpu.make_async_remote_copy(
            src_ref=source,
            dst_ref=target,
            send_sem=right_send.at[base + step],
            recv_sem=right_recv.at[base + sender],
            device_id=peers[step - 1],
            device_id_type=MESH,
        )

    scatter = [
        right_copy(send_ref.at[lax.rem(rep + step, REPS)], part_ref.at[rep], 0, step, rep)
        for step in range(1, REPS)
    ]
    for copy in scatter:
        copy.start()
    part_ref[rep] = send_ref[rep]
    for step in range(1, REPS):
        other = lax.rem(rep + step, REPS)
        right_copy(send_ref.at[other], part_ref.at[other], 0, step, other).wait_recv()
    mine_ref[...] = jnp.sum(part_ref[...].astype(jnp.float32), axis=0).astype(half_type)
    spread = [
        right_copy(mine_ref, whole_ref.at[rep], REPS, step, rep) for step in range(1, REPS)
    ]
    for copy in spread:
        copy.start()
    whole_ref[rep] = mine_ref[...]
    for step in range(1, REPS):
        other = lax.rem(rep + step, REPS)
        right_copy(mine_ref, whole_ref.at[other], REPS, step, other).wait_recv()
    for copy in scatter + spread + rows_out + shares_out + whole_out:
        copy.wait_send()

    def sent_piece(local, carry):
        send_piece(local).wait_send()
        return carry

    sent = 2 * shared_there
    lax.fori_loop((halves - ring) * shard, sent, sent_piece, 0)
    for block in range(blocks):
        save_matrix(block).wait()
    rows_across.wait()
    total_across.wait()
    for block in range(v_ref.shape[0]):
        load_moment(block).wait()


def update_kernel(
    rates_ref,
    m_hbm,
    v_ref,
    whole_ref,
    basis_cols,
    moment_hbm,
    master_hbm,
    new_master_hbm,
    new_moment_hbm,
    new_error_hbm,
    right_ref,
    error_ref,
    moment_ref,
    master_ref,
    moment_sem,
    master_sem,
    matrix_sem,
    error_out,
    moment_out,
    master_out,
):
    pieces = BLOCK // PIECE
    blocks = m_hbm.shape[0] * pieces
    early = v_ref.shape[0] * pieces
    slots = master_ref.shape[0]
    rate = rates_ref[0]

    def columns(block):
        return pl.ds(pl.multiple_of(block * PIECE, PIECE), PIECE)

    def load_master(block, slot):
        return pltpu.make_async_copy(
            master_hbm.at[:, columns(block)], master_ref.at[slot], master_sem.at[slot]
        )

    def load_matrix(block, slot):
        return pltpu.make_async_copy(
            m_hbm.at[
                lax.div(block, pieces),
                :,
                pl.ds(pl.multiple_of(lax.rem(block, pieces) * PIECE, PIECE), PIECE),
            ],
            error_ref.at[slot],
            matrix_sem.at[slot],
        )

    def load_moment(block, slot):
        return pltpu.make_async_copy(
            moment_hbm.at[:, columns(block)], moment_ref.at[slot], moment_sem.at[slot]
        )

    def out_error(block, slot):
        return pltpu.make_async_copy(
            error_ref.at[slot], new_error_hbm.at[0, :, columns(block)], error_out.at[slot]
        )

    def out_moment(block, slot):
        return pltpu.make_async_copy(
            moment_ref.at[slot], new_moment_hbm.at[:, columns(block)], moment_out.at[slot]
        )

    def out_master(block, slot):
        return pltpu.make_async_copy(
            master_ref.at[slot], new_master_hbm.at[:, columns(block)], master_out.at[slot]
        )

    ahead = slots - 2
    for block in range(ahead):
        load_matrix(block, block).start()
        load_master(block, block).start()

    def update_piece(whole, piece):
        block = whole * pieces + piece
        span = slice(piece * PIECE, (piece + 1) * PIECE)
        slot = lax.rem(block, slots)
        next_slot = lax.rem(block + ahead, slots)

        @pl.when(block >= 2)
        def _():
            out_error(block - 2, next_slot).wait()
            out_moment(block - 2, next_slot).wait()
            out_master(block - 2, next_slot).wait()

        @pl.when(block + ahead < blocks)
        def _():
            load_matrix(block + ahead, next_slot).start()
            load_master(block + ahead, next_slot).start()

            @pl.when(block + ahead >= early)
            def _():
                load_moment(block + ahead, next_slot).start()

        right = whole_ref[whole, :, span]
        right_ref[:, columns(block)] = right.astype(jnp.float32)
        approx = multiply(basis_cols[:, 0 : 2 * RANK], jnp.concatenate([right, right], axis=0))
        load_matrix(block, slot).wait()
        error_ref[slot] = error_ref[slot] - approx * (1.0 / REPS)
        out_error(block, slot).start()

        @pl.when(block < early)
        def _():
            moment_ref[slot] = (
                momentum_decay * v_ref[jnp.minimum(whole, v_ref.shape[0] - 1), :, span] + approx
            )

        @pl.when(block >= early)
        def _():
            load_moment(block, slot).wait()
            moment_ref[slot] = momentum_decay * moment_ref[slot] + approx

        out_moment(block, slot).start()
        load_master(block, slot).wait()
        master_ref[slot] = master_ref[slot] - rate * moment_ref[slot]
        out_master(block, slot).start()

    def update_block(whole, carry):
        for piece in range(pieces):
            update_piece(whole, piece)
        return carry

    lax.fori_loop(0, m_hbm.shape[0], update_block, 0)
    for block in range(blocks - 2, blocks):
        out_error(block, block % slots).wait()
        out_moment(block, block % slots).wait()
        out_master(block, block % slots).wait()


def compress(rates, sides, tail_left, tail_right, error, factor_rows, moment, master, sums, lines):
    rows, cols = master.shape
    blocks = cols // BLOCK
    depth = 3
    slots = 8
    hbm = pl.BlockSpec(memory_space=pltpu.HBM)
    vmem = pl.BlockSpec(memory_space=pltpu.VMEM)
    moments, whole, basis, total, gathered, unused, matrices = pl.pallas_call(
        tail_kernel,
        out_shape=(
            pltpu.VMEM((EARLY, rows, BLOCK), jnp.float32),
            pltpu.VMEM((blocks, RANK, BLOCK), half_type),
            pltpu.VMEM((rows, LANES), half_type),
            sds((2, REPS) + sums.shape[2:]),
            sds((2, REPS) + lines.shape),
            pltpu.HBM((rows, cols), half_type),
            pltpu.HBM((blocks, rows, BLOCK), jnp.float32),
        ),
        in_specs=[hbm] * 8 + [vmem, vmem, hbm, vmem, hbm, vmem, vmem],
        out_specs=[vmem] * 5 + [pl.BlockSpec(memory_space=pltpu.HBM)] * 2,
        scratch_shapes=[
            pltpu.VMEM((blocks, rows, BLOCK), jnp.float32),
            pltpu.VMEM((depth, rows, BLOCK), jnp.float32),
            pltpu.VMEM((depth, rows, BLOCK), half_type),
            pltpu.VMEM(sides[0].shape, half_type),
            pltpu.VMEM(sides[0].shape[::-1], half_type),
            pltpu.VMEM((4, sides[0].shape[0], PIECE), half_type),
            pltpu.VMEM((4, rows, PIECE), half_type),
            pltpu.VMEM((LANES, cols), half_type),
            pltpu.VMEM((rows, LANES), jnp.float32),
            pltpu.VMEM((RANK, rows), jnp.float32),
            pltpu.VMEM((4, RANK, rows), jnp.float32),
            pltpu.VMEM((4, RANK, rows), jnp.float32),
            pltpu.VMEM((2 * RANK, rows), half_type),
            pltpu.VMEM((blocks, RANK, BLOCK), half_type),
            pltpu.VMEM((blocks, RANK, BLOCK), half_type),
            pltpu.VMEM((RANK, BLOCK), half_type),
            pltpu.VMEM(sums.shape[1:], jnp.float32),
            pltpu.VMEM(sums.shape[1:], jnp.float32),
            pltpu.VMEM(sums.shape[2:], jnp.float32),
            pltpu.SemaphoreType.DMA((depth,)),
            pltpu.SemaphoreType.DMA((1,)),
            pltpu.SemaphoreType.DMA((4,)),
            pltpu.SemaphoreType.DMA((depth,)),
            pltpu.SemaphoreType.DMA((blocks,)),
            pltpu.SemaphoreType.DMA((8,)),
            pltpu.SemaphoreType.DMA((8,)),
            pltpu.SemaphoreType.DMA((2 * REPS,)),
            pltpu.SemaphoreType.DMA((2 * REPS,)),
            pltpu.SemaphoreType.DMA((4,)),
            pltpu.SemaphoreType.DMA((2 * blocks,)),
            pltpu.SemaphoreType.DMA((51,)),
            pltpu.SemaphoreType.DMA((51,)),
            pltpu.SemaphoreType.DMA((blocks,)),
        ],
        compiler_params=pltpu.CompilerParams(
            collective_id=2, has_side_effects=True, vmem_limit_bytes=EXCHANGE_BYTES
        ),
        name="compress",
    )(*sides, tail_left, tail_right, error, factor_rows, moment, sums, lines)
    updated = pl.pallas_call(
        update_kernel,
        out_shape=(
            sds(master.shape),
            sds(moment.shape),
            sds(error.shape),
            sds((RANK, cols)),
        ),
        in_specs=[pl.BlockSpec(memory_space=pltpu.SMEM), hbm, vmem, vmem, vmem, hbm, hbm],
        out_specs=[hbm, hbm, hbm, vmem],
        scratch_shapes=[
            pltpu.VMEM((slots, rows, PIECE), jnp.float32),
            pltpu.VMEM((slots, rows, PIECE), jnp.float32),
            pltpu.VMEM((slots, rows, PIECE), jnp.float32),
            pltpu.SemaphoreType.DMA((slots,)),
            pltpu.SemaphoreType.DMA((slots,)),
            pltpu.SemaphoreType.DMA((slots,)),
            pltpu.SemaphoreType.DMA((slots,)),
            pltpu.SemaphoreType.DMA((slots,)),
            pltpu.SemaphoreType.DMA((slots,)),
        ],
        compiler_params=pltpu.CompilerParams(vmem_limit_bytes=KERNEL_BYTES),
        name="update",
    )(rates, matrices, moments, whole, basis, moment, master)
    return lax.optimization_barrier((tuple(updated), total, gathered))


def small_kernel(
    rates_ref, sums_ref, lines_ref, moment_ref, master_ref, new_moment_ref, new_master_ref
):
    step = pl.program_id(0)
    height = moment_ref.shape[0]
    images = lines_ref.shape[1] * 8
    strips = D // LANES

    def piece(place):
        return lines_ref[1, :, place * 8 : (place + 1) * 8, :].reshape(images, LANES)

    labels = piece(strips)[:, 0:1]
    place = lax.broadcasted_iota(jnp.int32, (images, height), 1) + (step * height - P_DIM)
    chosen = (place.astype(jnp.float32) == labels).astype(half_type)
    high, low = split_two(jnp.concatenate([piece(strip) for strip in range(strips)], axis=1))
    new_moment_ref[...] = momentum_decay * moment_ref[...] + outer_sum(
        jnp.concatenate([chosen, chosen], axis=0), jnp.concatenate([high, low], axis=0)
    )

    def add(first, base):
        for strip in range(strips):
            span = slice(strip * LANES, (strip + 1) * LANES)
            new_moment_ref[first : first + P_DIM, span] += sums_ref[
                base + strip * P_DIM : base + (strip + 1) * P_DIM, :
            ]

    @pl.when(step == 0)
    def _():
        add(0, 0)

    @pl.when(step == pl.num_programs(0) - 1)
    def _():
        add(height - P_DIM, strips * P_DIM)

    new_master_ref[...] = master_ref[...] - rates_ref[1] * new_moment_ref[...]


def update_small(rates, total, gathered, moment, master):
    rows = moment.shape[0]
    steps = 3
    vmem = pl.BlockSpec(memory_space=pltpu.VMEM)
    block = pl.BlockSpec((rows // steps, D), lambda step: (step, 0))
    return pl.pallas_call(
        small_kernel,
        grid=(steps,),
        out_shape=(sds(moment.shape), sds(master.shape)),
        in_specs=[pl.BlockSpec(memory_space=pltpu.SMEM), vmem, vmem, block, block],
        out_specs=[block, block],
        name="update_small",
    )(rates, total.reshape(-1, LANES), gathered, moment, master)


GROUP = 2 * HEAD_DIM
CHUNK = 768
UNROLL = 6


def unit_rows(values):
    center = values - jnp.mean(values, axis=-1, keepdims=True)
    inverse = lax.rsqrt(jnp.mean(center * center, axis=-1, keepdims=True) + epsilon)
    return center * inverse, inverse


def unit_back(unit, inverse, grad):
    return inverse * (
        grad
        - jnp.mean(grad, axis=-1, keepdims=True)
        - unit * jnp.mean(grad * unit, axis=-1, keepdims=True)
    )


def gelu_both(values):
    scale = math.sqrt(2.0 / math.pi)
    square = values * values
    bent = jnp.tanh(scale * (values + 0.044715 * (values * square)))
    half = 0.5 * (1.0 + bent)
    slope = half + 0.5 * values * (1.0 - bent * bent) * (scale * (1.0 + 0.134145 * square))
    return values * half, slope


def token_sum(values):
    return jnp.sum(values, axis=0, keepdims=True)


def image_kernel(
    entries,
    patches_ref,
    targets_ref,
    active_ref,
    mod_bias_ref,
    place_ref,
    patch_weight_ref,
    head_weight_ref,
    qkv_bias_ref,
    output_bias_ref,
    up_bias_ref,
    down_bias_ref,
    patch_bias_ref,
    head_bias_ref,
    master_hbm,
    attn_in_ref,
    mixed_ref,
    mlp_in_ref,
    hidden_ref,
    grad_qkv_ref,
    grad_attn_ref,
    grad_pre_ref,
    grad_mlp_ref,
    both_grads_ref,
    grad_active_ref,
    grad_patch_ref,
    grad_head_ref,
    bias_qkv_ref,
    bias_output_ref,
    bias_up_ref,
    bias_down_ref,
    bias_patch_ref,
    bias_head_ref,
    loss_ref,
    weight_ref,
    qkv_ref,
    probs_ref,
    slope_ref,
    unit_start_ref,
    unit_mid_ref,
    stream_ref,
    attended_ref,
    mlp_out_ref,
    grad_mixed_ref,
    total_ref,
    stage_ref,
    mod_weight_ref,
    flat_mods_ref,
    mods_ref,
    got_mods_ref,
    mod_grad_ref,
    got_grads_ref,
    stage_sem,
    weight_send,
    weight_recv,
    mod_send,
    mod_recv,
):
    image = pl.program_id(0)
    last = pl.num_programs(0) - 1
    images = mods_ref.shape[0]
    edges = [0, 3 * D, 4 * D, 4 * D + FF, 4 * D + 2 * FF]
    shard = lax.axis_index("shard")
    partner = (1 - shard, lax.axis_index("rep"))
    cols = master_hbm.shape[1]
    first_count = cols // BLOCK
    all_count = edges[4] // BLOCK
    count = first_count - (2 * first_count - all_count) * shard
    depth = stage_ref.shape[0]
    loads = first_count - 2 * shard

    def load(block):
        slot = lax.rem(block, depth)
        return pltpu.make_async_copy(
            master_hbm.at[:, pl.ds(pl.multiple_of(block * BLOCK, BLOCK), BLOCK)],
            stage_ref.at[slot],
            stage_sem.at[slot],
        )

    def weight_copy(block):
        span = pl.ds(pl.multiple_of(block * BLOCK, BLOCK), BLOCK)
        return pltpu.make_async_remote_copy(
            src_ref=weight_ref.at[:, span],
            dst_ref=weight_ref.at[:, span],
            send_sem=weight_send.at[block],
            recv_sem=weight_recv.at[block],
            device_id=partner,
            device_id_type=MESH,
        )

    def mod_copy(source, target, place):
        return pltpu.make_async_remote_copy(
            src_ref=source,
            dst_ref=target,
            send_sem=mod_send.at[place],
            recv_sem=mod_recv.at[place],
            device_id=partner,
            device_id_type=MESH,
        )

    mods_across = mod_copy(flat_mods_ref, got_mods_ref, 0)
    grads_across = mod_copy(mod_grad_ref, got_grads_ref, 1)

    sums = [
        grad_patch_ref,
        grad_head_ref,
        bias_qkv_ref,
        bias_output_ref,
        bias_up_ref,
        bias_down_ref,
        bias_patch_ref,
        bias_head_ref,
        loss_ref,
    ]

    @pl.when(image == 0)
    def _():
        for block in range(2):
            load(block).start()
        barrier, greeted = greet([partner])
        pl.semaphore_wait(barrier, greeted)
        for total in sums:
            total[...] = jnp.zeros_like(total)

        def cast(block, carry):
            @pl.when(block + 2 < loads)
            def _():
                load(block + 2).start()

            load(block).wait()
            low_weight = stage_ref[lax.rem(block, depth)].astype(half_type)

            @pl.when(block < count)
            def _():
                place = shard * first_count + block
                weight_ref[:, pl.ds(pl.multiple_of(place * BLOCK, BLOCK), BLOCK)] = low_weight
                weight_copy(place).start()

            @pl.when(block >= count)
            def _():
                span = pl.ds(pl.multiple_of((block - count) * BLOCK, BLOCK), BLOCK)
                mod_weight_ref[:, span] = low_weight
                flat_mods_ref[:, span] = (
                    multiply(active_ref[...], low_weight) + mod_bias_ref[:, span]
                )
            return carry

        lax.fori_loop(0, loads, cast, 0)

        @pl.when(shard == 1)
        def _():
            mods_across.start()
            for place in range(8):
                mods_ref[:, place, :] = flat_mods_ref[0:images, place * D : (place + 1) * D]

        @pl.when(shard == 0)
        def _():
            mods_across.wait_recv()
            for place in range(8):
                mods_ref[:, place, :] = got_mods_ref[
                    images : 2 * images, place * D : (place + 1) * D
                ]

    stops = [-(-edge // BLOCK) for edge in edges]

    def arrived(part):
        @pl.when(jnp.logical_and(image == 0, shard == 1))
        def _():
            for block in range(stops[part], min(stops[part + 1], first_count)):
                weight_copy(block).wait_recv()

        if stops[part + 1] > first_count:

            @pl.when(jnp.logical_and(image == 0, shard == 0))
            def _():
                for block in range(first_count, all_count):
                    weight_copy(block).wait_recv()

    def modulation(place):
        return mods_ref[image, place : place + 1, :]

    def weight(first, width):
        return weight_ref[:, pl.ds(first, width)]

    patches = patches_ref[...]
    start = multiply(patches, patch_weight_ref[...]) + patch_bias_ref[...] + place_ref[...]
    stream_ref[...] = start
    unit, inverse_start = unit_rows(start)
    unit_start_ref[...] = unit
    attn_in_ref[...] = (unit * (1.0 + modulation(1)) + modulation(0)).astype(half_type)
    arrived(0)
    for part in range(3):
        span = slice(part * D, (part + 1) * D)
        qkv_ref[:, span] = (
            multiply(attn_in_ref[...], weight_ref[:, span]) + qkv_bias_ref[:, span]
        ).astype(half_type)

    scale = 1.0 / math.sqrt(HEAD_DIM)
    first_half = lax.broadcasted_iota(jnp.int32, (1, GROUP), 1) < HEAD_DIM

    def pair_slice(ref, part, pair):
        return ref[:, pl.ds(pl.multiple_of(part * D + pair * GROUP, GROUP), GROUP)]

    def halves(values):
        nothing = jnp.zeros_like(values)
        return jnp.where(first_half, values, nothing), jnp.where(first_half, nothing, values)

    def attend(pair, carry):
        queries = pair_slice(qkv_ref, 0, pair)
        keys = halves(pair_slice(qkv_ref, 1, pair))
        turned = pair_slice(qkv_ref, 2, pair).T
        rows = []
        for half in range(2):
            scores = multiply_trans(keys[half], queries) * scale
            weights = jnp.exp(scores - jnp.max(scores, axis=0, keepdims=True))
            probs = weights * (1.0 / jnp.sum(weights, axis=0, keepdims=True))
            probs_ref[2 * pair + half] = probs
            rows.append(
                multiply(
                    turned[half * HEAD_DIM : (half + 1) * HEAD_DIM], probs.astype(half_type)
                )
            )
        mixed_ref[:, pl.ds(pl.multiple_of(pair * GROUP, GROUP), GROUP)] = (
            jnp.concatenate(rows, axis=0).T.astype(half_type)
        )
        return carry

    lax.fori_loop(0, HEADS // 2, attend, 0, unroll=UNROLL)
    arrived(1)
    attended = multiply(mixed_ref[...], weight_ref[:, edges[1] : edges[2]]) + output_bias_ref[...]
    attended_ref[...] = attended
    middle = stream_ref[...] + modulation(2) * attended
    stream_ref[...] = middle
    unit, inverse_mid = unit_rows(middle)
    unit_mid_ref[...] = unit
    mlp_in_ref[...] = (unit * (1.0 + modulation(4)) + modulation(3)).astype(half_type)
    arrived(2)
    arrived(3)
    total_ref[...] = jnp.zeros_like(total_ref) + down_bias_ref[...]
    for part in range(FF // CHUNK):
        span = slice(part * CHUNK, (part + 1) * CHUNK)
        before = (
            multiply(mlp_in_ref[...], weight(edges[2] + part * CHUNK, CHUNK)) + up_bias_ref[:, span]
        )
        after, slope_part = gelu_both(before)
        slope_ref[:, span] = slope_part
        after = after.astype(half_type)
        hidden_ref[:, span] = after
        total_ref[...] += multiply_trans(after, weight(edges[3] + part * CHUNK, CHUNK))
    mlp_out_ref[...] = total_ref[...]
    unit, inverse_end = unit_rows(stream_ref[...] + modulation(5) * total_ref[...])
    final_in = (unit * (1.0 + modulation(7)) + modulation(6)).astype(half_type)
    error = (
        multiply_trans(final_in, head_weight_ref[...]) + head_bias_ref[...] - targets_ref[...]
    )
    loss_ref[...] += token_sum(error * error)
    grad_out = (error * (2.0 / entries)).astype(half_type)
    bias_head_ref[...] += token_sum(grad_out.astype(jnp.float32))
    grad_head_ref[...] += outer_sum(grad_out, final_in)

    grad_final = multiply(grad_out, head_weight_ref[...])
    mod_grad_ref[image, 6:7] = token_sum(grad_final)
    mod_grad_ref[image, 7:8] = token_sum(grad_final * unit)
    grad_stream = unit_back(unit, inverse_end, grad_final * (1.0 + modulation(7)))
    stream_ref[...] = grad_stream
    mod_grad_ref[image, 5:6] = token_sum(grad_stream * mlp_out_ref[...])
    grad_mlp = (grad_stream * modulation(5)).astype(half_type)
    grad_mlp_ref[...] = grad_mlp
    bias_down_ref[...] += token_sum(grad_mlp.astype(jnp.float32))
    total_ref[...] = jnp.zeros_like(total_ref)
    for part in range(FF // CHUNK):
        span = slice(part * CHUNK, (part + 1) * CHUNK)
        grad_pre = (
            multiply(grad_mlp_ref[...], weight(edges[3] + part * CHUNK, CHUNK)) * slope_ref[:, span]
        ).astype(half_type)
        grad_pre_ref[:, span] = grad_pre
        bias_up_ref[:, span] += token_sum(grad_pre.astype(jnp.float32))
        total_ref[...] += multiply_trans(grad_pre, weight(edges[2] + part * CHUNK, CHUNK))
    grad_in = total_ref[...]
    unit = unit_mid_ref[...]
    mod_grad_ref[image, 3:4] = token_sum(grad_in)
    mod_grad_ref[image, 4:5] = token_sum(grad_in * unit)
    grad_stream = stream_ref[...] + unit_back(unit, inverse_mid, grad_in * (1.0 + modulation(4)))
    stream_ref[...] = grad_stream
    mod_grad_ref[image, 2:3] = token_sum(grad_stream * attended_ref[...])
    grad_attn = (grad_stream * modulation(2)).astype(half_type)
    grad_attn_ref[...] = grad_attn
    bias_output_ref[...] += token_sum(grad_attn.astype(jnp.float32))
    grad_mixed_ref[...] = multiply_trans(grad_attn, weight_ref[:, edges[1] : edges[2]]).astype(
        half_type
    )

    def attend_back(pair, carry):
        queries = pair_slice(qkv_ref, 0, pair)
        keys_turned = pair_slice(qkv_ref, 1, pair).T
        values = halves(pair_slice(qkv_ref, 2, pair))
        grads = pair_slice(grad_mixed_ref, 0, pair)
        rows, key_grads, value_grads = [], [], []
        for half in range(2):
            probs = probs_ref[2 * pair + half]
            grad_probs = multiply_trans(values[half], grads)
            value_grads.append(multiply(probs.astype(half_type), grads))
            product = probs * grad_probs
            grad_scores = (product - probs * token_sum(product)).astype(half_type)
            key_grads.append(multiply(grad_scores, queries))
            rows.append(
                multiply(keys_turned[half * HEAD_DIM : (half + 1) * HEAD_DIM], grad_scores)
            )

        def put(part, values):
            grad_qkv_ref[:, pl.ds(pl.multiple_of(part * D + pair * GROUP, GROUP), GROUP)] = (
                values.astype(half_type)
            )

        put(0, jnp.concatenate(rows, axis=0).T * scale)
        put(1, jnp.where(first_half, key_grads[0], key_grads[1]) * scale)
        put(2, jnp.where(first_half, value_grads[0], value_grads[1]))
        return carry

    lax.fori_loop(0, HEADS // 2, attend_back, 0, unroll=UNROLL)
    bias_qkv_ref[...] += token_sum(grad_qkv_ref[...].astype(jnp.float32))
    grad_in = multiply_trans(grad_qkv_ref[...], weight_ref[:, : edges[1]])
    unit = unit_start_ref[...]
    mod_grad_ref[image, 0:1] = token_sum(grad_in)
    mod_grad_ref[image, 1:2] = token_sum(grad_in * unit)
    grad_start = (
        stream_ref[...] + unit_back(unit, inverse_start, grad_in * (1.0 + modulation(1)))
    ).astype(half_type)
    bias_patch_ref[...] += token_sum(grad_start.astype(jnp.float32))
    grad_patch_ref[...] += outer_sum(patches, grad_start)

    @pl.when(image == last)
    def _():
        grads_across.start()

        def sent(block, carry):
            weight_copy(shard * first_count + block).wait_send()
            return carry

        lax.fori_loop(0, count, sent, 0)
        @pl.when(shard == 1)
        def _():
            mods_across.wait_send()

        both_grads_ref[0:images] = mod_grad_ref[...]
        grads_across.wait()
        both_grads_ref[images : 2 * images] = got_grads_ref[...]
        grad_active_ref[...] = jnp.zeros_like(grad_active_ref)

        @pl.when(shard == 1)
        def _():
            for place in range(8):
                part = jnp.concatenate(
                    [mod_grad_ref[:, place, :], got_grads_ref[:, place, :]], axis=0
                ).astype(half_type)
                grad_active_ref[...] += multiply_trans(
                    part, mod_weight_ref[:, place * D : (place + 1) * D]
                )


def run_images(
    patches, targets, active, mod_bias, places, patch_weight, head_weight, biases, master, entries
):
    images = active.shape[0] // 2
    tokens = images * SEQ
    wide = 4 * D + 2 * FF

    def rows(width):
        return pl.BlockSpec((SEQ, width), lambda image: (image, 0))

    def fixed(array):
        return pl.BlockSpec(array.shape, lambda image: (0,) * len(array.shape))

    vector = [(P_DIM, D), (P_DIM, D), (1, 3 * D), (1, D), (1, FF), (1, D), (1, D), (1, P_DIM)]
    vector = [sds(shape) for shape in vector + [(1, P_DIM)]]
    saved = [D, D, D, FF, 3 * D, D, FF, D]
    return pl.pallas_call(
        functools.partial(image_kernel, entries),
        grid=(images,),
        out_shape=[sds((tokens, width), half_type) for width in saved]
        + [sds((2 * images, 8, D)), sds((2 * images, D))]
        + vector,
        in_specs=[rows(P_DIM), rows(P_DIM), fixed(active), fixed(mod_bias), fixed(places)]
        + [fixed(patch_weight), fixed(head_weight)]
        + [fixed(bias) for bias in biases]
        + [pl.BlockSpec(memory_space=pltpu.HBM)],
        out_specs=[rows(width) for width in saved] + [fixed(sds((2 * images, 8, D))), fixed(sds((2 * images, D)))] + [fixed(item) for item in vector],
        scratch_shapes=[
            pltpu.VMEM((D, wide), half_type),
            pltpu.VMEM((SEQ, 3 * D), half_type),
            pltpu.VMEM((HEADS, SEQ, SEQ), jnp.float32),
            pltpu.VMEM((SEQ, FF), jnp.float32),
            pltpu.VMEM((SEQ, D), jnp.float32),
            pltpu.VMEM((SEQ, D), jnp.float32),
            pltpu.VMEM((SEQ, D), jnp.float32),
            pltpu.VMEM((SEQ, D), jnp.float32),
            pltpu.VMEM((SEQ, D), jnp.float32),
            pltpu.VMEM((SEQ, D), half_type),
            pltpu.VMEM((SEQ, D), jnp.float32),
            pltpu.VMEM((3, D, BLOCK), jnp.float32),
            pltpu.VMEM((D, 8 * D), half_type),
            pltpu.VMEM((2 * images, 8 * D), jnp.float32),
            pltpu.VMEM((images, 8, D), jnp.float32),
            pltpu.VMEM((2 * images, 8 * D), jnp.float32),
            pltpu.VMEM((images, 8, D), jnp.float32),
            pltpu.VMEM((images, 8, D), jnp.float32),
            pltpu.SemaphoreType.DMA((3,)),
            pltpu.SemaphoreType.DMA((wide // BLOCK,)),
            pltpu.SemaphoreType.DMA((wide // BLOCK,)),
            pltpu.SemaphoreType.DMA((2,)),
            pltpu.SemaphoreType.DMA((2,)),
        ],
        compiler_params=pltpu.CompilerParams(
            collective_id=1, has_side_effects=True, vmem_limit_bytes=64_000_000
        ),
        name="images",
    )(patches, targets, active, mod_bias, places, patch_weight, head_weight, *biases, master)


def train_gradients(master, master_small, biases, noisy_patches, targets, timesteps, labels, entries):
    owner = lax.axis_index("shard") == 1
    last = master.shape[1]
    embed_second, embed_first = split_at(
        master, [last - D - FREQ, last - FREQ, last]
    )
    patch_weight, class_table, head_weight = split_small(master_small)
    (
        query_bias,
        value_bias,
        output_bias,
        up_bias,
        down_bias,
        modulate_bias,
        final_bias,
        second_bias,
        first_bias,
        patch_bias,
        head_bias,
    ) = split_bias(biases)
    images = noisy_patches.shape[0]
    frequency = timestep_features(timesteps).astype(half_type)
    embed_pre = multiply_trans(frequency.astype(jnp.float32), embed_first) + first_bias
    embed_hidden = jax.nn.silu(embed_pre).astype(half_type)
    time_embed = multiply(embed_hidden.astype(jnp.float32), embed_second) + second_bias
    chosen = (labels[:, None] == jnp.arange(NCLASS, dtype=jnp.int32)[None, :]).astype(jnp.float32)
    condition = time_embed + lax.dot_general(
        chosen,
        class_table,
        (((1,), (1,)), ((), ())),
        precision=highest,
        preferred_element_type=jnp.float32,
    )
    active = jax.nn.silu(condition).astype(half_type)
    mod_bias = jnp.concatenate([modulate_bias, final_bias]).reshape(1, 8 * D)
    qkv_bias = jnp.concatenate([query_bias, jnp.zeros_like(query_bias), value_bias])
    (
        attn_in,
        mixed,
        mlp_in,
        hidden,
        grad_qkv,
        grad_attn,
        grad_pre,
        grad_mlp,
        mod_grads,
        grad_active,
        grad_patch,
        grad_head,
        bias_qkv,
        bias_output,
        bias_up,
        bias_down,
        bias_patch,
        bias_head,
        losses,
    ) = run_images(
        noisy_patches.reshape(-1, P_DIM),
        targets.reshape(-1, P_DIM),
        active,
        mod_bias,
        jnp.asarray(position_constant()),
        patch_weight.T.astype(half_type),
        head_weight.T.astype(half_type),
        [item[None] for item in (qkv_bias, output_bias, up_bias, down_bias, patch_bias, head_bias)],
        master,
        entries,
    )
    grad_mods = mod_grads.reshape(-1, 8 * D).astype(half_type)
    bias_mods = column_sums(grad_mods)
    grad_condition = slope(jax.nn.silu, condition, grad_active)
    grad_embed = grad_condition.astype(half_type)
    grad_embed_hidden = multiply_trans(grad_embed.astype(jnp.float32), embed_second)
    grad_embed_pre = slope(jax.nn.silu, embed_pre, grad_embed_hidden).astype(half_type)
    tail_left = jnp.pad(
        jnp.concatenate([active, embed_hidden, grad_embed_pre]), ((0, 8), (0, 0))
    ).T
    tail_right = jnp.concatenate(
        [
            jnp.pad(grad_mods, ((0, 0), (0, D + FREQ))),
            jnp.pad(grad_embed, ((0, 0), (8 * D, FREQ))),
            jnp.pad(frequency, ((0, 16 - frequency.shape[0]), (9 * D, 0))),
        ]
    )
    sides = (attn_in, mixed, mlp_in, grad_mlp, grad_qkv, grad_attn, grad_pre, hidden)
    grad_bias = jnp.concatenate(
        [
            bias_qkv[0, :D],
            bias_qkv[0, 2 * D :],
            bias_output[0],
            bias_up[0],
            bias_down[0],
            jnp.where(
                owner,
                jnp.concatenate([bias_mods, column_sums(grad_embed), column_sums(grad_embed_pre)]),
                0.0,
            ),
            bias_patch[0],
            bias_head[0],
        ]
    )
    loss_part = jnp.sum(losses) / entries
    return sides, tail_left, tail_right, grad_patch, grad_head, grad_condition, grad_bias, loss_part


def on_pair(
    noisy_patches,
    targets,
    timesteps,
    labels,
    master_big,
    moment_big,
    error_big,
    factor_right,
    master_small,
    moment_small,
    biases,
    moment_bias,
    step_rates,
):
    shards = lax.axis_size("shard")
    replicas = lax.axis_size("rep")
    entries = noisy_patches.shape[0] * shards * replicas * SEQ * P_DIM
    own = jnp.stack([timesteps, labels])
    timesteps, labels = jnp.concatenate(
        [own, lax.ppermute(own, "shard", [(0, 1), (1, 0)])], axis=1
    )
    sides, tail_left, tail_right, grad_patch, grad_head, grad_condition, grad_bias, loss_part = (
        train_gradients(
            master_big, master_small, biases, noisy_patches, targets, timesteps, labels, entries
        )
    )
    images = labels.shape[0]
    strips = D // LANES

    def lines_of(matrix):
        return matrix.reshape(-1, strips, LANES).transpose(1, 0, 2)

    flat = jnp.concatenate(
        [
            lines_of(grad_patch).reshape(-1),
            lines_of(grad_head).reshape(-1),
            grad_bias,
            loss_part[None],
        ]
    )
    width = shards * replicas * 16 * LANES
    sums = jnp.pad(flat, (0, width - flat.shape[0])).reshape(shards, replicas, 16, LANES)
    label_lines = jnp.broadcast_to(labels.astype(jnp.float32)[None, :, None], (1, images, LANES))
    lines = jnp.concatenate(
        [
            lines_of(grad_condition),
            label_lines,
        ]
    ).reshape(-1, LANES)
    (new_master, new_moment, new_error, right_rows), total, gathered_lines = compress(
        step_rates,
        sides,
        tail_left,
        tail_right,
        error_big,
        factor_right.T,
        moment_big,
        master_big,
        sums,
        lines,
    )
    new_moment_small, new_master_small = update_small(
        step_rates, total, gathered_lines, moment_small.T, master_small.T
    )
    total = total.reshape(-1)
    bias_count = biases.shape[0]
    base = 2 * P_DIM * D
    total_loss = total[base + bias_count]
    new_moment_bias = momentum_decay * moment_bias + total[base : base + bias_count]
    new_biases = biases - step_rates[1] * new_moment_bias
    return (
        total_loss,
        new_master,
        new_moment,
        new_error,
        right_rows.T,
        new_master_small.T,
        new_moment_small.T,
        new_biases,
        new_moment_bias,
    )


def solution(mesh):
    in_specs = (
        P(("shard", "rep"), None),
        P(("shard", "rep"), None),
        P(("shard", "rep")),
        P(("shard", "rep")),
        P(None, "shard"),
        P(None, "shard"),
        P("rep", None, "shard"),
        P("shard", None),
        P(),
        P(),
        P(),
        P(),
        P(),
    )
    out_specs = (
        P(),
        P(None, "shard"),
        P(None, "shard"),
        P("rep", None, "shard"),
        P("shard", None),
        P(),
        P(),
        P(),
        P(),
    )
    fits = mesh.shape["shard"] == 2 and mesh.shape["rep"] == 16
    return jax.shard_map(
        on_pair if fits else on_device, mesh=mesh, in_specs=in_specs, out_specs=out_specs, check_vma=False
    )
```
